32 devices in a mesh: rep: 4 (over y, x), fsdp: 8 (over z, core).
Axes of the slice: x: 2, y: 2, z: 4, core: 2. Of those that a mesh axis runs over, the one named last changes fastest.
Arguments:
- tokens: bfloat16 [64, 512, 768], P(('rep', 'fsdp')), may hold values from -6 to 6
- memory: bfloat16 [64, 1024, 768], P(('rep', 'fsdp')), may hold values from -6 to 6
- prefix_len: int32 [64], P(('rep', 'fsdp')), may hold values from 51 to 256
- bucket_table: int32 [1023], replicated, may hold values from 0 to 31
- rel_bias: bfloat16 [384], P('fsdp'), may hold values from -4 to 4
- gain_self: bfloat16 [768], P('fsdp'), may hold values from 0.5 to 1.5
- self_query: bfloat16 [768, 768], P('fsdp'), may hold values from -0.099609375 to 0.099609375
- self_key: bfloat16 [768, 768], P('fsdp'), may hold values from -0.099609375 to 0.099609375
- self_value: bfloat16 [768, 768], P('fsdp'), may hold values from -0.21875 to 0.21875
- self_out: bfloat16 [768, 768], P('fsdp'), may hold values from -0.875 to 0.875
- gain_cross: bfloat16 [768], P('fsdp'), may hold values from 0.5 to 1.5
- cross_query: bfloat16 [768, 768], P('fsdp'), may hold values from -0.099609375 to 0.099609375
- cross_key: bfloat16 [768, 768], P('fsdp'), may hold values from -0.099609375 to 0.099609375
- cross_value: bfloat16 [768, 768], P('fsdp'), may hold values from -0.21875 to 0.21875
- cross_out: bfloat16 [768, 768], P('fsdp'), may hold values from -1.25 to 1.25
- gain_feed: bfloat16 [768], P('fsdp'), may hold values from 0.5 to 1.5
- gate_weight: bfloat16 [768, 2048], P('fsdp'), may hold values from -0.21875 to 0.21875
- up_weight: bfloat16 [768, 2048], P('fsdp'), may hold values from -0.21875 to 0.21875
- down_weight: bfloat16 [2048, 768], P('fsdp'), may hold values from -0.25 to 0.25
- out_grad: bfloat16 [64, 512, 768], P(('rep', 'fsdp')), may hold values from -6 to 6
Outputs:
- layer_out: bfloat16 [64, 512, 768], P(('rep', 'fsdp'))
- tokens_grad: float32 [64, 512, 768], P(('rep', 'fsdp'))
- memory_grad: float32 [64, 1024, 768], P(('rep', 'fsdp'))
- rel_bias_grad: float32 [384], P('fsdp')
- gain_self_grad: float32 [768], P('fsdp')
- self_query_grad: float32 [768, 768], P('fsdp', 'rep')
- self_key_grad: float32 [768, 768], P('fsdp', 'rep')
- self_value_grad: float32 [768, 768], P('fsdp', 'rep')
- self_out_grad: float32 [768, 768], P('fsdp', 'rep')
- gain_cross_grad: float32 [768], P('fsdp')
- cross_query_grad: float32 [768, 768], P('fsdp', 'rep')
- cross_key_grad: float32 [768, 768], P('fsdp', 'rep')
- cross_value_grad: float32 [768, 768], P('fsdp', 'rep')
- cross_out_grad: float32 [768, 768], P('fsdp', 'rep')
- gain_feed_grad: float32 [768], P('fsdp')
- gate_weight_grad: float32 [768, 2048], P('fsdp', 'rep')
- up_weight_grad: float32 [768, 2048], P('fsdp', 'rep')
- down_weight_grad: float32 [2048, 768], P('fsdp', 'rep')
The draws below stay inside these ranges and needn't reach their ends.
All inputs are finite; a program needn't handle non-finite values.
Results may differ from the reference program's by a relative error of at most 0.03.
Values may be sent and summed in bfloat16 or wider, within the bound.
A program may use at most 384 MiB of HBM per device.

```python
import math
import jax
import jax.numpy as jnp
from jax import lax

WIDTH = 768
FFN = 2048
NHEAD = 12
DHEAD = 64
BUCKETS = 32
LENGTH = 512
MEMROWS = 1024
NSEQ = 64


def set_ends(entries, rng, least, top_value):
    index_at = [jax.random.randint(jax.random.fold_in(rng, axis), (), 0, length) for axis, length in enumerate(entries.shape)]
    longest = entries.shape.index(max(entries.shape))
    beside = index_at[:longest] + [(index_at[longest] + 1) % entries.shape[longest]] + index_at[longest + 1:]
    return entries.at[tuple(index_at)].set(least).at[tuple(beside)].set(top_value)


def shard_levels(key, shape, shards, low, top_value):
    gain, own = 1.0, jax.random.fold_in(key, 6)
    for dim, shards_of in shards:
        draws = jnp.exp(jax.random.uniform(jax.random.fold_in(own, dim), (shards_of,), jnp.float32, low / len(shards), top_value / len(shards)))
        gain = gain * jnp.repeat(draws, shape[dim] // shards_of).reshape([-1 if axis == dim else 1 for axis in range(len(shape))])
    return gain


def gaussian(key, dims, spread, limit, cuts=(), kind=jnp.bfloat16):
    array = jax.random.normal(key, dims, jnp.float32) * spread
    if len(cuts) > 0:
        array = shard_levels(key, dims, cuts, -0.22, 0.18) * array
    return jnp.clip(array, min=-limit, max=limit).astype(kind)


def setup_inputs(seed: int = 0) -> dict:
    seeds = jax.random.split(jax.random.key(seed), 21)
    tokens = gaussian(seeds[0], (NSEQ, LENGTH, WIDTH), 1.0, 6.0, ((0, 32),))
    memory = gaussian(seeds[1], (NSEQ, MEMROWS, WIDTH), 1.0, 6.0, ((0, 32),))
    prefix_len = set_ends(jax.random.randint(seeds[2], (NSEQ,), LENGTH // 10, LENGTH // 2 + 1), jax.random.fold_in(seeds[2], 1), LENGTH // 10, (LENGTH // 2 + 1) - 1).astype(jnp.int32)
    bucket_table = set_ends(jax.random.randint(seeds[3], (2 * LENGTH - 1,), 0, BUCKETS), jax.random.fold_in(seeds[3], 1), 0, BUCKETS - 1).astype(jnp.int32)
    rel_bias = gaussian(seeds[4], (NHEAD * BUCKETS,), 1.0, 4.0, ((0, 8),))
    gain_self = jnp.clip(1.0 + 0.1 * jax.random.normal(seeds[5], (WIDTH,), jnp.float32), 0.5, 1.5).astype(jnp.bfloat16)
    self_query = gaussian(seeds[6], (WIDTH, WIDTH), 0.018, 0.099609375, ((0, 8),))
    self_key = gaussian(seeds[7], (WIDTH, WIDTH), 0.018, 0.099609375, ((0, 8),))
    self_value = gaussian(seeds[8], (WIDTH, WIDTH), WIDTH ** -0.5, 0.21875, ((0, 8),))
    self_out = gaussian(seeds[9], (WIDTH, WIDTH), (WIDTH // 16) ** -0.5, 0.875, ((0, 8),))
    gain_cross = jnp.clip(1.0 + 0.1 * jax.random.normal(seeds[10], (WIDTH,), jnp.float32), 0.5, 1.5).astype(jnp.bfloat16)
    cross_query = gaussian(seeds[11], (WIDTH, WIDTH), 0.018, 0.099609375, ((0, 8),))
    cross_key = gaussian(seeds[12], (WIDTH, WIDTH), 0.018, 0.099609375, ((0, 8),))
    cross_value = gaussian(seeds[13], (WIDTH, WIDTH), WIDTH ** -0.5, 0.21875, ((0, 8),))
    cross_out = gaussian(seeds[14], (WIDTH, WIDTH), (WIDTH // 32) ** -0.5, 1.25, ((0, 8),))
    gain_feed = jnp.clip(1.0 + 0.1 * jax.random.normal(seeds[15], (WIDTH,), jnp.float32), 0.5, 1.5).astype(jnp.bfloat16)
    gate_weight = gaussian(seeds[16], (WIDTH, FFN), WIDTH ** -0.5, 0.21875, ((0, 8),))
    up_weight = gaussian(seeds[17], (WIDTH, FFN), WIDTH ** -0.5, 0.21875, ((0, 8),))
    down_weight = gaussian(seeds[18], (FFN, WIDTH), (FFN // 4) ** -0.5, 0.25, ((0, 8),))
    out_grad = gaussian(seeds[19], (NSEQ, LENGTH, WIDTH), 1.0, 6.0, ((0, 32),))
    return {"tokens": tokens, "memory": memory, "prefix_len": prefix_len, "bucket_table": bucket_table, "rel_bias": rel_bias, "gain_self": gain_self, "self_query": self_query, "self_key": self_key, "self_value": self_value, "self_out": self_out, "gain_cross": gain_cross, "cross_query": cross_query, "cross_key": cross_key, "cross_value": cross_value, "cross_out": cross_out, "gain_feed": gain_feed, "gate_weight": gate_weight, "up_weight": up_weight, "down_weight": down_weight, "out_grad": out_grad}


EPSILON = 1e-06
CUBIC_TERM = 0.044715
SQRT_TWO_PI = 0.7978845608028654
NEGATIVE = -1000000000.0
PRECISE = lax.Precision.HIGHEST

@jax.custom_vjp
def low(v):
    return lax.optimization_barrier(v.astype(jnp.bfloat16)).astype(jnp.float32)

@jax.custom_vjp
def low_back(v):
    return v

def low_keep(v):
    return (low(v), None)

def low_pass(kept, grad):
    return (grad,)

def back_keep(v):
    return (v, None)

def back_low(kept, grad):
    return (low(grad),)
low.defvjp(low_keep, low_pass)
low_back.defvjp(back_keep, back_low)

def matmul(left_side, right_side):
    return jnp.dot(left_side, right_side, precision=PRECISE)

def rms_norm(values, gain_vec):
    return values * lax.rsqrt(lax.optimization_barrier(jnp.mean(values * values, axis=-1, keepdims=True)) + EPSILON) * gain_vec

def gelu_tanh(values):
    return 0.5 * values * (1.0 + jnp.tanh(SQRT_TWO_PI * (values + CUBIC_TERM * values * values * values)))

def split_heads(values):
    return values.reshape(values.shape[0], NHEAD, DHEAD)

def attention(queries, key_rows, value_rows, bias_terms, allowed):
    scores = jnp.einsum('qhd,khd->hqk', split_heads(queries), split_heads(key_rows), precision=PRECISE)
    if bias_terms is not None:
        scores = jnp.where(allowed[None], low_back(scores + bias_terms), NEGATIVE)
    else:
        scores = low_back(scores)
    row_top = lax.optimization_barrier(jnp.max(scores, axis=-1, keepdims=True))
    log_total = row_top + jnp.log(lax.optimization_barrier(jnp.sum(jnp.exp(scores - row_top), axis=-1, keepdims=True)))
    shares = low(jnp.exp(scores - log_total))
    context = jnp.einsum('hqk,khd->qhd', shares, split_heads(value_rows), precision=PRECISE)
    return low(low_back(context.reshape(queries.shape[0], -1)))

def decoder_layer(params, start_rows, memory_rows, bias_terms, allowed):
    bias_table, gain_first, query_self, key_self, value_self, out_self, gain_second, query_cross, key_cross, value_cross, out_cross, gain_third, gate_proj, up_proj, down_proj = params
    normed_first = low(rms_norm(start_rows, gain_first))
    queries = low(low_back(matmul(normed_first, query_self)))
    key_rows = low(low_back(matmul(normed_first, key_self)))
    value_rows = low(low_back(matmul(normed_first, value_self)))
    context = attention(queries, key_rows, value_rows, bias_terms, allowed)
    middle = start_rows + low_back(matmul(context, out_self))
    normed_second = low(rms_norm(middle, gain_second))
    query_two = low(low_back(matmul(normed_second, query_cross)))
    keys_two = low(low_back(matmul(memory_rows, key_cross)))
    values_two = low(low_back(matmul(memory_rows, value_cross)))
    context_two = attention(query_two, keys_two, values_two, None, None)
    later = middle + low_back(matmul(context_two, out_cross))
    normed_third = low(rms_norm(later, gain_third))
    gate_pre = low_back(matmul(normed_third, gate_proj))
    up_pre = low_back(matmul(normed_third, up_proj))
    hidden = low(gelu_tanh(gate_pre) * up_pre)
    return later + low_back(matmul(hidden, down_proj))

def reference(tokens, memory, prefix_len, bucket_table, rel_bias, gain_self, self_query, self_key, self_value, self_out, gain_cross, cross_query, cross_key, cross_value, cross_out, gain_feed, gate_weight, up_weight, down_weight, out_grad):
    params = tuple((item.astype(jnp.float32) for item in (rel_bias, gain_self, self_query, self_key, self_value, self_out, gain_cross, cross_query, cross_key, cross_value, cross_out, gain_feed, gate_weight, up_weight, down_weight)))
    row_count, length, width = tokens.shape
    mem_length = memory.shape[1]
    group_size = math.gcd(row_count, max(1, 2048 // length))
    step_count = row_count // group_size
    position = jnp.arange(length, dtype=jnp.int32)
    causal = position[None, :] <= position[:, None]
    buckets = bucket_table[(position[None, :] - position[:, None] + length - 1).astype(jnp.int32)]
    flat_tokens = tokens.astype(jnp.float32).reshape(step_count, group_size, length, width)
    flat_memory = memory.astype(jnp.float32).reshape(step_count, group_size, mem_length, width)
    flat_prefix = prefix_len.reshape(step_count, group_size).astype(jnp.int32)
    flat_grad = out_grad.astype(jnp.float32).reshape(step_count, group_size, length, width)

    def one_step(running, inputs):
        start_rows, memory_rows, prefix_rows, grad_rows = inputs

        def whole_batch(layer_params, start_all, memory_all):
            bias_terms = layer_params[0].reshape(NHEAD, BUCKETS)[:, buckets]

            def single(one_start, one_memory, one_prefix):
                allowed = causal | (position[None, :] < one_prefix)
                return decoder_layer(layer_params, one_start, one_memory, bias_terms, allowed)
            return jax.vmap(single)(start_all, memory_all, prefix_rows)
        result, pull_back = jax.vjp(whole_batch, params, start_rows, memory_rows)
        param_grads, start_grad, memory_grad = pull_back(grad_rows)
        running = jax.tree.map(jnp.add, running, param_grads)
        return (running, (result.astype(jnp.bfloat16), start_grad, memory_grad))
    initial = tuple((jnp.zeros_like(item) for item in params))
    totals, (layer_rows, start_grads, memory_grads) = lax.scan(one_step, initial, (flat_tokens, flat_memory, flat_prefix, flat_grad))
    layer_out = layer_rows.reshape(tokens.shape)
    tokens_grad = start_grads.reshape(tokens.shape)
    memory_grad = memory_grads.reshape(memory.shape)
    return (layer_out, tokens_grad, memory_grad, totals[0], totals[1], totals[2], totals[3], totals[4], totals[5], totals[6], totals[7], totals[8], totals[9], totals[10], totals[11], totals[12], totals[13], totals[14])
```

```python
import functools

import jax
import jax.numpy as jnp
from jax import lax
from jax.experimental import pallas as pl
from jax.experimental.pallas import tpu as pltpu
from jax.sharding import PartitionSpec as P

NHEAD = 12
DHEAD = 64
BUCKETS = 32
PAIRS = NHEAD // 2
LANES = 2 * DHEAD
PREFIX_MAX = 256

EPSILON = 1e-06
CUBIC_TERM = 0.044715
SQRT_TWO_PI = 0.7978845608028654
NEGATIVE = -1000000000.0

F32 = jnp.float32
BF16 = jnp.bfloat16
LAST_DIMS = (((1,), (1,)), ((), ()))
FIRST_DIMS = (((0,), (0,)), ((), ()))


def matmul(left_side, right_side):
    return jnp.dot(left_side, right_side, preferred_element_type=F32)


def weight_term(inputs, gradient):
    return lax.dot_general(inputs, gradient, FIRST_DIMS, preferred_element_type=F32)


def back_term(gradient, weight):
    return lax.dot_general(gradient, weight, LAST_DIMS, preferred_element_type=F32)


def inverse_rms(values):
    return lax.rsqrt(jnp.mean(values * values, axis=-1, keepdims=True) + EPSILON)


def gelu_tanh(values):
    return (
        0.5
        * values
        * (1.0 + jnp.tanh(SQRT_TWO_PI * (values + CUBIC_TERM * values * values * values)))
    )


def gelu_slope(values):
    tangent = jnp.tanh(SQRT_TWO_PI * (values + CUBIC_TERM * values * values * values))
    return 0.5 * (1.0 + tangent) + 0.5 * values * (1.0 - tangent * tangent) * SQRT_TWO_PI * (
        1.0 + 3.0 * CUBIC_TERM * values * values
    )


def norm_back(values, scale_rows, gain_vec, upstream):
    weighted = upstream * gain_vec
    gain_grad = jnp.sum(upstream * values * scale_rows, axis=0)
    input_grad = scale_rows * weighted - values * scale_rows * scale_rows * scale_rows * jnp.mean(
        values * weighted, axis=-1, keepdims=True
    )
    return (input_grad, gain_grad)


def one_head(rows, head):
    lane = lax.broadcasted_iota(jnp.int32, rows.shape, 1)
    keep = lane < DHEAD if head == 0 else lane >= DHEAD
    return jnp.where(keep, rows, jnp.zeros_like(rows))


def flipped(rows):
    return rows.astype(F32).T.astype(BF16)


def tree(fold, rows, groups):
    step = rows.shape[0] // groups
    total = rows[:step]
    for index in range(1, groups):
        total = fold(total, rows[index * step : (index + 1) * step])
    return total


def column_max(rows, groups):
    return jnp.max(tree(jnp.maximum, rows, groups), axis=0, keepdims=True)


def column_sum(rows, groups):
    return jnp.sum(tree(jnp.add, rows, groups), axis=0, keepdims=True)


def allowed_at(shape, key_start, query_start, prefix):
    key = lax.broadcasted_iota(jnp.int32, shape, 0) + key_start
    query = lax.broadcasted_iota(jnp.int32, shape, 1) + query_start
    return (key <= query) | (key < prefix)


def skew_kernel(table_ref, buckets_ref, out_ref):
    bucket = lax.broadcasted_iota(jnp.int32, (BUCKETS, buckets_ref.shape[1]), 0)
    onehot = (bucket == buckets_ref[...]).astype(BF16)
    by_offset = matmul(table_ref[...], onehot)
    width = out_ref.shape[2]
    total = by_offset.shape[1]
    for head in range(NHEAD):
        rows = jnp.broadcast_to(by_offset[head : head + 1], (LANES, total))
        rolled = pltpu.roll(rows, total - (LANES - 1), 1, stride=1, stride_axis=0)
        out_ref[head] = rolled[:, :width]


def skewed_bias(table, buckets_back, length):
    total = 2 * length
    return pl.pallas_call(
        skew_kernel,
        out_shape=jax.ShapeDtypeStruct((NHEAD, LANES, total - LANES), F32),
        name="skewed_bias",
    )(jnp.pad(table, ((0, 4), (0, 0))), buckets_back)


def self_forward(prefix_ref, qkv_ref, bias_ref, out_ref, lse_ref):
    length = qkv_ref.shape[0]
    block = 256
    prefix = prefix_ref[pl.program_id(0)]
    queries = qkv_ref[:, :LANES]
    keys = qkv_ref[:, LANES : 2 * LANES]
    values = flipped(qkv_ref[:, 2 * LANES :])
    for start in range(0, length, block):
        stop = start + block
        count = max(PREFIX_MAX, stop)
        outs = []
        for head in range(2):
            scores = back_term(keys[:count], one_head(queries[start:stop], head))
            parts = []
            for base in range(0, count, LANES):
                shift = length - LANES - base + start
                part = scores[base : base + LANES] + bias_ref[head, :, shift : shift + block]
                if base + LANES - 1 > start:
                    part = jnp.where(
                        allowed_at(part.shape, base, start, prefix), part, NEGATIVE
                    )
                parts.append(part)
            top = parts[0]
            for part in parts[1:]:
                top = jnp.maximum(top, part)
            top = column_max(top, 4)
            shares = [jnp.exp(part - top) for part in parts]
            total = shares[0]
            for share in shares[1:]:
                total = total + share
            total = column_sum(total, 4)
            share = jnp.concatenate([item.astype(BF16) for item in shares], axis=0)
            context = matmul(values[head * DHEAD : (head + 1) * DHEAD, :count], share)
            outs.append(context * (1.0 / total))
            lse_ref[head : head + 1, start:stop] = top + jnp.log(total)
        out_ref[start:stop, :] = jnp.concatenate(outs, axis=0).T.astype(BF16)


def cross_forward(query_ref, kv_ref, out_ref, lse_ref):
    length = query_ref.shape[0]
    keys = kv_ref[:, :LANES]
    values = flipped(kv_ref[:, LANES:])
    queries = query_ref[...]
    ahead = [back_term(keys, one_head(queries, head)) for head in range(2)]
    outs = []
    for head in range(2):
        scores = ahead[head]
        top = column_max(scores, 16)
        share = jnp.exp(scores - top)
        total = column_sum(share, 16)
        context = matmul(values[head * DHEAD : (head + 1) * DHEAD], share.astype(BF16))
        outs.append(context * (1.0 / total))
        lse_ref[head : head + 1, :] = top + jnp.log(total)
    out_ref[...] = jnp.concatenate(outs, axis=0).T.astype(BF16)


def cross_backward(query_ref, kv_ref, up_ref, context_ref, lse_ref, dq_ref, dkv_ref):
    length = query_ref.shape[0]
    block = 256
    keys = kv_ref[:, :LANES]
    values = kv_ref[:, LANES:]
    queries = query_ref[...]
    upstream = up_ref[...]
    keys_flipped = flipped(keys)
    inner = (upstream.astype(F32) * context_ref[...].astype(F32)).T
    key_grad = None
    value_grad = None
    for start in range(0, length, block):
        rows = slice(start, start + block)
        grads = []
        for head in range(2):
            sub = slice(head * DHEAD, (head + 1) * DHEAD)
            query = one_head(queries[rows], head)
            above = one_head(upstream[rows], head)
            row_inner = jnp.sum(inner[sub, rows], axis=0, keepdims=True)
            shares = jnp.exp(back_term(keys, query) - lse_ref[head : head + 1, rows])
            share_grad = back_term(values, above)
            score_grad = (shares * (share_grad - row_inner)).astype(BF16)
            value_part = matmul(shares.astype(BF16), above)
            key_part = matmul(score_grad, query)
            value_grad = value_part if value_grad is None else value_grad + value_part
            key_grad = key_part if key_grad is None else key_grad + key_part
            grads.append(matmul(keys_flipped[sub], score_grad))
        dq_ref[rows, :] = jnp.concatenate(grads, axis=0).T.astype(BF16)
    dkv_ref[:, :LANES] = key_grad.astype(BF16)
    dkv_ref[:, LANES:] = value_grad.astype(BF16)


def self_backward(
    prefix_ref, qkv_ref, up_ref, context_ref, lse_ref, bias_ref, grad_ref, diag_ref, acc_ref
):
    length = qkv_ref.shape[0]
    block = 256
    step = pl.program_id(1)
    prefix = prefix_ref[step]

    @pl.when(step == 0)
    def _():
        acc_ref[...] = jnp.zeros_like(acc_ref)

    queries = qkv_ref[:, :LANES]
    keys = qkv_ref[:, LANES : 2 * LANES]
    values = qkv_ref[:, 2 * LANES :]
    upstream = up_ref[...]
    keys_flipped = flipped(keys)
    inner = (upstream.astype(F32) * context_ref[...].astype(F32)).T
    count_all = length // block
    key_grad = [None] * count_all
    value_grad = [None] * count_all
    for start in range(0, length, block):
        stop = start + block
        count = max(PREFIX_MAX, stop)
        rows = slice(start, stop)
        grads = []
        for head in range(2):
            sub = slice(head * DHEAD, (head + 1) * DHEAD)
            query = one_head(queries[rows], head)
            above = one_head(upstream[rows], head)
            row_inner = jnp.sum(inner[sub, rows], axis=0, keepdims=True)
            row_lse = lse_ref[head : head + 1, rows]
            scores = back_term(keys[:count], query)
            share_grad = back_term(values[:count], above)
            shares = []
            score_grads = []
            for base in range(0, count, LANES):
                part = slice(base, base + LANES)
                shift = length - LANES - base + start
                share = jnp.exp(
                    scores[part] + bias_ref[head, :, shift : shift + block] - row_lse
                )
                if base + LANES - 1 > start:
                    share = jnp.where(allowed_at(share.shape, base, start, prefix), share, 0.0)
                score_grad = share * (share_grad[part] - row_inner)
                acc_ref[head, :, shift : shift + block] += score_grad
                shares.append(share.astype(BF16))
                score_grads.append(score_grad.astype(BF16))
            share = jnp.concatenate(shares, axis=0)
            score_grad = jnp.concatenate(score_grads, axis=0)
            value_part = matmul(share, above)
            key_part = matmul(score_grad, query)
            for index in range(count // block):
                part = slice(index * block, (index + 1) * block)
                if value_grad[index] is None:
                    value_grad[index] = value_part[part]
                    key_grad[index] = key_part[part]
                else:
                    value_grad[index] = value_grad[index] + value_part[part]
                    key_grad[index] = key_grad[index] + key_part[part]
            grads.append(matmul(keys_flipped[sub, :count], score_grad))
        grad_ref[rows, :LANES] = jnp.concatenate(grads, axis=0).T.astype(BF16)
    for index in range(count_all):
        part = slice(index * block, (index + 1) * block)
        grad_ref[part, LANES : 2 * LANES] = key_grad[index].astype(BF16)
        grad_ref[part, 2 * LANES :] = value_grad[index].astype(BF16)

    @pl.when(step == pl.num_programs(1) - 1)
    def _():
        row = lax.broadcasted_iota(jnp.int32, (LANES, 2 * length), 0)
        amount = LANES - 1 - row
        for head in range(2):
            skewed = jnp.concatenate(
                [acc_ref[head], jnp.zeros((LANES, LANES), F32)], axis=1
            )
            bit = 1
            while bit < LANES:
                skewed = jnp.where((amount & bit) != 0, pltpu.roll(skewed, bit, 1), skewed)
                bit *= 2
            diag_ref[head : head + 1, :] = jnp.sum(skewed, axis=0, keepdims=True)


def spec(shape, index):
    return pl.BlockSpec(shape, index)


def run_self_forward(prefix, qkv, bias, nseq):
    length = qkv.shape[0] // nseq
    return pl.pallas_call(
        self_forward,
        grid_spec=pltpu.PrefetchScalarGridSpec(
            num_scalar_prefetch=1,
            grid=(nseq, PAIRS),
            in_specs=[
                spec((length, 3 * LANES), lambda s, p, _: (s, p)),
                spec((2, LANES, 2 * length - LANES), lambda s, p, _: (p, 0, 0)),
            ],
            out_specs=[
                spec((length, LANES), lambda s, p, _: (s, p)),
                spec((None, None, 2, length), lambda s, p, _: (s, p, 0, 0)),
            ],
        ),
        out_shape=[
            jax.ShapeDtypeStruct((qkv.shape[0], PAIRS * LANES), BF16),
            jax.ShapeDtypeStruct((nseq, PAIRS, 2, length), F32),
        ],
        cost_estimate=pl.CostEstimate(
            flops=20_000_000_000, bytes_accessed=12_000_000, transcendentals=0
        ),
        name="self_forward",
    )(prefix, qkv, bias)


def run_cross_forward(query, kv, nseq):
    length = query.shape[0] // nseq
    count = kv.shape[0] // nseq
    return pl.pallas_call(
        cross_forward,
        grid=(nseq, PAIRS),
        in_specs=[
            spec((length, LANES), lambda s, p: (s, p)),
            spec((count, 2 * LANES), lambda s, p: (s, p)),
        ],
        out_specs=[
            spec((length, LANES), lambda s, p: (s, p)),
            spec((None, None, 2, length), lambda s, p: (s, p, 0, 0)),
        ],
        out_shape=[
            jax.ShapeDtypeStruct(query.shape, BF16),
            jax.ShapeDtypeStruct((nseq, PAIRS, 2, length), F32),
        ],
        cost_estimate=pl.CostEstimate(
            flops=24_000_000_000, bytes_accessed=10_000_000, transcendentals=0
        ),
        name="cross_forward",
    )(query, kv)


def run_cross_backward(query, kv, upstream, context, lse, nseq):
    length = query.shape[0] // nseq
    count = kv.shape[0] // nseq
    rows = spec((length, LANES), lambda s, p: (s, p))
    wide = spec((count, 2 * LANES), lambda s, p: (s, p))
    return pl.pallas_call(
        cross_backward,
        grid=(nseq, PAIRS),
        in_specs=[
            rows,
            wide,
            rows,
            rows,
            spec((None, None, 2, length), lambda s, p: (s, p, 0, 0)),
        ],
        out_specs=[rows, wide],
        out_shape=[
            jax.ShapeDtypeStruct(query.shape, BF16),
            jax.ShapeDtypeStruct(kv.shape, BF16),
        ],
        cost_estimate=pl.CostEstimate(
            flops=36_000_000_000, bytes_accessed=20_000_000, transcendentals=0
        ),
        name="cross_backward",
    )(query, kv, upstream, context, lse)


def run_self_backward(prefix, qkv, upstream, context, lse, bias, nseq):
    length = qkv.shape[0] // nseq
    rows = spec((length, LANES), lambda p, s, _: (s, p))
    wide = spec((length, 3 * LANES), lambda p, s, _: (s, p))
    return pl.pallas_call(
        self_backward,
        grid_spec=pltpu.PrefetchScalarGridSpec(
            num_scalar_prefetch=1,
            grid=(PAIRS, nseq),
            in_specs=[
                wide,
                rows,
                rows,
                spec((None, None, 2, length), lambda p, s, _: (s, p, 0, 0)),
                spec((2, LANES, 2 * length - LANES), lambda p, s, _: (p, 0, 0)),
            ],
            out_specs=[
                wide,
                spec((None, 2, 2 * length), lambda p, s, _: (p, 0, 0)),
            ],
            scratch_shapes=[pltpu.VMEM((2, LANES, 2 * length - LANES), F32)],
        ),
        out_shape=[
            jax.ShapeDtypeStruct(qkv.shape, BF16),
            jax.ShapeDtypeStruct((PAIRS, 2, 2 * length), F32),
        ],
        cost_estimate=pl.CostEstimate(
            flops=24_000_000_000, bytes_accessed=20_000_000, transcendentals=0
        ),
        name="self_backward",
    )(prefix, qkv, upstream, context, lse, bias)


def interleave(*parts):
    blocks = []
    for pair in range(PAIRS):
        for part in parts:
            blocks.append(part[:, pair * LANES : (pair + 1) * LANES])
    return jnp.concatenate(blocks, axis=1)


def deinterleave(block, count):
    rows = block.shape[0]
    split = block.reshape(rows, PAIRS, count, LANES)
    return [split[:, :, index].reshape(rows, PAIRS * LANES) for index in range(count)]


def gather(block):
    return lax.all_gather(block, "fsdp", axis=0, tiled=True)


def scatter(block):
    return lax.psum_scatter(block.astype(BF16), "fsdp", scatter_dimension=0, tiled=True)


def scatter_columns(parts):
    count = lax.axis_size("rep")
    rows = parts[0].shape[0]
    split = [part.reshape(rows, count, -1) for part in parts]
    joined = jnp.concatenate(split, axis=2).reshape(rows, -1)
    own = lax.psum_scatter(joined, "rep", scatter_dimension=1, tiled=True)
    sizes = [part.shape[1] // count for part in parts]
    outs = []
    start = 0
    for size in sizes:
        outs.append(own[:, start : start + size].astype(F32))
        start += size
    return outs


def body(
    tokens,
    memory,
    prefix_len,
    bucket_table,
    rel_bias,
    gain_self,
    self_query,
    self_key,
    self_value,
    self_out,
    gain_cross,
    cross_query,
    cross_key,
    cross_value,
    cross_out,
    gain_feed,
    gate_weight,
    up_weight,
    down_weight,
    out_grad,
):
    nseq, length, width = tokens.shape
    shard = gain_self.shape[0]
    groups = width // shard
    entries = rel_bias.shape[0]
    small = jnp.stack(
        [gain_self, gain_cross, gain_feed, jnp.pad(rel_bias, (0, shard - entries))], axis=1
    )
    small = jnp.pad(small, ((0, 0), (0, LANES - 4)))
    first = gather(
        jnp.concatenate([interleave(self_query, self_key, self_value), small], axis=1)
    )
    second = gather(
        jnp.concatenate(
            [self_out, cross_query, interleave(cross_key, cross_value), cross_out], axis=1
        )
    )
    gate_up = gather(jnp.concatenate([gate_weight, up_weight], axis=1))
    down = gather(down_weight)
    qkv_proj = first[:, : 3 * width]
    vectors = first[:, 3 * width : 3 * width + 4].T
    gain_first = vectors[0:1].astype(F32)
    gain_second = vectors[1:2].astype(F32)
    gain_third = vectors[2:3].astype(F32)
    table = vectors[3].reshape(groups, shard)[:, :entries].reshape(NHEAD, BUCKETS)
    out_self = second[:, :width]
    query_cross = second[:, width : 2 * width]
    kv_cross = second[:, 2 * width : 4 * width]
    out_cross = second[:, 4 * width :]
    ffn = gate_weight.shape[1]
    gate_proj = gate_up[:, :ffn]
    up_proj = gate_up[:, ffn:]

    buckets_back = jnp.pad(bucket_table[::-1], (0, 1)).reshape(1, 2 * length)
    bias = skewed_bias(table, buckets_back, length)

    rows = nseq * length
    start_rows = tokens.reshape(rows, width).astype(F32)
    memory_rows = memory.reshape(-1, width)
    upstream = out_grad.reshape(rows, width)

    scale_first = inverse_rms(start_rows)
    normed_first = (start_rows * scale_first * gain_first).astype(BF16)
    qkv = matmul(normed_first, qkv_proj).astype(BF16)
    context, lse_self = run_self_forward(prefix_len, qkv, bias, nseq)
    middle = start_rows + matmul(context, out_self)
    scale_second = inverse_rms(middle)
    normed_second = (middle * scale_second * gain_second).astype(BF16)
    query_two = matmul(normed_second, query_cross).astype(BF16)
    kv_two = matmul(memory_rows, kv_cross).astype(BF16)
    context_two, lse_cross = run_cross_forward(query_two, kv_two, nseq)
    later = middle + matmul(context_two, out_cross)
    scale_third = inverse_rms(later)
    normed_third = (later * scale_third * gain_third).astype(BF16)
    gate_pre = matmul(normed_third, gate_proj)
    up_pre = matmul(normed_third, up_proj)
    hidden = (gelu_tanh(gate_pre) * up_pre).astype(BF16)
    result = (later + matmul(hidden, down)).astype(BF16)

    down_own = scatter(weight_term(hidden, upstream))
    hidden_grad = back_term(upstream, down)
    gate_grad = (hidden_grad * up_pre * gelu_slope(gate_pre)).astype(BF16)
    lift_grad = (hidden_grad * gelu_tanh(gate_pre)).astype(BF16)
    feed_own = scatter(
        jnp.concatenate(
            [
                weight_term(normed_third, gate_grad).astype(BF16),
                weight_term(normed_third, lift_grad).astype(BF16),
            ],
            axis=1,
        )
    )
    third_grad = back_term(gate_grad, gate_proj) + back_term(lift_grad, up_proj)
    carry, gain_third_grad = norm_back(later, scale_third, gain_third, third_grad)
    later_grad = upstream.astype(F32) + carry
    branch_two = later_grad.astype(BF16)
    context_two_grad = back_term(branch_two, out_cross).astype(BF16)
    query_two_grad, kv_two_grad = run_cross_backward(
        query_two, kv_two, context_two_grad, context_two, lse_cross, nseq
    )
    cross_own = scatter(
        jnp.concatenate(
            [
                weight_term(normed_second, query_two_grad).astype(BF16),
                weight_term(memory_rows, kv_two_grad).astype(BF16),
                weight_term(context_two, branch_two).astype(BF16),
            ],
            axis=1,
        )
    )
    memory_grad = back_term(kv_two_grad, kv_cross)
    carry, gain_second_grad = norm_back(
        middle, scale_second, gain_second, back_term(query_two_grad, query_cross)
    )
    middle_grad = later_grad + carry
    branch_one = middle_grad.astype(BF16)
    context_grad = back_term(branch_one, out_self).astype(BF16)
    qkv_grad, diagonal = run_self_backward(
        prefix_len, qkv, context_grad, context, lse_self, bias, nseq
    )
    first_grad = back_term(qkv_grad, qkv_proj)
    carry, gain_first_grad = norm_back(start_rows, scale_first, gain_first, first_grad)
    tokens_grad = middle_grad + carry

    onehot = (
        buckets_back.reshape(-1, 1) == jnp.arange(BUCKETS, dtype=jnp.int32)[None, :]
    ).astype(F32)
    onehot = onehot * (jnp.arange(2 * length) < 2 * length - 1)[:, None]
    bias_grad = jnp.dot(
        diagonal.reshape(NHEAD, 2 * length), onehot, precision=lax.Precision.HIGHEST
    )
    bias_rows = jnp.pad(
        bias_grad.reshape(groups, entries), ((0, 0), (0, shard - entries))
    ).reshape(width)
    vector_block = jnp.pad(
        jnp.stack([gain_first_grad, gain_second_grad, gain_third_grad, bias_rows], axis=0),
        ((0, LANES - 4), (0, 0)),
    ).T
    self_own = scatter(
        jnp.concatenate(
            [
                weight_term(normed_first, qkv_grad).astype(BF16),
                weight_term(context, branch_one).astype(BF16),
                vector_block.astype(BF16),
            ],
            axis=1,
        )
    )

    (down_weight_grad,) = scatter_columns([down_own])
    key_own, value_own = deinterleave(cross_own[:, width : 3 * width], 2)
    gate_g, up_g, cq_g, ck_g, cv_g, co_g = scatter_columns(
        [
            feed_own[:, :ffn],
            feed_own[:, ffn:],
            cross_own[:, :width],
            key_own,
            value_own,
            cross_own[:, 3 * width :],
        ]
    )
    q_own, k_own, v_own = deinterleave(self_own[:, : 3 * width], 3)
    copies = jnp.tile(self_own[:, 4 * width :], (1, lax.axis_size("rep")))
    sq_g, sk_g, sv_g, so_g, vec = scatter_columns(
        [q_own, k_own, v_own, self_own[:, 3 * width : 4 * width], copies]
    )
    return (
        result.reshape(tokens.shape),
        tokens_grad.reshape(tokens.shape),
        memory_grad.reshape(memory.shape),
        vec[:entries, 3],
        vec[:, 0],
        sq_g,
        sk_g,
        sv_g,
        so_g,
        vec[:, 1],
        cq_g,
        ck_g,
        cv_g,
        co_g,
        vec[:, 2],
        gate_g,
        up_g,
        down_weight_grad,
    )


def solution(mesh):
    batch = P(("rep", "fsdp"), None, None)
    matrix = P("fsdp", None)
    vector = P("fsdp")
    split = P("fsdp", "rep")
    in_specs = (
        (batch, batch, P(("rep", "fsdp")), P(), vector, vector)
        + (matrix,) * 4
        + (vector,)
        + (matrix,) * 4
        + (vector,)
        + (matrix,) * 3
        + (batch,)
    )
    out_specs = (
        (batch, batch, batch, vector, vector)
        + (split,) * 4
        + (vector,)
        + (split,) * 4
        + (vector,)
        + (split,) * 3
    )
    return jax.shard_map(body, mesh=mesh, in_specs=in_specs, out_specs=out_specs, check_vma=False)
```

```python
import functools

import jax
import jax.numpy as jnp
from jax import lax
from jax.experimental import pallas as pl
from jax.experimental.pallas import tpu as pltpu
from jax.sharding import PartitionSpec as P

NHEAD = 12
DHEAD = 64
BUCKETS = 32
PAIRS = NHEAD // 2
LANES = 2 * DHEAD
PREFIX_MAX = 256

EPSILON = 1e-06
CUBIC_TERM = 0.044715
SQRT_TWO_PI = 0.7978845608028654
NEGATIVE = -1000000000.0

F32 = jnp.float32
BF16 = jnp.bfloat16
LAST_DIMS = (((1,), (1,)), ((), ()))
FIRST_DIMS = (((0,), (0,)), ((), ()))


def matmul(left_side, right_side):
    return jnp.dot(left_side, right_side, preferred_element_type=F32)


def weight_term(inputs, gradient):
    return lax.dot_general(inputs, gradient, FIRST_DIMS, preferred_element_type=F32)


def back_term(gradient, weight):
    return lax.dot_general(gradient, weight, LAST_DIMS, preferred_element_type=F32)


def inverse_rms(values):
    return lax.rsqrt(jnp.mean(values * values, axis=-1, keepdims=True) + EPSILON)


def gelu_tanh(values):
    return (
        0.5
        * values
        * (1.0 + jnp.tanh(SQRT_TWO_PI * (values + CUBIC_TERM * values * values * values)))
    )


def gelu_slope(values):
    tangent = jnp.tanh(SQRT_TWO_PI * (values + CUBIC_TERM * values * values * values))
    return 0.5 * (1.0 + tangent) + 0.5 * values * (1.0 - tangent * tangent) * SQRT_TWO_PI * (
        1.0 + 3.0 * CUBIC_TERM * values * values
    )


def norm_back(values, scale_rows, gain_vec, upstream):
    weighted = upstream * gain_vec
    gain_grad = jnp.sum(upstream * values * scale_rows, axis=0)
    input_grad = scale_rows * weighted - values * scale_rows * scale_rows * scale_rows * jnp.mean(
        values * weighted, axis=-1, keepdims=True
    )
    return (input_grad, gain_grad)


def one_head(rows, head):
    lane = lax.broadcasted_iota(jnp.int32, rows.shape, 1)
    keep = lane < DHEAD if head == 0 else lane >= DHEAD
    return jnp.where(keep, rows, jnp.zeros_like(rows))


def flipped(rows):
    return rows.astype(F32).T.astype(BF16)


def tree(fold, rows, groups):
    step = rows.shape[0] // groups
    total = rows[:step]
    for index in range(1, groups):
        total = fold(total, rows[index * step : (index + 1) * step])
    return total


def column_max(rows, groups):
    return jnp.max(tree(jnp.maximum, rows, groups), axis=0, keepdims=True)


def column_sum(rows, groups):
    return jnp.sum(tree(jnp.add, rows, groups), axis=0, keepdims=True)


def allowed_at(shape, key_start, query_start, prefix):
    key = lax.broadcasted_iota(jnp.int32, shape, 0) + key_start
    query = lax.broadcasted_iota(jnp.int32, shape, 1) + query_start
    return (key <= query) | (key < prefix)


def skew_kernel(table_ref, buckets_ref, out_ref):
    bucket = lax.broadcasted_iota(jnp.int32, (BUCKETS, buckets_ref.shape[1]), 0)
    onehot = (bucket == buckets_ref[...]).astype(BF16)
    by_offset = matmul(table_ref[...], onehot)
    width = out_ref.shape[2]
    total = by_offset.shape[1]
    for head in range(NHEAD):
        rows = jnp.broadcast_to(by_offset[head : head + 1], (LANES, total))
        rolled = pltpu.roll(rows, total - (LANES - 1), 1, stride=1, stride_axis=0)
        out_ref[head] = rolled[:, :width]


def skewed_bias(table, buckets_back, length):
    total = 2 * length
    return pl.pallas_call(
        skew_kernel,
        out_shape=jax.ShapeDtypeStruct((NHEAD, LANES, total - LANES), F32),
        name="skewed_bias",
    )(jnp.pad(table, ((0, 4), (0, 0))), buckets_back)


def self_forward(prefix_ref, query_ref, key_ref, value_ref, bias_ref, out_ref, lse_ref):
    length = query_ref.shape[0]
    block = 256
    prefix = prefix_ref[pl.program_id(0)]
    queries = query_ref[...]
    keys = key_ref[...]
    values = flipped(value_ref[...])
    for start in range(0, length, block):
        stop = start + block
        count = max(PREFIX_MAX, stop)
        outs = []
        for head in range(2):
            scores = back_term(keys[:count], one_head(queries[start:stop], head))
            parts = []
            for base in range(0, count, LANES):
                shift = length - LANES - base + start
                part = scores[base : base + LANES] + bias_ref[head, :, shift : shift + block]
                if base + LANES - 1 > start:
                    part = jnp.where(
                        allowed_at(part.shape, base, start, prefix), part, NEGATIVE
                    )
                parts.append(part)
            top = parts[0]
            for part in parts[1:]:
                top = jnp.maximum(top, part)
            top = column_max(top, 4)
            shares = [jnp.exp(part - top) for part in parts]
            total = shares[0]
            for share in shares[1:]:
                total = total + share
            total = column_sum(total, 4)
            share = jnp.concatenate([item.astype(BF16) for item in shares], axis=0)
            context = matmul(values[head * DHEAD : (head + 1) * DHEAD, :count], share)
            outs.append(context * (1.0 / total))
            lse_ref[head : head + 1, start:stop] = top + jnp.log(total)
        out_ref[start:stop, :] = jnp.concatenate(outs, axis=0).T.astype(BF16)


def cross_forward(query_ref, key_ref, value_ref, out_ref, lse_ref):
    keys = key_ref[...]
    values = flipped(value_ref[...])
    queries = query_ref[...]
    ahead = [back_term(keys, one_head(queries, head)) for head in range(2)]
    outs = []
    for head in range(2):
        scores = ahead[head]
        top = column_max(scores, 16)
        share = jnp.exp(scores - top)
        total = column_sum(share, 16)
        context = matmul(values[head * DHEAD : (head + 1) * DHEAD], share.astype(BF16))
        outs.append(context * (1.0 / total))
        lse_ref[head : head + 1, :] = top + jnp.log(total)
    out_ref[...] = jnp.concatenate(outs, axis=0).T.astype(BF16)


def cross_backward(
    query_ref, key_ref, value_ref, up_ref, context_ref, lse_ref, dq_ref, dk_ref, dv_ref
):
    length = query_ref.shape[0]
    block = 256
    keys = key_ref[...]
    values = value_ref[...]
    queries = query_ref[...]
    upstream = up_ref[...]
    keys_flipped = flipped(keys)
    inner = (upstream.astype(F32) * context_ref[...].astype(F32)).T
    key_grad = None
    value_grad = None
    for start in range(0, length, block):
        rows = slice(start, start + block)
        grads = []
        for head in range(2):
            sub = slice(head * DHEAD, (head + 1) * DHEAD)
            query = one_head(queries[rows], head)
            above = one_head(upstream[rows], head)
            row_inner = jnp.sum(inner[sub, rows], axis=0, keepdims=True)
            shares = jnp.exp(back_term(keys, query) - lse_ref[head : head + 1, rows])
            share_grad = back_term(values, above)
            score_grad = (shares * (share_grad - row_inner)).astype(BF16)
            value_part = matmul(shares.astype(BF16), above)
            key_part = matmul(score_grad, query)
            value_grad = value_part if value_grad is None else value_grad + value_part
            key_grad = key_part if key_grad is None else key_grad + key_part
            grads.append(matmul(keys_flipped[sub], score_grad))
        dq_ref[rows, :] = jnp.concatenate(grads, axis=0).T.astype(BF16)
    dk_ref[...] = key_grad.astype(BF16)
    dv_ref[...] = value_grad.astype(BF16)


def self_backward(
    prefix_ref,
    query_ref,
    key_ref,
    value_ref,
    up_ref,
    context_ref,
    lse_ref,
    bias_ref,
    dq_ref,
    dk_ref,
    dv_ref,
    diag_ref,
    acc_ref,
):
    length = query_ref.shape[0]
    block = 256
    step = pl.program_id(1)
    prefix = prefix_ref[step]

    @pl.when(step == 0)
    def _():
        acc_ref[...] = jnp.zeros_like(acc_ref)

    queries = query_ref[...]
    keys = key_ref[...]
    values = value_ref[...]
    upstream = up_ref[...]
    keys_flipped = flipped(keys)
    inner = (upstream.astype(F32) * context_ref[...].astype(F32)).T
    count_all = length // block
    key_grad = [None] * count_all
    value_grad = [None] * count_all
    for start in range(0, length, block):
        stop = start + block
        count = max(PREFIX_MAX, stop)
        rows = slice(start, stop)
        grads = []
        for head in range(2):
            sub = slice(head * DHEAD, (head + 1) * DHEAD)
            query = one_head(queries[rows], head)
            above = one_head(upstream[rows], head)
            row_inner = jnp.sum(inner[sub, rows], axis=0, keepdims=True)
            row_lse = lse_ref[head : head + 1, rows]
            scores = back_term(keys[:count], query)
            share_grad = back_term(values[:count], above)
            shares = []
            score_grads = []
            for base in range(0, count, LANES):
                part = slice(base, base + LANES)
                shift = length - LANES - base + start
                share = jnp.exp(
                    scores[part] + bias_ref[head, :, shift : shift + block] - row_lse
                )
                if base + LANES - 1 > start:
                    share = jnp.where(allowed_at(share.shape, base, start, prefix), share, 0.0)
                score_grad = share * (share_grad[part] - row_inner)
                acc_ref[head, :, shift : shift + block] += score_grad
                shares.append(share.astype(BF16))
                score_grads.append(score_grad.astype(BF16))
            share = jnp.concatenate(shares, axis=0)
            score_grad = jnp.concatenate(score_grads, axis=0)
            value_part = matmul(share, above)
            key_part = matmul(score_grad, query)
            for index in range(count // block):
                part = slice(index * block, (index + 1) * block)
                if value_grad[index] is None:
                    value_grad[index] = value_part[part]
                    key_grad[index] = key_part[part]
                else:
                    value_grad[index] = value_grad[index] + value_part[part]
                    key_grad[index] = key_grad[index] + key_part[part]
            grads.append(matmul(keys_flipped[sub, :count], score_grad))
        dq_ref[rows, :] = jnp.concatenate(grads, axis=0).T.astype(BF16)
    for index in range(count_all):
        part = slice(index * block, (index + 1) * block)
        dk_ref[part, :] = key_grad[index].astype(BF16)
        dv_ref[part, :] = value_grad[index].astype(BF16)

    @pl.when(step == pl.num_programs(1) - 1)
    def _():
        row = lax.broadcasted_iota(jnp.int32, (LANES, 2 * length), 0)
        amount = LANES - 1 - row
        for head in range(2):
            skewed = jnp.concatenate(
                [acc_ref[head], jnp.zeros((LANES, LANES), F32)], axis=1
            )
            bit = 1
            while bit < LANES:
                skewed = jnp.where((amount & bit) != 0, pltpu.roll(skewed, bit, 1), skewed)
                bit *= 2
            diag_ref[head : head + 1, :] = jnp.sum(skewed, axis=0, keepdims=True)


def spec(shape, index):
    return pl.BlockSpec(shape, index)


def run_self_forward(prefix, qkv, bias, nseq):
    length = qkv.shape[0] // nseq
    return pl.pallas_call(
        self_forward,
        grid_spec=pltpu.PrefetchScalarGridSpec(
            num_scalar_prefetch=1,
            grid=(nseq, PAIRS),
            in_specs=[
                spec((length, LANES), lambda s, p, _: (s, p)),
                spec((length, LANES), lambda s, p, _: (s, PAIRS + p)),
                spec((length, LANES), lambda s, p, _: (s, 2 * PAIRS + p)),
                spec((2, LANES, 2 * length - LANES), lambda s, p, _: (p, 0, 0)),
            ],
            out_specs=[
                spec((length, LANES), lambda s, p, _: (s, p)),
                spec((None, None, 2, length), lambda s, p, _: (s, p, 0, 0)),
            ],
        ),
        out_shape=[
            jax.ShapeDtypeStruct((qkv.shape[0], PAIRS * LANES), BF16),
            jax.ShapeDtypeStruct((nseq, PAIRS, 2, length), F32),
        ],
        cost_estimate=pl.CostEstimate(
            flops=20_000_000_000, bytes_accessed=12_000_000, transcendentals=0
        ),
        name="self_forward",
    )(prefix, qkv, qkv, qkv, bias)


def run_cross_forward(query, kv, nseq):
    length = query.shape[0] // nseq
    count = kv.shape[0] // nseq
    return pl.pallas_call(
        cross_forward,
        grid=(nseq, PAIRS),
        in_specs=[
            spec((length, LANES), lambda s, p: (s, p)),
            spec((count, LANES), lambda s, p: (s, p)),
            spec((count, LANES), lambda s, p: (s, PAIRS + p)),
        ],
        out_specs=[
            spec((length, LANES), lambda s, p: (s, p)),
            spec((None, None, 2, length), lambda s, p: (s, p, 0, 0)),
        ],
        out_shape=[
            jax.ShapeDtypeStruct(query.shape, BF16),
            jax.ShapeDtypeStruct((nseq, PAIRS, 2, length), F32),
        ],
        cost_estimate=pl.CostEstimate(
            flops=24_000_000_000, bytes_accessed=10_000_000, transcendentals=0
        ),
        name="cross_forward",
    )(query, kv, kv)


def run_cross_backward(query, kv, upstream, context, lse, nseq):
    length = query.shape[0] // nseq
    count = kv.shape[0] // nseq
    rows = spec((length, LANES), lambda s, p: (s, p))
    wide = spec((count, LANES), lambda s, p: (s, p))
    return pl.pallas_call(
        cross_backward,
        grid=(nseq, PAIRS),
        in_specs=[
            rows,
            wide,
            spec((count, LANES), lambda s, p: (s, PAIRS + p)),
            rows,
            rows,
            spec((None, None, 2, length), lambda s, p: (s, p, 0, 0)),
        ],
        out_specs=[rows, wide, wide],
        out_shape=[
            jax.ShapeDtypeStruct(query.shape, BF16),
            jax.ShapeDtypeStruct((kv.shape[0], PAIRS * LANES), BF16),
            jax.ShapeDtypeStruct((kv.shape[0], PAIRS * LANES), BF16),
        ],
        cost_estimate=pl.CostEstimate(
            flops=36_000_000_000, bytes_accessed=20_000_000, transcendentals=0
        ),
        name="cross_backward",
    )(query, kv, kv, upstream, context, lse)


def run_self_backward(prefix, qkv, upstream, context, lse, bias, nseq):
    length = qkv.shape[0] // nseq
    rows = spec((length, LANES), lambda p, s, _: (s, p))
    return pl.pallas_call(
        self_backward,
        grid_spec=pltpu.PrefetchScalarGridSpec(
            num_scalar_prefetch=1,
            grid=(PAIRS, nseq),
            in_specs=[
                rows,
                spec((length, LANES), lambda p, s, _: (s, PAIRS + p)),
                spec((length, LANES), lambda p, s, _: (s, 2 * PAIRS + p)),
                rows,
                rows,
                spec((None, None, 2, length), lambda p, s, _: (s, p, 0, 0)),
                spec((2, LANES, 2 * length - LANES), lambda p, s, _: (p, 0, 0)),
            ],
            out_specs=[
                rows,
                rows,
                rows,
                spec((None, 2, 2 * length), lambda p, s, _: (p, 0, 0)),
            ],
            scratch_shapes=[pltpu.VMEM((2, LANES, 2 * length - LANES), F32)],
        ),
        out_shape=[jax.ShapeDtypeStruct(upstream.shape, BF16)] * 3
        + [jax.ShapeDtypeStruct((PAIRS, 2, 2 * length), F32)],
        cost_estimate=pl.CostEstimate(
            flops=24_000_000_000, bytes_accessed=20_000_000, transcendentals=0
        ),
        name="self_backward",
    )(prefix, qkv, qkv, qkv, upstream, context, lse, bias)


MESH = pl.DeviceIdType.MESH


class Place:
    def __init__(self, line):
        self.line = line
        rep = lax.axis_index("rep")
        fsdp = lax.axis_index("fsdp")
        self.rep = rep
        self.fsdp = fsdp
        self.y = rep // 2
        self.x = rep % 2
        self.z = fsdp // 2
        self.core = fsdp % 2
        self.x_rep = self.y * 2 + 1 - self.x
        self.y_rep = (1 - self.y) * 2 + self.x

    def at_x(self):
        return {"rep": self.x_rep, "fsdp": self.fsdp}

    def at_y(self):
        return {"rep": self.y_rep, "fsdp": self.fsdp}

    def at_partner(self):
        return {"rep": self.rep, "fsdp": self.z * 2 + 1 - self.core}

    def at_line(self, side):
        return {"rep": self.rep, "fsdp": self.fsdp + (2 if side == 0 else -2)}

    def has_next(self, side):
        return self.z < self.line - 1 if side == 0 else self.z > 0

    def has_last(self, side):
        return self.has_next(1 - side)

    def arrives(self, side, hop):
        if side == 0:
            return self.z - 1 - hop >= 0
        return self.z + 1 + hop <= self.line - 1

    def source(self, side, hop):
        return self.z - 1 - hop if side == 0 else self.z + 1 + hop

    def at_far(self):
        half = self.line // 2
        return {"rep": self.rep, "fsdp": (self.z + half) % self.line * 2 + self.core}

    def greet(self, wide=False):
        barrier = pltpu.get_barrier_semaphore()
        targets = [self.at_x(), self.at_y(), self.at_partner()]
        if wide:
            targets.append({"rep": 3 - self.rep, "fsdp": self.fsdp})
            targets.append(self.at_far())
        for target in targets:
            pl.semaphore_signal(barrier, inc=1, device_id=target, device_id_type=MESH)
        for side in range(2):

            @pl.when(self.has_next(side))
            def _():
                pl.semaphore_signal(
                    barrier, inc=1, device_id=self.at_line(side), device_id_type=MESH
                )

        count = len(targets)
        for side in range(2):
            count = count + jnp.where(self.has_next(side), 1, 0)
        pl.semaphore_wait(barrier, count)


def remote(source, target, send, recv, device):
    return pltpu.make_async_remote_copy(
        src_ref=source,
        dst_ref=target,
        send_sem=send,
        recv_sem=recv,
        device_id=device,
        device_id_type=MESH,
    )


class GatherShape:
    def __init__(self, rows, columns, by_rows):
        self.rows = rows
        self.columns = columns
        self.by_rows = by_rows

    def full(self, ref, owner):
        return ref.at[pl.ds(pl.multiple_of(owner * self.rows, 32), self.rows)]

    def piece(self, ref, owner, part, half=None):
        base = owner * self.rows
        if self.by_rows:
            rows = self.rows // 4
            base = base + part * rows
        else:
            rows = self.rows
        if half is not None:
            rows = rows // 2
            base = base + half * rows
        row_slice = pl.ds(pl.multiple_of(base, 16), rows)
        if self.by_rows:
            return ref.at[row_slice]
        width = self.columns // 4
        return ref.at[row_slice, pl.ds(pl.multiple_of(part * width, LANES), width)]


def gather_sems(line):
    hops = line - 1
    return [pltpu.SemaphoreType.DMA((5, 2, 2, hops)), pltpu.SemaphoreType.DMA((4,))] + [
        pltpu.SemaphoreType.DMA((2, 2, hops))
    ]


def gather_steps(place, shape, src, own, dst, sems):
    hop_sem, own_sem, pair_sem = sems
    hops = place.line - 1
    me = place.fsdp

    def load():
        return pltpu.make_async_copy(src, own, own_sem.at[0])

    def keep():
        return pltpu.make_async_copy(own, shape.full(dst, me), own_sem.at[1])

    def own_pair():
        return remote(
            own, shape.full(dst, me), own_sem.at[2], own_sem.at[3], place.at_partner()
        )

    def owner(side, hop):
        return place.source(side, hop) * 2 + place.core

    def line_first(side):
        return remote(
            shape.piece(own, 0, place.rep),
            shape.piece(dst, me, place.rep),
            hop_sem.at[0, 0, side, 0],
            hop_sem.at[0, 1, side, 0],
            place.at_line(side),
        )

    def moved(kind, side, hop, block, device):
        return remote(
            block, block, hop_sem.at[kind, 0, side, hop], hop_sem.at[kind, 1, side, hop], device
        )

    def line_next(side, hop):
        block = shape.piece(dst, owner(side, hop - 1), place.rep)
        return moved(0, side, hop, block, place.at_line(side))

    def line_arrival(side, hop):
        block = shape.piece(dst, owner(side, hop), place.rep)
        return moved(0, side, hop, block, place.at_line(side))

    def plane(axis, side, hop):
        block = shape.piece(dst, owner(side, hop), place.rep)
        return moved(1 + axis, side, hop, block, place.at_x() if axis == 0 else place.at_y())

    def cross(axis, side, hop):
        part = place.x_rep if axis == 1 else place.y_rep
        block = shape.piece(dst, owner(side, hop), part, 1 - axis)
        return moved(3 + axis, side, hop, block, place.at_x() if axis == 0 else place.at_y())

    def pair(side, hop):
        block = shape.full(dst, owner(side, hop))
        return remote(
            block, block, pair_sem.at[0, side, hop], pair_sem.at[1, side, hop], place.at_partner()
        )

    def each(fn):
        def run():
            for hop in range(hops):
                for side in range(2):
                    pl.when(place.arrives(side, hop))(functools.partial(fn, side, hop))

        return run

    def start():
        load().start()
        load().wait()
        for side in range(2):
            pl.when(place.has_next(side))(lambda side=side: line_first(side).start())
        own_pair().start()
        keep().start()

    def arrive(side, hop):
        line_arrival(side, hop).wait_recv()
        if hop + 1 < hops:
            pl.when(place.has_next(side))(lambda: line_next(side, hop + 1).start())
        plane(0, side, hop).start()
        plane(1, side, hop).start()

    def turn(side, hop):
        plane(0, side, hop).wait_recv()
        cross(1, side, hop).start()
        plane(1, side, hop).wait_recv()
        cross(0, side, hop).start()

    def hand(side, hop):
        cross(0, side, hop).wait_recv()
        cross(1, side, hop).wait_recv()
        pair(side, hop).start()

    def finish():
        def last(side, hop):
            pair(side, hop).wait()
            for axis in range(2):
                plane(axis, side, hop).wait_send()
                cross(axis, side, hop).wait_send()
            if hop + 1 < hops:
                pl.when(place.has_next(side))(lambda: line_next(side, hop + 1).wait_send())

        each(last)()
        for side in range(2):
            pl.when(place.has_next(side))(lambda side=side: line_first(side).wait_send())
        own_pair().wait()
        keep().wait()

    return start, each(arrive), each(turn), each(hand), finish


def gather_kernel(shapes, line, *refs):
    count = len(shapes)
    sources = refs[:count]
    targets = refs[count : 2 * count]
    scratch = refs[2 * count :]
    place = Place(line)
    place.greet()
    plans = []
    for index, shape in enumerate(shapes):
        own, *sems = scratch[4 * index : 4 * index + 4]
        plans.append(gather_steps(place, shape, sources[index], own, targets[index], sems))
    for stage in range(5):
        for plan in plans:
            plan[stage]()


def fast_gather(blocks, line, by_rows, collective_id):
    shapes = [
        GatherShape(block.shape[0], block.shape[1], flag) for block, flag in zip(blocks, by_rows)
    ]
    scratch = []
    for shape in shapes:
        scratch.append(pltpu.VMEM((shape.rows, shape.columns), BF16))
        scratch.extend(gather_sems(line))
    anywhere = pl.BlockSpec(memory_space=pl.ANY)
    return pl.pallas_call(
        functools.partial(gather_kernel, shapes, line),
        in_specs=[anywhere] * len(blocks),
        out_specs=[anywhere] * len(blocks),
        out_shape=[
            jax.ShapeDtypeStruct((2 * line * s.rows, s.columns), BF16) for s in shapes
        ],
        scratch_shapes=scratch,
        compiler_params=pltpu.CompilerParams(collective_id=collective_id, has_side_effects=True),
        name="fast_gather",
    )(*blocks)


class ReduceShape:
    def __init__(self, kind, rows, columns, sources):
        self.kind = kind
        self.rows = rows
        self.sources = sources
        if kind == "rows":
            self.block = (rows // 8, columns)
        elif kind == "pair":
            self.block = (rows // 2, columns // 2)
        else:
            self.block = (rows // 2, columns)
        self.exchange = kind != "pair"
        self.part_rows = rows // 4 if kind == "rows" else rows
        self.part_columns = columns // 4

    def pieces(self, refs, owner, half, quarter):
        rows, columns = self.block
        if self.kind == "rows":
            base = owner * self.rows + quarter * (self.rows // 4) + half * rows
            return [(refs[0].at[pl.ds(pl.multiple_of(base, 16), rows)], 0, columns)]
        at = pl.ds(pl.multiple_of(owner * self.rows + half * rows, 16), rows)
        if self.kind == "four":
            return [(refs[quarter].at[at], 0, columns)]
        width = columns // 2
        cut = slice(quarter * width, (quarter + 1) * width)
        return [(refs[index].at[at, cut], index * width, width) for index in range(2)]

    def out_shape(self):
        if self.exchange:
            return jax.ShapeDtypeStruct((4, self.part_rows, self.part_columns), F32)
        return jax.ShapeDtypeStruct((self.rows, self.block[1]), F32)

    def scratch(self, line):
        rows, columns = self.block
        dma = pltpu.SemaphoreType.DMA
        buffers = [
            pltpu.VMEM((line, 8, rows, columns), BF16),
            pltpu.VMEM((line, 8, rows, columns), BF16),
            pltpu.VMEM((line, 2, 2, rows, columns), BF16),
            pltpu.VMEM((line, 2, rows, columns), BF16),
            pltpu.VMEM((line, 2, rows, columns), BF16),
            pltpu.VMEM((2, line, 2, rows, columns), BF16),
            pltpu.VMEM((4, self.part_rows, self.part_columns), F32),
            pltpu.VMEM((4, self.part_rows, self.part_columns), F32),
            dma((line,)),
            dma((2, line)),
            dma((2, line, 2)),
            dma((2, line, 2)),
            dma((2, 2, line)),
            dma((2, 3)),
        ]
        return buffers


REDUCE_SCRATCH = 14


def added(left, right):
    return (left.astype(F32) + right.astype(F32)).astype(BF16)


def reduce_steps(place, shape, refs, out, scratch):
    own, other, first_in, second_in, total, line_in, parts, gathered = scratch[:8]
    load_sem, pair_sem, first_sem, second_sem, line_sem, swap_sem = scratch[8:]
    line = place.line
    near = (place.x, place.y)
    far = (place.y, place.x)
    near_device = (place.at_x(), place.at_y())
    far_device = (place.at_y(), place.at_x())

    def quarter_of(half, index):
        high, low = index // 2, index % 2
        return low * 2 + high if half == 0 else high * 2 + low

    def start(z):
        for half in range(2):
            for index in range(4):
                quarter = quarter_of(half, index)
                slot = half * 4 + index
                mine = shape.pieces(refs, 2 * z + place.core, half, quarter)
                theirs = shape.pieces(refs, 2 * z + 1 - place.core, half, quarter)
                for (view, column, width), (view_two, _, _) in zip(mine, theirs):
                    cut = pl.ds(column, width)
                    remote(
                        view_two,
                        other.at[z, slot, :, cut],
                        pair_sem.at[0, z],
                        pair_sem.at[1, z],
                        place.at_partner(),
                    ).start()
                    pltpu.make_async_copy(
                        view, own.at[z, slot, :, cut], load_sem.at[z]
                    ).start()

    def pair_all(z):
        return remote(
            own.at[z], other.at[z], pair_sem.at[0, z], pair_sem.at[1, z], place.at_partner()
        )

    def first(z, half):
        return remote(
            own.at[z, pl.ds(half * 4 + (1 - near[half]) * 2, 2)],
            first_in.at[z, half],
            first_sem.at[0, z, half],
            first_sem.at[1, z, half],
            near_device[half],
        )

    def second(z, half):
        return remote(
            own.at[z, half * 4 + near[half] * 2 + 1 - far[half]],
            second_in.at[z, half],
            second_sem.at[0, z, half],
            second_sem.at[1, z, half],
            far_device[half],
        )

    def along(z, side):
        return remote(
            total.at[z],
            line_in.at[side, z],
            line_sem.at[0, side, z],
            line_sem.at[1, side, z],
            place.at_line(side),
        )

    def pair_add(z):
        pltpu.make_async_copy(own.at[z], own.at[z], load_sem.at[z]).wait()
        pair_all(z).wait_recv()

        @pl.loop(0, 8)
        def _(slot):
            own[z, slot] = added(own[z, slot], other[z, slot])

        for half in range(2):
            first(z, half).start()

    def first_add(z):
        for half in range(2):
            first(z, half).wait_recv()
            base = half * 4 + near[half] * 2

            @pl.loop(0, 2)
            def _(index):
                own[z, base + index] = added(own[z, base + index], first_in[z, half, index])

            second(z, half).start()

    def second_add(z):
        for half in range(2):
            second(z, half).wait_recv()
            mine = half * 4 + near[half] * 2 + far[half]
            total[z, half] = added(own[z, mine], second_in[z, half])

    def line_send(z, side):
        ahead = place.z < z if side == 0 else place.z > z

        @pl.when(ahead)
        def _():
            @pl.when(place.has_last(side))
            def _():
                along(z, side).wait_recv()

                @pl.loop(0, 2)
                def _(half):
                    total[z, half] = added(total[z, half], line_in[side, z, half])

            along(z, side).start()

    def line_end(z):
        @pl.when(place.z == z)
        def _():
            for side in range(2):
                pl.when(place.has_last(side))(lambda: along(z, side).wait_recv())

    def swap(rep_slot, device, index):
        return remote(
            parts.at[rep_slot],
            gathered.at[place.rep],
            swap_sem.at[0, index],
            swap_sem.at[1, index],
            device,
        )

    def swaps():
        corner = 3 - place.rep
        return [
            swap(place.x_rep, place.at_x(), 0),
            swap(place.y_rep, place.at_y(), 1),
            swap(corner, {"rep": corner, "fsdp": place.fsdp}, 2),
        ]

    def finish():
        rows, columns = shape.block
        me = place.z
        for half in range(2):
            result = total[me, half].astype(F32)
            for side in range(2):
                extra = line_in[side, me, half].astype(F32)
                result = result + jnp.where(place.has_last(side), extra, 0.0)
            at = slice(half * rows, (half + 1) * rows)
            if shape.exchange:
                width = shape.part_columns
                for index in range(4):
                    parts[index, at, :] = result[:, index * width : (index + 1) * width]
            else:
                out[at, :] = result
        if shape.exchange:
            for copy in swaps():
                copy.start()
            gathered[place.rep] = parts[place.rep]

    def drain():
        if shape.exchange:
            for copy in swaps():
                copy.wait()
            out[...] = gathered[...]
        for z in range(line):
            pair_all(z).wait_send()
            for half in range(2):
                first(z, half).wait_send()
                second(z, half).wait_send()
            for side in range(2):
                ahead = place.z < z if side == 0 else place.z > z
                pl.when(ahead)(lambda: along(z, side).wait_send())

    order = [line - 1, 0] + [z for z in range(line - 2, 0, -1)]

    def begin():
        for z in order:
            start(z)

    def pairs():
        for z in order:
            pair_add(z)

    def firsts():
        for z in order:
            first_add(z)

    def seconds():
        for index, z in enumerate(order):
            second_add(z)
            if index > 0:
                line_send(order[index - 1], 0)
                line_send(order[index - 1], 1)
        line_send(order[-1], 0)
        line_send(order[-1], 1)

    def close():
        for z in range(line):
            line_end(z)
        finish()

    return begin, pairs, firsts, seconds, close, drain


class VectorSum:
    def __init__(self, place, source, out, scratch):
        self.place = place
        self.source = source
        self.out = out
        self.current, self.incoming, self.sems = scratch
        side = place.z % 2
        near = place.fsdp + 2 - 4 * side
        self.devices = [
            place.at_partner(),
            place.at_x(),
            place.at_y(),
            {"rep": place.rep, "fsdp": near},
            place.at_far(),
        ]

    @staticmethod
    def scratch(shape):
        return [
            pltpu.VMEM((6,) + shape, F32),
            pltpu.VMEM((5,) + shape, F32),
            pltpu.SemaphoreType.DMA((2, 5)),
        ]

    def copy(self, index):
        return remote(
            self.current.at[index],
            self.incoming.at[index],
            self.sems.at[0, index],
            self.sems.at[1, index],
            self.devices[index],
        )

    def round(self, index):
        if index == 0:
            self.current[0] = self.source[...]
        else:
            self.copy(index - 1).wait_recv()
            self.current[index] = self.current[index - 1] + self.incoming[index - 1]
        if index < 5:
            self.copy(index).start()

    def finish(self):
        self.out[...] = self.current[5]
        for index in range(5):
            self.copy(index).wait_send()


def reduce_kernel(shapes, line, vector_count, *refs):
    sources = []
    at = 0
    for shape in shapes:
        sources.append(refs[at : at + shape.sources])
        at += shape.sources
    vector_refs = refs[at : at + vector_count]
    at += vector_count
    outs = refs[at : at + len(shapes)]
    at += len(shapes)
    vector_outs = refs[at : at + vector_count]
    at += vector_count
    place = Place(line)
    place.greet(wide=True)
    plans = []
    for index, shape in enumerate(shapes):
        part = refs[at : at + REDUCE_SCRATCH]
        at += REDUCE_SCRATCH
        plans.append(reduce_steps(place, shape, sources[index], outs[index], part))
    vectors = []
    if vector_count:
        vectors = [VectorSum(place, vector_refs[0], vector_outs[0], refs[at : at + 3])]

    def rounds(*indices):
        for vector in vectors:
            for index in indices:
                vector.round(index)

    rounds(0)
    for plan in plans:
        plan[0]()
    plans[0][1]()
    rounds(1)
    plans[0][2]()
    rounds(2)
    for index, plan in enumerate(plans):
        ahead = plans[index + 1] if index + 1 < len(plans) else None
        if ahead is not None:
            ahead[1]()
        plan[3]()
        if ahead is not None:
            ahead[2]()
    rounds(3)
    for plan in plans:
        plan[4]()
    rounds(4, 5)
    for plan in plans:
        plan[5]()
    for vector in vectors:
        vector.finish()


def fast_reduce(groups, kinds, line, collective_id, vector=None):
    shapes = []
    blocks = []
    scratch = []
    for group, kind in zip(groups, kinds):
        rows, columns = group[0].shape
        shape = ReduceShape(kind, rows // (2 * line), columns, len(group))
        shapes.append(shape)
        blocks.extend(group)
        scratch.extend(shape.scratch(line))
    anywhere = pl.BlockSpec(memory_space=pl.ANY)
    local = pl.BlockSpec(memory_space=pltpu.VMEM)
    in_specs = [anywhere] * len(blocks)
    out_shape = [shape.out_shape() for shape in shapes]
    if vector is not None:
        blocks.append(vector)
        in_specs.append(local)
        out_shape.append(jax.ShapeDtypeStruct(vector.shape, F32))
        scratch.extend(VectorSum.scratch(vector.shape))
    return pl.pallas_call(
        functools.partial(reduce_kernel, shapes, line, 0 if vector is None else 1),
        in_specs=in_specs,
        out_specs=[local] * len(out_shape),
        out_shape=out_shape,
        scratch_shapes=scratch,
        compiler_params=pltpu.CompilerParams(
            collective_id=collective_id, has_side_effects=True, vmem_limit_bytes=60 << 20
        ),
        name="fast_reduce",
    )(*blocks)


PLANE = 4
CHIP = 2
LINE = 4


def small_plane():
    return lax.axis_size("rep") == PLANE and lax.axis_size("fsdp") == CHIP * LINE


def gather(block):
    return lax.all_gather(block, "fsdp", axis=0, tiled=True)


def gather_all(blocks, by_rows, collective_id):
    if small_plane():
        return fast_gather(blocks, LINE, by_rows, collective_id)
    return [gather(block) for block in blocks]


def scatter(block):
    return lax.psum_scatter(block.astype(BF16), "fsdp", scatter_dimension=0, tiled=True)


def scatter_columns(parts):
    count = lax.axis_size("rep")
    rows = parts[0].shape[0]
    split = [part.reshape(rows, count, -1) for part in parts]
    joined = jnp.concatenate(split, axis=2).reshape(rows, -1)
    own = lax.psum_scatter(joined, "rep", scatter_dimension=1, tiled=True)
    sizes = [part.shape[1] // count for part in parts]
    outs = []
    start = 0
    for size in sizes:
        outs.append(own[:, start : start + size].astype(F32))
        start += size
    return outs


def scatter_last(groups, vector, collective_id):
    if small_plane():
        *outs, total = fast_reduce(
            groups, ["four"] * len(groups), LINE, collective_id, vector
        )
        return [[out[index] for index in range(4)] for out in outs], total
    outs = [scatter_columns([scatter(item) for item in group]) for group in groups]
    return outs, lax.psum(vector, ("rep", "fsdp"))


def body(
    tokens,
    memory,
    prefix_len,
    bucket_table,
    rel_bias,
    gain_self,
    self_query,
    self_key,
    self_value,
    self_out,
    gain_cross,
    cross_query,
    cross_key,
    cross_value,
    cross_out,
    gain_feed,
    gate_weight,
    up_weight,
    down_weight,
    out_grad,
):
    nseq, length, width = tokens.shape
    shard = gain_self.shape[0]
    groups = width // shard
    entries = rel_bias.shape[0]
    ffn = gate_weight.shape[1]
    small = jnp.stack(
        [gain_self, gain_cross, gain_feed, jnp.pad(rel_bias, (0, shard - entries))], axis=1
    )
    small = jnp.pad(small, ((0, 0), (0, 2 * LANES - 4)))
    gate_up = gather(jnp.concatenate([gate_weight, up_weight], axis=1))
    down = gather(down_weight)
    (first,) = gather_all(
        [jnp.concatenate([self_query, self_key, self_value, small], axis=1)], [False], 1
    )
    second_own = jnp.concatenate(
        [self_out, cross_query, cross_key, cross_value, cross_out, small], axis=1
    )
    second_own, first = lax.optimization_barrier((second_own, first))
    (second,) = gather_all([second_own], [False], 2)
    qkv_proj = first[:, : 3 * width]
    vectors = first[:, 3 * width : 3 * width + 4].T
    gain_first = vectors[0:1].astype(F32)
    gain_second = vectors[1:2].astype(F32)
    gain_third = vectors[2:3].astype(F32)
    table = vectors[3].reshape(groups, shard)[:, :entries].reshape(NHEAD, BUCKETS)
    out_self = second[:, :width]
    query_cross = second[:, width : 2 * width]
    kv_cross = second[:, 2 * width : 4 * width]
    out_cross = second[:, 4 * width : 5 * width]
    gate_proj = gate_up[:, :ffn]
    up_proj = gate_up[:, ffn:]

    buckets_back = jnp.pad(bucket_table[::-1], (0, 1)).reshape(1, 2 * length)
    bias = skewed_bias(table, buckets_back, length)

    rows = nseq * length
    start_rows = tokens.reshape(rows, width).astype(F32)
    memory_rows = memory.reshape(-1, width)
    upstream = out_grad.reshape(rows, width)

    scale_first = inverse_rms(start_rows)
    normed_first = (start_rows * scale_first * gain_first).astype(BF16)
    qkv = matmul(normed_first, qkv_proj).astype(BF16)
    context, lse_self = run_self_forward(prefix_len, qkv, bias, nseq)
    middle = start_rows + matmul(context, out_self)
    scale_second = inverse_rms(middle)
    normed_second = (middle * scale_second * gain_second).astype(BF16)
    query_two = matmul(normed_second, query_cross).astype(BF16)
    kv_two = matmul(memory_rows, kv_cross).astype(BF16)
    context_two, lse_cross = run_cross_forward(query_two, kv_two, nseq)
    later = middle + matmul(context_two, out_cross)
    scale_third = inverse_rms(later)
    normed_third = (later * scale_third * gain_third).astype(BF16)
    gate_pre = matmul(normed_third, gate_proj)
    up_pre = matmul(normed_third, up_proj)
    hidden = (gelu_tanh(gate_pre) * up_pre).astype(BF16)
    result = (later + matmul(hidden, down)).astype(BF16)

    down_term = weight_term(hidden, upstream).astype(BF16)
    hidden_grad = back_term(upstream, down)
    gate_grad = (hidden_grad * up_pre * gelu_slope(gate_pre)).astype(BF16)
    lift_grad = (hidden_grad * gelu_tanh(gate_pre)).astype(BF16)
    gate_term = weight_term(normed_third, gate_grad).astype(BF16)
    up_term = weight_term(normed_third, lift_grad).astype(BF16)
    gate_grad, lift_grad, down_term, gate_term, up_term = lax.optimization_barrier(
        (gate_grad, lift_grad, down_term, gate_term, up_term)
    )
    down_own = scatter(down_term)
    gate_own = scatter(gate_term)
    up_own = scatter(up_term)
    third_grad = back_term(gate_grad, gate_proj) + back_term(lift_grad, up_proj)
    carry, gain_third_grad = norm_back(later, scale_third, gain_third, third_grad)
    later_grad = upstream.astype(F32) + carry
    branch_two = later_grad.astype(BF16)
    context_two_grad = back_term(branch_two, out_cross).astype(BF16)
    query_two_grad, key_two_grad, value_two_grad = run_cross_backward(
        query_two, kv_two, context_two_grad, context_two, lse_cross, nseq
    )
    cross_terms = [
        weight_term(normed_second, query_two_grad).astype(BF16),
        weight_term(memory_rows, key_two_grad).astype(BF16),
        weight_term(memory_rows, value_two_grad).astype(BF16),
        weight_term(context_two, branch_two).astype(BF16),
    ]
    memory_grad = back_term(key_two_grad, kv_cross[:, :width]) + back_term(
        value_two_grad, kv_cross[:, width:]
    )
    carry, gain_second_grad = norm_back(
        middle, scale_second, gain_second, back_term(query_two_grad, query_cross)
    )
    middle_grad = later_grad + carry
    branch_one = middle_grad.astype(BF16)
    context_grad = back_term(branch_one, out_self).astype(BF16)
    query_grad, key_grad, value_grad, diagonal = run_self_backward(
        prefix_len, qkv, context_grad, context, lse_self, bias, nseq
    )
    first_grad = (
        back_term(query_grad, qkv_proj[:, :width])
        + back_term(key_grad, qkv_proj[:, width : 2 * width])
        + back_term(value_grad, qkv_proj[:, 2 * width :])
    )
    carry, gain_first_grad = norm_back(start_rows, scale_first, gain_first, first_grad)
    tokens_grad = middle_grad + carry

    onehot = (
        buckets_back.reshape(-1, 1) == jnp.arange(BUCKETS, dtype=jnp.int32)[None, :]
    ).astype(F32)
    onehot = onehot * (jnp.arange(2 * length) < 2 * length - 1)[:, None]
    bias_grad = jnp.dot(
        diagonal.reshape(NHEAD, 2 * length), onehot, precision=lax.Precision.HIGHEST
    )
    bias_rows = jnp.pad(
        bias_grad.reshape(groups, entries), ((0, 0), (0, shard - entries))
    ).reshape(width)
    vector_block = jnp.pad(
        jnp.stack([gain_first_grad, gain_second_grad, gain_third_grad, bias_rows], axis=0),
        ((0, 4), (0, 0)),
    )
    self_terms = [
        weight_term(normed_first, query_grad).astype(BF16),
        weight_term(normed_first, key_grad).astype(BF16),
        weight_term(normed_first, value_grad).astype(BF16),
        weight_term(context, branch_one).astype(BF16),
    ]
    (cross_out_grads, self_out_grads), totals = scatter_last(
        [cross_terms, self_terms], vector_block, 3
    )
    own = lax.dynamic_slice(
        totals, (0, lax.axis_index("fsdp") * shard), (totals.shape[0], shard)
    )
    (down_weight_grad,) = scatter_columns([down_own])
    gate_weight_grad, up_weight_grad = scatter_columns([gate_own, up_own])
    return (
        result.reshape(tokens.shape),
        tokens_grad.reshape(tokens.shape),
        memory_grad.reshape(memory.shape),
        own[3, :entries],
        own[0],
        *self_out_grads,
        own[1],
        *cross_out_grads,
        own[2],
        gate_weight_grad,
        up_weight_grad,
        down_weight_grad,
    )


def solution(mesh):
    batch = P(("rep", "fsdp"), None, None)
    matrix = P("fsdp", None)
    vector = P("fsdp")
    split = P("fsdp", "rep")
    in_specs = (
        (batch, batch, P(("rep", "fsdp")), P(), vector, vector)
        + (matrix,) * 4
        + (vector,)
        + (matrix,) * 4
        + (vector,)
        + (matrix,) * 3
        + (batch,)
    )
    out_specs = (
        (batch, batch, batch, vector, vector)
        + (split,) * 4
        + (vector,)
        + (split,) * 4
        + (vector,)
        + (split,) * 3
    )
    return jax.shard_map(body, mesh=mesh, in_specs=in_specs, out_specs=out_specs, check_vma=False)
```

```python
import functools

import jax
import jax.numpy as jnp
from jax import lax
from jax.experimental import pallas as pl
from jax.experimental.pallas import tpu as pltpu
from jax.sharding import PartitionSpec as P

NHEAD = 12
DHEAD = 64
BUCKETS = 32
PAIRS = NHEAD // 2
LANES = 2 * DHEAD
PREFIX_MAX = 256

EPSILON = 1e-06
CUBIC_TERM = 0.044715
SQRT_TWO_PI = 0.7978845608028654
NEGATIVE = -1000000000.0

F32 = jnp.float32
BF16 = jnp.bfloat16
LAST_DIMS = (((1,), (1,)), ((), ()))
FIRST_DIMS = (((0,), (0,)), ((), ()))


def matmul(left_side, right_side):
    return jnp.dot(left_side, right_side, preferred_element_type=F32)


def weight_term(inputs, gradient):
    return lax.dot_general(inputs, gradient, FIRST_DIMS, preferred_element_type=F32)


def back_term(gradient, weight):
    return lax.dot_general(gradient, weight, LAST_DIMS, preferred_element_type=F32)


def inverse_rms(values):
    return lax.rsqrt(jnp.mean(values * values, axis=-1, keepdims=True) + EPSILON)


def norm_back(values, scale_rows, gain_vec, upstream):
    weighted = upstream * gain_vec
    gain_grad = jnp.sum(upstream * values * scale_rows, axis=0)
    input_grad = scale_rows * weighted - values * scale_rows * scale_rows * scale_rows * jnp.mean(
        values * weighted, axis=-1, keepdims=True
    )
    return (input_grad, gain_grad)


def one_head(rows, head):
    lane = lax.broadcasted_iota(jnp.int32, rows.shape, 1)
    keep = lane < DHEAD if head == 0 else lane >= DHEAD
    return jnp.where(keep, rows, jnp.zeros_like(rows))


def flipped(rows):
    return rows.astype(F32).T.astype(BF16)


def tree(fold, rows, groups):
    step = rows.shape[0] // groups
    total = rows[:step]
    for index in range(1, groups):
        total = fold(total, rows[index * step : (index + 1) * step])
    return total


def column_max(rows, groups):
    return jnp.max(tree(jnp.maximum, rows, groups), axis=0, keepdims=True)


def column_sum(rows, groups):
    return jnp.sum(tree(jnp.add, rows, groups), axis=0, keepdims=True)


def allowed_at(shape, key_start, query_start, prefix):
    key = lax.broadcasted_iota(jnp.int32, shape, 0) + key_start
    query = lax.broadcasted_iota(jnp.int32, shape, 1) + query_start
    return (key <= query) | (key < prefix)


def skew_kernel(table_ref, buckets_ref, out_ref):
    bucket = lax.broadcasted_iota(jnp.int32, (BUCKETS, buckets_ref.shape[1]), 0)
    onehot = (bucket == buckets_ref[...]).astype(BF16)
    by_offset = matmul(table_ref[...], onehot)
    width = out_ref.shape[2]
    total = by_offset.shape[1]
    for head in range(NHEAD):
        rows = jnp.broadcast_to(by_offset[head : head + 1], (LANES, total))
        rolled = pltpu.roll(rows, total - (LANES - 1), 1, stride=1, stride_axis=0)
        out_ref[head] = rolled[:, :width]


def skewed_bias(table, buckets_back, length):
    total = 2 * length
    return pl.pallas_call(
        skew_kernel,
        out_shape=jax.ShapeDtypeStruct((NHEAD, LANES, total - LANES), F32),
        name="skewed_bias",
    )(jnp.pad(table, ((0, 4), (0, 0))), buckets_back)


def self_forward(prefix_ref, query_ref, key_ref, value_ref, bias_ref, out_ref, lse_ref):
    length = query_ref.shape[0]
    block = 256
    prefix = prefix_ref[pl.program_id(0)]
    queries = query_ref[...]
    keys = key_ref[...]
    values = flipped(value_ref[...])
    for start in range(0, length, block):
        stop = start + block
        count = max(PREFIX_MAX, stop)
        outs = []
        for head in range(2):
            scores = back_term(keys[:count], one_head(queries[start:stop], head))
            parts = []
            for base in range(0, count, LANES):
                shift = length - LANES - base + start
                part = scores[base : base + LANES] + bias_ref[head, :, shift : shift + block]
                if base + LANES - 1 > start:
                    part = jnp.where(
                        allowed_at(part.shape, base, start, prefix), part, NEGATIVE
                    )
                parts.append(part)
            top = parts[0]
            for part in parts[1:]:
                top = jnp.maximum(top, part)
            top = column_max(top, 4)
            shares = [jnp.exp(part - top) for part in parts]
            total = shares[0]
            for share in shares[1:]:
                total = total + share
            total = column_sum(total, 4)
            share = jnp.concatenate([item.astype(BF16) for item in shares], axis=0)
            context = matmul(values[head * DHEAD : (head + 1) * DHEAD, :count], share)
            outs.append(context * (1.0 / total))
            lse_ref[head : head + 1, start:stop] = top + jnp.log(total)
        out_ref[start:stop, :] = jnp.concatenate(outs, axis=0).T.astype(BF16)


def cross_forward(query_ref, key_ref, value_ref, out_ref, lse_ref):
    keys = key_ref[...]
    values = flipped(value_ref[...])
    queries = query_ref[...]
    ahead = [back_term(keys, one_head(queries, head)) for head in range(2)]
    outs = []
    for head in range(2):
        scores = ahead[head]
        top = column_max(scores, 16)
        share = jnp.exp(scores - top)
        total = column_sum(share, 16)
        context = matmul(values[head * DHEAD : (head + 1) * DHEAD], share.astype(BF16))
        outs.append(context * (1.0 / total))
        lse_ref[head : head + 1, :] = top + jnp.log(total)
    out_ref[...] = jnp.concatenate(outs, axis=0).T.astype(BF16)


def cross_backward(
    query_ref, key_ref, value_ref, up_ref, context_ref, lse_ref, dq_ref, dk_ref, dv_ref
):
    length = query_ref.shape[0]
    block = 256
    keys = key_ref[...]
    values = value_ref[...]
    queries = query_ref[...]
    upstream = up_ref[...]
    keys_flipped = flipped(keys)
    inner = (upstream.astype(F32) * context_ref[...].astype(F32)).T
    key_grad = None
    value_grad = None
    for start in range(0, length, block):
        rows = slice(start, start + block)
        grads = []
        for head in range(2):
            sub = slice(head * DHEAD, (head + 1) * DHEAD)
            query = one_head(queries[rows], head)
            above = one_head(upstream[rows], head)
            row_inner = jnp.sum(inner[sub, rows], axis=0, keepdims=True)
            shares = jnp.exp(back_term(keys, query) - lse_ref[head : head + 1, rows])
            share_grad = back_term(values, above)
            score_grad = (shares * (share_grad - row_inner)).astype(BF16)
            value_part = matmul(shares.astype(BF16), above)
            key_part = matmul(score_grad, query)
            value_grad = value_part if value_grad is None else value_grad + value_part
            key_grad = key_part if key_grad is None else key_grad + key_part
            grads.append(matmul(keys_flipped[sub], score_grad))
        dq_ref[rows, :] = jnp.concatenate(grads, axis=0).T.astype(BF16)
    dk_ref[...] = key_grad.astype(BF16)
    dv_ref[...] = value_grad.astype(BF16)


def self_backward(
    prefix_ref,
    query_ref,
    key_ref,
    value_ref,
    up_ref,
    context_ref,
    lse_ref,
    bias_ref,
    dq_ref,
    dk_ref,
    dv_ref,
    diag_ref,
    acc_ref,
):
    length = query_ref.shape[0]
    block = 256
    step = pl.program_id(1)
    prefix = prefix_ref[step]

    @pl.when(step == 0)
    def _():
        acc_ref[...] = jnp.zeros_like(acc_ref)

    queries = query_ref[...]
    keys = key_ref[...]
    values = value_ref[...]
    upstream = up_ref[...]
    keys_flipped = flipped(keys)
    inner = (upstream.astype(F32) * context_ref[...].astype(F32)).T
    count_all = length // block
    key_grad = [None] * count_all
    value_grad = [None] * count_all
    for start in range(0, length, block):
        stop = start + block
        count = max(PREFIX_MAX, stop)
        rows = slice(start, stop)
        grads = []
        for head in range(2):
            sub = slice(head * DHEAD, (head + 1) * DHEAD)
            query = one_head(queries[rows], head)
            above = one_head(upstream[rows], head)
            row_inner = jnp.sum(inner[sub, rows], axis=0, keepdims=True)
            row_lse = lse_ref[head : head + 1, rows]
            scores = back_term(keys[:count], query)
            share_grad = back_term(values[:count], above)
            shares = []
            score_grads = []
            for base in range(0, count, LANES):
                part = slice(base, base + LANES)
                shift = length - LANES - base + start
                share = jnp.exp(
                    scores[part] + bias_ref[head, :, shift : shift + block] - row_lse
                )
                if base + LANES - 1 > start:
                    share = jnp.where(allowed_at(share.shape, base, start, prefix), share, 0.0)
                score_grad = share * (share_grad[part] - row_inner)
                acc_ref[head, :, shift : shift + block] += score_grad
                shares.append(share.astype(BF16))
                score_grads.append(score_grad.astype(BF16))
            share = jnp.concatenate(shares, axis=0)
            score_grad = jnp.concatenate(score_grads, axis=0)
            value_part = matmul(share, above)
            key_part = matmul(score_grad, query)
            for index in range(count // block):
                part = slice(index * block, (index + 1) * block)
                if value_grad[index] is None:
                    value_grad[index] = value_part[part]
                    key_grad[index] = key_part[part]
                else:
                    value_grad[index] = value_grad[index] + value_part[part]
                    key_grad[index] = key_grad[index] + key_part[part]
            grads.append(matmul(keys_flipped[sub, :count], score_grad))
        dq_ref[rows, :] = jnp.concatenate(grads, axis=0).T.astype(BF16)
    for index in range(count_all):
        part = slice(index * block, (index + 1) * block)
        dk_ref[part, :] = key_grad[index].astype(BF16)
        dv_ref[part, :] = value_grad[index].astype(BF16)

    @pl.when(step == pl.num_programs(1) - 1)
    def _():
        total = 2 * length
        for head in range(2):
            rows = jnp.concatenate([acc_ref[head], jnp.zeros((LANES, LANES), F32)], axis=1)
            half = LANES // 2
            while half >= 1:
                rows = rows[:half] + pltpu.roll(rows[half:], total - half, 1)
                half //= 2
            diag_ref[head : head + 1, :] = pltpu.roll(rows, LANES - 1, 1)


def spec(shape, index):
    return pl.BlockSpec(shape, index)


def run_self_forward(prefix, qkv, bias, nseq):
    length = qkv.shape[0] // nseq
    return pl.pallas_call(
        self_forward,
        grid_spec=pltpu.PrefetchScalarGridSpec(
            num_scalar_prefetch=1,
            grid=(nseq, PAIRS),
            in_specs=[
                spec((length, LANES), lambda s, p, _: (s, p)),
                spec((length, LANES), lambda s, p, _: (s, PAIRS + p)),
                spec((length, LANES), lambda s, p, _: (s, 2 * PAIRS + p)),
                spec((2, LANES, 2 * length - LANES), lambda s, p, _: (p, 0, 0)),
            ],
            out_specs=[
                spec((length, LANES), lambda s, p, _: (s, p)),
                spec((None, None, 2, length), lambda s, p, _: (s, p, 0, 0)),
            ],
        ),
        out_shape=[
            jax.ShapeDtypeStruct((qkv.shape[0], PAIRS * LANES), BF16),
            jax.ShapeDtypeStruct((nseq, PAIRS, 2, length), F32),
        ],
        cost_estimate=pl.CostEstimate(
            flops=20_000_000_000, bytes_accessed=12_000_000, transcendentals=0
        ),
        name="self_forward",
    )(prefix, qkv, qkv, qkv, bias)


def run_cross_forward(query, kv, nseq):
    length = query.shape[0] // nseq
    count = kv.shape[0] // nseq
    return pl.pallas_call(
        cross_forward,
        grid=(nseq, PAIRS),
        in_specs=[
            spec((length, LANES), lambda s, p: (s, p)),
            spec((count, LANES), lambda s, p: (s, p)),
            spec((count, LANES), lambda s, p: (s, PAIRS + p)),
        ],
        out_specs=[
            spec((length, LANES), lambda s, p: (s, p)),
            spec((None, None, 2, length), lambda s, p: (s, p, 0, 0)),
        ],
        out_shape=[
            jax.ShapeDtypeStruct(query.shape, BF16),
            jax.ShapeDtypeStruct((nseq, PAIRS, 2, length), F32),
        ],
        cost_estimate=pl.CostEstimate(
            flops=24_000_000_000, bytes_accessed=10_000_000, transcendentals=0
        ),
        name="cross_forward",
    )(query, kv, kv)


def run_cross_backward(query, kv, upstream, context, lse, nseq):
    length = query.shape[0] // nseq
    count = kv.shape[0] // nseq
    rows = spec((length, LANES), lambda s, p: (s, p))
    wide = spec((count, LANES), lambda s, p: (s, p))
    return pl.pallas_call(
        cross_backward,
        grid=(nseq, PAIRS),
        in_specs=[
            rows,
            wide,
            spec((count, LANES), lambda s, p: (s, PAIRS + p)),
            rows,
            rows,
            spec((None, None, 2, length), lambda s, p: (s, p, 0, 0)),
        ],
        out_specs=[rows, wide, wide],
        out_shape=[
            jax.ShapeDtypeStruct(query.shape, BF16),
            jax.ShapeDtypeStruct((kv.shape[0], PAIRS * LANES), BF16),
            jax.ShapeDtypeStruct((kv.shape[0], PAIRS * LANES), BF16),
        ],
        cost_estimate=pl.CostEstimate(
            flops=36_000_000_000, bytes_accessed=20_000_000, transcendentals=0
        ),
        name="cross_backward",
    )(query, kv, kv, upstream, context, lse)


def run_self_backward(prefix, qkv, upstream, context, lse, bias, nseq):
    length = qkv.shape[0] // nseq
    rows = spec((length, LANES), lambda p, s, _: (s, p))
    return pl.pallas_call(
        self_backward,
        grid_spec=pltpu.PrefetchScalarGridSpec(
            num_scalar_prefetch=1,
            grid=(PAIRS, nseq),
            in_specs=[
                rows,
                spec((length, LANES), lambda p, s, _: (s, PAIRS + p)),
                spec((length, LANES), lambda p, s, _: (s, 2 * PAIRS + p)),
                rows,
                rows,
                spec((None, None, 2, length), lambda p, s, _: (s, p, 0, 0)),
                spec((2, LANES, 2 * length - LANES), lambda p, s, _: (p, 0, 0)),
            ],
            out_specs=[
                rows,
                rows,
                rows,
                spec((None, 2, 2 * length), lambda p, s, _: (p, 0, 0)),
            ],
            scratch_shapes=[pltpu.VMEM((2, LANES, 2 * length - LANES), F32)],
        ),
        out_shape=[jax.ShapeDtypeStruct(upstream.shape, BF16)] * 3
        + [jax.ShapeDtypeStruct((PAIRS, 2, 2 * length), F32)],
        cost_estimate=pl.CostEstimate(
            flops=24_000_000_000, bytes_accessed=20_000_000, transcendentals=0
        ),
        name="self_backward",
    )(prefix, qkv, qkv, qkv, upstream, context, lse, bias)


FEED_BLOCK = 256


def feed_kernel(
    middle_ref,
    context_ref,
    out_proj_ref,
    gain_ref,
    up_grad_ref,
    gate_ref,
    up_ref,
    down_ref,
    result_ref,
    later_grad_ref,
    branch_ref,
    context_grad_ref,
    gain_grad_ref,
    down_term_ref,
    pair_term_ref,
    later_ref,
    normed_ref,
    flipped_ref,
    result_acc,
    third_acc,
):
    step = pl.program_id(0)
    count = middle_ref.shape[0]
    chunk = 256
    chunks = [slice(start, start + chunk) for start in range(0, count, chunk)]

    @pl.when(step == 0)
    def _():
        for rows in chunks:
            later = middle_ref[rows] + matmul(context_ref[rows], out_proj_ref[...])
            normed = (later * inverse_rms(later) * gain_ref[...]).astype(BF16)
            later_ref[rows] = later
            normed_ref[rows] = normed
            flipped_ref[:, rows] = flipped(normed)
            result_acc[rows] = jnp.zeros_like(later)
            third_acc[rows] = jnp.zeros_like(later)

    gate_proj = gate_ref[...]
    up_proj = up_ref[...]
    down_proj = down_ref[...]
    hidden_flipped = []
    gate_grads = []
    lift_grads = []
    for rows in chunks:
        normed = normed_ref[rows]
        gate = matmul(normed, gate_proj)
        lift = matmul(normed, up_proj)
        hidden_grad = back_term(up_grad_ref[rows], down_proj)
        square = gate * gate
        tangent = jnp.tanh(SQRT_TWO_PI * gate * (1.0 + CUBIC_TERM * square))
        half = 0.5 * (1.0 + tangent)
        active = gate * half
        slope = half + 0.5 * gate * (1.0 - tangent * tangent) * (
            SQRT_TWO_PI + 3.0 * CUBIC_TERM * SQRT_TWO_PI * square
        )
        hidden = active * lift
        gate_grad = (hidden_grad * lift * slope).astype(BF16)
        lift_grad = (hidden_grad * active).astype(BF16)
        hidden_flipped.append(hidden.T.astype(BF16))
        gate_grads.append(gate_grad)
        lift_grads.append(lift_grad)
        result_acc[rows] += matmul(hidden.astype(BF16), down_proj)
        third_acc[rows] += back_term(gate_grad, gate_proj) + back_term(lift_grad, up_proj)
    hidden_flipped = jnp.concatenate(hidden_flipped, axis=1)
    down_term_ref[...] = matmul(hidden_flipped, up_grad_ref[...]).astype(BF16)
    gate_grads = jnp.concatenate(gate_grads, axis=0)
    lift_grads = jnp.concatenate(lift_grads, axis=0)
    pair_term_ref[:, :FEED_BLOCK] = matmul(flipped_ref[...], gate_grads).astype(BF16)
    pair_term_ref[:, FEED_BLOCK:] = matmul(flipped_ref[...], lift_grads).astype(BF16)

    @pl.when(step == pl.num_programs(0) - 1)
    def _():
        gain_grad = jnp.zeros(gain_ref.shape, F32)
        for rows in chunks:
            later = later_ref[rows]
            result_ref[rows] = (later + result_acc[rows]).astype(BF16)
            carry, part = norm_back(later, inverse_rms(later), gain_ref[...], third_acc[rows])
            gain_grad = gain_grad + part[None, :]
            later_grad = up_grad_ref[rows].astype(F32) + carry
            branch = later_grad.astype(BF16)
            later_grad_ref[rows] = later_grad
            branch_ref[rows] = branch
            context_grad_ref[rows] = back_term(branch, out_proj_ref[...]).astype(BF16)
        gain_grad_ref[...] = gain_grad


def run_feed(middle, context, out_proj, gain, upstream, gate_up, down):
    count, width = middle.shape
    ffn = down.shape[0]
    blocks = ffn // FEED_BLOCK

    def whole(shape, **extra):
        return pl.BlockSpec(shape, lambda j: (0, 0), **extra)

    once = {"pipeline_mode": pl.Buffered(1)}
    rows = (count, width)
    return pl.pallas_call(
        feed_kernel,
        grid=(blocks,),
        in_specs=[
            whole(rows, **once),
            whole(rows, **once),
            whole((width, width), **once),
            whole((1, width)),
            whole(rows, **once),
            spec((width, FEED_BLOCK), lambda j: (0, j)),
            spec((width, FEED_BLOCK), lambda j: (0, blocks + j)),
            spec((FEED_BLOCK, width), lambda j: (j, 0)),
        ],
        out_specs=[
            whole(rows),
            whole(rows),
            whole(rows),
            whole(rows),
            whole((1, width)),
            spec((FEED_BLOCK, width), lambda j: (j, 0)),
            spec((width, 2 * FEED_BLOCK), lambda j: (0, j)),
        ],
        out_shape=[
            jax.ShapeDtypeStruct(rows, BF16),
            jax.ShapeDtypeStruct(rows, F32),
            jax.ShapeDtypeStruct(rows, BF16),
            jax.ShapeDtypeStruct(rows, BF16),
            jax.ShapeDtypeStruct((1, width), F32),
            jax.ShapeDtypeStruct((ffn, width), BF16),
            jax.ShapeDtypeStruct((width, 2 * ffn), BF16),
        ],
        scratch_shapes=[
            pltpu.VMEM(rows, F32),
            pltpu.VMEM(rows, BF16),
            pltpu.VMEM((width, count), BF16),
            pltpu.VMEM(rows, F32),
            pltpu.VMEM(rows, F32),
        ],
        cost_estimate=pl.CostEstimate(
            flops=32_000_000_000, bytes_accessed=40_000_000, transcendentals=0
        ),
        compiler_params=pltpu.CompilerParams(vmem_limit_bytes=60 << 20),
        name="feed",
    )(middle, context, out_proj, gain, upstream, gate_up, gate_up, down)


MESH = pl.DeviceIdType.MESH


class Place:
    def __init__(self, line):
        self.line = line
        rep = lax.axis_index("rep")
        fsdp = lax.axis_index("fsdp")
        self.rep = rep
        self.fsdp = fsdp
        self.y = rep // 2
        self.x = rep % 2
        self.z = fsdp // 2
        self.core = fsdp % 2
        self.x_rep = self.y * 2 + 1 - self.x
        self.y_rep = (1 - self.y) * 2 + self.x

    def at_x(self):
        return {"rep": self.x_rep, "fsdp": self.fsdp}

    def at_y(self):
        return {"rep": self.y_rep, "fsdp": self.fsdp}

    def at_partner(self):
        return {"rep": self.rep, "fsdp": self.z * 2 + 1 - self.core}

    def at_line(self, side):
        return {"rep": self.rep, "fsdp": self.fsdp + (2 if side == 0 else -2)}

    def has_next(self, side):
        return self.z < self.line - 1 if side == 0 else self.z > 0

    def has_last(self, side):
        return self.has_next(1 - side)

    def arrives(self, side, hop):
        if side == 0:
            return self.z - 1 - hop >= 0
        return self.z + 1 + hop <= self.line - 1

    def source(self, side, hop):
        return self.z - 1 - hop if side == 0 else self.z + 1 + hop

    def at_far(self):
        half = self.line // 2
        return {"rep": self.rep, "fsdp": (self.z + half) % self.line * 2 + self.core}

    def greet(self, wide=False):
        barrier = pltpu.get_barrier_semaphore()
        targets = [self.at_x(), self.at_y(), self.at_partner()]
        if wide:
            targets.append({"rep": 3 - self.rep, "fsdp": self.fsdp})
            targets.append(self.at_far())
        for target in targets:
            pl.semaphore_signal(barrier, inc=1, device_id=target, device_id_type=MESH)
        for side in range(2):

            @pl.when(self.has_next(side))
            def _():
                pl.semaphore_signal(
                    barrier, inc=1, device_id=self.at_line(side), device_id_type=MESH
                )

        count = len(targets)
        for side in range(2):
            count = count + jnp.where(self.has_next(side), 1, 0)
        pl.semaphore_wait(barrier, count)


def remote(source, target, send, recv, device):
    return pltpu.make_async_remote_copy(
        src_ref=source,
        dst_ref=target,
        send_sem=send,
        recv_sem=recv,
        device_id=device,
        device_id_type=MESH,
    )


class GatherShape:
    def __init__(self, parts, by_rows):
        self.rows = parts[0].shape[0]
        self.widths = [part.shape[1] for part in parts]
        self.starts = [sum(self.widths[:index]) for index in range(len(parts))]
        self.columns = sum(self.widths)
        self.by_rows = by_rows

    def full(self, ref, owner):
        return ref.at[pl.ds(pl.multiple_of(owner * self.rows, 32), self.rows)]

    def piece(self, ref, owner, part, half=None):
        base = owner * self.rows
        if self.by_rows:
            rows = self.rows // 4
            base = base + part * rows
        else:
            rows = self.rows
        if half is not None:
            rows = rows // 2
            base = base + half * rows
        row_slice = pl.ds(pl.multiple_of(base, 16), rows)
        if self.by_rows:
            return ref.at[row_slice]
        width = self.columns // 4
        return ref.at[row_slice, pl.ds(pl.multiple_of(part * width, LANES), width)]


def gather_sems(line):
    hops = line - 1
    return [pltpu.SemaphoreType.DMA((5, 2, 2, hops)), pltpu.SemaphoreType.DMA((4,))] + [
        pltpu.SemaphoreType.DMA((2, 2, hops))
    ]


def gather_steps(place, shape, src, own, dst, sems):
    hop_sem, own_sem, pair_sem = sems
    hops = place.line - 1
    me = place.fsdp

    def load(index):
        at = pl.ds(shape.starts[index], shape.widths[index])
        return pltpu.make_async_copy(src[index], own.at[:, at], own_sem.at[0])

    def loaded():
        return pltpu.make_async_copy(own, own, own_sem.at[0])

    def keep():
        return pltpu.make_async_copy(own, shape.full(dst, me), own_sem.at[1])

    def own_pair():
        return remote(
            own, shape.full(dst, me), own_sem.at[2], own_sem.at[3], place.at_partner()
        )

    def owner(side, hop):
        return place.source(side, hop) * 2 + place.core

    def line_first(side):
        return remote(
            shape.piece(own, 0, place.rep),
            shape.piece(dst, me, place.rep),
            hop_sem.at[0, 0, side, 0],
            hop_sem.at[0, 1, side, 0],
            place.at_line(side),
        )

    def moved(kind, side, hop, block, device):
        return remote(
            block, block, hop_sem.at[kind, 0, side, hop], hop_sem.at[kind, 1, side, hop], device
        )

    def line_next(side, hop):
        block = shape.piece(dst, owner(side, hop - 1), place.rep)
        return moved(0, side, hop, block, place.at_line(side))

    def line_arrival(side, hop):
        block = shape.piece(dst, owner(side, hop), place.rep)
        return moved(0, side, hop, block, place.at_line(side))

    def plane(axis, side, hop):
        block = shape.piece(dst, owner(side, hop), place.rep)
        return moved(1 + axis, side, hop, block, place.at_x() if axis == 0 else place.at_y())

    def cross(axis, side, hop):
        part = place.x_rep if axis == 1 else place.y_rep
        block = shape.piece(dst, owner(side, hop), part, 1 - axis)
        return moved(3 + axis, side, hop, block, place.at_x() if axis == 0 else place.at_y())

    def pair(side, hop):
        block = shape.full(dst, owner(side, hop))
        return remote(
            block, block, pair_sem.at[0, side, hop], pair_sem.at[1, side, hop], place.at_partner()
        )

    def each(fn):
        def run():
            for hop in range(hops):
                for side in range(2):
                    pl.when(place.arrives(side, hop))(functools.partial(fn, side, hop))

        return run

    def start():
        for index in range(len(src)):
            load(index).start()
        loaded().wait()
        for side in range(2):
            pl.when(place.has_next(side))(lambda side=side: line_first(side).start())
        own_pair().start()
        keep().start()

    def arrive(side, hop):
        line_arrival(side, hop).wait_recv()
        if hop + 1 < hops:
            pl.when(place.has_next(side))(lambda: line_next(side, hop + 1).start())
        plane(0, side, hop).start()
        plane(1, side, hop).start()

    def turn(side, hop):
        plane(0, side, hop).wait_recv()
        cross(1, side, hop).start()
        plane(1, side, hop).wait_recv()
        cross(0, side, hop).start()

    def hand(side, hop):
        cross(0, side, hop).wait_recv()
        cross(1, side, hop).wait_recv()
        pair(side, hop).start()

    def finish():
        def last(side, hop):
            pair(side, hop).wait()
            for axis in range(2):
                plane(axis, side, hop).wait_send()
                cross(axis, side, hop).wait_send()
            if hop + 1 < hops:
                pl.when(place.has_next(side))(lambda: line_next(side, hop + 1).wait_send())

        each(last)()
        for side in range(2):
            pl.when(place.has_next(side))(lambda side=side: line_first(side).wait_send())
        own_pair().wait()
        keep().wait()

    return start, each(arrive), each(turn), each(hand), finish


def gather_kernel(shapes, line, *refs):
    count = len(shapes)
    sources = []
    at = 0
    for shape in shapes:
        sources.append(refs[at : at + len(shape.widths)])
        at += len(shape.widths)
    targets = refs[at : at + count]
    scratch = refs[at + count :]
    place = Place(line)
    place.greet()
    plans = []
    for index, shape in enumerate(shapes):
        own, *sems = scratch[4 * index : 4 * index + 4]
        plans.append(gather_steps(place, shape, sources[index], own, targets[index], sems))
    for stage in range(5):
        for plan in plans:
            plan[stage]()


def fast_gather(groups, line, by_rows, collective_id):
    shapes = [GatherShape(group, flag) for group, flag in zip(groups, by_rows)]
    scratch = []
    for shape in shapes:
        scratch.append(pltpu.VMEM((shape.rows, shape.columns), BF16))
        scratch.extend(gather_sems(line))
    anywhere = pl.BlockSpec(memory_space=pl.ANY)
    blocks = [block for group in groups for block in group]
    return pl.pallas_call(
        functools.partial(gather_kernel, shapes, line),
        in_specs=[anywhere] * len(blocks),
        out_specs=[anywhere] * len(groups),
        out_shape=[
            jax.ShapeDtypeStruct((2 * line * s.rows, s.columns), BF16) for s in shapes
        ],
        scratch_shapes=scratch,
        compiler_params=pltpu.CompilerParams(collective_id=collective_id, has_side_effects=True),
        name="fast_gather",
    )(*blocks)


class ReduceShape:
    def __init__(self, kind, rows, columns, sources):
        self.kind = kind
        self.rows = rows
        self.sources = sources
        if kind == "rows":
            self.block = (rows // 8, columns)
        elif kind == "pair":
            self.block = (rows // 2, columns // 2)
        else:
            self.block = (rows // 2, columns)
        self.exchange = kind != "pair"
        self.part_rows = rows // 4 if kind == "rows" else rows
        self.part_columns = columns // 4

    def pieces(self, refs, owner, half, quarter):
        rows, columns = self.block
        if self.kind == "rows":
            base = owner * self.rows + quarter * (self.rows // 4) + half * rows
            return [(refs[0].at[pl.ds(pl.multiple_of(base, 16), rows)], 0, columns)]
        at = pl.ds(pl.multiple_of(owner * self.rows + half * rows, 16), rows)
        if self.kind == "four":
            return [(refs[quarter].at[at], 0, columns)]
        width = columns // 2
        cut = slice(quarter * width, (quarter + 1) * width)
        return [(refs[index].at[at, cut], index * width, width) for index in range(2)]

    def out_shape(self):
        if self.exchange:
            return jax.ShapeDtypeStruct((4, self.part_rows, self.part_columns), F32)
        return jax.ShapeDtypeStruct((self.rows, self.block[1]), F32)

    def scratch(self, line):
        rows, columns = self.block
        dma = pltpu.SemaphoreType.DMA
        buffers = [
            pltpu.VMEM((line, 8, rows, columns), BF16),
            pltpu.VMEM((line, 8, rows, columns), BF16),
            pltpu.VMEM((line, 2, 2, rows, columns), BF16),
            pltpu.VMEM((line, 2, rows, columns), BF16),
            pltpu.VMEM((line, 2, rows, columns), BF16),
            pltpu.VMEM((2, line, 2, rows, columns), BF16),
            pltpu.VMEM((4, self.part_rows, self.part_columns), F32),
            pltpu.VMEM((4, self.part_rows, self.part_columns), F32),
            dma((line,)),
            dma((2, line)),
            dma((2, line, 2)),
            dma((2, line, 2)),
            dma((2, 2, line)),
            dma((2, 3)),
        ]
        return buffers


REDUCE_SCRATCH = 14


def added(left, right):
    return (left.astype(F32) + right.astype(F32)).astype(BF16)


def reduce_steps(place, shape, refs, out, scratch):
    own, other, first_in, second_in, total, line_in, parts, gathered = scratch[:8]
    load_sem, pair_sem, first_sem, second_sem, line_sem, swap_sem = scratch[8:]
    line = place.line
    near = (place.x, place.y)
    far = (place.y, place.x)
    near_device = (place.at_x(), place.at_y())
    far_device = (place.at_y(), place.at_x())

    def quarter_of(half, index):
        high, low = index // 2, index % 2
        return low * 2 + high if half == 0 else high * 2 + low

    def start(z):
        for half in range(2):
            for index in range(4):
                quarter = quarter_of(half, index)
                slot = half * 4 + index
                mine = shape.pieces(refs, 2 * z + place.core, half, quarter)
                theirs = shape.pieces(refs, 2 * z + 1 - place.core, half, quarter)
                for (view, column, width), (view_two, _, _) in zip(mine, theirs):
                    cut = pl.ds(column, width)
                    remote(
                        view_two,
                        other.at[z, slot, :, cut],
                        pair_sem.at[0, z],
                        pair_sem.at[1, z],
                        place.at_partner(),
                    ).start()
                    pltpu.make_async_copy(
                        view, own.at[z, slot, :, cut], load_sem.at[z]
                    ).start()

    def pair_all(z):
        return remote(
            own.at[z], other.at[z], pair_sem.at[0, z], pair_sem.at[1, z], place.at_partner()
        )

    def first(z, half):
        return remote(
            own.at[z, pl.ds(half * 4 + (1 - near[half]) * 2, 2)],
            first_in.at[z, half],
            first_sem.at[0, z, half],
            first_sem.at[1, z, half],
            near_device[half],
        )

    def second(z, half):
        return remote(
            own.at[z, half * 4 + near[half] * 2 + 1 - far[half]],
            second_in.at[z, half],
            second_sem.at[0, z, half],
            second_sem.at[1, z, half],
            far_device[half],
        )

    def along(z, side):
        return remote(
            total.at[z],
            line_in.at[side, z],
            line_sem.at[0, side, z],
            line_sem.at[1, side, z],
            place.at_line(side),
        )

    def pair_add(z):
        pltpu.make_async_copy(own.at[z], own.at[z], load_sem.at[z]).wait()
        pair_all(z).wait_recv()

        @pl.loop(0, 8)
        def _(slot):
            own[z, slot] = added(own[z, slot], other[z, slot])

        for half in range(2):
            first(z, half).start()

    def first_add(z):
        for half in range(2):
            first(z, half).wait_recv()
            base = half * 4 + near[half] * 2

            @pl.loop(0, 2)
            def _(index):
                own[z, base + index] = added(own[z, base + index], first_in[z, half, index])

            second(z, half).start()

    def second_add(z):
        for half in range(2):
            second(z, half).wait_recv()
            mine = half * 4 + near[half] * 2 + far[half]
            total[z, half] = added(own[z, mine], second_in[z, half])

    def line_send(z, side):
        ahead = place.z < z if side == 0 else place.z > z

        @pl.when(ahead)
        def _():
            @pl.when(place.has_last(side))
            def _():
                along(z, side).wait_recv()

                @pl.loop(0, 2)
                def _(half):
                    total[z, half] = added(total[z, half], line_in[side, z, half])

            along(z, side).start()

    def line_end(z):
        @pl.when(place.z == z)
        def _():
            for side in range(2):
                pl.when(place.has_last(side))(lambda: along(z, side).wait_recv())

    def swap(rep_slot, device, index):
        return remote(
            parts.at[rep_slot],
            gathered.at[place.rep],
            swap_sem.at[0, index],
            swap_sem.at[1, index],
            device,
        )

    def swaps():
        corner = 3 - place.rep
        return [
            swap(place.x_rep, place.at_x(), 0),
            swap(place.y_rep, place.at_y(), 1),
            swap(corner, {"rep": corner, "fsdp": place.fsdp}, 2),
        ]

    def finish():
        rows, columns = shape.block
        me = place.z
        for half in range(2):
            result = total[me, half].astype(F32)
            for side in range(2):
                extra = line_in[side, me, half].astype(F32)
                result = result + jnp.where(place.has_last(side), extra, 0.0)
            at = slice(half * rows, (half + 1) * rows)
            if shape.exchange:
                width = shape.part_columns
                for index in range(4):
                    parts[index, at, :] = result[:, index * width : (index + 1) * width]
            else:
                out[at, :] = result
        if shape.exchange:
            for copy in swaps():
                copy.start()
            gathered[place.rep] = parts[place.rep]

    def drain():
        if shape.exchange:
            for copy in swaps():
                copy.wait()
            out[...] = gathered[...]
        for z in range(line):
            pair_all(z).wait_send()
            for half in range(2):
                first(z, half).wait_send()
                second(z, half).wait_send()
            for side in range(2):
                ahead = place.z < z if side == 0 else place.z > z
                pl.when(ahead)(lambda: along(z, side).wait_send())

    order = [line - 1, 0] + [z for z in range(line - 2, 0, -1)]

    def begin():
        for z in order:
            start(z)

    def pairs():
        for z in order:
            pair_add(z)

    def firsts():
        for z in order:
            first_add(z)

    def seconds():
        for index, z in enumerate(order):
            second_add(z)
            if index > 0:
                line_send(order[index - 1], 0)
                line_send(order[index - 1], 1)
        line_send(order[-1], 0)
        line_send(order[-1], 1)

    def close():
        for z in range(line):
            line_end(z)
        finish()

    return begin, pairs, firsts, seconds, close, drain


class VectorSum:
    def __init__(self, place, source, out, scratch):
        self.place = place
        self.source = source
        self.out = out
        self.current, self.incoming, self.sems = scratch
        side = place.z % 2
        near = place.fsdp + 2 - 4 * side
        self.devices = [
            place.at_partner(),
            place.at_x(),
            place.at_y(),
            {"rep": place.rep, "fsdp": near},
            place.at_far(),
        ]

    @staticmethod
    def scratch(shape):
        return [
            pltpu.VMEM((6,) + shape, F32),
            pltpu.VMEM((5,) + shape, F32),
            pltpu.SemaphoreType.DMA((2, 5)),
        ]

    def copy(self, index):
        return remote(
            self.current.at[index],
            self.incoming.at[index],
            self.sems.at[0, index],
            self.sems.at[1, index],
            self.devices[index],
        )

    def round(self, index):
        if index == 0:
            self.current[0] = self.source[...]
        else:
            self.copy(index - 1).wait_recv()
            self.current[index] = self.current[index - 1] + self.incoming[index - 1]
        if index < 5:
            self.copy(index).start()

    def finish(self):
        self.out[...] = self.current[5]
        for index in range(5):
            self.copy(index).wait_send()


def reduce_kernel(shapes, line, vector_count, *refs):
    sources = []
    at = 0
    for shape in shapes:
        sources.append(refs[at : at + shape.sources])
        at += shape.sources
    vector_refs = refs[at : at + vector_count]
    at += vector_count
    outs = refs[at : at + len(shapes)]
    at += len(shapes)
    vector_outs = refs[at : at + vector_count]
    at += vector_count
    place = Place(line)
    place.greet(wide=True)
    plans = []
    for index, shape in enumerate(shapes):
        part = refs[at : at + REDUCE_SCRATCH]
        at += REDUCE_SCRATCH
        plans.append(reduce_steps(place, shape, sources[index], outs[index], part))
    vectors = []
    if vector_count:
        vectors = [VectorSum(place, vector_refs[0], vector_outs[0], refs[at : at + 3])]

    def rounds(*indices):
        for vector in vectors:
            for index in indices:
                vector.round(index)

    rounds(0)
    for plan in plans:
        plan[0]()
    plans[0][1]()
    rounds(1)
    plans[0][2]()
    rounds(2)
    for index, plan in enumerate(plans):
        ahead = plans[index + 1] if index + 1 < len(plans) else None
        if ahead is not None:
            ahead[1]()
        plan[3]()
        if ahead is not None:
            ahead[2]()
    rounds(3)
    for plan in plans:
        plan[4]()
    rounds(4, 5)
    for plan in plans:
        plan[5]()
    for vector in vectors:
        vector.finish()


def fast_reduce(groups, kinds, line, collective_id, vector=None):
    shapes = []
    blocks = []
    scratch = []
    for group, kind in zip(groups, kinds):
        rows, columns = group[0].shape
        shape = ReduceShape(kind, rows // (2 * line), columns, len(group))
        shapes.append(shape)
        blocks.extend(group)
        scratch.extend(shape.scratch(line))
    anywhere = pl.BlockSpec(memory_space=pl.ANY)
    local = pl.BlockSpec(memory_space=pltpu.VMEM)
    in_specs = [anywhere] * len(blocks)
    out_shape = [shape.out_shape() for shape in shapes]
    if vector is not None:
        blocks.append(vector)
        in_specs.append(local)
        out_shape.append(jax.ShapeDtypeStruct(vector.shape, F32))
        scratch.extend(VectorSum.scratch(vector.shape))
    return pl.pallas_call(
        functools.partial(reduce_kernel, shapes, line, 0 if vector is None else 1),
        in_specs=in_specs,
        out_specs=[local] * len(out_shape),
        out_shape=out_shape,
        scratch_shapes=scratch,
        compiler_params=pltpu.CompilerParams(
            collective_id=collective_id, has_side_effects=True, vmem_limit_bytes=60 << 20
        ),
        name="fast_reduce",
    )(*blocks)


PLANE = 4
CHIP = 2
LINE = 4


def small_plane():
    return lax.axis_size("rep") == PLANE and lax.axis_size("fsdp") == CHIP * LINE


def gather(block):
    return lax.all_gather(block, "fsdp", axis=0, tiled=True)


def gather_all(groups, by_rows, collective_id):
    if small_plane():
        return fast_gather(groups, LINE, by_rows, collective_id)
    return [gather(jnp.concatenate(group, axis=1)) for group in groups]


def scatter(block):
    return lax.psum_scatter(block.astype(BF16), "fsdp", scatter_dimension=0, tiled=True)


def column_blocks(block):
    rows = block.shape[0]
    return block.reshape(rows, lax.axis_size("rep"), -1).swapaxes(0, 1)


def scatter_columns(parts):
    count = lax.axis_size("rep")
    rows = parts[0].shape[0]
    split = [part.reshape(rows, count, -1) for part in parts]
    joined = jnp.concatenate(split, axis=2).reshape(rows, -1)
    own = lax.psum_scatter(joined, "rep", scatter_dimension=1, tiled=True)
    sizes = [part.shape[1] // count for part in parts]
    outs = []
    start = 0
    for size in sizes:
        outs.append(own[:, start : start + size].astype(F32))
        start += size
    return outs


def scatter_last(groups, vector, collective_id):
    if small_plane():
        *outs, total = fast_reduce(
            groups, ["four"] * len(groups), LINE, collective_id, vector
        )
        return [[out[index] for index in range(4)] for out in outs], total
    outs = [scatter_columns([scatter(item) for item in group]) for group in groups]
    return outs, lax.psum(vector, ("rep", "fsdp"))


def body(
    tokens,
    memory,
    prefix_len,
    bucket_table,
    rel_bias,
    gain_self,
    self_query,
    self_key,
    self_value,
    self_out,
    gain_cross,
    cross_query,
    cross_key,
    cross_value,
    cross_out,
    gain_feed,
    gate_weight,
    up_weight,
    down_weight,
    out_grad,
):
    nseq, length, width = tokens.shape
    shard = gain_self.shape[0]
    groups = width // shard
    entries = rel_bias.shape[0]
    small = jnp.stack(
        [gain_self, gain_cross, gain_feed, jnp.pad(rel_bias, (0, shard - entries))], axis=1
    )
    small = jnp.pad(small, ((0, 0), (0, 2 * LANES - 4)))
    first, second = gather_all(
        [
            [self_query, self_key, self_value, small],
            [self_out, cross_query, cross_key, cross_value, cross_out, small],
        ],
        [False, False],
        1,
    )
    gate_up_own = jnp.concatenate([gate_weight, up_weight], axis=1)
    gate_up_own, down_rows, first, second = lax.optimization_barrier(
        (gate_up_own, down_weight, first, second)
    )
    gate_up = gather(gate_up_own)
    down = gather(down_rows)
    qkv_proj = first[:, : 3 * width]
    vectors = first[:, 3 * width : 3 * width + 4].T
    gain_first = vectors[0:1].astype(F32)
    gain_second = vectors[1:2].astype(F32)
    gain_third = vectors[2:3].astype(F32)
    table = vectors[3].reshape(groups, shard)[:, :entries].reshape(NHEAD, BUCKETS)
    out_self = second[:, :width]
    query_cross = second[:, width : 2 * width]
    kv_cross = second[:, 2 * width : 4 * width]
    out_cross = second[:, 4 * width : 5 * width]

    buckets_back = jnp.pad(bucket_table[::-1], (0, 1)).reshape(1, 2 * length)
    bias = skewed_bias(table, buckets_back, length)

    rows = nseq * length
    start_rows = tokens.reshape(rows, width).astype(F32)
    memory_rows = memory.reshape(-1, width)
    upstream = out_grad.reshape(rows, width)

    scale_first = inverse_rms(start_rows)
    normed_first = (start_rows * scale_first * gain_first).astype(BF16)
    qkv = matmul(normed_first, qkv_proj).astype(BF16)
    context, lse_self = run_self_forward(prefix_len, qkv, bias, nseq)
    middle = start_rows + matmul(context, out_self)
    scale_second = inverse_rms(middle)
    normed_second = (middle * scale_second * gain_second).astype(BF16)
    query_two = matmul(normed_second, query_cross).astype(BF16)
    kv_two = matmul(memory_rows, kv_cross).astype(BF16)
    context_two, lse_cross = run_cross_forward(query_two, kv_two, nseq)
    (
        result,
        later_grad,
        branch_two,
        context_two_grad,
        gain_third_grad,
        down_term,
        pair_term,
    ) = run_feed(middle, context_two, out_cross, gain_third, upstream, gate_up, down)
    gain_third_grad = gain_third_grad[0]
    down_own = scatter(down_term)
    pair_own = scatter(pair_term)
    query_two_grad, key_two_grad, value_two_grad = run_cross_backward(
        query_two, kv_two, context_two_grad, context_two, lse_cross, nseq
    )
    cross_terms = [
        weight_term(normed_second, query_two_grad).astype(BF16),
        weight_term(memory_rows, key_two_grad).astype(BF16),
        weight_term(memory_rows, value_two_grad).astype(BF16),
        weight_term(context_two, branch_two).astype(BF16),
    ]
    memory_grad = back_term(key_two_grad, kv_cross[:, :width]) + back_term(
        value_two_grad, kv_cross[:, width:]
    )
    carry, gain_second_grad = norm_back(
        middle, scale_second, gain_second, back_term(query_two_grad, query_cross)
    )
    middle_grad = later_grad + carry
    branch_one = middle_grad.astype(BF16)
    context_grad = back_term(branch_one, out_self).astype(BF16)
    query_grad, key_grad, value_grad, diagonal = run_self_backward(
        prefix_len, qkv, context_grad, context, lse_self, bias, nseq
    )
    first_grad = (
        back_term(query_grad, qkv_proj[:, :width])
        + back_term(key_grad, qkv_proj[:, width : 2 * width])
        + back_term(value_grad, qkv_proj[:, 2 * width :])
    )
    carry, gain_first_grad = norm_back(start_rows, scale_first, gain_first, first_grad)
    tokens_grad = middle_grad + carry

    onehot = (
        buckets_back.reshape(-1, 1) == jnp.arange(BUCKETS, dtype=jnp.int32)[None, :]
    ).astype(F32)
    onehot = onehot * (jnp.arange(2 * length) < 2 * length - 1)[:, None]
    bias_grad = jnp.dot(
        diagonal.reshape(NHEAD, 2 * length), onehot, precision=lax.Precision.HIGHEST
    )
    bias_rows = jnp.pad(
        bias_grad.reshape(groups, entries), ((0, 0), (0, shard - entries))
    ).reshape(width)
    vector_block = jnp.pad(
        jnp.stack([gain_first_grad, gain_second_grad, gain_third_grad, bias_rows], axis=0),
        ((0, 4), (0, 0)),
    )
    self_terms = [
        weight_term(normed_first, query_grad).astype(BF16),
        weight_term(normed_first, key_grad).astype(BF16),
        weight_term(normed_first, value_grad).astype(BF16),
        weight_term(context, branch_one).astype(BF16),
    ]
    down_split = column_blocks(down_own)
    pair_split = column_blocks(pair_own)
    down_split, pair_split, self_terms = lax.optimization_barrier(
        (down_split, pair_split, self_terms)
    )
    down_weight_grad = lax.psum_scatter(down_split, "rep").astype(F32)
    pair_grad = lax.psum_scatter(pair_split, "rep").astype(F32)
    pair_grad = pair_grad.reshape(shard, -1, 2, FEED_BLOCK)
    gate_weight_grad = pair_grad[:, :, 0].reshape(shard, -1)
    up_weight_grad = pair_grad[:, :, 1].reshape(shard, -1)
    (cross_out_grads, self_out_grads), totals = scatter_last(
        [cross_terms, self_terms], vector_block, 3
    )
    own = lax.dynamic_slice(
        totals, (0, lax.axis_index("fsdp") * shard), (totals.shape[0], shard)
    )
    return (
        result.reshape(tokens.shape),
        tokens_grad.reshape(tokens.shape),
        memory_grad.reshape(memory.shape),
        own[3, :entries],
        own[0],
        *self_out_grads,
        own[1],
        *cross_out_grads,
        own[2],
        gate_weight_grad,
        up_weight_grad,
        down_weight_grad,
    )


def solution(mesh):
    batch = P(("rep", "fsdp"), None, None)
    matrix = P("fsdp", None)
    vector = P("fsdp")
    split = P("fsdp", "rep")
    in_specs = (
        (batch, batch, P(("rep", "fsdp")), P(), vector, vector)
        + (matrix,) * 4
        + (vector,)
        + (matrix,) * 4
        + (vector,)
        + (matrix,) * 3
        + (batch,)
    )
    out_specs = (
        (batch, batch, batch, vector, vector)
        + (split,) * 4
        + (vector,)
        + (split,) * 4
        + (vector,)
        + (split,) * 3
    )
    return jax.shard_map(body, mesh=mesh, in_specs=in_specs, out_specs=out_specs, check_vma=False)
```

```python
import functools

import jax
import jax.numpy as jnp
from jax import lax
from jax.experimental import pallas as pl
from jax.experimental.pallas import tpu as pltpu
from jax.sharding import PartitionSpec as P

NHEAD = 12
DHEAD = 64
BUCKETS = 32
PAIRS = NHEAD // 2
LANES = 2 * DHEAD
PREFIX_MAX = 256

EPSILON = 1e-06
CUBIC_TERM = 0.044715
SQRT_TWO_PI = 0.7978845608028654
NEGATIVE = -1000000000.0

F32 = jnp.float32
BF16 = jnp.bfloat16
LAST_DIMS = (((1,), (1,)), ((), ()))


def matmul(left_side, right_side):
    return jnp.dot(left_side, right_side, preferred_element_type=F32)


def back_term(gradient, weight):
    return lax.dot_general(gradient, weight, LAST_DIMS, preferred_element_type=F32)


def inverse_rms(values):
    return lax.rsqrt(jnp.mean(values * values, axis=-1, keepdims=True) + EPSILON)


def norm_back(values, scale_rows, gain_vec, upstream):
    weighted = upstream * gain_vec
    gain_grad = jnp.sum(upstream * values * scale_rows, axis=0)
    input_grad = scale_rows * weighted - values * scale_rows * scale_rows * scale_rows * jnp.mean(
        values * weighted, axis=-1, keepdims=True
    )
    return (input_grad, gain_grad)


def one_head(rows, head):
    lane = lax.broadcasted_iota(jnp.int32, rows.shape, 1)
    keep = lane < DHEAD if head == 0 else lane >= DHEAD
    return jnp.where(keep, rows, jnp.zeros_like(rows))


def flipped(rows):
    return rows.astype(F32).T.astype(BF16)


def tree(fold, rows, groups):
    step = rows.shape[0] // groups
    total = rows[:step]
    for index in range(1, groups):
        total = fold(total, rows[index * step : (index + 1) * step])
    return total


def column_max(rows, groups):
    return jnp.max(tree(jnp.maximum, rows, groups), axis=0, keepdims=True)


def column_sum(rows, groups):
    return jnp.sum(tree(jnp.add, rows, groups), axis=0, keepdims=True)


def allowed_at(shape, key_start, query_start, prefix):
    key = lax.broadcasted_iota(jnp.int32, shape, 0) + key_start
    query = lax.broadcasted_iota(jnp.int32, shape, 1) + query_start
    return (key <= query) | (key < prefix)


def skew_kernel(table_ref, buckets_ref, out_ref):
    bucket = lax.broadcasted_iota(jnp.int32, (BUCKETS, buckets_ref.shape[1]), 0)
    onehot = (bucket == buckets_ref[...]).astype(BF16)
    by_offset = matmul(table_ref[...], onehot)
    width = out_ref.shape[2]
    total = by_offset.shape[1]
    for head in range(NHEAD):
        rows = jnp.broadcast_to(by_offset[head : head + 1], (LANES, total))
        rolled = pltpu.roll(rows, total - (LANES - 1), 1, stride=1, stride_axis=0)
        out_ref[head] = rolled[:, :width]


def skewed_bias(table, buckets_back, length):
    total = 2 * length
    return pl.pallas_call(
        skew_kernel,
        out_shape=jax.ShapeDtypeStruct((NHEAD, LANES, total - LANES), F32),
        name="skewed_bias",
    )(jnp.pad(table, ((0, 4), (0, 0))), buckets_back)


HEADROOM = 70.0


def self_forward(prefix_ref, query_ref, key_ref, value_ref, bias_ref, out_ref, lse_ref):
    length = query_ref.shape[0]
    block = 256
    prefix = prefix_ref[pl.program_id(0)]
    queries = query_ref[...]
    keys = key_ref[...]
    values = flipped(value_ref[...])

    def run(exact):
        excess = jnp.zeros((1, block), F32)
        for start in range(0, length, block):
            stop = start + block
            count = max(PREFIX_MAX, stop)
            outs = []
            for head in range(2):
                scores = back_term(keys[:count], one_head(queries[start:stop], head))
                parts = []
                for base in range(0, count, LANES):
                    shift = length - LANES - base + start
                    part = scores[base : base + LANES] + bias_ref[head, :, shift : shift + block]
                    if base + LANES - 1 > start:
                        part = jnp.where(
                            allowed_at(part.shape, base, start, prefix), part, NEGATIVE
                        )
                    parts.append(part)
                top = parts[0]
                for part in parts[1:]:
                    top = jnp.maximum(top, part)
                top = column_max(top, 4)
                anchor = top if exact else column_max(parts[0], 4)
                if not exact:
                    excess = jnp.maximum(excess, top - anchor)
                shares = [jnp.exp(part - anchor) for part in parts]
                total = shares[0]
                for share in shares[1:]:
                    total = total + share
                total = column_sum(total, 4)
                share = jnp.concatenate([item.astype(BF16) for item in shares], axis=0)
                context = matmul(values[head * DHEAD : (head + 1) * DHEAD, :count], share)
                outs.append(context * (1.0 / total))
                lse_ref[head : head + 1, start:stop] = anchor + jnp.log(total)
            out_ref[start:stop, :] = jnp.concatenate(outs, axis=0).T.astype(BF16)
        return jnp.max(excess)

    excess = run(False)

    @pl.when(excess > HEADROOM)
    def _():
        run(True)


def cross_forward(query_ref, key_ref, value_ref, out_ref, lse_ref):
    keys = key_ref[...]
    values = flipped(value_ref[...])
    queries = query_ref[...]

    def run(exact):
        excess = jnp.zeros((1, queries.shape[0]), F32)
        ahead = [back_term(keys, one_head(queries, head)) for head in range(2)]
        outs = []
        for head in range(2):
            scores = ahead[head]
            top = column_max(scores, 16)
            anchor = top if exact else column_max(scores[: 2 * LANES], 8)
            if not exact:
                excess = jnp.maximum(excess, top - anchor)
            share = jnp.exp(scores - anchor)
            total = column_sum(share, 16)
            context = matmul(values[head * DHEAD : (head + 1) * DHEAD], share.astype(BF16))
            outs.append(context * (1.0 / total))
            lse_ref[head : head + 1, :] = anchor + jnp.log(total)
        out_ref[...] = jnp.concatenate(outs, axis=0).T.astype(BF16)
        return jnp.max(excess)

    excess = run(False)

    @pl.when(excess > HEADROOM)
    def _():
        run(True)


def cross_backward(
    query_ref, key_ref, value_ref, up_ref, context_ref, lse_ref, dq_ref, dk_ref, dv_ref
):
    length = query_ref.shape[0]
    block = 256
    keys = key_ref[...]
    values = value_ref[...]
    queries = query_ref[...]
    upstream = up_ref[...]
    keys_flipped = flipped(keys)
    inner = (upstream.astype(F32) * context_ref[...].astype(F32)).T
    key_grad = None
    value_grad = None
    for start in range(0, length, block):
        rows = slice(start, start + block)
        grads = []
        for head in range(2):
            sub = slice(head * DHEAD, (head + 1) * DHEAD)
            query = one_head(queries[rows], head)
            above = one_head(upstream[rows], head)
            row_inner = jnp.sum(inner[sub, rows], axis=0, keepdims=True)
            shares = jnp.exp(back_term(keys, query) - lse_ref[head : head + 1, rows])
            share_grad = back_term(values, above)
            score_grad = (shares * (share_grad - row_inner)).astype(BF16)
            value_part = matmul(shares.astype(BF16), above)
            key_part = matmul(score_grad, query)
            value_grad = value_part if value_grad is None else value_grad + value_part
            key_grad = key_part if key_grad is None else key_grad + key_part
            grads.append(matmul(keys_flipped[sub], score_grad))
        dq_ref[rows, :] = jnp.concatenate(grads, axis=0).T.astype(BF16)
    dk_ref[...] = key_grad.astype(BF16)
    dv_ref[...] = value_grad.astype(BF16)


def self_backward(
    prefix_ref,
    query_ref,
    key_ref,
    value_ref,
    up_ref,
    context_ref,
    lse_ref,
    bias_ref,
    dq_ref,
    dk_ref,
    dv_ref,
    diag_ref,
    acc_ref,
):
    length = query_ref.shape[0]
    block = 256
    step = pl.program_id(1)
    prefix = prefix_ref[step]

    @pl.when(step == 0)
    def _():
        acc_ref[...] = jnp.zeros_like(acc_ref)

    queries = query_ref[...]
    keys = key_ref[...]
    values = value_ref[...]
    upstream = up_ref[...]
    keys_flipped = flipped(keys)
    inner = (upstream.astype(F32) * context_ref[...].astype(F32)).T
    count_all = length // block
    key_grad = [None] * count_all
    value_grad = [None] * count_all
    for start in range(0, length, block):
        stop = start + block
        count = max(PREFIX_MAX, stop)
        rows = slice(start, stop)
        grads = []
        for head in range(2):
            sub = slice(head * DHEAD, (head + 1) * DHEAD)
            query = one_head(queries[rows], head)
            above = one_head(upstream[rows], head)
            row_inner = jnp.sum(inner[sub, rows], axis=0, keepdims=True)
            row_lse = lse_ref[head : head + 1, rows]
            scores = back_term(keys[:count], query)
            share_grad = back_term(values[:count], above)
            shares = []
            score_grads = []
            for base in range(0, count, LANES):
                part = slice(base, base + LANES)
                shift = length - LANES - base + start
                share = jnp.exp(
                    scores[part] + bias_ref[head, :, shift : shift + block] - row_lse
                )
                if base + LANES - 1 > start:
                    share = jnp.where(allowed_at(share.shape, base, start, prefix), share, 0.0)
                score_grad = share * (share_grad[part] - row_inner)
                acc_ref[head, :, shift : shift + block] += score_grad
                shares.append(share.astype(BF16))
                score_grads.append(score_grad.astype(BF16))
            share = jnp.concatenate(shares, axis=0)
            score_grad = jnp.concatenate(score_grads, axis=0)
            value_part = matmul(share, above)
            key_part = matmul(score_grad, query)
            for index in range(count // block):
                part = slice(index * block, (index + 1) * block)
                if value_grad[index] is None:
                    value_grad[index] = value_part[part]
                    key_grad[index] = key_part[part]
                else:
                    value_grad[index] = value_grad[index] + value_part[part]
                    key_grad[index] = key_grad[index] + key_part[part]
            grads.append(matmul(keys_flipped[sub, :count], score_grad))
        dq_ref[rows, :] = jnp.concatenate(grads, axis=0).T.astype(BF16)
    for index in range(count_all):
        part = slice(index * block, (index + 1) * block)
        dk_ref[part, :] = key_grad[index].astype(BF16)
        dv_ref[part, :] = value_grad[index].astype(BF16)

    @pl.when(step == pl.num_programs(1) - 1)
    def _():
        total = 2 * length
        for head in range(2):
            rows = jnp.concatenate([acc_ref[head], jnp.zeros((LANES, LANES), F32)], axis=1)
            half = LANES // 2
            while half >= 1:
                rows = rows[:half] + pltpu.roll(rows[half:], total - half, 1)
                half //= 2
            diag_ref[head : head + 1, :] = pltpu.roll(rows, LANES - 1, 1)


def spec(shape, index):
    return pl.BlockSpec(shape, index)


def run_self_forward(prefix, qkv, bias, nseq):
    length = qkv.shape[0] // nseq
    return pl.pallas_call(
        self_forward,
        grid_spec=pltpu.PrefetchScalarGridSpec(
            num_scalar_prefetch=1,
            grid=(nseq, PAIRS),
            in_specs=[
                spec((length, LANES), lambda s, p, _: (s, p)),
                spec((length, LANES), lambda s, p, _: (s, PAIRS + p)),
                spec((length, LANES), lambda s, p, _: (s, 2 * PAIRS + p)),
                spec((2, LANES, 2 * length - LANES), lambda s, p, _: (p, 0, 0)),
            ],
            out_specs=[
                spec((length, LANES), lambda s, p, _: (s, p)),
                spec((None, None, 2, length), lambda s, p, _: (s, p, 0, 0)),
            ],
        ),
        out_shape=[
            jax.ShapeDtypeStruct((qkv.shape[0], PAIRS * LANES), BF16),
            jax.ShapeDtypeStruct((nseq, PAIRS, 2, length), F32),
        ],
        cost_estimate=pl.CostEstimate(
            flops=20_000_000_000, bytes_accessed=12_000_000, transcendentals=0
        ),
        name="self_forward",
    )(prefix, qkv, qkv, qkv, bias)


def run_cross_forward(query, kv, nseq):
    length = query.shape[0] // nseq
    count = kv.shape[0] // nseq
    return pl.pallas_call(
        cross_forward,
        grid=(nseq, PAIRS),
        in_specs=[
            spec((length, LANES), lambda s, p: (s, p)),
            spec((count, LANES), lambda s, p: (s, p)),
            spec((count, LANES), lambda s, p: (s, PAIRS + p)),
        ],
        out_specs=[
            spec((length, LANES), lambda s, p: (s, p)),
            spec((None, None, 2, length), lambda s, p: (s, p, 0, 0)),
        ],
        out_shape=[
            jax.ShapeDtypeStruct(query.shape, BF16),
            jax.ShapeDtypeStruct((nseq, PAIRS, 2, length), F32),
        ],
        cost_estimate=pl.CostEstimate(
            flops=24_000_000_000, bytes_accessed=10_000_000, transcendentals=0
        ),
        name="cross_forward",
    )(query, kv, kv)


def run_cross_backward(query, kv, upstream, context, lse, nseq):
    length = query.shape[0] // nseq
    count = kv.shape[0] // nseq
    rows = spec((length, LANES), lambda s, p: (s, p))
    wide = spec((count, LANES), lambda s, p: (s, p))
    return pl.pallas_call(
        cross_backward,
        grid=(nseq, PAIRS),
        in_specs=[
            rows,
            wide,
            spec((count, LANES), lambda s, p: (s, PAIRS + p)),
            rows,
            rows,
            spec((None, None, 2, length), lambda s, p: (s, p, 0, 0)),
        ],
        out_specs=[rows, wide, wide],
        out_shape=[
            jax.ShapeDtypeStruct(query.shape, BF16),
            jax.ShapeDtypeStruct((kv.shape[0], PAIRS * LANES), BF16),
            jax.ShapeDtypeStruct((kv.shape[0], PAIRS * LANES), BF16),
        ],
        cost_estimate=pl.CostEstimate(
            flops=36_000_000_000, bytes_accessed=20_000_000, transcendentals=0
        ),
        name="cross_backward",
    )(query, kv, kv, upstream, context, lse)


def run_self_backward(prefix, qkv, upstream, context, lse, bias, nseq):
    length = qkv.shape[0] // nseq
    rows = spec((length, LANES), lambda p, s, _: (s, p))
    return pl.pallas_call(
        self_backward,
        grid_spec=pltpu.PrefetchScalarGridSpec(
            num_scalar_prefetch=1,
            grid=(PAIRS, nseq),
            in_specs=[
                rows,
                spec((length, LANES), lambda p, s, _: (s, PAIRS + p)),
                spec((length, LANES), lambda p, s, _: (s, 2 * PAIRS + p)),
                rows,
                rows,
                spec((None, None, 2, length), lambda p, s, _: (s, p, 0, 0)),
                spec((2, LANES, 2 * length - LANES), lambda p, s, _: (p, 0, 0)),
            ],
            out_specs=[
                rows,
                rows,
                rows,
                spec((None, 2, 2 * length), lambda p, s, _: (p, 0, 0)),
            ],
            scratch_shapes=[pltpu.VMEM((2, LANES, 2 * length - LANES), F32)],
        ),
        out_shape=[jax.ShapeDtypeStruct(upstream.shape, BF16)] * 3
        + [jax.ShapeDtypeStruct((PAIRS, 2, 2 * length), F32)],
        cost_estimate=pl.CostEstimate(
            flops=24_000_000_000, bytes_accessed=20_000_000, transcendentals=0
        ),
        name="self_backward",
    )(prefix, qkv, qkv, qkv, upstream, context, lse, bias)


FEED_BLOCK = 256


def feed_kernel(
    middle_ref,
    context_ref,
    out_proj_ref,
    gain_ref,
    up_grad_ref,
    gate_ref,
    up_ref,
    down_ref,
    result_ref,
    later_grad_ref,
    branch_ref,
    context_grad_ref,
    gain_grad_ref,
    down_term_ref,
    pair_term_ref,
    later_ref,
    normed_ref,
    flipped_ref,
    result_acc,
    third_acc,
):
    step = pl.program_id(0)
    count = middle_ref.shape[0]
    chunk = 256
    chunks = [slice(start, start + chunk) for start in range(0, count, chunk)]

    @pl.when(step == 0)
    def _():
        for rows in chunks:
            later = middle_ref[rows] + matmul(context_ref[rows], out_proj_ref[...])
            normed = (later * inverse_rms(later) * gain_ref[...]).astype(BF16)
            later_ref[rows] = later
            normed_ref[rows] = normed
            flipped_ref[:, rows] = flipped(normed)
            result_acc[rows] = jnp.zeros_like(later)
            third_acc[rows] = jnp.zeros_like(later)

    gate_proj = gate_ref[...]
    up_proj = up_ref[...]
    down_proj = down_ref[...]
    hidden_flipped = []
    gate_grads = []
    lift_grads = []
    for rows in chunks:
        normed = normed_ref[rows]
        gate = matmul(normed, gate_proj)
        lift = matmul(normed, up_proj)
        hidden_grad = back_term(up_grad_ref[rows], down_proj)
        square = gate * gate
        tangent = jnp.tanh(SQRT_TWO_PI * gate * (1.0 + CUBIC_TERM * square))
        half = 0.5 * (1.0 + tangent)
        active = gate * half
        slope = half + 0.5 * gate * (1.0 - tangent * tangent) * (
            SQRT_TWO_PI + 3.0 * CUBIC_TERM * SQRT_TWO_PI * square
        )
        hidden = active * lift
        gate_grad = (hidden_grad * lift * slope).astype(BF16)
        lift_grad = (hidden_grad * active).astype(BF16)
        hidden_flipped.append(hidden.T.astype(BF16))
        gate_grads.append(gate_grad)
        lift_grads.append(lift_grad)
        result_acc[rows] += matmul(hidden.astype(BF16), down_proj)
        third_acc[rows] += back_term(gate_grad, gate_proj) + back_term(lift_grad, up_proj)
    hidden_flipped = jnp.concatenate(hidden_flipped, axis=1)
    down_term_ref[...] = matmul(hidden_flipped, up_grad_ref[...]).astype(BF16)
    gate_grads = jnp.concatenate(gate_grads, axis=0)
    lift_grads = jnp.concatenate(lift_grads, axis=0)
    pair_term_ref[:, :FEED_BLOCK] = matmul(flipped_ref[...], gate_grads).astype(BF16)
    pair_term_ref[:, FEED_BLOCK:] = matmul(flipped_ref[...], lift_grads).astype(BF16)

    @pl.when(step == pl.num_programs(0) - 1)
    def _():
        gain_grad = jnp.zeros(gain_ref.shape, F32)
        for rows in chunks:
            later = later_ref[rows]
            result_ref[rows] = (later + result_acc[rows]).astype(BF16)
            carry, part = norm_back(later, inverse_rms(later), gain_ref[...], third_acc[rows])
            gain_grad = gain_grad + part[None, :]
            later_grad = up_grad_ref[rows].astype(F32) + carry
            branch = later_grad.astype(BF16)
            later_grad_ref[rows] = later_grad
            branch_ref[rows] = branch
            context_grad_ref[rows] = back_term(branch, out_proj_ref[...]).astype(BF16)
        gain_grad_ref[...] = gain_grad


def run_feed(middle, context, out_proj, out_block, gain, upstream, gate_up, down):
    count, width = middle.shape
    ffn = down.shape[0]
    blocks = ffn // FEED_BLOCK

    def whole(shape, **extra):
        return pl.BlockSpec(shape, lambda j: (0, 0), **extra)

    once = {"pipeline_mode": pl.Buffered(1)}
    rows = (count, width)
    return pl.pallas_call(
        feed_kernel,
        grid=(blocks,),
        in_specs=[
            whole(rows, **once),
            whole(rows, **once),
            pl.BlockSpec((width, width), lambda j: (0, out_block), **once),
            whole((1, width)),
            whole(rows, **once),
            spec((width, FEED_BLOCK), lambda j: (0, j)),
            spec((width, FEED_BLOCK), lambda j: (0, blocks + j)),
            spec((FEED_BLOCK, width), lambda j: (j, 0)),
        ],
        out_specs=[
            whole(rows),
            whole(rows),
            whole(rows),
            whole(rows),
            whole((1, width)),
            spec((FEED_BLOCK, width), lambda j: (j, 0)),
            spec((width, 2 * FEED_BLOCK), lambda j: (0, j)),
        ],
        out_shape=[
            jax.ShapeDtypeStruct(rows, BF16),
            jax.ShapeDtypeStruct(rows, F32),
            jax.ShapeDtypeStruct(rows, BF16),
            jax.ShapeDtypeStruct(rows, BF16),
            jax.ShapeDtypeStruct((1, width), F32),
            jax.ShapeDtypeStruct((ffn, width), BF16),
            jax.ShapeDtypeStruct((width, 2 * ffn), BF16),
        ],
        scratch_shapes=[
            pltpu.VMEM(rows, F32),
            pltpu.VMEM(rows, BF16),
            pltpu.VMEM((width, count), BF16),
            pltpu.VMEM(rows, F32),
            pltpu.VMEM(rows, F32),
        ],
        cost_estimate=pl.CostEstimate(
            flops=32_000_000_000, bytes_accessed=40_000_000, transcendentals=0
        ),
        compiler_params=pltpu.CompilerParams(vmem_limit_bytes=60 << 20),
        name="feed",
    )(middle, context, out_proj, gain, upstream, gate_up, gate_up, down)


def close_kernel(count, project, *refs):
    values_ref, carry_ref, gain_ref, left_ref, right_ref = refs[:5]
    grad_refs = refs[5 : 5 + count]
    weight_refs = refs[5 + count : 5 + 2 * count]
    at = 5 + 2 * count
    if project:
        proj_ref = refs[at]
        at += 1
    out_ref, gain_grad_ref = refs[at : at + 2]
    term_refs = refs[at + 2 : at + 3 + count]
    at += 3 + count
    if project:
        branch_ref, projected_ref = refs[at : at + 2]
        at += 2
    sums = refs[at : at + 1 + count]
    gain_sum = refs[at + 1 + count]
    step = pl.program_id(0)

    @pl.when(step == 0)
    def _():
        gain_sum[...] = jnp.zeros_like(gain_sum)
        for total in sums:
            total[...] = jnp.zeros_like(total)

    values = values_ref[...].astype(F32)
    gain = gain_ref[...]
    scale = inverse_rms(values)
    normed = (values * scale * gain).T.astype(BF16)
    upstream = None
    for index in range(count):
        grad = grad_refs[index][...]
        sums[index][...] += matmul(normed, grad)
        part = back_term(grad, weight_refs[index][...])
        upstream = part if upstream is None else upstream + part
    sums[count][...] += matmul(flipped(left_ref[...]), right_ref[...])
    carry, part = norm_back(values, scale, gain, upstream)
    gain_sum[...] += part[None, :]
    result = carry_ref[...] + carry
    out_ref[...] = result
    if project:
        branch = result.astype(BF16)
        branch_ref[...] = branch
        projected_ref[...] = back_term(branch, proj_ref[...]).astype(BF16)

    @pl.when(step == pl.num_programs(0) - 1)
    def _():
        gain_grad_ref[...] = gain_sum[...]
        for term, total in zip(term_refs, sums):
            term[...] = total[...].astype(BF16)


def run_close(values, carry, gain, left, right, grads, weights, project, name):
    rows, width = values.shape
    count = len(grads)
    block = 256
    wide = spec((block, width), lambda i: (i, 0))

    def columns(index):
        return pl.BlockSpec((width, width), lambda i: (0, index), pipeline_mode=pl.Buffered(1))

    whole = [spec((1, width), lambda i: (0, 0))]
    square = [spec((width, width), lambda i: (0, 0))] * (count + 1)
    extra = [] if project is None else [project]
    out_shape = [
        jax.ShapeDtypeStruct((rows, width), F32),
        jax.ShapeDtypeStruct((1, width), F32),
    ] + [jax.ShapeDtypeStruct((width, width), BF16)] * (count + 1)
    out_shape += [jax.ShapeDtypeStruct((rows, width), BF16)] * (2 * len(extra))
    return pl.pallas_call(
        functools.partial(close_kernel, count, project is not None),
        grid=(rows // block,),
        in_specs=[wide, wide]
        + whole
        + [wide] * (2 + count)
        + [columns(index) for _, index in weights + extra],
        out_specs=[wide] + whole + square + [wide] * (2 * len(extra)),
        out_shape=out_shape,
        scratch_shapes=[pltpu.VMEM((width, width), F32)] * (count + 1)
        + [pltpu.VMEM((1, width), F32)],
        cost_estimate=pl.CostEstimate(
            flops=8_000_000_000, bytes_accessed=25_000_000, transcendentals=0
        ),
        compiler_params=pltpu.CompilerParams(vmem_limit_bytes=60 << 20),
        name=name,
    )(values, carry, gain, left, right, *grads, *[item for item, _ in weights + extra])


def memory_kernel(
    memory_ref, key_grad_ref, value_grad_ref, key_ref, value_ref, out_ref, *rest
):
    key_term_ref, value_term_ref, key_sum, value_sum = rest
    step = pl.program_id(0)

    @pl.when(step == 0)
    def _():
        key_sum[...] = jnp.zeros_like(key_sum)
        value_sum[...] = jnp.zeros_like(value_sum)

    rows = flipped(memory_ref[...])
    key_grad = key_grad_ref[...]
    value_grad = value_grad_ref[...]
    out_ref[...] = back_term(key_grad, key_ref[...]) + back_term(value_grad, value_ref[...])
    key_sum[...] += matmul(rows, key_grad)
    value_sum[...] += matmul(rows, value_grad)

    @pl.when(step == pl.num_programs(0) - 1)
    def _():
        key_term_ref[...] = key_sum[...].astype(BF16)
        value_term_ref[...] = value_sum[...].astype(BF16)


def run_memory(memory, key_grad, value_grad, weights, key_block, value_block):
    rows, width = memory.shape
    block = 512
    wide = spec((block, width), lambda i: (i, 0))
    square = spec((width, width), lambda i: (0, 0))

    def columns(index):
        return pl.BlockSpec((width, width), lambda i: (0, index), pipeline_mode=pl.Buffered(1))

    return pl.pallas_call(
        memory_kernel,
        grid=(rows // block,),
        in_specs=[wide, wide, wide, columns(key_block), columns(value_block)],
        out_specs=[wide, square, square],
        out_shape=[
            jax.ShapeDtypeStruct((rows, width), F32),
            jax.ShapeDtypeStruct((width, width), BF16),
            jax.ShapeDtypeStruct((width, width), BF16),
        ],
        scratch_shapes=[pltpu.VMEM((width, width), F32)] * 2,
        cost_estimate=pl.CostEstimate(
            flops=10_000_000_000, bytes_accessed=18_000_000, transcendentals=0
        ),
        compiler_params=pltpu.CompilerParams(vmem_limit_bytes=60 << 20),
        name="memory_close",
    )(memory, key_grad, value_grad, weights, weights)


MESH = pl.DeviceIdType.MESH


class Place:
    def __init__(self, line):
        self.line = line
        rep = lax.axis_index("rep")
        fsdp = lax.axis_index("fsdp")
        self.rep = rep
        self.fsdp = fsdp
        self.y = rep // 2
        self.x = rep % 2
        self.z = fsdp // 2
        self.core = fsdp % 2
        self.x_rep = self.y * 2 + 1 - self.x
        self.y_rep = (1 - self.y) * 2 + self.x

    def at_x(self):
        return {"rep": self.x_rep, "fsdp": self.fsdp}

    def at_y(self):
        return {"rep": self.y_rep, "fsdp": self.fsdp}

    def at_partner(self):
        return {"rep": self.rep, "fsdp": self.z * 2 + 1 - self.core}

    def at_line(self, side):
        return {"rep": self.rep, "fsdp": self.fsdp + (2 if side == 0 else -2)}

    def has_next(self, side):
        return self.z < self.line - 1 if side == 0 else self.z > 0

    def has_last(self, side):
        return self.has_next(1 - side)

    def arrives(self, side, hop):
        if side == 0:
            return self.z - 1 - hop >= 0
        return self.z + 1 + hop <= self.line - 1

    def source(self, side, hop):
        return self.z - 1 - hop if side == 0 else self.z + 1 + hop

    def at_far(self):
        half = self.line // 2
        return {"rep": self.rep, "fsdp": (self.z + half) % self.line * 2 + self.core}

    def greet(self, wide=False):
        barrier = pltpu.get_barrier_semaphore()
        targets = [self.at_x(), self.at_y(), self.at_partner()]
        if wide:
            targets.append({"rep": 3 - self.rep, "fsdp": self.fsdp})
            targets.append(self.at_far())
        for target in targets:
            pl.semaphore_signal(barrier, inc=1, device_id=target, device_id_type=MESH)
        for side in range(2):

            @pl.when(self.has_next(side))
            def _():
                pl.semaphore_signal(
                    barrier, inc=1, device_id=self.at_line(side), device_id_type=MESH
                )

        count = len(targets)
        for side in range(2):
            count = count + jnp.where(self.has_next(side), 1, 0)
        pl.semaphore_wait(barrier, count)


def remote(source, target, send, recv, device):
    return pltpu.make_async_remote_copy(
        src_ref=source,
        dst_ref=target,
        send_sem=send,
        recv_sem=recv,
        device_id=device,
        device_id_type=MESH,
    )


class GatherShape:
    def __init__(self, parts, by_rows):
        self.rows = parts[0].shape[0]
        self.widths = [part.shape[1] for part in parts]
        self.starts = [sum(self.widths[:index]) for index in range(len(parts))]
        self.columns = sum(self.widths)
        self.by_rows = by_rows

    def full(self, ref, owner):
        return ref.at[pl.ds(pl.multiple_of(owner * self.rows, 32), self.rows)]

    def piece(self, ref, owner, part, half=None):
        base = owner * self.rows
        if self.by_rows:
            rows = self.rows // 4
            base = base + part * rows
        else:
            rows = self.rows
        if half is not None:
            rows = rows // 2
            base = base + half * rows
        row_slice = pl.ds(pl.multiple_of(base, 16), rows)
        if self.by_rows:
            return ref.at[row_slice]
        width = self.columns // 4
        return ref.at[row_slice, pl.ds(pl.multiple_of(part * width, LANES), width)]


def gather_sems(line):
    hops = line - 1
    return [pltpu.SemaphoreType.DMA((5, 2, 2, hops)), pltpu.SemaphoreType.DMA((4,))] + [
        pltpu.SemaphoreType.DMA((2, 2, hops))
    ]


def gather_steps(place, shape, src, own, dst, sems):
    hop_sem, own_sem, pair_sem = sems
    hops = place.line - 1
    me = place.fsdp

    def load(index):
        at = pl.ds(shape.starts[index], shape.widths[index])
        return pltpu.make_async_copy(src[index], own.at[:, at], own_sem.at[0])

    def loaded():
        return pltpu.make_async_copy(own, own, own_sem.at[0])

    def keep():
        return pltpu.make_async_copy(own, shape.full(dst, me), own_sem.at[1])

    def own_pair():
        return remote(
            own, shape.full(dst, me), own_sem.at[2], own_sem.at[3], place.at_partner()
        )

    def owner(side, hop):
        return place.source(side, hop) * 2 + place.core

    def line_first(side):
        return remote(
            shape.piece(own, 0, place.rep),
            shape.piece(dst, me, place.rep),
            hop_sem.at[0, 0, side, 0],
            hop_sem.at[0, 1, side, 0],
            place.at_line(side),
        )

    def moved(kind, side, hop, block, device):
        return remote(
            block, block, hop_sem.at[kind, 0, side, hop], hop_sem.at[kind, 1, side, hop], device
        )

    def line_next(side, hop):
        block = shape.piece(dst, owner(side, hop - 1), place.rep)
        return moved(0, side, hop, block, place.at_line(side))

    def line_arrival(side, hop):
        block = shape.piece(dst, owner(side, hop), place.rep)
        return moved(0, side, hop, block, place.at_line(side))

    def plane(axis, side, hop):
        block = shape.piece(dst, owner(side, hop), place.rep)
        return moved(1 + axis, side, hop, block, place.at_x() if axis == 0 else place.at_y())

    def cross(axis, side, hop):
        part = place.x_rep if axis == 1 else place.y_rep
        block = shape.piece(dst, owner(side, hop), part, 1 - axis)
        return moved(3 + axis, side, hop, block, place.at_x() if axis == 0 else place.at_y())

    def pair(side, hop):
        block = shape.full(dst, owner(side, hop))
        return remote(
            block, block, pair_sem.at[0, side, hop], pair_sem.at[1, side, hop], place.at_partner()
        )

    def each(fn):
        def run():
            for hop in range(hops):
                for side in range(2):
                    pl.when(place.arrives(side, hop))(functools.partial(fn, side, hop))

        return run

    def start():
        for index in range(len(src)):
            load(index).start()
        loaded().wait()
        for side in range(2):
            pl.when(place.has_next(side))(lambda side=side: line_first(side).start())
        own_pair().start()
        keep().start()

    def arrive(side, hop):
        line_arrival(side, hop).wait_recv()
        if hop + 1 < hops:
            pl.when(place.has_next(side))(lambda: line_next(side, hop + 1).start())
        plane(0, side, hop).start()
        plane(1, side, hop).start()

    def turn(side, hop):
        plane(0, side, hop).wait_recv()
        cross(1, side, hop).start()
        plane(1, side, hop).wait_recv()
        cross(0, side, hop).start()

    def hand(side, hop):
        cross(0, side, hop).wait_recv()
        cross(1, side, hop).wait_recv()
        pair(side, hop).start()

    def finish():
        def last(side, hop):
            pair(side, hop).wait()
            for axis in range(2):
                plane(axis, side, hop).wait_send()
                cross(axis, side, hop).wait_send()
            if hop + 1 < hops:
                pl.when(place.has_next(side))(lambda: line_next(side, hop + 1).wait_send())

        each(last)()
        for side in range(2):
            pl.when(place.has_next(side))(lambda side=side: line_first(side).wait_send())
        own_pair().wait()
        keep().wait()

    return start, each(arrive), each(turn), each(hand), finish


def gather_kernel(shapes, line, *refs):
    count = len(shapes)
    sources = []
    at = 0
    for shape in shapes:
        sources.append(refs[at : at + len(shape.widths)])
        at += len(shape.widths)
    targets = refs[at : at + count]
    scratch = refs[at + count :]
    place = Place(line)
    place.greet()
    plans = []
    for index, shape in enumerate(shapes):
        own, *sems = scratch[4 * index : 4 * index + 4]
        plans.append(gather_steps(place, shape, sources[index], own, targets[index], sems))
    for stage in range(5):
        for plan in plans:
            plan[stage]()


def fast_gather(groups, line, by_rows, collective_id):
    shapes = [GatherShape(group, flag) for group, flag in zip(groups, by_rows)]
    scratch = []
    for shape in shapes:
        scratch.append(pltpu.VMEM((shape.rows, shape.columns), BF16))
        scratch.extend(gather_sems(line))
    anywhere = pl.BlockSpec(memory_space=pl.ANY)
    blocks = [block for group in groups for block in group]
    return pl.pallas_call(
        functools.partial(gather_kernel, shapes, line),
        in_specs=[anywhere] * len(blocks),
        out_specs=[anywhere] * len(groups),
        out_shape=[
            jax.ShapeDtypeStruct((2 * line * s.rows, s.columns), BF16) for s in shapes
        ],
        scratch_shapes=scratch,
        compiler_params=pltpu.CompilerParams(collective_id=collective_id, has_side_effects=True),
        name="fast_gather",
    )(*blocks)


class ReduceShape:
    def __init__(self, kind, rows, columns, sources):
        self.kind = kind
        self.rows = rows
        self.sources = sources
        if kind == "rows":
            self.block = (rows // 8, columns)
        elif kind == "pair":
            self.block = (rows // 2, columns // 2)
        else:
            self.block = (rows // 2, columns)
        self.exchange = kind != "pair"
        self.part_rows = rows // 4 if kind == "rows" else rows
        self.part_columns = columns // 4

    def pieces(self, refs, owner, half, quarter):
        rows, columns = self.block
        if self.kind == "rows":
            base = owner * self.rows + quarter * (self.rows // 4) + half * rows
            return [(refs[0].at[pl.ds(pl.multiple_of(base, 16), rows)], 0, columns)]
        at = pl.ds(pl.multiple_of(owner * self.rows + half * rows, 16), rows)
        if self.kind == "four":
            return [(refs[quarter].at[at], 0, columns)]
        width = columns // 2
        cut = slice(quarter * width, (quarter + 1) * width)
        return [(refs[index].at[at, cut], index * width, width) for index in range(2)]

    def out_shape(self):
        if self.exchange:
            return jax.ShapeDtypeStruct((4, self.part_rows, self.part_columns), F32)
        return jax.ShapeDtypeStruct((self.rows, self.block[1]), F32)

    def scratch(self, line):
        rows, columns = self.block
        dma = pltpu.SemaphoreType.DMA
        buffers = [
            pltpu.VMEM((line, 8, rows, columns), BF16),
            pltpu.VMEM((line, 8, rows, columns), BF16),
            pltpu.VMEM((line, 2, 2, rows, columns), BF16),
            pltpu.VMEM((line, 2, rows, columns), BF16),
            pltpu.VMEM((line, 2, rows, columns), BF16),
            pltpu.VMEM((2, line, 2, rows, columns), BF16),
            pltpu.VMEM((4, self.part_rows, self.part_columns), F32),
            pltpu.VMEM((4, self.part_rows, self.part_columns), F32),
            dma((line,)),
            dma((2, line)),
            dma((2, line, 2)),
            dma((2, line, 2)),
            dma((2, 2, line)),
            dma((2, 3)),
        ]
        return buffers


REDUCE_SCRATCH = 14


def added(left, right):
    return (left.astype(F32) + right.astype(F32)).astype(BF16)


def reduce_steps(place, shape, refs, out, scratch):
    own, other, first_in, second_in, total, line_in, parts, gathered = scratch[:8]
    load_sem, pair_sem, first_sem, second_sem, line_sem, swap_sem = scratch[8:]
    line = place.line
    near = (place.x, place.y)
    far = (place.y, place.x)
    near_device = (place.at_x(), place.at_y())
    far_device = (place.at_y(), place.at_x())

    def quarter_of(half, index):
        high, low = index // 2, index % 2
        return low * 2 + high if half == 0 else high * 2 + low

    def start(z):
        for half in range(2):
            for index in range(4):
                quarter = quarter_of(half, index)
                slot = half * 4 + index
                mine = shape.pieces(refs, 2 * z + place.core, half, quarter)
                theirs = shape.pieces(refs, 2 * z + 1 - place.core, half, quarter)
                for (view, column, width), (view_two, _, _) in zip(mine, theirs):
                    cut = pl.ds(column, width)
                    remote(
                        view_two,
                        other.at[z, slot, :, cut],
                        pair_sem.at[0, z],
                        pair_sem.at[1, z],
                        place.at_partner(),
                    ).start()
                    pltpu.make_async_copy(
                        view, own.at[z, slot, :, cut], load_sem.at[z]
                    ).start()

    def pair_all(z):
        return remote(
            own.at[z], other.at[z], pair_sem.at[0, z], pair_sem.at[1, z], place.at_partner()
        )

    def first(z, half):
        return remote(
            own.at[z, pl.ds(half * 4 + (1 - near[half]) * 2, 2)],
            first_in.at[z, half],
            first_sem.at[0, z, half],
            first_sem.at[1, z, half],
            near_device[half],
        )

    def second(z, half):
        return remote(
            own.at[z, half * 4 + near[half] * 2 + 1 - far[half]],
            second_in.at[z, half],
            second_sem.at[0, z, half],
            second_sem.at[1, z, half],
            far_device[half],
        )

    def along(z, side):
        return remote(
            total.at[z],
            line_in.at[side, z],
            line_sem.at[0, side, z],
            line_sem.at[1, side, z],
            place.at_line(side),
        )

    def pair_add(z):
        pltpu.make_async_copy(own.at[z], own.at[z], load_sem.at[z]).wait()
        pair_all(z).wait_recv()

        @pl.loop(0, 8)
        def _(slot):
            own[z, slot] = added(own[z, slot], other[z, slot])

        for half in range(2):
            first(z, half).start()

    def first_add(z):
        for half in range(2):
            first(z, half).wait_recv()
            base = half * 4 + near[half] * 2

            @pl.loop(0, 2)
            def _(index):
                own[z, base + index] = added(own[z, base + index], first_in[z, half, index])

            second(z, half).start()

    def second_add(z):
        for half in range(2):
            second(z, half).wait_recv()
            mine = half * 4 + near[half] * 2 + far[half]
            total[z, half] = added(own[z, mine], second_in[z, half])

    def line_send(z, side):
        ahead = place.z < z if side == 0 else place.z > z

        @pl.when(ahead)
        def _():
            @pl.when(place.has_last(side))
            def _():
                along(z, side).wait_recv()

                @pl.loop(0, 2)
                def _(half):
                    total[z, half] = added(total[z, half], line_in[side, z, half])

            along(z, side).start()

    def line_end(z):
        @pl.when(place.z == z)
        def _():
            for side in range(2):
                pl.when(place.has_last(side))(lambda: along(z, side).wait_recv())

    def swap(rep_slot, device, index):
        return remote(
            parts.at[rep_slot],
            gathered.at[place.rep],
            swap_sem.at[0, index],
            swap_sem.at[1, index],
            device,
        )

    def swaps():
        corner = 3 - place.rep
        return [
            swap(place.x_rep, place.at_x(), 0),
            swap(place.y_rep, place.at_y(), 1),
            swap(corner, {"rep": corner, "fsdp": place.fsdp}, 2),
        ]

    def finish():
        rows, columns = shape.block
        me = place.z
        for half in range(2):
            result = total[me, half].astype(F32)
            for side in range(2):
                extra = line_in[side, me, half].astype(F32)
                result = result + jnp.where(place.has_last(side), extra, 0.0)
            at = slice(half * rows, (half + 1) * rows)
            if shape.exchange:
                width = shape.part_columns
                for index in range(4):
                    parts[index, at, :] = result[:, index * width : (index + 1) * width]
            else:
                out[at, :] = result
        if shape.exchange:
            for copy in swaps():
                copy.start()
            gathered[place.rep] = parts[place.rep]

    def drain():
        if shape.exchange:
            for copy in swaps():
                copy.wait()
            out[...] = gathered[...]
        for z in range(line):
            pair_all(z).wait_send()
            for half in range(2):
                first(z, half).wait_send()
                second(z, half).wait_send()
            for side in range(2):
                ahead = place.z < z if side == 0 else place.z > z
                pl.when(ahead)(lambda: along(z, side).wait_send())

    order = [line - 1, 0] + [z for z in range(line - 2, 0, -1)]

    def begin():
        for z in order:
            start(z)

    def pairs():
        for z in order:
            pair_add(z)

    def firsts():
        for z in order:
            first_add(z)

    def seconds():
        for index, z in enumerate(order):
            second_add(z)
            if index > 0:
                line_send(order[index - 1], 0)
                line_send(order[index - 1], 1)
        line_send(order[-1], 0)
        line_send(order[-1], 1)

    def close():
        for z in range(line):
            line_end(z)
        finish()

    return begin, pairs, firsts, seconds, close, drain


class VectorSum:
    def __init__(self, place, source, out, scratch):
        self.place = place
        self.source = source
        self.out = out
        self.current, self.incoming, self.sems = scratch
        side = place.z % 2
        near = place.fsdp + 2 - 4 * side
        self.devices = [
            place.at_partner(),
            place.at_x(),
            place.at_y(),
            {"rep": place.rep, "fsdp": near},
            place.at_far(),
        ]

    @staticmethod
    def scratch(shape):
        return [
            pltpu.VMEM((6,) + shape, F32),
            pltpu.VMEM((5,) + shape, F32),
            pltpu.SemaphoreType.DMA((2, 5)),
        ]

    def copy(self, index):
        return remote(
            self.current.at[index],
            self.incoming.at[index],
            self.sems.at[0, index],
            self.sems.at[1, index],
            self.devices[index],
        )

    def round(self, index):
        if index == 0:
            self.current[0] = self.source[...]
        else:
            self.copy(index - 1).wait_recv()
            self.current[index] = self.current[index - 1] + self.incoming[index - 1]
        if index < 5:
            self.copy(index).start()

    def finish(self):
        self.out[...] = self.current[5]
        for index in range(5):
            self.copy(index).wait_send()


def reduce_kernel(shapes, line, vector_count, *refs):
    sources = []
    at = 0
    for shape in shapes:
        sources.append(refs[at : at + shape.sources])
        at += shape.sources
    vector_refs = refs[at : at + vector_count]
    at += vector_count
    outs = refs[at : at + len(shapes)]
    at += len(shapes)
    vector_outs = refs[at : at + vector_count]
    at += vector_count
    place = Place(line)
    place.greet(wide=True)
    plans = []
    for index, shape in enumerate(shapes):
        part = refs[at : at + REDUCE_SCRATCH]
        at += REDUCE_SCRATCH
        plans.append(reduce_steps(place, shape, sources[index], outs[index], part))
    vectors = []
    if vector_count:
        vectors = [VectorSum(place, vector_refs[0], vector_outs[0], refs[at : at + 3])]

    def rounds(*indices):
        for vector in vectors:
            for index in indices:
                vector.round(index)

    rounds(0)
    for plan in plans:
        plan[0]()
    plans[0][1]()
    rounds(1)
    plans[0][2]()
    rounds(2)
    for index, plan in enumerate(plans):
        ahead = plans[index + 1] if index + 1 < len(plans) else None
        if ahead is not None:
            ahead[1]()
        plan[3]()
        if ahead is not None:
            ahead[2]()
    rounds(3)
    for plan in plans:
        plan[4]()
    rounds(4, 5)
    for plan in plans:
        plan[5]()
    for vector in vectors:
        vector.finish()


def fast_reduce(groups, kinds, line, collective_id, vector=None):
    shapes = []
    blocks = []
    scratch = []
    for group, kind in zip(groups, kinds):
        rows, columns = group[0].shape
        shape = ReduceShape(kind, rows // (2 * line), columns, len(group))
        shapes.append(shape)
        blocks.extend(group)
        scratch.extend(shape.scratch(line))
    anywhere = pl.BlockSpec(memory_space=pl.ANY)
    local = pl.BlockSpec(memory_space=pltpu.VMEM)
    in_specs = [anywhere] * len(blocks)
    out_shape = [shape.out_shape() for shape in shapes]
    if vector is not None:
        blocks.append(vector)
        in_specs.append(local)
        out_shape.append(jax.ShapeDtypeStruct(vector.shape, F32))
        scratch.extend(VectorSum.scratch(vector.shape))
    return pl.pallas_call(
        functools.partial(reduce_kernel, shapes, line, 0 if vector is None else 1),
        in_specs=in_specs,
        out_specs=[local] * len(out_shape),
        out_shape=out_shape,
        scratch_shapes=scratch,
        compiler_params=pltpu.CompilerParams(
            collective_id=collective_id, has_side_effects=True, vmem_limit_bytes=60 << 20
        ),
        name="fast_reduce",
    )(*blocks)


PLANE = 4
CHIP = 2
LINE = 4


def small_plane():
    return lax.axis_size("rep") == PLANE and lax.axis_size("fsdp") == CHIP * LINE


def gather(block):
    return lax.all_gather(block, "fsdp", axis=0, tiled=True)


def gather_all(groups, by_rows, collective_id):
    if small_plane():
        return fast_gather(groups, LINE, by_rows, collective_id)
    return [gather(jnp.concatenate(group, axis=1)) for group in groups]


def scatter(block):
    return lax.psum_scatter(block.astype(BF16), "fsdp", scatter_dimension=0, tiled=True)


def column_blocks(block):
    rows = block.shape[0]
    return block.reshape(rows, lax.axis_size("rep"), -1).swapaxes(0, 1)


def scatter_columns(parts):
    count = lax.axis_size("rep")
    rows = parts[0].shape[0]
    split = [part.reshape(rows, count, -1) for part in parts]
    joined = jnp.concatenate(split, axis=2).reshape(rows, -1)
    own = lax.psum_scatter(joined, "rep", scatter_dimension=1, tiled=True)
    sizes = [part.shape[1] // count for part in parts]
    outs = []
    start = 0
    for size in sizes:
        outs.append(own[:, start : start + size].astype(F32))
        start += size
    return outs


def scatter_last(groups, vector, collective_id):
    if small_plane():
        *outs, total = fast_reduce(
            groups, ["four"] * len(groups), LINE, collective_id, vector
        )
        return [[out[index] for index in range(4)] for out in outs], total
    outs = [scatter_columns([scatter(item) for item in group]) for group in groups]
    return outs, lax.psum(vector, ("rep", "fsdp"))


def body(
    tokens,
    memory,
    prefix_len,
    bucket_table,
    rel_bias,
    gain_self,
    self_query,
    self_key,
    self_value,
    self_out,
    gain_cross,
    cross_query,
    cross_key,
    cross_value,
    cross_out,
    gain_feed,
    gate_weight,
    up_weight,
    down_weight,
    out_grad,
):
    nseq, length, width = tokens.shape
    shard = gain_self.shape[0]
    groups = width // shard
    entries = rel_bias.shape[0]
    small = jnp.stack(
        [gain_self, gain_cross, gain_feed, jnp.pad(rel_bias, (0, shard - entries))], axis=1
    )
    small = jnp.pad(small, ((0, 0), (0, 2 * LANES - 4)))
    first, second = gather_all(
        [
            [self_query, self_key, self_value, small],
            [self_out, cross_query, cross_key, cross_value, cross_out, small],
        ],
        [False, False],
        1,
    )
    gate_up_own = jnp.concatenate([gate_weight, up_weight], axis=1)
    gate_up_own, down_rows, first, second = lax.optimization_barrier(
        (gate_up_own, down_weight, first, second)
    )
    gate_up = gather(gate_up_own)
    down = gather(down_rows)
    qkv_proj = first[:, : 3 * width]
    vectors = lax.optimization_barrier(first[:, 3 * width : 3 * width + LANES])[:, :4].T
    gain_first = vectors[0:1].astype(F32)
    gain_second = vectors[1:2].astype(F32)
    gain_third = vectors[2:3].astype(F32)
    table = vectors[3].reshape(groups, shard)[:, :entries].reshape(NHEAD, BUCKETS)
    out_self = second[:, :width]
    query_cross = second[:, width : 2 * width]
    kv_cross = second[:, 2 * width : 4 * width]

    buckets_back = jnp.pad(bucket_table[::-1], (0, 1)).reshape(1, 2 * length)
    bias = skewed_bias(table, buckets_back, length)

    rows = nseq * length
    start_rows = tokens.reshape(rows, width).astype(F32)
    memory_rows = memory.reshape(-1, width)
    upstream = out_grad.reshape(rows, width)

    scale_first = inverse_rms(start_rows)
    normed_first = (start_rows * scale_first * gain_first).astype(BF16)
    qkv = matmul(normed_first, qkv_proj).astype(BF16)
    context, lse_self = run_self_forward(prefix_len, qkv, bias, nseq)
    middle = start_rows + matmul(context, out_self)
    scale_second = inverse_rms(middle)
    normed_second = (middle * scale_second * gain_second).astype(BF16)
    query_two = matmul(normed_second, query_cross).astype(BF16)
    kv_two = matmul(memory_rows, kv_cross).astype(BF16)
    context_two, lse_cross = run_cross_forward(query_two, kv_two, nseq)
    (
        result,
        later_grad,
        branch_two,
        context_two_grad,
        gain_third_grad,
        down_term,
        pair_term,
    ) = run_feed(middle, context_two, second, 4, gain_third, upstream, gate_up, down)
    down_own = scatter(down_term)
    pair_own = scatter(pair_term)
    query_two_grad, key_two_grad, value_two_grad = run_cross_backward(
        query_two, kv_two, context_two_grad, context_two, lse_cross, nseq
    )
    (
        middle_grad,
        gain_second_grad,
        query_term,
        out_term,
        branch_one,
        context_grad,
    ) = run_close(
        middle,
        later_grad,
        gain_second,
        context_two,
        branch_two,
        [query_two_grad],
        [(second, 1)],
        (second, 0),
        "cross_close",
    )
    memory_grad, key_term, value_term = run_memory(
        memory_rows, key_two_grad, value_two_grad, second, 2, 3
    )
    cross_terms = [query_term, key_term, value_term, out_term]
    query_grad, key_grad, value_grad, diagonal = run_self_backward(
        prefix_len, qkv, context_grad, context, lse_self, bias, nseq
    )
    tokens_grad, gain_first_grad, *self_terms = run_close(
        tokens.reshape(rows, width),
        middle_grad,
        gain_first,
        context,
        branch_one,
        [query_grad, key_grad, value_grad],
        [(first, 0), (first, 1), (first, 2)],
        None,
        "self_close",
    )

    onehot = (
        buckets_back.reshape(-1, 1) == jnp.arange(BUCKETS, dtype=jnp.int32)[None, :]
    ).astype(F32)
    onehot = onehot * (jnp.arange(2 * length) < 2 * length - 1)[:, None]
    bias_grad = jnp.dot(
        diagonal.reshape(NHEAD, 2 * length), onehot, precision=lax.Precision.HIGHEST
    )
    bias_rows = jnp.pad(
        bias_grad.reshape(groups, entries), ((0, 0), (0, shard - entries))
    ).reshape(width)
    vector_block = jnp.pad(
        jnp.concatenate(
            [gain_first_grad, gain_second_grad, gain_third_grad, bias_rows[None]], axis=0
        ),
        ((0, 4), (0, 0)),
    )
    down_split = column_blocks(down_own)
    pair_split = column_blocks(pair_own)
    down_split, pair_split, self_terms = lax.optimization_barrier(
        (down_split, pair_split, self_terms)
    )
    down_weight_grad = lax.psum_scatter(down_split, "rep").astype(F32)
    pair_grad = lax.psum_scatter(pair_split, "rep").astype(F32)
    pair_grad = pair_grad.reshape(shard, -1, 2, FEED_BLOCK)
    gate_weight_grad = pair_grad[:, :, 0].reshape(shard, -1)
    up_weight_grad = pair_grad[:, :, 1].reshape(shard, -1)
    (cross_out_grads, self_out_grads), totals = scatter_last(
        [cross_terms, self_terms], vector_block, 3
    )
    own = lax.dynamic_slice(
        totals, (0, lax.axis_index("fsdp") * shard), (totals.shape[0], shard)
    )
    return (
        result.reshape(tokens.shape),
        tokens_grad.reshape(tokens.shape),
        memory_grad.reshape(memory.shape),
        own[3, :entries],
        own[0],
        *self_out_grads,
        own[1],
        *cross_out_grads,
        own[2],
        gate_weight_grad,
        up_weight_grad,
        down_weight_grad,
    )


def solution(mesh):
    batch = P(("rep", "fsdp"), None, None)
    matrix = P("fsdp", None)
    vector = P("fsdp")
    split = P("fsdp", "rep")
    in_specs = (
        (batch, batch, P(("rep", "fsdp")), P(), vector, vector)
        + (matrix,) * 4
        + (vector,)
        + (matrix,) * 4
        + (vector,)
        + (matrix,) * 3
        + (batch,)
    )
    out_specs = (
        (batch, batch, batch, vector, vector)
        + (split,) * 4
        + (vector,)
        + (split,) * 4
        + (vector,)
        + (split,) * 3
    )
    return jax.shard_map(body, mesh=mesh, in_specs=in_specs, out_specs=out_specs, check_vma=False)
```

```python
import functools

import jax
import jax.numpy as jnp
from jax import lax
from jax.experimental import pallas as pl
from jax.experimental.pallas import tpu as pltpu
from jax.sharding import PartitionSpec as P

NHEAD = 12
DHEAD = 64
BUCKETS = 32
PAIRS = NHEAD // 2
LANES = 2 * DHEAD
PREFIX_MAX = 256

EPSILON = 1e-06
CUBIC_TERM = 0.044715
SQRT_TWO_PI = 0.7978845608028654
NEGATIVE = -1000000000.0

F32 = jnp.float32
BF16 = jnp.bfloat16
LAST_DIMS = (((1,), (1,)), ((), ()))


def matmul(left_side, right_side):
    return jnp.dot(left_side, right_side, preferred_element_type=F32)


def back_term(gradient, weight):
    return lax.dot_general(gradient, weight, LAST_DIMS, preferred_element_type=F32)


def inverse_rms(values):
    return lax.rsqrt(jnp.mean(values * values, axis=-1, keepdims=True) + EPSILON)


def norm_back(values, scale_rows, gain_vec, upstream):
    weighted = upstream * gain_vec
    gain_grad = jnp.sum(upstream * values * scale_rows, axis=0)
    input_grad = scale_rows * weighted - values * scale_rows * scale_rows * scale_rows * jnp.mean(
        values * weighted, axis=-1, keepdims=True
    )
    return (input_grad, gain_grad)


def one_head(rows, head):
    lane = lax.broadcasted_iota(jnp.int32, rows.shape, 1)
    keep = lane < DHEAD if head == 0 else lane >= DHEAD
    return jnp.where(keep, rows, jnp.zeros_like(rows))


def flipped(rows):
    return rows.astype(F32).T.astype(BF16)


def tree(fold, rows, groups):
    step = rows.shape[0] // groups
    total = rows[:step]
    for index in range(1, groups):
        total = fold(total, rows[index * step : (index + 1) * step])
    return total


def column_max(rows, groups):
    return jnp.max(tree(jnp.maximum, rows, groups), axis=0, keepdims=True)


def column_sum(rows, groups):
    return jnp.sum(tree(jnp.add, rows, groups), axis=0, keepdims=True)


def allowed_at(shape, key_start, query_start, prefix):
    key = lax.broadcasted_iota(jnp.int32, shape, 0) + key_start
    query = lax.broadcasted_iota(jnp.int32, shape, 1) + query_start
    return (key <= query) | (key < prefix)


def skew_kernel(table_ref, buckets_ref, out_ref):
    bucket = lax.broadcasted_iota(jnp.int32, (BUCKETS, buckets_ref.shape[1]), 0)
    onehot = (bucket == buckets_ref[...]).astype(BF16)
    by_offset = matmul(table_ref[...], onehot)
    width = out_ref.shape[2]
    total = by_offset.shape[1]
    for head in range(NHEAD):
        rows = jnp.broadcast_to(by_offset[head : head + 1], (LANES, total))
        rolled = pltpu.roll(rows, total - (LANES - 1), 1, stride=1, stride_axis=0)
        out_ref[head] = rolled[:, :width]


def skewed_bias(table, buckets_back, length):
    total = 2 * length
    return pl.pallas_call(
        skew_kernel,
        out_shape=jax.ShapeDtypeStruct((NHEAD, LANES, total - LANES), F32),
        name="skewed_bias",
    )(jnp.pad(table, ((0, 4), (0, 0))), buckets_back)


HEADROOM = 70.0


def self_forward(prefix_ref, query_ref, key_ref, value_ref, bias_ref, out_ref, lse_ref):
    length = query_ref.shape[0]
    block = 256
    prefix = prefix_ref[pl.program_id(0)]
    queries = query_ref[...]
    keys = key_ref[...]
    values = flipped(value_ref[...])

    def run(exact):
        excess = jnp.zeros((1, block), F32)
        for start in range(0, length, block):
            stop = start + block
            count = max(PREFIX_MAX, stop)
            outs = []
            for head in range(2):
                scores = back_term(keys[:count], one_head(queries[start:stop], head))
                parts = []
                for base in range(0, count, LANES):
                    shift = length - LANES - base + start
                    part = scores[base : base + LANES] + bias_ref[head, :, shift : shift + block]
                    if base + LANES - 1 > start:
                        part = jnp.where(
                            allowed_at(part.shape, base, start, prefix), part, NEGATIVE
                        )
                    parts.append(part)
                top = parts[0]
                for part in parts[1:]:
                    top = jnp.maximum(top, part)
                top = column_max(top, 4)
                anchor = top if exact else column_max(parts[0], 4)
                if not exact:
                    excess = jnp.maximum(excess, top - anchor)
                shares = [jnp.exp(part - anchor) for part in parts]
                total = shares[0]
                for share in shares[1:]:
                    total = total + share
                total = column_sum(total, 4)
                share = jnp.concatenate([item.astype(BF16) for item in shares], axis=0)
                context = matmul(values[head * DHEAD : (head + 1) * DHEAD, :count], share)
                outs.append(context * (1.0 / total))
                lse_ref[head : head + 1, start:stop] = anchor + jnp.log(total)
            out_ref[start:stop, :] = jnp.concatenate(outs, axis=0).T.astype(BF16)
        return jnp.max(excess)

    excess = run(False)

    @pl.when(excess > HEADROOM)
    def _():
        run(True)


def cross_forward(query_ref, key_ref, value_ref, out_ref, lse_ref):
    keys = key_ref[...]
    values = flipped(value_ref[...])
    queries = query_ref[...]

    def run(exact):
        excess = jnp.zeros((1, queries.shape[0]), F32)
        ahead = [back_term(keys, one_head(queries, head)) for head in range(2)]
        outs = []
        for head in range(2):
            scores = ahead[head]
            top = column_max(scores, 16)
            anchor = top if exact else column_max(scores[: 2 * LANES], 8)
            if not exact:
                excess = jnp.maximum(excess, top - anchor)
            share = jnp.exp(scores - anchor)
            total = column_sum(share, 16)
            context = matmul(values[head * DHEAD : (head + 1) * DHEAD], share.astype(BF16))
            outs.append(context * (1.0 / total))
            lse_ref[head : head + 1, :] = anchor + jnp.log(total)
        out_ref[...] = jnp.concatenate(outs, axis=0).T.astype(BF16)
        return jnp.max(excess)

    excess = run(False)

    @pl.when(excess > HEADROOM)
    def _():
        run(True)


def cross_backward(
    query_ref, key_ref, value_ref, up_ref, context_ref, lse_ref, dq_ref, dk_ref, dv_ref
):
    length = query_ref.shape[0]
    block = 256
    keys = key_ref[...]
    values = value_ref[...]
    queries = query_ref[...]
    upstream = up_ref[...]
    keys_flipped = flipped(keys)
    inner = (upstream.astype(F32) * context_ref[...].astype(F32)).T
    key_grad = None
    value_grad = None
    for start in range(0, length, block):
        rows = slice(start, start + block)
        grads = []
        for head in range(2):
            sub = slice(head * DHEAD, (head + 1) * DHEAD)
            query = one_head(queries[rows], head)
            above = one_head(upstream[rows], head)
            row_inner = jnp.sum(inner[sub, rows], axis=0, keepdims=True)
            shares = jnp.exp(back_term(keys, query) - lse_ref[head : head + 1, rows])
            share_grad = back_term(values, above)
            score_grad = (shares * (share_grad - row_inner)).astype(BF16)
            value_part = matmul(shares.astype(BF16), above)
            key_part = matmul(score_grad, query)
            value_grad = value_part if value_grad is None else value_grad + value_part
            key_grad = key_part if key_grad is None else key_grad + key_part
            grads.append(matmul(keys_flipped[sub], score_grad))
        dq_ref[rows, :] = jnp.concatenate(grads, axis=0).T.astype(BF16)
    dk_ref[...] = key_grad.astype(BF16)
    dv_ref[...] = value_grad.astype(BF16)


def self_backward(
    prefix_ref,
    query_ref,
    key_ref,
    value_ref,
    up_ref,
    context_ref,
    lse_ref,
    bias_ref,
    dq_ref,
    dk_ref,
    dv_ref,
    diag_ref,
    acc_ref,
):
    length = query_ref.shape[0]
    block = 256
    step = pl.program_id(1)
    prefix = prefix_ref[step]

    @pl.when(step == 0)
    def _():
        acc_ref[...] = jnp.zeros_like(acc_ref)

    queries = query_ref[...]
    keys = key_ref[...]
    values = value_ref[...]
    upstream = up_ref[...]
    keys_flipped = flipped(keys)
    inner = (upstream.astype(F32) * context_ref[...].astype(F32)).T
    count_all = length // block
    key_grad = [None] * count_all
    value_grad = [None] * count_all
    for start in range(0, length, block):
        stop = start + block
        count = max(PREFIX_MAX, stop)
        rows = slice(start, stop)
        grads = []
        for head in range(2):
            sub = slice(head * DHEAD, (head + 1) * DHEAD)
            query = one_head(queries[rows], head)
            above = one_head(upstream[rows], head)
            row_inner = jnp.sum(inner[sub, rows], axis=0, keepdims=True)
            row_lse = lse_ref[head : head + 1, rows]
            scores = back_term(keys[:count], query)
            share_grad = back_term(values[:count], above)
            shares = []
            score_grads = []
            for base in range(0, count, LANES):
                part = slice(base, base + LANES)
                shift = length - LANES - base + start
                share = jnp.exp(
                    scores[part] + bias_ref[head, :, shift : shift + block] - row_lse
                )
                if base + LANES - 1 > start:
                    share = jnp.where(allowed_at(share.shape, base, start, prefix), share, 0.0)
                score_grad = share * (share_grad[part] - row_inner)
                acc_ref[head, :, shift : shift + block] += score_grad
                shares.append(share.astype(BF16))
                score_grads.append(score_grad.astype(BF16))
            share = jnp.concatenate(shares, axis=0)
            score_grad = jnp.concatenate(score_grads, axis=0)
            value_part = matmul(share, above)
            key_part = matmul(score_grad, query)
            for index in range(count // block):
                part = slice(index * block, (index + 1) * block)
                if value_grad[index] is None:
                    value_grad[index] = value_part[part]
                    key_grad[index] = key_part[part]
                else:
                    value_grad[index] = value_grad[index] + value_part[part]
                    key_grad[index] = key_grad[index] + key_part[part]
            grads.append(matmul(keys_flipped[sub, :count], score_grad))
        dq_ref[rows, :] = jnp.concatenate(grads, axis=0).T.astype(BF16)
    for index in range(count_all):
        part = slice(index * block, (index + 1) * block)
        dk_ref[part, :] = key_grad[index].astype(BF16)
        dv_ref[part, :] = value_grad[index].astype(BF16)

    @pl.when(step == pl.num_programs(1) - 1)
    def _():
        total = 2 * length
        for head in range(2):
            rows = jnp.concatenate([acc_ref[head], jnp.zeros((LANES, LANES), F32)], axis=1)
            half = LANES // 2
            while half >= 1:
                rows = rows[:half] + pltpu.roll(rows[half:], total - half, 1)
                half //= 2
            diag_ref[head : head + 1, :] = pltpu.roll(rows, LANES - 1, 1)


def spec(shape, index):
    return pl.BlockSpec(shape, index)


def run_self_forward(prefix, qkv, bias, nseq):
    length = qkv.shape[0] // nseq
    return pl.pallas_call(
        self_forward,
        grid_spec=pltpu.PrefetchScalarGridSpec(
            num_scalar_prefetch=1,
            grid=(nseq, PAIRS),
            in_specs=[
                spec((length, LANES), lambda s, p, _: (s, p)),
                spec((length, LANES), lambda s, p, _: (s, PAIRS + p)),
                spec((length, LANES), lambda s, p, _: (s, 2 * PAIRS + p)),
                spec((2, LANES, 2 * length - LANES), lambda s, p, _: (p, 0, 0)),
            ],
            out_specs=[
                spec((length, LANES), lambda s, p, _: (s, p)),
                spec((None, None, 2, length), lambda s, p, _: (s, p, 0, 0)),
            ],
        ),
        out_shape=[
            jax.ShapeDtypeStruct((qkv.shape[0], PAIRS * LANES), BF16),
            jax.ShapeDtypeStruct((nseq, PAIRS, 2, length), F32),
        ],
        cost_estimate=pl.CostEstimate(
            flops=20_000_000_000, bytes_accessed=12_000_000, transcendentals=0
        ),
        name="self_forward",
    )(prefix, qkv, qkv, qkv, bias)


def run_cross_forward(query, kv, nseq):
    length = query.shape[0] // nseq
    count = kv.shape[0] // nseq
    return pl.pallas_call(
        cross_forward,
        grid=(nseq, PAIRS),
        in_specs=[
            spec((length, LANES), lambda s, p: (s, p)),
            spec((count, LANES), lambda s, p: (s, p)),
            spec((count, LANES), lambda s, p: (s, PAIRS + p)),
        ],
        out_specs=[
            spec((length, LANES), lambda s, p: (s, p)),
            spec((None, None, 2, length), lambda s, p: (s, p, 0, 0)),
        ],
        out_shape=[
            jax.ShapeDtypeStruct(query.shape, BF16),
            jax.ShapeDtypeStruct((nseq, PAIRS, 2, length), F32),
        ],
        cost_estimate=pl.CostEstimate(
            flops=24_000_000_000, bytes_accessed=10_000_000, transcendentals=0
        ),
        name="cross_forward",
    )(query, kv, kv)


def run_cross_backward(query, kv, upstream, context, lse, nseq):
    length = query.shape[0] // nseq
    count = kv.shape[0] // nseq
    rows = spec((length, LANES), lambda s, p: (s, p))
    wide = spec((count, LANES), lambda s, p: (s, p))
    return pl.pallas_call(
        cross_backward,
        grid=(nseq, PAIRS),
        in_specs=[
            rows,
            wide,
            spec((count, LANES), lambda s, p: (s, PAIRS + p)),
            rows,
            rows,
            spec((None, None, 2, length), lambda s, p: (s, p, 0, 0)),
        ],
        out_specs=[rows, wide, wide],
        out_shape=[
            jax.ShapeDtypeStruct(query.shape, BF16),
            jax.ShapeDtypeStruct((kv.shape[0], PAIRS * LANES), BF16),
            jax.ShapeDtypeStruct((kv.shape[0], PAIRS * LANES), BF16),
        ],
        cost_estimate=pl.CostEstimate(
            flops=36_000_000_000, bytes_accessed=20_000_000, transcendentals=0
        ),
        name="cross_backward",
    )(query, kv, kv, upstream, context, lse)


def run_self_backward(prefix, qkv, upstream, context, lse, bias, nseq):
    length = qkv.shape[0] // nseq
    rows = spec((length, LANES), lambda p, s, _: (s, p))
    return pl.pallas_call(
        self_backward,
        grid_spec=pltpu.PrefetchScalarGridSpec(
            num_scalar_prefetch=1,
            grid=(PAIRS, nseq),
            in_specs=[
                rows,
                spec((length, LANES), lambda p, s, _: (s, PAIRS + p)),
                spec((length, LANES), lambda p, s, _: (s, 2 * PAIRS + p)),
                rows,
                rows,
                spec((None, None, 2, length), lambda p, s, _: (s, p, 0, 0)),
                spec((2, LANES, 2 * length - LANES), lambda p, s, _: (p, 0, 0)),
            ],
            out_specs=[
                rows,
                rows,
                rows,
                spec((None, 2, 2 * length), lambda p, s, _: (p, 0, 0)),
            ],
            scratch_shapes=[pltpu.VMEM((2, LANES, 2 * length - LANES), F32)],
        ),
        out_shape=[jax.ShapeDtypeStruct(upstream.shape, BF16)] * 3
        + [jax.ShapeDtypeStruct((PAIRS, 2, 2 * length), F32)],
        cost_estimate=pl.CostEstimate(
            flops=24_000_000_000, bytes_accessed=20_000_000, transcendentals=0
        ),
        name="self_backward",
    )(prefix, qkv, qkv, qkv, upstream, context, lse, bias)


FEED_BLOCK = 256


def feed_kernel(
    middle_ref,
    context_ref,
    out_proj_ref,
    gain_ref,
    up_grad_ref,
    gate_ref,
    up_ref,
    down_ref,
    result_ref,
    later_grad_ref,
    branch_ref,
    context_grad_ref,
    gain_grad_ref,
    down_term_ref,
    pair_term_ref,
    later_ref,
    normed_ref,
    flipped_ref,
    result_acc,
    third_acc,
):
    step = pl.program_id(0)
    count = middle_ref.shape[0]
    chunk = 256
    chunks = [slice(start, start + chunk) for start in range(0, count, chunk)]

    @pl.when(step == 0)
    def _():
        for rows in chunks:
            later = middle_ref[rows] + matmul(context_ref[rows], out_proj_ref[...])
            normed = (later * inverse_rms(later) * gain_ref[...]).astype(BF16)
            later_ref[rows] = later
            normed_ref[rows] = normed
            flipped_ref[:, rows] = flipped(normed)
            result_acc[rows] = jnp.zeros_like(later)
            third_acc[rows] = jnp.zeros_like(later)

    gate_proj = gate_ref[...]
    up_proj = up_ref[...]
    down_proj = down_ref[...]
    hidden_flipped = []
    gate_grads = []
    lift_grads = []
    for rows in chunks:
        normed = normed_ref[rows]
        gate = matmul(normed, gate_proj)
        lift = matmul(normed, up_proj)
        hidden_grad = back_term(up_grad_ref[rows], down_proj)
        square = gate * gate
        tangent = jnp.tanh(SQRT_TWO_PI * gate * (1.0 + CUBIC_TERM * square))
        half = 0.5 * (1.0 + tangent)
        active = gate * half
        slope = half + 0.5 * gate * (1.0 - tangent * tangent) * (
            SQRT_TWO_PI + 3.0 * CUBIC_TERM * SQRT_TWO_PI * square
        )
        hidden = active * lift
        gate_grad = (hidden_grad * lift * slope).astype(BF16)
        lift_grad = (hidden_grad * active).astype(BF16)
        hidden_flipped.append(hidden.T.astype(BF16))
        gate_grads.append(gate_grad)
        lift_grads.append(lift_grad)
        result_acc[rows] += matmul(hidden.astype(BF16), down_proj)
        third_acc[rows] += back_term(gate_grad, gate_proj) + back_term(lift_grad, up_proj)
    hidden_flipped = jnp.concatenate(hidden_flipped, axis=1)
    down_term_ref[...] = matmul(hidden_flipped, up_grad_ref[...]).astype(BF16)
    gate_grads = jnp.concatenate(gate_grads, axis=0)
    lift_grads = jnp.concatenate(lift_grads, axis=0)
    pair_term_ref[:, :FEED_BLOCK] = matmul(flipped_ref[...], gate_grads).astype(BF16)
    pair_term_ref[:, FEED_BLOCK:] = matmul(flipped_ref[...], lift_grads).astype(BF16)

    @pl.when(step == pl.num_programs(0) - 1)
    def _():
        gain_grad = jnp.zeros(gain_ref.shape, F32)
        for rows in chunks:
            later = later_ref[rows]
            result_ref[rows] = (later + result_acc[rows]).astype(BF16)
            carry, part = norm_back(later, inverse_rms(later), gain_ref[...], third_acc[rows])
            gain_grad = gain_grad + part[None, :]
            later_grad = up_grad_ref[rows].astype(F32) + carry
            branch = later_grad.astype(BF16)
            later_grad_ref[rows] = later_grad
            branch_ref[rows] = branch
            context_grad_ref[rows] = back_term(branch, out_proj_ref[...]).astype(BF16)
        gain_grad_ref[...] = gain_grad


def run_feed(middle, context, out_proj, out_block, gain, upstream, gate_up, down):
    count, width = middle.shape
    ffn = down.shape[0]
    blocks = ffn // FEED_BLOCK

    def whole(shape, **extra):
        return pl.BlockSpec(shape, lambda j: (0, 0), **extra)

    once = {"pipeline_mode": pl.Buffered(1)}
    rows = (count, width)
    return pl.pallas_call(
        feed_kernel,
        grid=(blocks,),
        in_specs=[
            whole(rows, **once),
            whole(rows, **once),
            pl.BlockSpec((width, width), lambda j: (0, out_block), **once),
            whole((1, width)),
            whole(rows, **once),
            spec((width, FEED_BLOCK), lambda j: (0, j)),
            spec((width, FEED_BLOCK), lambda j: (0, blocks + j)),
            spec((FEED_BLOCK, width), lambda j: (j, 0)),
        ],
        out_specs=[
            whole(rows),
            whole(rows),
            whole(rows),
            whole(rows),
            whole((1, width)),
            spec((FEED_BLOCK, width), lambda j: (j, 0)),
            spec((width, 2 * FEED_BLOCK), lambda j: (0, j)),
        ],
        out_shape=[
            jax.ShapeDtypeStruct(rows, BF16),
            jax.ShapeDtypeStruct(rows, F32),
            jax.ShapeDtypeStruct(rows, BF16),
            jax.ShapeDtypeStruct(rows, BF16),
            jax.ShapeDtypeStruct((1, width), F32),
            jax.ShapeDtypeStruct((ffn, width), BF16),
            jax.ShapeDtypeStruct((width, 2 * ffn), BF16),
        ],
        scratch_shapes=[
            pltpu.VMEM(rows, F32),
            pltpu.VMEM(rows, BF16),
            pltpu.VMEM((width, count), BF16),
            pltpu.VMEM(rows, F32),
            pltpu.VMEM(rows, F32),
        ],
        cost_estimate=pl.CostEstimate(
            flops=32_000_000_000, bytes_accessed=40_000_000, transcendentals=0
        ),
        compiler_params=pltpu.CompilerParams(vmem_limit_bytes=60 << 20),
        name="feed",
    )(middle, context, out_proj, gain, upstream, gate_up, gate_up, down)


def close_kernel(count, project, *refs):
    values_ref, carry_ref, gain_ref, left_ref, right_ref = refs[:5]
    grad_refs = refs[5 : 5 + count]
    weight_refs = refs[5 + count : 5 + 2 * count]
    at = 5 + 2 * count
    if project:
        proj_ref = refs[at]
        at += 1
    out_ref, gain_grad_ref = refs[at : at + 2]
    term_refs = refs[at + 2 : at + 3 + count]
    at += 3 + count
    if project:
        branch_ref, projected_ref = refs[at : at + 2]
        at += 2
    sums = refs[at : at + 1 + count]
    gain_sum = refs[at + 1 + count]
    step = pl.program_id(0)

    @pl.when(step == 0)
    def _():
        gain_sum[...] = jnp.zeros_like(gain_sum)
        for total in sums:
            total[...] = jnp.zeros_like(total)

    values = values_ref[...].astype(F32)
    gain = gain_ref[...]
    scale = inverse_rms(values)
    normed = (values * scale * gain).T.astype(BF16)
    upstream = None
    for index in range(count):
        grad = grad_refs[index][...]
        sums[index][...] += matmul(normed, grad)
        part = back_term(grad, weight_refs[index][...])
        upstream = part if upstream is None else upstream + part
    sums[count][...] += matmul(flipped(left_ref[...]), right_ref[...])
    carry, part = norm_back(values, scale, gain, upstream)
    gain_sum[...] += part[None, :]
    result = carry_ref[...] + carry
    out_ref[...] = result
    if project:
        branch = result.astype(BF16)
        branch_ref[...] = branch
        projected_ref[...] = back_term(branch, proj_ref[...]).astype(BF16)

    @pl.when(step == pl.num_programs(0) - 1)
    def _():
        gain_grad_ref[...] = gain_sum[...]
        for term, total in zip(term_refs, sums):
            term[...] = total[...].astype(BF16)


def run_close(values, carry, gain, left, right, grads, weights, project, name):
    rows, width = values.shape
    count = len(grads)
    block = 512
    wide = spec((block, width), lambda i: (i, 0))

    def columns(index):
        return pl.BlockSpec((width, width), lambda i: (0, index), pipeline_mode=pl.Buffered(1))

    whole = [spec((1, width), lambda i: (0, 0))]
    square = [spec((width, width), lambda i: (0, 0))] * (count + 1)
    extra = [] if project is None else [project]
    out_shape = [
        jax.ShapeDtypeStruct((rows, width), F32),
        jax.ShapeDtypeStruct((1, width), F32),
    ] + [jax.ShapeDtypeStruct((width, width), BF16)] * (count + 1)
    out_shape += [jax.ShapeDtypeStruct((rows, width), BF16)] * (2 * len(extra))
    return pl.pallas_call(
        functools.partial(close_kernel, count, project is not None),
        grid=(rows // block,),
        in_specs=[wide, wide]
        + whole
        + [wide] * (2 + count)
        + [columns(index) for _, index in weights + extra],
        out_specs=[wide] + whole + square + [wide] * (2 * len(extra)),
        out_shape=out_shape,
        scratch_shapes=[pltpu.VMEM((width, width), F32)] * (count + 1)
        + [pltpu.VMEM((1, width), F32)],
        cost_estimate=pl.CostEstimate(
            flops=8_000_000_000, bytes_accessed=25_000_000, transcendentals=0
        ),
        compiler_params=pltpu.CompilerParams(vmem_limit_bytes=60 << 20),
        name=name,
    )(values, carry, gain, left, right, *grads, *[item for item, _ in weights + extra])


def memory_kernel(
    memory_ref, key_grad_ref, value_grad_ref, key_ref, value_ref, out_ref, *rest
):
    key_term_ref, value_term_ref, key_sum, value_sum = rest
    step = pl.program_id(0)

    @pl.when(step == 0)
    def _():
        key_sum[...] = jnp.zeros_like(key_sum)
        value_sum[...] = jnp.zeros_like(value_sum)

    rows = flipped(memory_ref[...])
    key_grad = key_grad_ref[...]
    value_grad = value_grad_ref[...]
    out_ref[...] = back_term(key_grad, key_ref[...]) + back_term(value_grad, value_ref[...])
    key_sum[...] += matmul(rows, key_grad)
    value_sum[...] += matmul(rows, value_grad)

    @pl.when(step == pl.num_programs(0) - 1)
    def _():
        key_term_ref[...] = key_sum[...].astype(BF16)
        value_term_ref[...] = value_sum[...].astype(BF16)


def run_memory(memory, key_grad, value_grad, weights, key_block, value_block):
    rows, width = memory.shape
    block = 1024
    wide = spec((block, width), lambda i: (i, 0))
    square = spec((width, width), lambda i: (0, 0))

    def columns(index):
        return pl.BlockSpec((width, width), lambda i: (0, index), pipeline_mode=pl.Buffered(1))

    return pl.pallas_call(
        memory_kernel,
        grid=(rows // block,),
        in_specs=[wide, wide, wide, columns(key_block), columns(value_block)],
        out_specs=[wide, square, square],
        out_shape=[
            jax.ShapeDtypeStruct((rows, width), F32),
            jax.ShapeDtypeStruct((width, width), BF16),
            jax.ShapeDtypeStruct((width, width), BF16),
        ],
        scratch_shapes=[pltpu.VMEM((width, width), F32)] * 2,
        cost_estimate=pl.CostEstimate(
            flops=10_000_000_000, bytes_accessed=18_000_000, transcendentals=0
        ),
        compiler_params=pltpu.CompilerParams(vmem_limit_bytes=60 << 20),
        name="memory_close",
    )(memory, key_grad, value_grad, weights, weights)


MESH = pl.DeviceIdType.MESH


class Place:
    def __init__(self, line):
        self.line = line
        rep = lax.axis_index("rep")
        fsdp = lax.axis_index("fsdp")
        self.rep = rep
        self.fsdp = fsdp
        self.y = rep // 2
        self.x = rep % 2
        self.z = fsdp // 2
        self.core = fsdp % 2
        self.x_rep = self.y * 2 + 1 - self.x
        self.y_rep = (1 - self.y) * 2 + self.x

    def at_x(self):
        return {"rep": self.x_rep, "fsdp": self.fsdp}

    def at_y(self):
        return {"rep": self.y_rep, "fsdp": self.fsdp}

    def at_partner(self):
        return {"rep": self.rep, "fsdp": self.z * 2 + 1 - self.core}

    def at_line(self, side):
        return {"rep": self.rep, "fsdp": self.fsdp + (2 if side == 0 else -2)}

    def has_next(self, side):
        return self.z < self.line - 1 if side == 0 else self.z > 0

    def has_last(self, side):
        return self.has_next(1 - side)

    def arrives(self, side, hop):
        if side == 0:
            return self.z - 1 - hop >= 0
        return self.z + 1 + hop <= self.line - 1

    def source(self, side, hop):
        return self.z - 1 - hop if side == 0 else self.z + 1 + hop

    def at_far(self):
        half = self.line // 2
        return {"rep": self.rep, "fsdp": (self.z + half) % self.line * 2 + self.core}

    def greet(self, wide=False):
        barrier = pltpu.get_barrier_semaphore()
        targets = [self.at_x(), self.at_y(), self.at_partner()]
        if wide:
            targets.append({"rep": 3 - self.rep, "fsdp": self.fsdp})
            targets.append(self.at_far())
        for target in targets:
            pl.semaphore_signal(barrier, inc=1, device_id=target, device_id_type=MESH)
        for side in range(2):

            @pl.when(self.has_next(side))
            def _():
                pl.semaphore_signal(
                    barrier, inc=1, device_id=self.at_line(side), device_id_type=MESH
                )

        count = len(targets)
        for side in range(2):
            count = count + jnp.where(self.has_next(side), 1, 0)
        pl.semaphore_wait(barrier, count)


def remote(source, target, send, recv, device):
    return pltpu.make_async_remote_copy(
        src_ref=source,
        dst_ref=target,
        send_sem=send,
        recv_sem=recv,
        device_id=device,
        device_id_type=MESH,
    )


class GatherShape:
    def __init__(self, parts, by_rows):
        self.rows = parts[0].shape[0]
        self.widths = [part.shape[1] for part in parts]
        self.starts = [sum(self.widths[:index]) for index in range(len(parts))]
        self.columns = sum(self.widths)
        self.by_rows = by_rows

    def full(self, ref, owner):
        return ref.at[pl.ds(pl.multiple_of(owner * self.rows, 32), self.rows)]

    def piece(self, ref, owner, part, half=None):
        base = owner * self.rows
        if self.by_rows:
            rows = self.rows // 4
            base = base + part * rows
        else:
            rows = self.rows
        if half is not None:
            rows = rows // 2
            base = base + half * rows
        row_slice = pl.ds(pl.multiple_of(base, 16), rows)
        if self.by_rows:
            return ref.at[row_slice]
        width = self.columns // 4
        return ref.at[row_slice, pl.ds(pl.multiple_of(part * width, LANES), width)]


def gather_sems(line):
    hops = line - 1
    return [pltpu.SemaphoreType.DMA((5, 2, 2, hops)), pltpu.SemaphoreType.DMA((4,))] + [
        pltpu.SemaphoreType.DMA((2, 2, hops))
    ]


def gather_steps(place, shape, src, own, dst, sems):
    hop_sem, own_sem, pair_sem = sems
    hops = place.line - 1
    me = place.fsdp

    def load(index):
        at = pl.ds(shape.starts[index], shape.widths[index])
        return pltpu.make_async_copy(src[index], own.at[:, at], own_sem.at[0])

    def loaded():
        return pltpu.make_async_copy(own, own, own_sem.at[0])

    def keep():
        return pltpu.make_async_copy(own, shape.full(dst, me), own_sem.at[1])

    def own_pair():
        return remote(
            own, shape.full(dst, me), own_sem.at[2], own_sem.at[3], place.at_partner()
        )

    def owner(side, hop):
        return place.source(side, hop) * 2 + place.core

    def line_first(side):
        return remote(
            shape.piece(own, 0, place.rep),
            shape.piece(dst, me, place.rep),
            hop_sem.at[0, 0, side, 0],
            hop_sem.at[0, 1, side, 0],
            place.at_line(side),
        )

    def moved(kind, side, hop, block, device):
        return remote(
            block, block, hop_sem.at[kind, 0, side, hop], hop_sem.at[kind, 1, side, hop], device
        )

    def line_next(side, hop):
        block = shape.piece(dst, owner(side, hop - 1), place.rep)
        return moved(0, side, hop, block, place.at_line(side))

    def line_arrival(side, hop):
        block = shape.piece(dst, owner(side, hop), place.rep)
        return moved(0, side, hop, block, place.at_line(side))

    def plane(axis, side, hop):
        block = shape.piece(dst, owner(side, hop), place.rep)
        return moved(1 + axis, side, hop, block, place.at_x() if axis == 0 else place.at_y())

    def cross(axis, side, hop):
        part = place.x_rep if axis == 1 else place.y_rep
        block = shape.piece(dst, owner(side, hop), part, 1 - axis)
        return moved(3 + axis, side, hop, block, place.at_x() if axis == 0 else place.at_y())

    def pair(side, hop):
        block = shape.full(dst, owner(side, hop))
        return remote(
            block, block, pair_sem.at[0, side, hop], pair_sem.at[1, side, hop], place.at_partner()
        )

    def each(fn):
        def run():
            for hop in range(hops):
                for side in range(2):
                    pl.when(place.arrives(side, hop))(functools.partial(fn, side, hop))

        return run

    def start():
        for index in range(len(src)):
            load(index).start()
        loaded().wait()
        for side in range(2):
            pl.when(place.has_next(side))(lambda side=side: line_first(side).start())
        own_pair().start()
        keep().start()

    def arrive(side, hop):
        line_arrival(side, hop).wait_recv()
        if hop + 1 < hops:
            pl.when(place.has_next(side))(lambda: line_next(side, hop + 1).start())
        plane(0, side, hop).start()
        plane(1, side, hop).start()

    def turn(side, hop):
        plane(0, side, hop).wait_recv()
        cross(1, side, hop).start()
        plane(1, side, hop).wait_recv()
        cross(0, side, hop).start()

    def hand(side, hop):
        cross(0, side, hop).wait_recv()
        cross(1, side, hop).wait_recv()
        pair(side, hop).start()

    def finish():
        def last(side, hop):
            pair(side, hop).wait()
            for axis in range(2):
                plane(axis, side, hop).wait_send()
                cross(axis, side, hop).wait_send()
            if hop + 1 < hops:
                pl.when(place.has_next(side))(lambda: line_next(side, hop + 1).wait_send())

        each(last)()
        for side in range(2):
            pl.when(place.has_next(side))(lambda side=side: line_first(side).wait_send())
        own_pair().wait()
        keep().wait()

    return start, each(arrive), each(turn), each(hand), finish


def gather_kernel(shapes, line, *refs):
    count = len(shapes)
    sources = []
    at = 0
    for shape in shapes:
        sources.append(refs[at : at + len(shape.widths)])
        at += len(shape.widths)
    targets = refs[at : at + count]
    scratch = refs[at + count :]
    place = Place(line)
    place.greet()
    plans = []
    for index, shape in enumerate(shapes):
        own, *sems = scratch[4 * index : 4 * index + 4]
        plans.append(gather_steps(place, shape, sources[index], own, targets[index], sems))
    for stage in range(5):
        for plan in plans:
            plan[stage]()


def fast_gather(groups, line, by_rows, collective_id):
    shapes = [GatherShape(group, flag) for group, flag in zip(groups, by_rows)]
    scratch = []
    for shape in shapes:
        scratch.append(pltpu.VMEM((shape.rows, shape.columns), BF16))
        scratch.extend(gather_sems(line))
    anywhere = pl.BlockSpec(memory_space=pl.ANY)
    blocks = [block for group in groups for block in group]
    return pl.pallas_call(
        functools.partial(gather_kernel, shapes, line),
        in_specs=[anywhere] * len(blocks),
        out_specs=[anywhere] * len(groups),
        out_shape=[
            jax.ShapeDtypeStruct((2 * line * s.rows, s.columns), BF16) for s in shapes
        ],
        scratch_shapes=scratch,
        compiler_params=pltpu.CompilerParams(collective_id=collective_id, has_side_effects=True),
        name="fast_gather",
    )(*blocks)


class ReduceShape:
    def __init__(self, kind, rows, columns, sources):
        self.kind = kind
        self.rows = rows
        self.sources = sources
        if kind == "rows":
            self.block = (rows // 8, columns)
        elif kind == "pair":
            self.block = (rows // 2, columns // 2)
        else:
            self.block = (rows // 2, columns)
        self.exchange = kind != "pair"
        self.part_rows = rows // 4 if kind == "rows" else rows
        self.part_columns = columns // 4

    def pieces(self, refs, owner, half, quarter):
        rows, columns = self.block
        if self.kind == "rows":
            base = owner * self.rows + quarter * (self.rows // 4) + half * rows
            return [(refs[0].at[pl.ds(pl.multiple_of(base, 16), rows)], 0, columns)]
        at = pl.ds(pl.multiple_of(owner * self.rows + half * rows, 16), rows)
        if self.kind == "four":
            return [(refs[quarter].at[at], 0, columns)]
        width = columns // 2
        cut = slice(quarter * width, (quarter + 1) * width)
        return [(refs[index].at[at, cut], index * width, width) for index in range(2)]

    def out_shape(self):
        if self.exchange:
            return jax.ShapeDtypeStruct((4, self.part_rows, self.part_columns), F32)
        return jax.ShapeDtypeStruct((self.rows, self.block[1]), F32)

    def scratch(self, line):
        rows, columns = self.block
        dma = pltpu.SemaphoreType.DMA
        buffers = [
            pltpu.VMEM((line, 8, rows, columns), BF16),
            pltpu.VMEM((line, 8, rows, columns), BF16),
            pltpu.VMEM((line, 2, 2, rows, columns), BF16),
            pltpu.VMEM((line, 2, rows, columns), BF16),
            pltpu.VMEM((line, 2, rows, columns), BF16),
            pltpu.VMEM((2, line, 2, rows, columns), BF16),
            pltpu.VMEM((4, self.part_rows, self.part_columns), F32),
            pltpu.VMEM((4, self.part_rows, self.part_columns), F32),
            dma((line,)),
            dma((2, line)),
            dma((2, line, 2)),
            dma((2, line, 2)),
            dma((2, 2, line)),
            dma((2, 3)),
        ]
        return buffers


REDUCE_SCRATCH = 14


def added(left, right):
    return (left.astype(F32) + right.astype(F32)).astype(BF16)


def reduce_steps(place, shape, refs, out, scratch):
    own, other, first_in, second_in, total, line_in, parts, gathered = scratch[:8]
    load_sem, pair_sem, first_sem, second_sem, line_sem, swap_sem = scratch[8:]
    line = place.line
    near = (place.x, place.y)
    far = (place.y, place.x)
    near_device = (place.at_x(), place.at_y())
    far_device = (place.at_y(), place.at_x())

    def quarter_of(half, index):
        high, low = index // 2, index % 2
        return low * 2 + high if half == 0 else high * 2 + low

    def start(z):
        for half in range(2):
            for index in range(4):
                quarter = quarter_of(half, index)
                slot = half * 4 + index
                mine = shape.pieces(refs, 2 * z + place.core, half, quarter)
                theirs = shape.pieces(refs, 2 * z + 1 - place.core, half, quarter)
                for (view, column, width), (view_two, _, _) in zip(mine, theirs):
                    cut = pl.ds(column, width)
                    remote(
                        view_two,
                        other.at[z, slot, :, cut],
                        pair_sem.at[0, z],
                        pair_sem.at[1, z],
                        place.at_partner(),
                    ).start()
                    pltpu.make_async_copy(
                        view, own.at[z, slot, :, cut], load_sem.at[z]
                    ).start()

    def pair_all(z):
        return remote(
            own.at[z], other.at[z], pair_sem.at[0, z], pair_sem.at[1, z], place.at_partner()
        )

    def first(z, half):
        return remote(
            own.at[z, pl.ds(half * 4 + (1 - near[half]) * 2, 2)],
            first_in.at[z, half],
            first_sem.at[0, z, half],
            first_sem.at[1, z, half],
            near_device[half],
        )

    def second(z, half):
        return remote(
            own.at[z, half * 4 + near[half] * 2 + 1 - far[half]],
            second_in.at[z, half],
            second_sem.at[0, z, half],
            second_sem.at[1, z, half],
            far_device[half],
        )

    def along(z, side):
        return remote(
            total.at[z],
            line_in.at[side, z],
            line_sem.at[0, side, z],
            line_sem.at[1, side, z],
            place.at_line(side),
        )

    def pair_add(z):
        pltpu.make_async_copy(own.at[z], own.at[z], load_sem.at[z]).wait()
        pair_all(z).wait_recv()

        @pl.loop(0, 8)
        def _(slot):
            own[z, slot] = added(own[z, slot], other[z, slot])

        for half in range(2):
            first(z, half).start()

    def first_add(z):
        for half in range(2):
            first(z, half).wait_recv()
            base = half * 4 + near[half] * 2

            @pl.loop(0, 2)
            def _(index):
                own[z, base + index] = added(own[z, base + index], first_in[z, half, index])

            second(z, half).start()

    def second_add(z):
        for half in range(2):
            second(z, half).wait_recv()
            mine = half * 4 + near[half] * 2 + far[half]
            total[z, half] = added(own[z, mine], second_in[z, half])

    def line_send(z, side):
        ahead = place.z < z if side == 0 else place.z > z

        @pl.when(ahead)
        def _():
            @pl.when(place.has_last(side))
            def _():
                along(z, side).wait_recv()

                @pl.loop(0, 2)
                def _(half):
                    total[z, half] = added(total[z, half], line_in[side, z, half])

            along(z, side).start()

    def line_end(z):
        @pl.when(place.z == z)
        def _():
            for side in range(2):
                pl.when(place.has_last(side))(lambda: along(z, side).wait_recv())

    def swap(rep_slot, device, index):
        return remote(
            parts.at[rep_slot],
            gathered.at[place.rep],
            swap_sem.at[0, index],
            swap_sem.at[1, index],
            device,
        )

    def swaps():
        corner = 3 - place.rep
        return [
            swap(place.x_rep, place.at_x(), 0),
            swap(place.y_rep, place.at_y(), 1),
            swap(corner, {"rep": corner, "fsdp": place.fsdp}, 2),
        ]

    def finish():
        rows, columns = shape.block
        me = place.z
        for half in range(2):
            result = total[me, half].astype(F32)
            for side in range(2):
                extra = line_in[side, me, half].astype(F32)
                result = result + jnp.where(place.has_last(side), extra, 0.0)
            at = slice(half * rows, (half + 1) * rows)
            if shape.exchange:
                width = shape.part_columns
                for index in range(4):
                    parts[index, at, :] = result[:, index * width : (index + 1) * width]
            else:
                out[at, :] = result
        if shape.exchange:
            for copy in swaps():
                copy.start()
            gathered[place.rep] = parts[place.rep]

    def drain():
        if shape.exchange:
            for copy in swaps():
                copy.wait()
            out[...] = gathered[...]
        for z in range(line):
            pair_all(z).wait_send()
            for half in range(2):
                first(z, half).wait_send()
                second(z, half).wait_send()
            for side in range(2):
                ahead = place.z < z if side == 0 else place.z > z
                pl.when(ahead)(lambda: along(z, side).wait_send())

    order = [line - 1, 0] + [z for z in range(line - 2, 0, -1)]

    def begin():
        for z in order:
            start(z)

    def pairs():
        for z in order:
            pair_add(z)

    def firsts():
        for z in order:
            first_add(z)

    def seconds():
        for index, z in enumerate(order):
            second_add(z)
            if index > 0:
                line_send(order[index - 1], 0)
                line_send(order[index - 1], 1)
        line_send(order[-1], 0)
        line_send(order[-1], 1)

    def close():
        for z in range(line):
            line_end(z)
        finish()

    return begin, pairs, firsts, seconds, close, drain


class VectorSum:
    def __init__(self, place, source, out, scratch):
        self.place = place
        self.source = source
        self.out = out
        self.current, self.incoming, self.sems = scratch
        side = place.z % 2
        near = place.fsdp + 2 - 4 * side
        self.devices = [
            place.at_partner(),
            place.at_x(),
            place.at_y(),
            {"rep": place.rep, "fsdp": near},
            place.at_far(),
        ]

    @staticmethod
    def scratch(shape):
        return [
            pltpu.VMEM((6,) + shape, F32),
            pltpu.VMEM((5,) + shape, F32),
            pltpu.SemaphoreType.DMA((2, 5)),
        ]

    def copy(self, index):
        return remote(
            self.current.at[index],
            self.incoming.at[index],
            self.sems.at[0, index],
            self.sems.at[1, index],
            self.devices[index],
        )

    def round(self, index):
        if index == 0:
            self.current[0] = self.source[...]
        else:
            self.copy(index - 1).wait_recv()
            self.current[index] = self.current[index - 1] + self.incoming[index - 1]
        if index < 5:
            self.copy(index).start()

    def finish(self):
        self.out[...] = self.current[5]
        for index in range(5):
            self.copy(index).wait_send()


def reduce_kernel(shapes, line, vector_count, *refs):
    sources = []
    at = 0
    for shape in shapes:
        sources.append(refs[at : at + shape.sources])
        at += shape.sources
    vector_refs = refs[at : at + vector_count]
    at += vector_count
    outs = refs[at : at + len(shapes)]
    at += len(shapes)
    vector_outs = refs[at : at + vector_count]
    at += vector_count
    place = Place(line)
    place.greet(wide=True)
    plans = []
    for index, shape in enumerate(shapes):
        part = refs[at : at + REDUCE_SCRATCH]
        at += REDUCE_SCRATCH
        plans.append(reduce_steps(place, shape, sources[index], outs[index], part))
    vectors = []
    if vector_count:
        vectors = [VectorSum(place, vector_refs[0], vector_outs[0], refs[at : at + 3])]

    def rounds(*indices):
        for vector in vectors:
            for index in indices:
                vector.round(index)

    rounds(0)
    for plan in plans:
        plan[0]()
    plans[0][1]()
    rounds(1)
    plans[0][2]()
    rounds(2)
    for index, plan in enumerate(plans):
        ahead = plans[index + 1] if index + 1 < len(plans) else None
        if ahead is not None:
            ahead[1]()
        plan[3]()
        if ahead is not None:
            ahead[2]()
    rounds(3)
    for plan in plans:
        plan[4]()
    rounds(4, 5)
    for plan in plans:
        plan[5]()
    for vector in vectors:
        vector.finish()


def fast_reduce(groups, kinds, line, collective_id, vector=None):
    shapes = []
    blocks = []
    scratch = []
    for group, kind in zip(groups, kinds):
        rows, columns = group[0].shape
        shape = ReduceShape(kind, rows // (2 * line), columns, len(group))
        shapes.append(shape)
        blocks.extend(group)
        scratch.extend(shape.scratch(line))
    anywhere = pl.BlockSpec(memory_space=pl.ANY)
    local = pl.BlockSpec(memory_space=pltpu.VMEM)
    in_specs = [anywhere] * len(blocks)
    out_shape = [shape.out_shape() for shape in shapes]
    if vector is not None:
        blocks.append(vector)
        in_specs.append(local)
        out_shape.append(jax.ShapeDtypeStruct(vector.shape, F32))
        scratch.extend(VectorSum.scratch(vector.shape))
    return pl.pallas_call(
        functools.partial(reduce_kernel, shapes, line, 0 if vector is None else 1),
        in_specs=in_specs,
        out_specs=[local] * len(out_shape),
        out_shape=out_shape,
        scratch_shapes=scratch,
        compiler_params=pltpu.CompilerParams(
            collective_id=collective_id, has_side_effects=True, vmem_limit_bytes=60 << 20
        ),
        name="fast_reduce",
    )(*blocks)


PLANE = 4
CHIP = 2
LINE = 4


def small_plane():
    return lax.axis_size("rep") == PLANE and lax.axis_size("fsdp") == CHIP * LINE


def gather(block):
    return lax.all_gather(block, "fsdp", axis=0, tiled=True)


def gather_all(groups, by_rows, collective_id):
    if small_plane():
        return fast_gather(groups, LINE, by_rows, collective_id)
    return [gather(jnp.concatenate(group, axis=1)) for group in groups]


def scatter(block):
    return lax.psum_scatter(block.astype(BF16), "fsdp", scatter_dimension=0, tiled=True)


def column_blocks(block):
    rows = block.shape[0]
    return block.reshape(rows, lax.axis_size("rep"), -1).swapaxes(0, 1)


def scatter_columns(parts):
    count = lax.axis_size("rep")
    rows = parts[0].shape[0]
    split = [part.reshape(rows, count, -1) for part in parts]
    joined = jnp.concatenate(split, axis=2).reshape(rows, -1)
    own = lax.psum_scatter(joined, "rep", scatter_dimension=1, tiled=True)
    sizes = [part.shape[1] // count for part in parts]
    outs = []
    start = 0
    for size in sizes:
        outs.append(own[:, start : start + size].astype(F32))
        start += size
    return outs


def scatter_last(groups, vector, collective_id):
    if small_plane():
        *outs, total = fast_reduce(
            groups, ["four"] * len(groups), LINE, collective_id, vector
        )
        return [[out[index] for index in range(4)] for out in outs], total
    outs = [scatter_columns([scatter(item) for item in group]) for group in groups]
    return outs, lax.psum(vector, ("rep", "fsdp"))


def body(
    tokens,
    memory,
    prefix_len,
    bucket_table,
    rel_bias,
    gain_self,
    self_query,
    self_key,
    self_value,
    self_out,
    gain_cross,
    cross_query,
    cross_key,
    cross_value,
    cross_out,
    gain_feed,
    gate_weight,
    up_weight,
    down_weight,
    out_grad,
):
    nseq, length, width = tokens.shape
    shard = gain_self.shape[0]
    groups = width // shard
    entries = rel_bias.shape[0]
    small = jnp.stack(
        [gain_self, gain_cross, gain_feed, jnp.pad(rel_bias, (0, shard - entries))], axis=1
    )
    small = jnp.pad(small, ((0, 0), (0, 2 * LANES - 4)))
    first, second, down = gather_all(
        [
            [self_query, self_key, self_value, small],
            [self_out, cross_query, cross_key, cross_value, cross_out, small],
            [down_weight],
        ],
        [False, False, True],
        1,
    )
    gate_up_own = jnp.concatenate([gate_weight, up_weight], axis=1)
    gate_up_own, first, second, down = lax.optimization_barrier(
        (gate_up_own, first, second, down)
    )
    gate_up = gather(gate_up_own)
    qkv_proj = first[:, : 3 * width]
    picks = jnp.eye(8, LANES, dtype=BF16)
    vectors = back_term(picks, first[:, 3 * width : 3 * width + LANES])
    gain_first = vectors[0:1]
    gain_second = vectors[1:2]
    gain_third = vectors[2:3]
    table = vectors[3].astype(BF16).reshape(groups, shard)[:, :entries]
    table = table.reshape(NHEAD, BUCKETS)
    out_self = second[:, :width]
    query_cross = second[:, width : 2 * width]
    kv_cross = second[:, 2 * width : 4 * width]

    buckets_back = jnp.pad(bucket_table[::-1], (0, 1)).reshape(1, 2 * length)
    bias = skewed_bias(table, buckets_back, length)

    rows = nseq * length
    start_rows = tokens.reshape(rows, width).astype(F32)
    memory_rows = memory.reshape(-1, width)
    upstream = out_grad.reshape(rows, width)

    scale_first = inverse_rms(start_rows)
    normed_first = (start_rows * scale_first * gain_first).astype(BF16)
    qkv = matmul(normed_first, qkv_proj).astype(BF16)
    context, lse_self = run_self_forward(prefix_len, qkv, bias, nseq)
    middle = start_rows + matmul(context, out_self)
    scale_second = inverse_rms(middle)
    normed_second = (middle * scale_second * gain_second).astype(BF16)
    query_two = matmul(normed_second, query_cross).astype(BF16)
    kv_two = matmul(memory_rows, kv_cross).astype(BF16)
    context_two, lse_cross = run_cross_forward(query_two, kv_two, nseq)
    (
        result,
        later_grad,
        branch_two,
        context_two_grad,
        gain_third_grad,
        down_term,
        pair_term,
    ) = run_feed(middle, context_two, second, 4, gain_third, upstream, gate_up, down)
    down_own = scatter(down_term)
    pair_own = scatter(pair_term)
    query_two_grad, key_two_grad, value_two_grad = run_cross_backward(
        query_two, kv_two, context_two_grad, context_two, lse_cross, nseq
    )
    (
        middle_grad,
        gain_second_grad,
        query_term,
        out_term,
        branch_one,
        context_grad,
    ) = run_close(
        middle,
        later_grad,
        gain_second,
        context_two,
        branch_two,
        [query_two_grad],
        [(second, 1)],
        (second, 0),
        "cross_close",
    )
    memory_grad, key_term, value_term = run_memory(
        memory_rows, key_two_grad, value_two_grad, second, 2, 3
    )
    cross_terms = [query_term, key_term, value_term, out_term]
    query_grad, key_grad, value_grad, diagonal = run_self_backward(
        prefix_len, qkv, context_grad, context, lse_self, bias, nseq
    )
    tokens_grad, gain_first_grad, *self_terms = run_close(
        tokens.reshape(rows, width),
        middle_grad,
        gain_first,
        context,
        branch_one,
        [query_grad, key_grad, value_grad],
        [(first, 0), (first, 1), (first, 2)],
        None,
        "self_close",
    )

    onehot = (
        buckets_back.reshape(-1, 1) == jnp.arange(BUCKETS, dtype=jnp.int32)[None, :]
    ).astype(F32)
    onehot = onehot * (jnp.arange(2 * length) < 2 * length - 1)[:, None]
    bias_grad = jnp.dot(
        diagonal.reshape(NHEAD, 2 * length), onehot, precision=lax.Precision.HIGHEST
    )
    bias_rows = jnp.pad(
        bias_grad.reshape(groups, entries), ((0, 0), (0, shard - entries))
    ).reshape(width)
    vector_block = jnp.pad(
        jnp.concatenate(
            [gain_first_grad, gain_second_grad, gain_third_grad, bias_rows[None]], axis=0
        ),
        ((0, 4), (0, 0)),
    )
    down_own, pair_own, memory_grad, self_terms = lax.optimization_barrier(
        (down_own, pair_own, memory_grad, self_terms)
    )
    down_split = column_blocks(down_own)
    pair_split = column_blocks(pair_own)
    down_split, pair_split, self_terms = lax.optimization_barrier(
        (down_split, pair_split, self_terms)
    )
    down_weight_grad = lax.psum_scatter(down_split, "rep").astype(F32)
    pair_grad = lax.psum_scatter(pair_split, "rep").astype(F32)
    pair_grad = pair_grad.reshape(shard, -1, 2, FEED_BLOCK)
    gate_weight_grad = pair_grad[:, :, 0].reshape(shard, -1)
    up_weight_grad = pair_grad[:, :, 1].reshape(shard, -1)
    (cross_out_grads, self_out_grads), totals = scatter_last(
        [cross_terms, self_terms], vector_block, 3
    )
    own = lax.dynamic_slice(
        totals, (0, lax.axis_index("fsdp") * shard), (totals.shape[0], shard)
    )
    return (
        result.reshape(tokens.shape),
        tokens_grad.reshape(tokens.shape),
        memory_grad.reshape(memory.shape),
        own[3, :entries],
        own[0],
        *self_out_grads,
        own[1],
        *cross_out_grads,
        own[2],
        gate_weight_grad,
        up_weight_grad,
        down_weight_grad,
    )


def solution(mesh):
    batch = P(("rep", "fsdp"), None, None)
    matrix = P("fsdp", None)
    vector = P("fsdp")
    split = P("fsdp", "rep")
    in_specs = (
        (batch, batch, P(("rep", "fsdp")), P(), vector, vector)
        + (matrix,) * 4
        + (vector,)
        + (matrix,) * 4
        + (vector,)
        + (matrix,) * 3
        + (batch,)
    )
    out_specs = (
        (batch, batch, batch, vector, vector)
        + (split,) * 4
        + (vector,)
        + (split,) * 4
        + (vector,)
        + (split,) * 3
    )
    return jax.shard_map(body, mesh=mesh, in_specs=in_specs, out_specs=out_specs, check_vma=False)
```

```python
import functools

import jax
import jax.numpy as jnp
from jax import lax
from jax.experimental import pallas as pl
from jax.experimental.pallas import tpu as pltpu
from jax.sharding import PartitionSpec as P

NHEAD = 12
DHEAD = 64
BUCKETS = 32
PAIRS = NHEAD // 2
LANES = 2 * DHEAD
PREFIX_MAX = 256

EPSILON = 1e-06
CUBIC_TERM = 0.044715
SQRT_TWO_PI = 0.7978845608028654
NEGATIVE = -1000000000.0

F32 = jnp.float32
BF16 = jnp.bfloat16
LAST_DIMS = (((1,), (1,)), ((), ()))


def matmul(left_side, right_side):
    return jnp.dot(left_side, right_side, preferred_element_type=F32)


def back_term(gradient, weight):
    return lax.dot_general(gradient, weight, LAST_DIMS, preferred_element_type=F32)


def inverse_rms(values):
    return lax.rsqrt(jnp.mean(values * values, axis=-1, keepdims=True) + EPSILON)


def norm_back(values, scale_rows, gain_vec, upstream):
    weighted = upstream * gain_vec
    gain_grad = jnp.sum(upstream * values * scale_rows, axis=0)
    input_grad = scale_rows * weighted - values * scale_rows * scale_rows * scale_rows * jnp.mean(
        values * weighted, axis=-1, keepdims=True
    )
    return (input_grad, gain_grad)


def one_head(rows, head):
    lane = lax.broadcasted_iota(jnp.int32, rows.shape, 1)
    keep = lane < DHEAD if head == 0 else lane >= DHEAD
    return jnp.where(keep, rows, jnp.zeros_like(rows))


def flipped(rows):
    return rows.astype(F32).T.astype(BF16)


def tree(fold, rows, groups):
    step = rows.shape[0] // groups
    total = rows[:step]
    for index in range(1, groups):
        total = fold(total, rows[index * step : (index + 1) * step])
    return total


def column_max(rows, groups):
    return jnp.max(tree(jnp.maximum, rows, groups), axis=0, keepdims=True)


def column_sum(rows, groups):
    return jnp.sum(tree(jnp.add, rows, groups), axis=0, keepdims=True)


def allowed_at(shape, key_start, query_start, prefix):
    key = lax.broadcasted_iota(jnp.int32, shape, 0) + key_start
    query = lax.broadcasted_iota(jnp.int32, shape, 1) + query_start
    return (key <= query) | (key < prefix)


def skew_kernel(table_ref, buckets_ref, out_ref):
    bucket = lax.broadcasted_iota(jnp.int32, (BUCKETS, buckets_ref.shape[1]), 0)
    onehot = (bucket == buckets_ref[...]).astype(BF16)
    by_offset = matmul(table_ref[...], onehot)
    width = out_ref.shape[2]
    total = by_offset.shape[1]
    for head in range(NHEAD):
        rows = jnp.broadcast_to(by_offset[head : head + 1], (LANES, total))
        rolled = pltpu.roll(rows, total - (LANES - 1), 1, stride=1, stride_axis=0)
        out_ref[head] = rolled[:, :width]


def skewed_bias(table, buckets_back, length):
    total = 2 * length
    return pl.pallas_call(
        skew_kernel,
        out_shape=jax.ShapeDtypeStruct((NHEAD, LANES, total - LANES), F32),
        name="skewed_bias",
    )(jnp.pad(table, ((0, 4), (0, 0))), buckets_back)


HEADROOM = 70.0


def self_forward(prefix_ref, query_ref, key_ref, value_ref, bias_ref, out_ref, lse_ref):
    length = query_ref.shape[0]
    block = 256
    prefix = prefix_ref[pl.program_id(0)]
    queries = query_ref[...]
    keys = key_ref[...]
    values = flipped(value_ref[...])

    def run(exact):
        excess = jnp.zeros((1, block), F32)
        for start in range(0, length, block):
            stop = start + block
            count = max(PREFIX_MAX, stop)
            outs = []
            for head in range(2):
                scores = back_term(keys[:count], one_head(queries[start:stop], head))
                parts = []
                for base in range(0, count, LANES):
                    shift = length - LANES - base + start
                    part = scores[base : base + LANES] + bias_ref[head, :, shift : shift + block]
                    if base + LANES - 1 > start:
                        part = jnp.where(
                            allowed_at(part.shape, base, start, prefix), part, NEGATIVE
                        )
                    parts.append(part)
                top = parts[0]
                for part in parts[1:]:
                    top = jnp.maximum(top, part)
                top = column_max(top, 4)
                anchor = top if exact else column_max(parts[0], 4)
                if not exact:
                    excess = jnp.maximum(excess, top - anchor)
                shares = [jnp.exp(part - anchor) for part in parts]
                total = shares[0]
                for share in shares[1:]:
                    total = total + share
                total = column_sum(total, 4)
                share = jnp.concatenate([item.astype(BF16) for item in shares], axis=0)
                context = matmul(values[head * DHEAD : (head + 1) * DHEAD, :count], share)
                outs.append(context * (1.0 / total))
                lse_ref[head : head + 1, start:stop] = anchor + jnp.log(total)
            out_ref[start:stop, :] = jnp.concatenate(outs, axis=0).T.astype(BF16)
        return jnp.max(excess)

    excess = run(False)

    @pl.when(excess > HEADROOM)
    def _():
        run(True)


def cross_forward(query_ref, key_ref, value_ref, out_ref, lse_ref):
    keys = key_ref[...]
    values = flipped(value_ref[...])
    queries = query_ref[...]

    def run(exact):
        excess = jnp.zeros((1, queries.shape[0]), F32)
        ahead = [back_term(keys, one_head(queries, head)) for head in range(2)]
        outs = []
        for head in range(2):
            scores = ahead[head]
            top = column_max(scores, 16)
            anchor = top if exact else column_max(scores[: 2 * LANES], 8)
            if not exact:
                excess = jnp.maximum(excess, top - anchor)
            share = jnp.exp(scores - anchor)
            total = column_sum(share, 16)
            context = matmul(values[head * DHEAD : (head + 1) * DHEAD], share.astype(BF16))
            outs.append(context * (1.0 / total))
            lse_ref[head : head + 1, :] = anchor + jnp.log(total)
        out_ref[...] = jnp.concatenate(outs, axis=0).T.astype(BF16)
        return jnp.max(excess)

    excess = run(False)

    @pl.when(excess > HEADROOM)
    def _():
        run(True)


def cross_backward(
    query_ref, key_ref, value_ref, up_ref, context_ref, lse_ref, dq_ref, dk_ref, dv_ref
):
    length = query_ref.shape[0]
    block = 256
    keys = key_ref[...]
    values = value_ref[...]
    queries = query_ref[...]
    upstream = up_ref[...]
    keys_flipped = flipped(keys)
    inner = (upstream.astype(F32) * context_ref[...].astype(F32)).T
    key_grad = None
    value_grad = None
    for start in range(0, length, block):
        rows = slice(start, start + block)
        grads = []
        for head in range(2):
            sub = slice(head * DHEAD, (head + 1) * DHEAD)
            query = one_head(queries[rows], head)
            above = one_head(upstream[rows], head)
            row_inner = jnp.sum(inner[sub, rows], axis=0, keepdims=True)
            shares = jnp.exp(back_term(keys, query) - lse_ref[head : head + 1, rows])
            share_grad = back_term(values, above)
            score_grad = (shares * (share_grad - row_inner)).astype(BF16)
            value_part = matmul(shares.astype(BF16), above)
            key_part = matmul(score_grad, query)
            value_grad = value_part if value_grad is None else value_grad + value_part
            key_grad = key_part if key_grad is None else key_grad + key_part
            grads.append(matmul(keys_flipped[sub], score_grad))
        dq_ref[rows, :] = jnp.concatenate(grads, axis=0).T.astype(BF16)
    dk_ref[...] = key_grad.astype(BF16)
    dv_ref[...] = value_grad.astype(BF16)


def self_backward(
    prefix_ref,
    query_ref,
    key_ref,
    value_ref,
    up_ref,
    context_ref,
    lse_ref,
    bias_ref,
    dq_ref,
    dk_ref,
    dv_ref,
    diag_ref,
    acc_ref,
):
    length = query_ref.shape[0]
    block = 256
    step = pl.program_id(1)
    prefix = prefix_ref[step]

    @pl.when(step == 0)
    def _():
        acc_ref[...] = jnp.zeros_like(acc_ref)

    queries = query_ref[...]
    keys = key_ref[...]
    values = value_ref[...]
    upstream = up_ref[...]
    keys_flipped = flipped(keys)
    inner = (upstream.astype(F32) * context_ref[...].astype(F32)).T
    count_all = length // block
    key_grad = [None] * count_all
    value_grad = [None] * count_all
    for start in range(0, length, block):
        stop = start + block
        count = max(PREFIX_MAX, stop)
        rows = slice(start, stop)
        grads = []
        for head in range(2):
            sub = slice(head * DHEAD, (head + 1) * DHEAD)
            query = one_head(queries[rows], head)
            above = one_head(upstream[rows], head)
            row_inner = jnp.sum(inner[sub, rows], axis=0, keepdims=True)
            row_lse = lse_ref[head : head + 1, rows]
            scores = back_term(keys[:count], query)
            share_grad = back_term(values[:count], above)
            shares = []
            score_grads = []
            for base in range(0, count, LANES):
                part = slice(base, base + LANES)
                shift = length - LANES - base + start
                share = jnp.exp(
                    scores[part] + bias_ref[head, :, shift : shift + block] - row_lse
                )
                if base + LANES - 1 > start:
                    share = jnp.where(allowed_at(share.shape, base, start, prefix), share, 0.0)
                score_grad = share * (share_grad[part] - row_inner)
                acc_ref[head, :, shift : shift + block] += score_grad
                shares.append(share.astype(BF16))
                score_grads.append(score_grad.astype(BF16))
            share = jnp.concatenate(shares, axis=0)
            score_grad = jnp.concatenate(score_grads, axis=0)
            value_part = matmul(share, above)
            key_part = matmul(score_grad, query)
            for index in range(count // block):
                part = slice(index * block, (index + 1) * block)
                if value_grad[index] is None:
                    value_grad[index] = value_part[part]
                    key_grad[index] = key_part[part]
                else:
                    value_grad[index] = value_grad[index] + value_part[part]
                    key_grad[index] = key_grad[index] + key_part[part]
            grads.append(matmul(keys_flipped[sub, :count], score_grad))
        dq_ref[rows, :] = jnp.concatenate(grads, axis=0).T.astype(BF16)
    for index in range(count_all):
        part = slice(index * block, (index + 1) * block)
        dk_ref[part, :] = key_grad[index].astype(BF16)
        dv_ref[part, :] = value_grad[index].astype(BF16)

    @pl.when(step == pl.num_programs(1) - 1)
    def _():
        total = 2 * length
        for head in range(2):
            rows = jnp.concatenate([acc_ref[head], jnp.zeros((LANES, LANES), F32)], axis=1)
            half = LANES // 2
            while half >= 1:
                rows = rows[:half] + pltpu.roll(rows[half:], total - half, 1)
                half //= 2
            diag_ref[head : head + 1, :] = pltpu.roll(rows, LANES - 1, 1)


def spec(shape, index):
    return pl.BlockSpec(shape, index)


def run_self_forward(prefix, qkv, bias, nseq):
    length = qkv.shape[0] // nseq
    return pl.pallas_call(
        self_forward,
        grid_spec=pltpu.PrefetchScalarGridSpec(
            num_scalar_prefetch=1,
            grid=(nseq, PAIRS),
            in_specs=[
                spec((length, LANES), lambda s, p, _: (s, p)),
                spec((length, LANES), lambda s, p, _: (s, PAIRS + p)),
                spec((length, LANES), lambda s, p, _: (s, 2 * PAIRS + p)),
                spec((2, LANES, 2 * length - LANES), lambda s, p, _: (p, 0, 0)),
            ],
            out_specs=[
                spec((length, LANES), lambda s, p, _: (s, p)),
                spec((None, None, 2, length), lambda s, p, _: (s, p, 0, 0)),
            ],
        ),
        out_shape=[
            jax.ShapeDtypeStruct((qkv.shape[0], PAIRS * LANES), BF16),
            jax.ShapeDtypeStruct((nseq, PAIRS, 2, length), F32),
        ],
        cost_estimate=pl.CostEstimate(
            flops=20_000_000_000, bytes_accessed=12_000_000, transcendentals=0
        ),
        name="self_forward",
    )(prefix, qkv, qkv, qkv, bias)


def run_cross_forward(query, kv, nseq):
    length = query.shape[0] // nseq
    count = kv.shape[0] // nseq
    return pl.pallas_call(
        cross_forward,
        grid=(nseq, PAIRS),
        in_specs=[
            spec((length, LANES), lambda s, p: (s, p)),
            spec((count, LANES), lambda s, p: (s, p)),
            spec((count, LANES), lambda s, p: (s, PAIRS + p)),
        ],
        out_specs=[
            spec((length, LANES), lambda s, p: (s, p)),
            spec((None, None, 2, length), lambda s, p: (s, p, 0, 0)),
        ],
        out_shape=[
            jax.ShapeDtypeStruct(query.shape, BF16),
            jax.ShapeDtypeStruct((nseq, PAIRS, 2, length), F32),
        ],
        cost_estimate=pl.CostEstimate(
            flops=24_000_000_000, bytes_accessed=10_000_000, transcendentals=0
        ),
        name="cross_forward",
    )(query, kv, kv)


def run_cross_backward(query, kv, upstream, context, lse, nseq):
    length = query.shape[0] // nseq
    count = kv.shape[0] // nseq
    rows = spec((length, LANES), lambda s, p: (s, p))
    wide = spec((count, LANES), lambda s, p: (s, p))
    return pl.pallas_call(
        cross_backward,
        grid=(nseq, PAIRS),
        in_specs=[
            rows,
            wide,
            spec((count, LANES), lambda s, p: (s, PAIRS + p)),
            rows,
            rows,
            spec((None, None, 2, length), lambda s, p: (s, p, 0, 0)),
        ],
        out_specs=[rows, wide, wide],
        out_shape=[
            jax.ShapeDtypeStruct(query.shape, BF16),
            jax.ShapeDtypeStruct((kv.shape[0], PAIRS * LANES), BF16),
            jax.ShapeDtypeStruct((kv.shape[0], PAIRS * LANES), BF16),
        ],
        cost_estimate=pl.CostEstimate(
            flops=36_000_000_000, bytes_accessed=20_000_000, transcendentals=0
        ),
        name="cross_backward",
    )(query, kv, kv, upstream, context, lse)


def run_self_backward(prefix, qkv, upstream, context, lse, bias, nseq, carried=None):
    length = qkv.shape[0] // nseq
    rows = spec((length, LANES), lambda p, s, _: (s, p))
    group = []
    kernel = self_backward
    extra_out_specs = []
    extra_out_shape = []
    extra_scratch = []
    params = None
    if carried is not None:
        group, collective_id = carried
        shape = square_shape(group, LINE)
        kernel = functools.partial(carried_backward, shape, LINE, PAIRS * nseq)
        total = shape.total_shape(LINE)
        extra_out_specs = [spec(total, lambda p, s, _: (0, 0, 0, 0))]
        extra_out_shape = [jax.ShapeDtypeStruct(total, BF16)]
        extra_scratch = shape.plane_scratch(LINE)
        params = pltpu.CompilerParams(
            collective_id=collective_id, has_side_effects=True, vmem_limit_bytes=60 << 20
        )
    return pl.pallas_call(
        kernel,
        grid_spec=pltpu.PrefetchScalarGridSpec(
            num_scalar_prefetch=1,
            grid=(PAIRS, nseq),
            in_specs=[
                rows,
                spec((length, LANES), lambda p, s, _: (s, PAIRS + p)),
                spec((length, LANES), lambda p, s, _: (s, 2 * PAIRS + p)),
                rows,
                rows,
                spec((None, None, 2, length), lambda p, s, _: (s, p, 0, 0)),
                spec((2, LANES, 2 * length - LANES), lambda p, s, _: (p, 0, 0)),
            ]
            + [pl.BlockSpec(memory_space=pl.ANY)] * len(group),
            out_specs=[
                rows,
                rows,
                rows,
                spec((None, 2, 2 * length), lambda p, s, _: (p, 0, 0)),
            ]
            + extra_out_specs,
            scratch_shapes=[pltpu.VMEM((2, LANES, 2 * length - LANES), F32)] + extra_scratch,
        ),
        out_shape=[jax.ShapeDtypeStruct(upstream.shape, BF16)] * 3
        + [jax.ShapeDtypeStruct((PAIRS, 2, 2 * length), F32)]
        + extra_out_shape,
        cost_estimate=pl.CostEstimate(
            flops=24_000_000_000, bytes_accessed=20_000_000, transcendentals=0
        ),
        compiler_params=params,
        name="self_backward",
    )(prefix, qkv, qkv, qkv, upstream, context, lse, bias, *group)


FEED_BLOCK = 256


def feed_kernel(
    middle_ref,
    context_ref,
    out_proj_ref,
    gain_ref,
    up_grad_ref,
    gate_ref,
    up_ref,
    down_ref,
    result_ref,
    later_grad_ref,
    branch_ref,
    context_grad_ref,
    gain_grad_ref,
    down_term_ref,
    pair_term_ref,
    later_ref,
    normed_ref,
    flipped_ref,
    result_acc,
    third_acc,
):
    step = pl.program_id(0)
    count = middle_ref.shape[0]
    chunk = 256
    chunks = [slice(start, start + chunk) for start in range(0, count, chunk)]

    @pl.when(step == 0)
    def _():
        for rows in chunks:
            later = middle_ref[rows] + matmul(context_ref[rows], out_proj_ref[...])
            normed = (later * inverse_rms(later) * gain_ref[...]).astype(BF16)
            later_ref[rows] = later
            normed_ref[rows] = normed
            flipped_ref[:, rows] = flipped(normed)
            result_acc[rows] = jnp.zeros_like(later)
            third_acc[rows] = jnp.zeros_like(later)

    gate_proj = gate_ref[...]
    up_proj = up_ref[...]
    down_proj = down_ref[...]
    hidden_flipped = []
    gate_grads = []
    lift_grads = []
    for rows in chunks:
        normed = normed_ref[rows]
        gate = matmul(normed, gate_proj)
        lift = matmul(normed, up_proj)
        hidden_grad = back_term(up_grad_ref[rows], down_proj)
        square = gate * gate
        tangent = jnp.tanh(SQRT_TWO_PI * gate * (1.0 + CUBIC_TERM * square))
        half = 0.5 * (1.0 + tangent)
        active = gate * half
        slope = half + 0.5 * gate * (1.0 - tangent * tangent) * (
            SQRT_TWO_PI + 3.0 * CUBIC_TERM * SQRT_TWO_PI * square
        )
        hidden = active * lift
        gate_grad = (hidden_grad * lift * slope).astype(BF16)
        lift_grad = (hidden_grad * active).astype(BF16)
        hidden_flipped.append(hidden.T.astype(BF16))
        gate_grads.append(gate_grad)
        lift_grads.append(lift_grad)
        result_acc[rows] += matmul(hidden.astype(BF16), down_proj)
        third_acc[rows] += back_term(gate_grad, gate_proj) + back_term(lift_grad, up_proj)
    hidden_flipped = jnp.concatenate(hidden_flipped, axis=1)
    down_term_ref[...] = matmul(hidden_flipped, up_grad_ref[...]).astype(BF16)
    gate_grads = jnp.concatenate(gate_grads, axis=0)
    lift_grads = jnp.concatenate(lift_grads, axis=0)
    pair_term_ref[:, :FEED_BLOCK] = matmul(flipped_ref[...], gate_grads).astype(BF16)
    pair_term_ref[:, FEED_BLOCK:] = matmul(flipped_ref[...], lift_grads).astype(BF16)

    @pl.when(step == pl.num_programs(0) - 1)
    def _():
        gain_grad = jnp.zeros(gain_ref.shape, F32)
        for rows in chunks:
            later = later_ref[rows]
            result_ref[rows] = (later + result_acc[rows]).astype(BF16)
            carry, part = norm_back(later, inverse_rms(later), gain_ref[...], third_acc[rows])
            gain_grad = gain_grad + part[None, :]
            later_grad = up_grad_ref[rows].astype(F32) + carry
            branch = later_grad.astype(BF16)
            later_grad_ref[rows] = later_grad
            branch_ref[rows] = branch
            context_grad_ref[rows] = back_term(branch, out_proj_ref[...]).astype(BF16)
        gain_grad_ref[...] = gain_grad


def run_feed(middle, context, out_proj, out_block, gain, upstream, gate_up, down):
    count, width = middle.shape
    ffn = down.shape[0]
    blocks = ffn // FEED_BLOCK

    def whole(shape, **extra):
        return pl.BlockSpec(shape, lambda j: (0, 0), **extra)

    once = {"pipeline_mode": pl.Buffered(1)}
    rows = (count, width)
    return pl.pallas_call(
        feed_kernel,
        grid=(blocks,),
        in_specs=[
            whole(rows, **once),
            whole(rows, **once),
            pl.BlockSpec((width, width), lambda j: (0, out_block), **once),
            whole((1, width)),
            whole(rows, **once),
            spec((width, FEED_BLOCK), lambda j: (0, j)),
            spec((width, FEED_BLOCK), lambda j: (0, blocks + j)),
            spec((FEED_BLOCK, width), lambda j: (j, 0)),
        ],
        out_specs=[
            whole(rows),
            whole(rows),
            whole(rows),
            whole(rows),
            whole((1, width)),
            spec((FEED_BLOCK, width), lambda j: (j, 0)),
            spec((width, 2 * FEED_BLOCK), lambda j: (0, j)),
        ],
        out_shape=[
            jax.ShapeDtypeStruct(rows, BF16),
            jax.ShapeDtypeStruct(rows, F32),
            jax.ShapeDtypeStruct(rows, BF16),
            jax.ShapeDtypeStruct(rows, BF16),
            jax.ShapeDtypeStruct((1, width), F32),
            jax.ShapeDtypeStruct((ffn, width), BF16),
            jax.ShapeDtypeStruct((width, 2 * ffn), BF16),
        ],
        scratch_shapes=[
            pltpu.VMEM(rows, F32),
            pltpu.VMEM(rows, BF16),
            pltpu.VMEM((width, count), BF16),
            pltpu.VMEM(rows, F32),
            pltpu.VMEM(rows, F32),
        ],
        cost_estimate=pl.CostEstimate(
            flops=32_000_000_000, bytes_accessed=40_000_000, transcendentals=0
        ),
        compiler_params=pltpu.CompilerParams(vmem_limit_bytes=60 << 20),
        name="feed",
    )(middle, context, out_proj, gain, upstream, gate_up, gate_up, down)


def close_kernel(count, project, *refs):
    values_ref, carry_ref, gain_ref, left_ref, right_ref = refs[:5]
    grad_refs = refs[5 : 5 + count]
    weight_refs = refs[5 + count : 5 + 2 * count]
    at = 5 + 2 * count
    if project:
        proj_ref = refs[at]
        at += 1
    out_ref, gain_grad_ref = refs[at : at + 2]
    term_refs = refs[at + 2 : at + 3 + count]
    at += 3 + count
    if project:
        branch_ref, projected_ref = refs[at : at + 2]
        at += 2
    sums = refs[at : at + 1 + count]
    gain_sum = refs[at + 1 + count]
    step = pl.program_id(0)

    @pl.when(step == 0)
    def _():
        gain_sum[...] = jnp.zeros_like(gain_sum)
        for total in sums:
            total[...] = jnp.zeros_like(total)

    values = values_ref[...].astype(F32)
    gain = gain_ref[...]
    scale = inverse_rms(values)
    normed = (values * scale * gain).T.astype(BF16)
    upstream = None
    for index in range(count):
        grad = grad_refs[index][...]
        sums[index][...] += matmul(normed, grad)
        part = back_term(grad, weight_refs[index][...])
        upstream = part if upstream is None else upstream + part
    sums[count][...] += matmul(flipped(left_ref[...]), right_ref[...])
    carry, part = norm_back(values, scale, gain, upstream)
    gain_sum[...] += part[None, :]
    result = carry_ref[...] + carry
    out_ref[...] = result
    if project:
        branch = result.astype(BF16)
        branch_ref[...] = branch
        projected_ref[...] = back_term(branch, proj_ref[...]).astype(BF16)

    @pl.when(step == pl.num_programs(0) - 1)
    def _():
        gain_grad_ref[...] = gain_sum[...]
        for term, total in zip(term_refs, sums):
            term[...] = total[...].astype(BF16)


def run_close(values, carry, gain, left, right, grads, weights, project, name):
    rows, width = values.shape
    count = len(grads)
    block = 512
    wide = spec((block, width), lambda i: (i, 0))

    def columns(index):
        return pl.BlockSpec((width, width), lambda i: (0, index), pipeline_mode=pl.Buffered(1))

    whole = [spec((1, width), lambda i: (0, 0))]
    square = [spec((width, width), lambda i: (0, 0))] * (count + 1)
    extra = [] if project is None else [project]
    out_shape = [
        jax.ShapeDtypeStruct((rows, width), F32),
        jax.ShapeDtypeStruct((1, width), F32),
    ] + [jax.ShapeDtypeStruct((width, width), BF16)] * (count + 1)
    out_shape += [jax.ShapeDtypeStruct((rows, width), BF16)] * (2 * len(extra))
    return pl.pallas_call(
        functools.partial(close_kernel, count, project is not None),
        grid=(rows // block,),
        in_specs=[wide, wide]
        + whole
        + [wide] * (2 + count)
        + [columns(index) for _, index in weights + extra],
        out_specs=[wide] + whole + square + [wide] * (2 * len(extra)),
        out_shape=out_shape,
        scratch_shapes=[pltpu.VMEM((width, width), F32)] * (count + 1)
        + [pltpu.VMEM((1, width), F32)],
        cost_estimate=pl.CostEstimate(
            flops=8_000_000_000, bytes_accessed=25_000_000, transcendentals=0
        ),
        compiler_params=pltpu.CompilerParams(vmem_limit_bytes=60 << 20),
        name=name,
    )(values, carry, gain, left, right, *grads, *[item for item, _ in weights + extra])


def memory_kernel(
    memory_ref, key_grad_ref, value_grad_ref, key_ref, value_ref, out_ref, *rest
):
    key_term_ref, value_term_ref, key_sum, value_sum = rest
    step = pl.program_id(0)

    @pl.when(step == 0)
    def _():
        key_sum[...] = jnp.zeros_like(key_sum)
        value_sum[...] = jnp.zeros_like(value_sum)

    rows = flipped(memory_ref[...])
    key_grad = key_grad_ref[...]
    value_grad = value_grad_ref[...]
    out_ref[...] = back_term(key_grad, key_ref[...]) + back_term(value_grad, value_ref[...])
    key_sum[...] += matmul(rows, key_grad)
    value_sum[...] += matmul(rows, value_grad)

    @pl.when(step == pl.num_programs(0) - 1)
    def _():
        key_term_ref[...] = key_sum[...].astype(BF16)
        value_term_ref[...] = value_sum[...].astype(BF16)


def run_memory(memory, key_grad, value_grad, weights, key_block, value_block):
    rows, width = memory.shape
    block = 1024
    wide = spec((block, width), lambda i: (i, 0))
    square = spec((width, width), lambda i: (0, 0))

    def columns(index):
        return pl.BlockSpec((width, width), lambda i: (0, index), pipeline_mode=pl.Buffered(1))

    return pl.pallas_call(
        memory_kernel,
        grid=(rows // block,),
        in_specs=[wide, wide, wide, columns(key_block), columns(value_block)],
        out_specs=[wide, square, square],
        out_shape=[
            jax.ShapeDtypeStruct((rows, width), F32),
            jax.ShapeDtypeStruct((width, width), BF16),
            jax.ShapeDtypeStruct((width, width), BF16),
        ],
        scratch_shapes=[pltpu.VMEM((width, width), F32)] * 2,
        cost_estimate=pl.CostEstimate(
            flops=10_000_000_000, bytes_accessed=18_000_000, transcendentals=0
        ),
        compiler_params=pltpu.CompilerParams(vmem_limit_bytes=60 << 20),
        name="memory_close",
    )(memory, key_grad, value_grad, weights, weights)


MESH = pl.DeviceIdType.MESH


class Place:
    def __init__(self, line):
        self.line = line
        rep = lax.axis_index("rep")
        fsdp = lax.axis_index("fsdp")
        self.rep = rep
        self.fsdp = fsdp
        self.y = rep // 2
        self.x = rep % 2
        self.z = fsdp // 2
        self.core = fsdp % 2
        self.x_rep = self.y * 2 + 1 - self.x
        self.y_rep = (1 - self.y) * 2 + self.x

    def at_x(self):
        return {"rep": self.x_rep, "fsdp": self.fsdp}

    def at_y(self):
        return {"rep": self.y_rep, "fsdp": self.fsdp}

    def at_partner(self):
        return {"rep": self.rep, "fsdp": self.z * 2 + 1 - self.core}

    def at_line(self, side):
        return {"rep": self.rep, "fsdp": self.fsdp + (2 if side == 0 else -2)}

    def has_next(self, side):
        return self.z < self.line - 1 if side == 0 else self.z > 0

    def has_last(self, side):
        return self.has_next(1 - side)

    def arrives(self, side, hop):
        if side == 0:
            return self.z - 1 - hop >= 0
        return self.z + 1 + hop <= self.line - 1

    def source(self, side, hop):
        return self.z - 1 - hop if side == 0 else self.z + 1 + hop

    def at_far(self):
        half = self.line // 2
        return {"rep": self.rep, "fsdp": (self.z + half) % self.line * 2 + self.core}

    def greet(self, wide=False):
        barrier = pltpu.get_barrier_semaphore()
        targets = [self.at_x(), self.at_y(), self.at_partner()]
        if wide:
            targets.append({"rep": 3 - self.rep, "fsdp": self.fsdp})
            targets.append(self.at_far())
        for target in targets:
            pl.semaphore_signal(barrier, inc=1, device_id=target, device_id_type=MESH)
        for side in range(2):

            @pl.when(self.has_next(side))
            def _():
                pl.semaphore_signal(
                    barrier, inc=1, device_id=self.at_line(side), device_id_type=MESH
                )

        count = len(targets)
        for side in range(2):
            count = count + jnp.where(self.has_next(side), 1, 0)
        pl.semaphore_wait(barrier, count)


def remote(source, target, send, recv, device):
    return pltpu.make_async_remote_copy(
        src_ref=source,
        dst_ref=target,
        send_sem=send,
        recv_sem=recv,
        device_id=device,
        device_id_type=MESH,
    )


class GatherShape:
    def __init__(self, parts, by_rows):
        self.rows = parts[0].shape[0]
        self.widths = [part.shape[1] for part in parts]
        self.starts = [sum(self.widths[:index]) for index in range(len(parts))]
        self.columns = sum(self.widths)
        self.by_rows = by_rows

    def full(self, ref, owner):
        return ref.at[pl.ds(pl.multiple_of(owner * self.rows, 32), self.rows)]

    def piece(self, ref, owner, part, half=None):
        base = owner * self.rows
        if self.by_rows:
            rows = self.rows // 4
            base = base + part * rows
        else:
            rows = self.rows
        if half is not None:
            rows = rows // 2
            base = base + half * rows
        row_slice = pl.ds(pl.multiple_of(base, 16), rows)
        if self.by_rows:
            return ref.at[row_slice]
        width = self.columns // 4
        return ref.at[row_slice, pl.ds(pl.multiple_of(part * width, LANES), width)]


def gather_sems(line):
    hops = line - 1
    return [pltpu.SemaphoreType.DMA((5, 2, 2, hops)), pltpu.SemaphoreType.DMA((4,))] + [
        pltpu.SemaphoreType.DMA((2, 2, hops))
    ]


def gather_steps(place, shape, src, own, dst, sems):
    hop_sem, own_sem, pair_sem = sems
    hops = place.line - 1
    me = place.fsdp

    def load(index):
        at = pl.ds(shape.starts[index], shape.widths[index])
        return pltpu.make_async_copy(src[index], own.at[:, at], own_sem.at[0])

    def loaded():
        return pltpu.make_async_copy(own, own, own_sem.at[0])

    def keep():
        return pltpu.make_async_copy(own, shape.full(dst, me), own_sem.at[1])

    def own_pair():
        return remote(
            own, shape.full(dst, me), own_sem.at[2], own_sem.at[3], place.at_partner()
        )

    def owner(side, hop):
        return place.source(side, hop) * 2 + place.core

    def line_first(side):
        return remote(
            shape.piece(own, 0, place.rep),
            shape.piece(dst, me, place.rep),
            hop_sem.at[0, 0, side, 0],
            hop_sem.at[0, 1, side, 0],
            place.at_line(side),
        )

    def moved(kind, side, hop, block, device):
        return remote(
            block, block, hop_sem.at[kind, 0, side, hop], hop_sem.at[kind, 1, side, hop], device
        )

    def line_next(side, hop):
        block = shape.piece(dst, owner(side, hop - 1), place.rep)
        return moved(0, side, hop, block, place.at_line(side))

    def line_arrival(side, hop):
        block = shape.piece(dst, owner(side, hop), place.rep)
        return moved(0, side, hop, block, place.at_line(side))

    def plane(axis, side, hop):
        block = shape.piece(dst, owner(side, hop), place.rep)
        return moved(1 + axis, side, hop, block, place.at_x() if axis == 0 else place.at_y())

    def cross(axis, side, hop):
        part = place.x_rep if axis == 1 else place.y_rep
        block = shape.piece(dst, owner(side, hop), part, 1 - axis)
        return moved(3 + axis, side, hop, block, place.at_x() if axis == 0 else place.at_y())

    def pair(side, hop):
        block = shape.full(dst, owner(side, hop))
        return remote(
            block, block, pair_sem.at[0, side, hop], pair_sem.at[1, side, hop], place.at_partner()
        )

    def each(fn):
        def run():
            for hop in range(hops):
                for side in range(2):
                    pl.when(place.arrives(side, hop))(functools.partial(fn, side, hop))

        return run

    def start():
        for index in range(len(src)):
            load(index).start()
        loaded().wait()
        for side in range(2):
            pl.when(place.has_next(side))(lambda side=side: line_first(side).start())
        own_pair().start()
        keep().start()

    def arrive(side, hop):
        line_arrival(side, hop).wait_recv()
        if hop + 1 < hops:
            pl.when(place.has_next(side))(lambda: line_next(side, hop + 1).start())
        plane(0, side, hop).start()
        plane(1, side, hop).start()

    def turn(side, hop):
        plane(0, side, hop).wait_recv()
        cross(1, side, hop).start()
        plane(1, side, hop).wait_recv()
        cross(0, side, hop).start()

    def hand(side, hop):
        cross(0, side, hop).wait_recv()
        cross(1, side, hop).wait_recv()
        pair(side, hop).start()

    def finish():
        def last(side, hop):
            pair(side, hop).wait()
            for axis in range(2):
                plane(axis, side, hop).wait_send()
                cross(axis, side, hop).wait_send()
            if hop + 1 < hops:
                pl.when(place.has_next(side))(lambda: line_next(side, hop + 1).wait_send())

        each(last)()
        for side in range(2):
            pl.when(place.has_next(side))(lambda side=side: line_first(side).wait_send())
        own_pair().wait()
        keep().wait()

    return start, each(arrive), each(turn), each(hand), finish


def gather_kernel(shapes, line, *refs):
    count = len(shapes)
    sources = []
    at = 0
    for shape in shapes:
        sources.append(refs[at : at + len(shape.widths)])
        at += len(shape.widths)
    targets = refs[at : at + count]
    scratch = refs[at + count :]
    place = Place(line)
    place.greet()
    plans = []
    for index, shape in enumerate(shapes):
        own, *sems = scratch[4 * index : 4 * index + 4]
        plans.append(gather_steps(place, shape, sources[index], own, targets[index], sems))
    for stage in range(5):
        for plan in plans:
            plan[stage]()


def fast_gather(groups, line, by_rows, collective_id):
    shapes = [GatherShape(group, flag) for group, flag in zip(groups, by_rows)]
    scratch = []
    for shape in shapes:
        scratch.append(pltpu.VMEM((shape.rows, shape.columns), BF16))
        scratch.extend(gather_sems(line))
    anywhere = pl.BlockSpec(memory_space=pl.ANY)
    blocks = [block for group in groups for block in group]
    return pl.pallas_call(
        functools.partial(gather_kernel, shapes, line),
        in_specs=[anywhere] * len(blocks),
        out_specs=[anywhere] * len(groups),
        out_shape=[
            jax.ShapeDtypeStruct((2 * line * s.rows, s.columns), BF16) for s in shapes
        ],
        scratch_shapes=scratch,
        compiler_params=pltpu.CompilerParams(collective_id=collective_id, has_side_effects=True),
        name="fast_gather",
    )(*blocks)


class ReduceShape:
    def __init__(self, kind, rows, columns, sources):
        self.kind = kind
        self.rows = rows
        self.sources = sources
        if kind == "rows":
            self.block = (rows // 8, columns)
        elif kind == "pair":
            self.block = (rows // 2, columns // 2)
        else:
            self.block = (rows // 2, columns)
        self.exchange = kind != "pair"
        self.part_rows = rows // 4 if kind == "rows" else rows
        self.part_columns = columns // 4

    def pieces(self, refs, owner, half, quarter):
        rows, columns = self.block
        if self.kind == "rows":
            base = owner * self.rows + quarter * (self.rows // 4) + half * rows
            return [(refs[0].at[pl.ds(pl.multiple_of(base, 16), rows)], 0, columns)]
        at = pl.ds(pl.multiple_of(owner * self.rows + half * rows, 16), rows)
        if self.kind == "four":
            return [(refs[quarter].at[at], 0, columns)]
        width = columns // 2
        cut = slice(quarter * width, (quarter + 1) * width)
        return [(refs[index].at[at, cut], index * width, width) for index in range(2)]

    def out_shape(self):
        if self.exchange:
            return jax.ShapeDtypeStruct((4, self.part_rows, self.part_columns), F32)
        return jax.ShapeDtypeStruct((self.rows, self.block[1]), F32)

    def total_shape(self, line):
        return (line, 2) + self.block

    def plane_scratch(self, line):
        rows, columns = self.block
        dma = pltpu.SemaphoreType.DMA
        return [
            pltpu.VMEM((line, 8, rows, columns), BF16),
            pltpu.VMEM((line, 8, rows, columns), BF16),
            pltpu.VMEM((line, 2, 2, rows, columns), BF16),
            pltpu.VMEM((line, 2, rows, columns), BF16),
            dma((line,)),
            dma((2, line)),
            dma((2, line, 2)),
            dma((2, line, 2)),
        ]

    def line_scratch(self, line):
        dma = pltpu.SemaphoreType.DMA
        return [
            pltpu.VMEM(self.total_shape(line), BF16),
            pltpu.VMEM((2,) + self.total_shape(line), BF16),
            pltpu.VMEM((4, self.part_rows, self.part_columns), F32),
            pltpu.VMEM((4, self.part_rows, self.part_columns), F32),
            dma((1,)),
            dma((2, 2, line)),
            dma((2, 3)),
        ]


PLANE_SCRATCH = 8
LINE_SCRATCH = 7


def reduce_order(line):
    return [line - 1, 0] + list(range(line - 2, 0, -1))


def added(left, right):
    return (left.astype(F32) + right.astype(F32)).astype(BF16)


def plane_steps(place, shape, refs, total, scratch):
    own, other, first_in, second_in, load_sem, pair_sem, first_sem, second_sem = scratch
    near = (place.x, place.y)
    far = (place.y, place.x)
    near_device = (place.at_x(), place.at_y())
    far_device = (place.at_y(), place.at_x())

    def quarter_of(half, index):
        high, low = index // 2, index % 2
        return low * 2 + high if half == 0 else high * 2 + low

    def start(z):
        for half in range(2):
            for index in range(4):
                quarter = quarter_of(half, index)
                slot = half * 4 + index
                mine = shape.pieces(refs, 2 * z + place.core, half, quarter)
                theirs = shape.pieces(refs, 2 * z + 1 - place.core, half, quarter)
                for (view, column, width), (view_two, _, _) in zip(mine, theirs):
                    cut = pl.ds(column, width)
                    remote(
                        view_two,
                        other.at[z, slot, :, cut],
                        pair_sem.at[0, z],
                        pair_sem.at[1, z],
                        place.at_partner(),
                    ).start()
                    pltpu.make_async_copy(
                        view, own.at[z, slot, :, cut], load_sem.at[z]
                    ).start()

    def pair_all(z):
        return remote(
            own.at[z], other.at[z], pair_sem.at[0, z], pair_sem.at[1, z], place.at_partner()
        )

    def first(z, half):
        return remote(
            own.at[z, pl.ds(half * 4 + (1 - near[half]) * 2, 2)],
            first_in.at[z, half],
            first_sem.at[0, z, half],
            first_sem.at[1, z, half],
            near_device[half],
        )

    def second(z, half):
        return remote(
            own.at[z, half * 4 + near[half] * 2 + 1 - far[half]],
            second_in.at[z, half],
            second_sem.at[0, z, half],
            second_sem.at[1, z, half],
            far_device[half],
        )

    def pair_add(z):
        pltpu.make_async_copy(own.at[z], own.at[z], load_sem.at[z]).wait()
        pair_all(z).wait_recv()

        @pl.loop(0, 8)
        def _(slot):
            own[z, slot] = added(own[z, slot], other[z, slot])

        for half in range(2):
            first(z, half).start()

    def first_add(z):
        for half in range(2):
            first(z, half).wait_recv()
            base = half * 4 + near[half] * 2

            @pl.loop(0, 2)
            def _(index):
                own[z, base + index] = added(own[z, base + index], first_in[z, half, index])

            second(z, half).start()

    def second_add(z):
        for half in range(2):
            second(z, half).wait_recv()
            mine = half * 4 + near[half] * 2 + far[half]
            total[z, half] = added(own[z, mine], second_in[z, half])

    def drain(z):
        pair_all(z).wait_send()
        for half in range(2):
            first(z, half).wait_send()
            second(z, half).wait_send()

    return start, pair_add, first_add, second_add, drain


def line_steps(place, shape, source, out, scratch):
    total, line_in, parts, gathered, load_sem, line_sem, swap_sem = scratch
    line = place.line

    def load():
        return pltpu.make_async_copy(source, total, load_sem.at[0])

    def along(z, side):
        return remote(
            total.at[z],
            line_in.at[side, z],
            line_sem.at[0, side, z],
            line_sem.at[1, side, z],
            place.at_line(side),
        )

    def line_send(z, side):
        ahead = place.z < z if side == 0 else place.z > z

        @pl.when(ahead)
        def _():
            @pl.when(place.has_last(side))
            def _():
                along(z, side).wait_recv()

                @pl.loop(0, 2)
                def _(half):
                    total[z, half] = added(total[z, half], line_in[side, z, half])

            along(z, side).start()

    def line_end(z):
        @pl.when(place.z == z)
        def _():
            for side in range(2):
                pl.when(place.has_last(side))(lambda: along(z, side).wait_recv())

    def swap(rep_slot, device, index):
        return remote(
            parts.at[rep_slot],
            gathered.at[place.rep],
            swap_sem.at[0, index],
            swap_sem.at[1, index],
            device,
        )

    def swaps():
        corner = 3 - place.rep
        return [
            swap(place.x_rep, place.at_x(), 0),
            swap(place.y_rep, place.at_y(), 1),
            swap(corner, {"rep": corner, "fsdp": place.fsdp}, 2),
        ]

    def finish():
        rows, columns = shape.block
        me = place.z
        for half in range(2):
            result = total[me, half].astype(F32)
            for side in range(2):
                extra = line_in[side, me, half].astype(F32)
                result = result + jnp.where(place.has_last(side), extra, 0.0)
            at = slice(half * rows, (half + 1) * rows)
            if shape.exchange:
                width = shape.part_columns
                for index in range(4):
                    parts[index, at, :] = result[:, index * width : (index + 1) * width]
            else:
                out[at, :] = result
        if shape.exchange:
            for copy in swaps():
                copy.start()
            gathered[place.rep] = parts[place.rep]

    def send(z):
        line_send(z, 0)
        line_send(z, 1)

    def close():
        for z in range(line):
            line_end(z)
        finish()

    def drain():
        if shape.exchange:
            for copy in swaps():
                copy.wait()
            out[...] = gathered[...]
        for z in range(line):
            for side in range(2):
                ahead = place.z < z if side == 0 else place.z > z
                pl.when(ahead)(lambda: along(z, side).wait_send())

    return load, send, close, drain


class VectorSum:
    def __init__(self, place, source, out, scratch):
        self.place = place
        self.source = source
        self.out = out
        self.current, self.incoming, self.sems = scratch
        side = place.z % 2
        near = place.fsdp + 2 - 4 * side
        self.devices = [
            place.at_partner(),
            place.at_x(),
            place.at_y(),
            {"rep": place.rep, "fsdp": near},
            place.at_far(),
        ]

    @staticmethod
    def scratch(shape):
        return [
            pltpu.VMEM((6,) + shape, F32),
            pltpu.VMEM((5,) + shape, F32),
            pltpu.SemaphoreType.DMA((2, 5)),
        ]

    def copy(self, index):
        return remote(
            self.current.at[index],
            self.incoming.at[index],
            self.sems.at[0, index],
            self.sems.at[1, index],
            self.devices[index],
        )

    def round(self, index):
        if index == 0:
            self.current[0] = self.source[...]
        else:
            self.copy(index - 1).wait_recv()
            self.current[index] = self.current[index - 1] + self.incoming[index - 1]
        if index < 5:
            self.copy(index).start()

    def finish(self):
        self.out[...] = self.current[5]
        for index in range(5):
            self.copy(index).wait_send()


def carried_backward(shape, line, steps, *refs):
    count = shape.sources
    local, sources, outs = refs[:8], refs[8 : 8 + count], refs[8 + count : 12 + count]
    total, acc_ref, *scratch = refs[12 + count :]
    place = Place(line)
    order = reduce_order(line)
    start, pair_add, first_add, second_add, drain = plane_steps(
        place, shape, sources, total, scratch
    )
    step = pl.program_id(0) * pl.num_programs(1) + pl.program_id(1)

    @pl.when(step == 0)
    def _():
        place.greet()
        for z in order:
            start(z)

    @pl.when(step == 1)
    def _():
        for z in order:
            pair_add(z)

    for index, z in enumerate(order):
        pl.when(step == min(3 + 2 * index - index // 2, steps - 1))(
            functools.partial(first_add, z)
        )
    self_backward(*local, *outs, acc_ref)

    @pl.when(step == steps - 1)
    def _():
        for z in order:
            second_add(z)
        for z in order:
            drain(z)


def reduce_kernel(ready_shape, shape, line, *refs):
    count = shape.sources
    ready, sources, vector_ref = refs[0], refs[1 : 1 + count], refs[1 + count]
    ready_out, out, vector_out = refs[2 + count : 5 + count]
    scratch = refs[5 + count :]
    ready_scratch, scratch = scratch[:LINE_SCRATCH], scratch[LINE_SCRATCH:]
    line_scratch, scratch = scratch[:LINE_SCRATCH], scratch[LINE_SCRATCH:]
    plane_scratch, scratch = scratch[:PLANE_SCRATCH], scratch[PLANE_SCRATCH:]
    place = Place(line)
    place.greet(wide=True)
    order = reduce_order(line)
    start, pair_add, first_add, second_add, drain = plane_steps(
        place, shape, sources, line_scratch[0], plane_scratch
    )
    ready_load, ready_send, ready_close, ready_drain = line_steps(
        place, ready_shape, ready, ready_out, ready_scratch
    )
    _, send, close, line_drain = line_steps(place, shape, None, out, line_scratch)
    vector = VectorSum(place, vector_ref, vector_out, scratch)
    for z in order:
        start(z)
    ready_load().start()
    vector.round(0)
    for index, z in enumerate(order):
        pair_add(z)
        if index == 0:
            ready_load().wait()
    vector.round(1)
    for index, z in enumerate(order):
        ready_send(z)
        first_add(z)
        if index == 1:
            vector.round(2)
    ready_close()
    vector.round(3)
    for index, z in enumerate(order):
        second_add(z)
        if index > 0:
            send(order[index - 1])
    send(order[-1])
    vector.round(4)
    close()
    vector.round(5)
    ready_drain()
    line_drain()
    for z in order:
        drain(z)
    vector.finish()


def square_shape(group, line):
    rows, columns = group[0].shape
    return ReduceShape("four", rows // (2 * line), columns, len(group))


def fast_reduce(ready, group, line, collective_id, vector):
    shape = square_shape(group, line)
    anywhere = pl.BlockSpec(memory_space=pl.ANY)
    local = pl.BlockSpec(memory_space=pltpu.VMEM)
    out_shape = [shape.out_shape()] * 2 + [jax.ShapeDtypeStruct(vector.shape, F32)]
    return pl.pallas_call(
        functools.partial(reduce_kernel, shape, shape, line),
        in_specs=[anywhere] * (1 + len(group)) + [local],
        out_specs=[local] * 3,
        out_shape=out_shape,
        scratch_shapes=shape.line_scratch(line)
        + shape.line_scratch(line)
        + shape.plane_scratch(line)
        + VectorSum.scratch(vector.shape),
        compiler_params=pltpu.CompilerParams(
            collective_id=collective_id, has_side_effects=True, vmem_limit_bytes=60 << 20
        ),
        name="fast_reduce",
    )(ready, *group, vector)


PLANE = 4
CHIP = 2
LINE = 4


def small_plane():
    return lax.axis_size("rep") == PLANE and lax.axis_size("fsdp") == CHIP * LINE


def gather(block):
    return lax.all_gather(block, "fsdp", axis=0, tiled=True)


def gather_all(groups, by_rows, collective_id):
    if small_plane():
        return fast_gather(groups, LINE, by_rows, collective_id)
    return [gather(jnp.concatenate(group, axis=1)) for group in groups]


def scatter(block):
    return lax.psum_scatter(block.astype(BF16), "fsdp", scatter_dimension=0, tiled=True)


def column_blocks(block):
    rows = block.shape[0]
    return block.reshape(rows, lax.axis_size("rep"), -1).swapaxes(0, 1)


def scatter_columns(parts):
    count = lax.axis_size("rep")
    rows = parts[0].shape[0]
    split = [part.reshape(rows, count, -1) for part in parts]
    joined = jnp.concatenate(split, axis=2).reshape(rows, -1)
    own = lax.psum_scatter(joined, "rep", scatter_dimension=1, tiled=True)
    sizes = [part.shape[1] // count for part in parts]
    outs = []
    start = 0
    for size in sizes:
        outs.append(own[:, start : start + size].astype(F32))
        start += size
    return outs


def scatter_last(ready, groups, vector, collective_id):
    if ready is not None:
        *outs, total = fast_reduce(ready, groups[1], LINE, collective_id, vector)
        return [[out[index] for index in range(4)] for out in outs], total
    outs = [scatter_columns([scatter(item) for item in group]) for group in groups]
    return outs, lax.psum(vector, ("rep", "fsdp"))


def body(
    tokens,
    memory,
    prefix_len,
    bucket_table,
    rel_bias,
    gain_self,
    self_query,
    self_key,
    self_value,
    self_out,
    gain_cross,
    cross_query,
    cross_key,
    cross_value,
    cross_out,
    gain_feed,
    gate_weight,
    up_weight,
    down_weight,
    out_grad,
):
    nseq, length, width = tokens.shape
    shard = gain_self.shape[0]
    groups = width // shard
    entries = rel_bias.shape[0]
    small = jnp.stack(
        [gain_self, gain_cross, gain_feed, jnp.pad(rel_bias, (0, shard - entries))], axis=1
    )
    small = jnp.pad(small, ((0, 0), (0, 2 * LANES - 4)))
    first, second, down = gather_all(
        [
            [self_query, self_key, self_value, small],
            [self_out, cross_query, cross_key, cross_value, cross_out, small],
            [down_weight],
        ],
        [False, False, True],
        1,
    )
    gate_up_own = jnp.concatenate([gate_weight, up_weight], axis=1)
    gate_up_own, first, second, down = lax.optimization_barrier(
        (gate_up_own, first, second, down)
    )
    gate_up = gather(gate_up_own)
    qkv_proj = first[:, : 3 * width]
    picks = jnp.eye(8, LANES, dtype=BF16)
    vectors = back_term(picks, first[:, 3 * width : 3 * width + LANES])
    gain_first = vectors[0:1]
    gain_second = vectors[1:2]
    gain_third = vectors[2:3]
    table = vectors[3].astype(BF16).reshape(groups, shard)[:, :entries]
    table = table.reshape(NHEAD, BUCKETS)
    out_self = second[:, :width]
    query_cross = second[:, width : 2 * width]
    kv_cross = second[:, 2 * width : 4 * width]

    buckets_back = jnp.pad(bucket_table[::-1], (0, 1)).reshape(1, 2 * length)
    bias = skewed_bias(table, buckets_back, length)

    rows = nseq * length
    start_rows = tokens.reshape(rows, width).astype(F32)
    memory_rows = memory.reshape(-1, width)
    upstream = out_grad.reshape(rows, width)

    scale_first = inverse_rms(start_rows)
    normed_first = (start_rows * scale_first * gain_first).astype(BF16)
    qkv = matmul(normed_first, qkv_proj).astype(BF16)
    context, lse_self = run_self_forward(prefix_len, qkv, bias, nseq)
    middle = start_rows + matmul(context, out_self)
    scale_second = inverse_rms(middle)
    normed_second = (middle * scale_second * gain_second).astype(BF16)
    query_two = matmul(normed_second, query_cross).astype(BF16)
    kv_two = matmul(memory_rows, kv_cross).astype(BF16)
    context_two, lse_cross = run_cross_forward(query_two, kv_two, nseq)
    (
        result,
        later_grad,
        branch_two,
        context_two_grad,
        gain_third_grad,
        down_term,
        pair_term,
    ) = run_feed(middle, context_two, second, 4, gain_third, upstream, gate_up, down)
    down_own = scatter(down_term)
    pair_own = scatter(pair_term)
    query_two_grad, key_two_grad, value_two_grad = run_cross_backward(
        query_two, kv_two, context_two_grad, context_two, lse_cross, nseq
    )
    (
        middle_grad,
        gain_second_grad,
        query_term,
        out_term,
        branch_one,
        context_grad,
    ) = run_close(
        middle,
        later_grad,
        gain_second,
        context_two,
        branch_two,
        [query_two_grad],
        [(second, 1)],
        (second, 0),
        "cross_close",
    )
    memory_grad, key_term, value_term = run_memory(
        memory_rows, key_two_grad, value_two_grad, second, 2, 3
    )
    cross_terms = [query_term, key_term, value_term, out_term]
    query_grad, key_grad, value_grad, diagonal, *sums = run_self_backward(
        prefix_len,
        qkv,
        context_grad,
        context,
        lse_self,
        bias,
        nseq,
        (cross_terms, 2) if small_plane() else None,
    )
    tokens_grad, gain_first_grad, *self_terms = run_close(
        tokens.reshape(rows, width),
        middle_grad,
        gain_first,
        context,
        branch_one,
        [query_grad, key_grad, value_grad],
        [(first, 0), (first, 1), (first, 2)],
        None,
        "self_close",
    )

    onehot = (
        buckets_back.reshape(-1, 1) == jnp.arange(BUCKETS, dtype=jnp.int32)[None, :]
    ).astype(F32)
    onehot = onehot * (jnp.arange(2 * length) < 2 * length - 1)[:, None]
    bias_grad = jnp.dot(
        diagonal.reshape(NHEAD, 2 * length), onehot, precision=lax.Precision.HIGHEST
    )
    bias_rows = jnp.pad(
        bias_grad.reshape(groups, entries), ((0, 0), (0, shard - entries))
    ).reshape(width)
    vector_block = jnp.pad(
        jnp.concatenate(
            [gain_first_grad, gain_second_grad, gain_third_grad, bias_rows[None]], axis=0
        ),
        ((0, 4), (0, 0)),
    )
    down_own, pair_own, memory_grad, self_terms = lax.optimization_barrier(
        (down_own, pair_own, memory_grad, self_terms)
    )
    down_split = column_blocks(down_own)
    pair_split = column_blocks(pair_own)
    down_split, pair_split, self_terms = lax.optimization_barrier(
        (down_split, pair_split, self_terms)
    )
    down_weight_grad = lax.psum_scatter(down_split, "rep").astype(F32)
    pair_grad = lax.psum_scatter(pair_split, "rep").astype(F32)
    pair_grad = pair_grad.reshape(shard, -1, 2, FEED_BLOCK)
    gate_weight_grad = pair_grad[:, :, 0].reshape(shard, -1)
    up_weight_grad = pair_grad[:, :, 1].reshape(shard, -1)
    (cross_out_grads, self_out_grads), totals = scatter_last(
        sums[0] if sums else None, [cross_terms, self_terms], vector_block, 3
    )
    own = lax.dynamic_slice(
        totals, (0, lax.axis_index("fsdp") * shard), (totals.shape[0], shard)
    )
    return (
        result.reshape(tokens.shape),
        tokens_grad.reshape(tokens.shape),
        memory_grad.reshape(memory.shape),
        own[3, :entries],
        own[0],
        *self_out_grads,
        own[1],
        *cross_out_grads,
        own[2],
        gate_weight_grad,
        up_weight_grad,
        down_weight_grad,
    )


def solution(mesh):
    batch = P(("rep", "fsdp"), None, None)
    matrix = P("fsdp", None)
    vector = P("fsdp")
    split = P("fsdp", "rep")
    in_specs = (
        (batch, batch, P(("rep", "fsdp")), P(), vector, vector)
        + (matrix,) * 4
        + (vector,)
        + (matrix,) * 4
        + (vector,)
        + (matrix,) * 3
        + (batch,)
    )
    out_specs = (
        (batch, batch, batch, vector, vector)
        + (split,) * 4
        + (vector,)
        + (split,) * 4
        + (vector,)
        + (split,) * 3
    )
    return jax.shard_map(body, mesh=mesh, in_specs=in_specs, out_specs=out_specs, check_vma=False)
```

```python
import functools

import jax
import jax.numpy as jnp
from jax import lax
from jax.experimental import pallas as pl
from jax.experimental.pallas import tpu as pltpu
from jax.sharding import PartitionSpec as P

NHEAD = 12
DHEAD = 64
BUCKETS = 32
PAIRS = NHEAD // 2
LANES = 2 * DHEAD
PREFIX_MAX = 256

EPSILON = 1e-06
CUBIC_TERM = 0.044715
SQRT_TWO_PI = 0.7978845608028654
NEGATIVE = -1000000000.0

F32 = jnp.float32
BF16 = jnp.bfloat16
LAST_DIMS = (((1,), (1,)), ((), ()))


def matmul(left_side, right_side):
    return jnp.dot(left_side, right_side, preferred_element_type=F32)


def back_term(gradient, weight):
    return lax.dot_general(gradient, weight, LAST_DIMS, preferred_element_type=F32)


def inverse_rms(values):
    return lax.rsqrt(jnp.mean(values * values, axis=-1, keepdims=True) + EPSILON)


def norm_back(values, scale_rows, gain_vec, upstream):
    weighted = upstream * gain_vec
    gain_grad = jnp.sum(upstream * values * scale_rows, axis=0)
    input_grad = scale_rows * weighted - values * scale_rows * scale_rows * scale_rows * jnp.mean(
        values * weighted, axis=-1, keepdims=True
    )
    return (input_grad, gain_grad)


def one_head(rows, head):
    lane = lax.broadcasted_iota(jnp.int32, rows.shape, 1)
    keep = lane < DHEAD if head == 0 else lane >= DHEAD
    return jnp.where(keep, rows, jnp.zeros_like(rows))


def flipped(rows):
    return rows.astype(F32).T.astype(BF16)


def tree(fold, rows, groups):
    step = rows.shape[0] // groups
    total = rows[:step]
    for index in range(1, groups):
        total = fold(total, rows[index * step : (index + 1) * step])
    return total


def column_max(rows, groups):
    return jnp.max(tree(jnp.maximum, rows, groups), axis=0, keepdims=True)


def column_sum(rows, groups):
    return jnp.sum(tree(jnp.add, rows, groups), axis=0, keepdims=True)


def allowed_at(shape, key_start, query_start, prefix):
    key = lax.broadcasted_iota(jnp.int32, shape, 0) + key_start
    query = lax.broadcasted_iota(jnp.int32, shape, 1) + query_start
    return (key <= query) | (key < prefix)


def skew_kernel(table_ref, buckets_ref, out_ref):
    bucket = lax.broadcasted_iota(jnp.int32, (BUCKETS, buckets_ref.shape[1]), 0)
    onehot = (bucket == buckets_ref[...]).astype(BF16)
    by_offset = matmul(table_ref[...], onehot)
    width = out_ref.shape[2]
    total = by_offset.shape[1]
    for head in range(NHEAD):
        rows = jnp.broadcast_to(by_offset[head : head + 1], (LANES, total))
        rolled = pltpu.roll(rows, total - (LANES - 1), 1, stride=1, stride_axis=0)
        out_ref[head] = rolled[:, :width]


def skewed_bias(table, buckets_back, length):
    total = 2 * length
    return pl.pallas_call(
        skew_kernel,
        out_shape=jax.ShapeDtypeStruct((NHEAD, LANES, total - LANES), F32),
        name="skewed_bias",
    )(jnp.pad(table, ((0, 4), (0, 0))), buckets_back)


HEADROOM = 70.0


def self_forward(prefix_ref, query_ref, key_ref, value_ref, bias_ref, out_ref, lse_ref):
    length = query_ref.shape[0]
    block = 256
    prefix = prefix_ref[pl.program_id(0)]
    queries = query_ref[...]
    keys = key_ref[...]
    values = flipped(value_ref[...])

    def run(exact):
        excess = jnp.zeros((1, block), F32)
        for start in range(0, length, block):
            stop = start + block
            count = max(PREFIX_MAX, stop)
            outs = []
            for head in range(2):
                scores = back_term(keys[:count], one_head(queries[start:stop], head))
                parts = []
                for base in range(0, count, LANES):
                    shift = length - LANES - base + start
                    part = scores[base : base + LANES] + bias_ref[head, :, shift : shift + block]
                    if base + LANES - 1 > start:
                        part = jnp.where(
                            allowed_at(part.shape, base, start, prefix), part, NEGATIVE
                        )
                    parts.append(part)
                top = parts[0]
                for part in parts[1:]:
                    top = jnp.maximum(top, part)
                top = column_max(top, 4)
                anchor = top if exact else column_max(parts[0], 4)
                if not exact:
                    excess = jnp.maximum(excess, top - anchor)
                shares = [jnp.exp(part - anchor) for part in parts]
                total = shares[0]
                for share in shares[1:]:
                    total = total + share
                total = column_sum(total, 4)
                share = jnp.concatenate([item.astype(BF16) for item in shares], axis=0)
                context = matmul(values[head * DHEAD : (head + 1) * DHEAD, :count], share)
                outs.append(context * (1.0 / total))
                lse_ref[head : head + 1, start:stop] = anchor + jnp.log(total)
            out_ref[start:stop, :] = jnp.concatenate(outs, axis=0).T.astype(BF16)
        return jnp.max(excess)

    excess = run(False)

    @pl.when(excess > HEADROOM)
    def _():
        run(True)


def cross_forward(query_ref, key_ref, value_ref, out_ref, lse_ref):
    keys = key_ref[...]
    values = flipped(value_ref[...])
    queries = query_ref[...]

    def run(exact):
        excess = jnp.zeros((1, queries.shape[0]), F32)
        ahead = [back_term(keys, one_head(queries, head)) for head in range(2)]
        outs = []
        for head in range(2):
            scores = ahead[head]
            top = column_max(scores, 16)
            anchor = top if exact else column_max(scores[: 2 * LANES], 8)
            if not exact:
                excess = jnp.maximum(excess, top - anchor)
            share = jnp.exp(scores - anchor)
            total = column_sum(share, 16)
            context = matmul(values[head * DHEAD : (head + 1) * DHEAD], share.astype(BF16))
            outs.append(context * (1.0 / total))
            lse_ref[head : head + 1, :] = anchor + jnp.log(total)
        out_ref[...] = jnp.concatenate(outs, axis=0).T.astype(BF16)
        return jnp.max(excess)

    excess = run(False)

    @pl.when(excess > HEADROOM)
    def _():
        run(True)


def cross_backward(
    query_ref, key_ref, value_ref, up_ref, context_ref, lse_ref, dq_ref, dk_ref, dv_ref
):
    length = query_ref.shape[0]
    block = 256
    keys = key_ref[...]
    values = value_ref[...]
    queries = query_ref[...]
    upstream = up_ref[...]
    keys_flipped = flipped(keys)
    inner = (upstream.astype(F32) * context_ref[...].astype(F32)).T
    key_grad = None
    value_grad = None
    for start in range(0, length, block):
        rows = slice(start, start + block)
        grads = []
        for head in range(2):
            sub = slice(head * DHEAD, (head + 1) * DHEAD)
            query = one_head(queries[rows], head)
            above = one_head(upstream[rows], head)
            row_inner = jnp.sum(inner[sub, rows], axis=0, keepdims=True)
            shares = jnp.exp(back_term(keys, query) - lse_ref[head : head + 1, rows])
            share_grad = back_term(values, above)
            score_grad = (shares * (share_grad - row_inner)).astype(BF16)
            value_part = matmul(shares.astype(BF16), above)
            key_part = matmul(score_grad, query)
            value_grad = value_part if value_grad is None else value_grad + value_part
            key_grad = key_part if key_grad is None else key_grad + key_part
            grads.append(matmul(keys_flipped[sub], score_grad))
        dq_ref[rows, :] = jnp.concatenate(grads, axis=0).T.astype(BF16)
    dk_ref[...] = key_grad.astype(BF16)
    dv_ref[...] = value_grad.astype(BF16)


def self_backward(
    prefix_ref,
    query_ref,
    key_ref,
    value_ref,
    up_ref,
    context_ref,
    lse_ref,
    bias_ref,
    dq_ref,
    dk_ref,
    dv_ref,
    diag_ref,
    acc_ref,
):
    length = query_ref.shape[0]
    block = 256
    step = pl.program_id(1)
    prefix = prefix_ref[step]

    @pl.when(step == 0)
    def _():
        acc_ref[...] = jnp.zeros_like(acc_ref)

    queries = query_ref[...]
    keys = key_ref[...]
    values = value_ref[...]
    upstream = up_ref[...]
    keys_flipped = flipped(keys)
    inner = (upstream.astype(F32) * context_ref[...].astype(F32)).T
    count_all = length // block
    key_grad = [None] * count_all
    value_grad = [None] * count_all
    for start in range(0, length, block):
        stop = start + block
        count = max(PREFIX_MAX, stop)
        rows = slice(start, stop)
        grads = []
        for head in range(2):
            sub = slice(head * DHEAD, (head + 1) * DHEAD)
            query = one_head(queries[rows], head)
            above = one_head(upstream[rows], head)
            row_inner = jnp.sum(inner[sub, rows], axis=0, keepdims=True)
            row_lse = lse_ref[head : head + 1, rows]
            scores = back_term(keys[:count], query)
            share_grad = back_term(values[:count], above)
            shares = []
            score_grads = []
            for base in range(0, count, LANES):
                part = slice(base, base + LANES)
                shift = length - LANES - base + start
                share = jnp.exp(
                    scores[part] + bias_ref[head, :, shift : shift + block] - row_lse
                )
                if base + LANES - 1 > start:
                    share = jnp.where(allowed_at(share.shape, base, start, prefix), share, 0.0)
                score_grad = share * (share_grad[part] - row_inner)
                acc_ref[head, :, shift : shift + block] += score_grad
                shares.append(share.astype(BF16))
                score_grads.append(score_grad.astype(BF16))
            share = jnp.concatenate(shares, axis=0)
            score_grad = jnp.concatenate(score_grads, axis=0)
            value_part = matmul(share, above)
            key_part = matmul(score_grad, query)
            for index in range(count // block):
                part = slice(index * block, (index + 1) * block)
                if value_grad[index] is None:
                    value_grad[index] = value_part[part]
                    key_grad[index] = key_part[part]
                else:
                    value_grad[index] = value_grad[index] + value_part[part]
                    key_grad[index] = key_grad[index] + key_part[part]
            grads.append(matmul(keys_flipped[sub, :count], score_grad))
        dq_ref[rows, :] = jnp.concatenate(grads, axis=0).T.astype(BF16)
    for index in range(count_all):
        part = slice(index * block, (index + 1) * block)
        dk_ref[part, :] = key_grad[index].astype(BF16)
        dv_ref[part, :] = value_grad[index].astype(BF16)

    @pl.when(step == pl.num_programs(1) - 1)
    def _():
        total = 2 * length
        for head in range(2):
            rows = jnp.concatenate([acc_ref[head], jnp.zeros((LANES, LANES), F32)], axis=1)
            half = LANES // 2
            while half >= 1:
                rows = rows[:half] + pltpu.roll(rows[half:], total - half, 1)
                half //= 2
            diag_ref[head : head + 1, :] = pltpu.roll(rows, LANES - 1, 1)


def spec(shape, index):
    return pl.BlockSpec(shape, index)


def run_self_forward(prefix, qkv, bias, nseq):
    length = qkv.shape[0] // nseq
    return pl.pallas_call(
        self_forward,
        grid_spec=pltpu.PrefetchScalarGridSpec(
            num_scalar_prefetch=1,
            grid=(nseq, PAIRS),
            in_specs=[
                spec((length, LANES), lambda s, p, _: (s, p)),
                spec((length, LANES), lambda s, p, _: (s, PAIRS + p)),
                spec((length, LANES), lambda s, p, _: (s, 2 * PAIRS + p)),
                spec((2, LANES, 2 * length - LANES), lambda s, p, _: (p, 0, 0)),
            ],
            out_specs=[
                spec((length, LANES), lambda s, p, _: (s, p)),
                spec((None, None, 2, length), lambda s, p, _: (s, p, 0, 0)),
            ],
        ),
        out_shape=[
            jax.ShapeDtypeStruct((qkv.shape[0], PAIRS * LANES), BF16),
            jax.ShapeDtypeStruct((nseq, PAIRS, 2, length), F32),
        ],
        cost_estimate=pl.CostEstimate(
            flops=20_000_000_000, bytes_accessed=12_000_000, transcendentals=0
        ),
        name="self_forward",
    )(prefix, qkv, qkv, qkv, bias)


def run_cross_forward(query, kv, nseq):
    length = query.shape[0] // nseq
    count = kv.shape[0] // nseq
    return pl.pallas_call(
        cross_forward,
        grid=(nseq, PAIRS),
        in_specs=[
            spec((length, LANES), lambda s, p: (s, p)),
            spec((count, LANES), lambda s, p: (s, p)),
            spec((count, LANES), lambda s, p: (s, PAIRS + p)),
        ],
        out_specs=[
            spec((length, LANES), lambda s, p: (s, p)),
            spec((None, None, 2, length), lambda s, p: (s, p, 0, 0)),
        ],
        out_shape=[
            jax.ShapeDtypeStruct(query.shape, BF16),
            jax.ShapeDtypeStruct((nseq, PAIRS, 2, length), F32),
        ],
        cost_estimate=pl.CostEstimate(
            flops=24_000_000_000, bytes_accessed=10_000_000, transcendentals=0
        ),
        name="cross_forward",
    )(query, kv, kv)


def carry(carried, steps, inner, inputs, outputs):
    if carried is None:
        return inner, [], [], [], [], None
    group, kind, collective_id = carried
    shape = group_shape(group, kind, LINE)
    kernel = functools.partial(
        carried_kernel, shape, LINE, steps, inner, inputs, outputs
    )
    total = shape.total_shape(LINE)
    params = pltpu.CompilerParams(
        collective_id=collective_id, has_side_effects=True, vmem_limit_bytes=60 << 20
    )
    return (
        kernel,
        group,
        [pl.BlockSpec(total, lambda *_: (0, 0, 0, 0))],
        [jax.ShapeDtypeStruct(total, BF16)],
        shape.plane_scratch(LINE),
        params,
    )


def run_cross_backward(query, kv, upstream, context, lse, nseq, carried=None):
    length = query.shape[0] // nseq
    count = kv.shape[0] // nseq
    rows = spec((length, LANES), lambda s, p: (s, p))
    wide = spec((count, LANES), lambda s, p: (s, p))
    kernel, group, total_specs, totals, scratch, params = carry(
        carried, PAIRS * nseq, cross_backward, 6, 3
    )
    return pl.pallas_call(
        kernel,
        grid=(nseq, PAIRS),
        in_specs=[
            rows,
            wide,
            spec((count, LANES), lambda s, p: (s, PAIRS + p)),
            rows,
            rows,
            spec((None, None, 2, length), lambda s, p: (s, p, 0, 0)),
        ]
        + [pl.BlockSpec(memory_space=pl.ANY)] * len(group),
        out_specs=[rows, wide, wide] + total_specs,
        out_shape=[
            jax.ShapeDtypeStruct(query.shape, BF16),
            jax.ShapeDtypeStruct((kv.shape[0], PAIRS * LANES), BF16),
            jax.ShapeDtypeStruct((kv.shape[0], PAIRS * LANES), BF16),
        ]
        + totals,
        scratch_shapes=scratch,
        cost_estimate=pl.CostEstimate(
            flops=36_000_000_000, bytes_accessed=20_000_000, transcendentals=0
        ),
        compiler_params=params,
        name="cross_backward",
    )(query, kv, kv, upstream, context, lse, *group)


def run_self_backward(prefix, qkv, upstream, context, lse, bias, nseq, carried=None):
    length = qkv.shape[0] // nseq
    rows = spec((length, LANES), lambda p, s, _: (s, p))
    kernel, group, total_specs, totals, scratch, params = carry(
        carried, PAIRS * nseq, self_backward, 8, 4
    )
    return pl.pallas_call(
        kernel,
        grid_spec=pltpu.PrefetchScalarGridSpec(
            num_scalar_prefetch=1,
            grid=(PAIRS, nseq),
            in_specs=[
                rows,
                spec((length, LANES), lambda p, s, _: (s, PAIRS + p)),
                spec((length, LANES), lambda p, s, _: (s, 2 * PAIRS + p)),
                rows,
                rows,
                spec((None, None, 2, length), lambda p, s, _: (s, p, 0, 0)),
                spec((2, LANES, 2 * length - LANES), lambda p, s, _: (p, 0, 0)),
            ]
            + [pl.BlockSpec(memory_space=pl.ANY)] * len(group),
            out_specs=[
                rows,
                rows,
                rows,
                spec((None, 2, 2 * length), lambda p, s, _: (p, 0, 0)),
            ]
            + total_specs,
            scratch_shapes=[pltpu.VMEM((2, LANES, 2 * length - LANES), F32)] + scratch,
        ),
        out_shape=[jax.ShapeDtypeStruct(upstream.shape, BF16)] * 3
        + [jax.ShapeDtypeStruct((PAIRS, 2, 2 * length), F32)]
        + totals,
        cost_estimate=pl.CostEstimate(
            flops=24_000_000_000, bytes_accessed=20_000_000, transcendentals=0
        ),
        compiler_params=params,
        name="self_backward",
    )(prefix, qkv, qkv, qkv, upstream, context, lse, bias, *group)


FEED_BLOCK = 256


def feed_kernel(
    middle_ref,
    context_ref,
    out_proj_ref,
    gain_ref,
    up_grad_ref,
    gate_ref,
    up_ref,
    down_ref,
    result_ref,
    later_grad_ref,
    branch_ref,
    context_grad_ref,
    gain_grad_ref,
    down_term_ref,
    pair_term_ref,
    later_ref,
    normed_ref,
    flipped_ref,
    result_acc,
    third_acc,
):
    step = pl.program_id(0)
    count = middle_ref.shape[0]
    chunk = 256
    chunks = [slice(start, start + chunk) for start in range(0, count, chunk)]

    @pl.when(step == 0)
    def _():
        for rows in chunks:
            later = middle_ref[rows] + matmul(context_ref[rows], out_proj_ref[...])
            normed = (later * inverse_rms(later) * gain_ref[...]).astype(BF16)
            later_ref[rows] = later
            normed_ref[rows] = normed
            flipped_ref[:, rows] = flipped(normed)
            result_acc[rows] = jnp.zeros_like(later)
            third_acc[rows] = jnp.zeros_like(later)

    gate_proj = gate_ref[...]
    up_proj = up_ref[...]
    down_proj = down_ref[...]
    hidden_flipped = []
    gate_grads = []
    lift_grads = []
    for rows in chunks:
        normed = normed_ref[rows]
        gate = matmul(normed, gate_proj)
        lift = matmul(normed, up_proj)
        hidden_grad = back_term(up_grad_ref[rows], down_proj)
        square = gate * gate
        tangent = jnp.tanh(SQRT_TWO_PI * gate * (1.0 + CUBIC_TERM * square))
        half = 0.5 * (1.0 + tangent)
        active = gate * half
        slope = half + 0.5 * gate * (1.0 - tangent * tangent) * (
            SQRT_TWO_PI + 3.0 * CUBIC_TERM * SQRT_TWO_PI * square
        )
        hidden = active * lift
        gate_grad = (hidden_grad * lift * slope).astype(BF16)
        lift_grad = (hidden_grad * active).astype(BF16)
        hidden_flipped.append(hidden.T.astype(BF16))
        gate_grads.append(gate_grad)
        lift_grads.append(lift_grad)
        result_acc[rows] += matmul(hidden.astype(BF16), down_proj)
        third_acc[rows] += back_term(gate_grad, gate_proj) + back_term(lift_grad, up_proj)
    hidden_flipped = jnp.concatenate(hidden_flipped, axis=1)
    down_term_ref[...] = matmul(hidden_flipped, up_grad_ref[...]).astype(BF16)
    gate_grads = jnp.concatenate(gate_grads, axis=0)
    lift_grads = jnp.concatenate(lift_grads, axis=0)
    pair_term_ref[:, :FEED_BLOCK] = matmul(flipped_ref[...], gate_grads).astype(BF16)
    pair_term_ref[:, FEED_BLOCK:] = matmul(flipped_ref[...], lift_grads).astype(BF16)

    @pl.when(step == pl.num_programs(0) - 1)
    def _():
        gain_grad = jnp.zeros(gain_ref.shape, F32)
        for rows in chunks:
            later = later_ref[rows]
            result_ref[rows] = (later + result_acc[rows]).astype(BF16)
            carry, part = norm_back(later, inverse_rms(later), gain_ref[...], third_acc[rows])
            gain_grad = gain_grad + part[None, :]
            later_grad = up_grad_ref[rows].astype(F32) + carry
            branch = later_grad.astype(BF16)
            later_grad_ref[rows] = later_grad
            branch_ref[rows] = branch
            context_grad_ref[rows] = back_term(branch, out_proj_ref[...]).astype(BF16)
        gain_grad_ref[...] = gain_grad


def run_feed(middle, context, out_proj, out_block, gain, upstream, gate_up, down):
    count, width = middle.shape
    ffn = down.shape[0]
    blocks = ffn // FEED_BLOCK

    def whole(shape, **extra):
        return pl.BlockSpec(shape, lambda j: (0, 0), **extra)

    once = {"pipeline_mode": pl.Buffered(1)}
    rows = (count, width)
    return pl.pallas_call(
        feed_kernel,
        grid=(blocks,),
        in_specs=[
            whole(rows, **once),
            whole(rows, **once),
            pl.BlockSpec((width, width), lambda j: (0, out_block), **once),
            whole((1, width)),
            whole(rows, **once),
            spec((width, FEED_BLOCK), lambda j: (0, j)),
            spec((width, FEED_BLOCK), lambda j: (0, blocks + j)),
            spec((FEED_BLOCK, width), lambda j: (j, 0)),
        ],
        out_specs=[
            whole(rows),
            whole(rows),
            whole(rows),
            whole(rows),
            whole((1, width)),
            spec((FEED_BLOCK, width), lambda j: (j, 0)),
            spec((width, 2 * FEED_BLOCK), lambda j: (0, j)),
        ],
        out_shape=[
            jax.ShapeDtypeStruct(rows, BF16),
            jax.ShapeDtypeStruct(rows, F32),
            jax.ShapeDtypeStruct(rows, BF16),
            jax.ShapeDtypeStruct(rows, BF16),
            jax.ShapeDtypeStruct((1, width), F32),
            jax.ShapeDtypeStruct((ffn, width), BF16),
            jax.ShapeDtypeStruct((width, 2 * ffn), BF16),
        ],
        scratch_shapes=[
            pltpu.VMEM(rows, F32),
            pltpu.VMEM(rows, BF16),
            pltpu.VMEM((width, count), BF16),
            pltpu.VMEM(rows, F32),
            pltpu.VMEM(rows, F32),
        ],
        cost_estimate=pl.CostEstimate(
            flops=32_000_000_000, bytes_accessed=40_000_000, transcendentals=0
        ),
        compiler_params=pltpu.CompilerParams(vmem_limit_bytes=60 << 20),
        name="feed",
    )(middle, context, out_proj, gain, upstream, gate_up, gate_up, down)


def close_kernel(count, project, *refs):
    values_ref, carry_ref, gain_ref, left_ref, right_ref = refs[:5]
    grad_refs = refs[5 : 5 + count]
    weight_refs = refs[5 + count : 5 + 2 * count]
    at = 5 + 2 * count
    if project:
        proj_ref = refs[at]
        at += 1
    out_ref, gain_grad_ref = refs[at : at + 2]
    term_refs = refs[at + 2 : at + 3 + count]
    at += 3 + count
    if project:
        branch_ref, projected_ref = refs[at : at + 2]
        at += 2
    sums = refs[at : at + 1 + count]
    gain_sum = refs[at + 1 + count]
    step = pl.program_id(0)

    @pl.when(step == 0)
    def _():
        gain_sum[...] = jnp.zeros_like(gain_sum)
        for total in sums:
            total[...] = jnp.zeros_like(total)

    values = values_ref[...].astype(F32)
    gain = gain_ref[...]
    scale = inverse_rms(values)
    normed = (values * scale * gain).T.astype(BF16)
    upstream = None
    for index in range(count):
        grad = grad_refs[index][...]
        sums[index][...] += matmul(normed, grad)
        part = back_term(grad, weight_refs[index][...])
        upstream = part if upstream is None else upstream + part
    sums[count][...] += matmul(flipped(left_ref[...]), right_ref[...])
    carry, part = norm_back(values, scale, gain, upstream)
    gain_sum[...] += part[None, :]
    result = carry_ref[...] + carry
    out_ref[...] = result
    if project:
        branch = result.astype(BF16)
        branch_ref[...] = branch
        projected_ref[...] = back_term(branch, proj_ref[...]).astype(BF16)

    @pl.when(step == pl.num_programs(0) - 1)
    def _():
        gain_grad_ref[...] = gain_sum[...]
        for term, total in zip(term_refs, sums):
            term[...] = total[...].astype(BF16)


def run_close(values, carry, gain, left, right, grads, weights, project, name):
    rows, width = values.shape
    count = len(grads)
    block = 512
    wide = spec((block, width), lambda i: (i, 0))

    def columns(index):
        return pl.BlockSpec((width, width), lambda i: (0, index), pipeline_mode=pl.Buffered(1))

    whole = [spec((1, width), lambda i: (0, 0))]
    square = [spec((width, width), lambda i: (0, 0))] * (count + 1)
    extra = [] if project is None else [project]
    out_shape = [
        jax.ShapeDtypeStruct((rows, width), F32),
        jax.ShapeDtypeStruct((1, width), F32),
    ] + [jax.ShapeDtypeStruct((width, width), BF16)] * (count + 1)
    out_shape += [jax.ShapeDtypeStruct((rows, width), BF16)] * (2 * len(extra))
    return pl.pallas_call(
        functools.partial(close_kernel, count, project is not None),
        grid=(rows // block,),
        in_specs=[wide, wide]
        + whole
        + [wide] * (2 + count)
        + [columns(index) for _, index in weights + extra],
        out_specs=[wide] + whole + square + [wide] * (2 * len(extra)),
        out_shape=out_shape,
        scratch_shapes=[pltpu.VMEM((width, width), F32)] * (count + 1)
        + [pltpu.VMEM((1, width), F32)],
        cost_estimate=pl.CostEstimate(
            flops=8_000_000_000, bytes_accessed=25_000_000, transcendentals=0
        ),
        compiler_params=pltpu.CompilerParams(vmem_limit_bytes=60 << 20),
        name=name,
    )(values, carry, gain, left, right, *grads, *[item for item, _ in weights + extra])


def memory_kernel(
    memory_ref, key_grad_ref, value_grad_ref, key_ref, value_ref, out_ref, *rest
):
    key_term_ref, value_term_ref, key_sum, value_sum = rest
    step = pl.program_id(0)

    @pl.when(step == 0)
    def _():
        key_sum[...] = jnp.zeros_like(key_sum)
        value_sum[...] = jnp.zeros_like(value_sum)

    rows = flipped(memory_ref[...])
    key_grad = key_grad_ref[...]
    value_grad = value_grad_ref[...]
    out_ref[...] = back_term(key_grad, key_ref[...]) + back_term(value_grad, value_ref[...])
    key_sum[...] += matmul(rows, key_grad)
    value_sum[...] += matmul(rows, value_grad)

    @pl.when(step == pl.num_programs(0) - 1)
    def _():
        key_term_ref[...] = key_sum[...].astype(BF16)
        value_term_ref[...] = value_sum[...].astype(BF16)


def run_memory(memory, key_grad, value_grad, weights, key_block, value_block):
    rows, width = memory.shape
    block = 1024
    wide = spec((block, width), lambda i: (i, 0))
    square = spec((width, width), lambda i: (0, 0))

    def columns(index):
        return pl.BlockSpec((width, width), lambda i: (0, index), pipeline_mode=pl.Buffered(1))

    return pl.pallas_call(
        memory_kernel,
        grid=(rows // block,),
        in_specs=[wide, wide, wide, columns(key_block), columns(value_block)],
        out_specs=[wide, square, square],
        out_shape=[
            jax.ShapeDtypeStruct((rows, width), F32),
            jax.ShapeDtypeStruct((width, width), BF16),
            jax.ShapeDtypeStruct((width, width), BF16),
        ],
        scratch_shapes=[pltpu.VMEM((width, width), F32)] * 2,
        cost_estimate=pl.CostEstimate(
            flops=10_000_000_000, bytes_accessed=18_000_000, transcendentals=0
        ),
        compiler_params=pltpu.CompilerParams(vmem_limit_bytes=60 << 20),
        name="memory_close",
    )(memory, key_grad, value_grad, weights, weights)


MESH = pl.DeviceIdType.MESH


class Place:
    def __init__(self, line):
        self.line = line
        rep = lax.axis_index("rep")
        fsdp = lax.axis_index("fsdp")
        self.rep = rep
        self.fsdp = fsdp
        self.y = rep // 2
        self.x = rep % 2
        self.z = fsdp // 2
        self.core = fsdp % 2
        self.x_rep = self.y * 2 + 1 - self.x
        self.y_rep = (1 - self.y) * 2 + self.x

    def at_x(self):
        return {"rep": self.x_rep, "fsdp": self.fsdp}

    def at_y(self):
        return {"rep": self.y_rep, "fsdp": self.fsdp}

    def at_partner(self):
        return {"rep": self.rep, "fsdp": self.z * 2 + 1 - self.core}

    def at_line(self, side):
        return {"rep": self.rep, "fsdp": self.fsdp + (2 if side == 0 else -2)}

    def has_next(self, side):
        return self.z < self.line - 1 if side == 0 else self.z > 0

    def has_last(self, side):
        return self.has_next(1 - side)

    def arrives(self, side, hop):
        if side == 0:
            return self.z - 1 - hop >= 0
        return self.z + 1 + hop <= self.line - 1

    def source(self, side, hop):
        return self.z - 1 - hop if side == 0 else self.z + 1 + hop

    def at_far(self):
        half = self.line // 2
        return {"rep": self.rep, "fsdp": (self.z + half) % self.line * 2 + self.core}

    def greet(self, wide=False):
        barrier = pltpu.get_barrier_semaphore()
        targets = [self.at_x(), self.at_y(), self.at_partner()]
        if wide:
            targets.append({"rep": 3 - self.rep, "fsdp": self.fsdp})
            targets.append(self.at_far())
        for target in targets:
            pl.semaphore_signal(barrier, inc=1, device_id=target, device_id_type=MESH)
        for side in range(2):

            @pl.when(self.has_next(side))
            def _():
                pl.semaphore_signal(
                    barrier, inc=1, device_id=self.at_line(side), device_id_type=MESH
                )

        count = len(targets)
        for side in range(2):
            count = count + jnp.where(self.has_next(side), 1, 0)
        pl.semaphore_wait(barrier, count)


def remote(source, target, send, recv, device):
    return pltpu.make_async_remote_copy(
        src_ref=source,
        dst_ref=target,
        send_sem=send,
        recv_sem=recv,
        device_id=device,
        device_id_type=MESH,
    )


class GatherShape:
    def __init__(self, parts, by_rows):
        self.rows = parts[0].shape[0]
        self.widths = [part.shape[1] for part in parts]
        self.starts = [sum(self.widths[:index]) for index in range(len(parts))]
        self.columns = sum(self.widths)
        self.by_rows = by_rows

    def full(self, ref, owner):
        return ref.at[pl.ds(pl.multiple_of(owner * self.rows, 32), self.rows)]

    def piece(self, ref, owner, part, half=None):
        base = owner * self.rows
        if self.by_rows:
            rows = self.rows // 4
            base = base + part * rows
        else:
            rows = self.rows
        if half is not None:
            rows = rows // 2
            base = base + half * rows
        row_slice = pl.ds(pl.multiple_of(base, 16), rows)
        if self.by_rows:
            return ref.at[row_slice]
        width = self.columns // 4
        return ref.at[row_slice, pl.ds(pl.multiple_of(part * width, LANES), width)]


def gather_sems(line):
    hops = line - 1
    return [pltpu.SemaphoreType.DMA((5, 2, 2, hops)), pltpu.SemaphoreType.DMA((4,))] + [
        pltpu.SemaphoreType.DMA((2, 2, hops))
    ]


def gather_steps(place, shape, src, own, dst, sems):
    hop_sem, own_sem, pair_sem = sems
    hops = place.line - 1
    me = place.fsdp

    def load(index):
        at = pl.ds(shape.starts[index], shape.widths[index])
        return pltpu.make_async_copy(src[index], own.at[:, at], own_sem.at[0])

    def loaded():
        return pltpu.make_async_copy(own, own, own_sem.at[0])

    def keep():
        return pltpu.make_async_copy(own, shape.full(dst, me), own_sem.at[1])

    def own_pair():
        return remote(
            own, shape.full(dst, me), own_sem.at[2], own_sem.at[3], place.at_partner()
        )

    def owner(side, hop):
        return place.source(side, hop) * 2 + place.core

    def line_first(side):
        return remote(
            shape.piece(own, 0, place.rep),
            shape.piece(dst, me, place.rep),
            hop_sem.at[0, 0, side, 0],
            hop_sem.at[0, 1, side, 0],
            place.at_line(side),
        )

    def moved(kind, side, hop, block, device):
        return remote(
            block, block, hop_sem.at[kind, 0, side, hop], hop_sem.at[kind, 1, side, hop], device
        )

    def line_next(side, hop):
        block = shape.piece(dst, owner(side, hop - 1), place.rep)
        return moved(0, side, hop, block, place.at_line(side))

    def line_arrival(side, hop):
        block = shape.piece(dst, owner(side, hop), place.rep)
        return moved(0, side, hop, block, place.at_line(side))

    def plane(axis, side, hop):
        block = shape.piece(dst, owner(side, hop), place.rep)
        return moved(1 + axis, side, hop, block, place.at_x() if axis == 0 else place.at_y())

    def cross(axis, side, hop):
        part = place.x_rep if axis == 1 else place.y_rep
        block = shape.piece(dst, owner(side, hop), part, 1 - axis)
        return moved(3 + axis, side, hop, block, place.at_x() if axis == 0 else place.at_y())

    def pair(side, hop):
        block = shape.full(dst, owner(side, hop))
        return remote(
            block, block, pair_sem.at[0, side, hop], pair_sem.at[1, side, hop], place.at_partner()
        )

    def each(fn):
        def run(hop):
            for side in range(2):
                pl.when(place.arrives(side, hop))(functools.partial(fn, side, hop))

        return run

    def start():
        for index in range(len(src)):
            load(index).start()
        loaded().wait()
        for side in range(2):
            pl.when(place.has_next(side))(lambda side=side: line_first(side).start())
        own_pair().start()
        keep().start()

    def arrive(side, hop):
        line_arrival(side, hop).wait_recv()
        if hop + 1 < hops:
            pl.when(place.has_next(side))(lambda: line_next(side, hop + 1).start())
        plane(0, side, hop).start()
        plane(1, side, hop).start()

    def turn(side, hop):
        plane(0, side, hop).wait_recv()
        cross(1, side, hop).start()
        plane(1, side, hop).wait_recv()
        cross(0, side, hop).start()

    def hand(side, hop):
        cross(0, side, hop).wait_recv()
        cross(1, side, hop).wait_recv()
        pair(side, hop).start()

    def finish():
        def last(side, hop):
            pair(side, hop).wait()
            for axis in range(2):
                plane(axis, side, hop).wait_send()
                cross(axis, side, hop).wait_send()
            if hop + 1 < hops:
                pl.when(place.has_next(side))(lambda: line_next(side, hop + 1).wait_send())

        for hop in range(hops):
            each(last)(hop)
        for side in range(2):
            pl.when(place.has_next(side))(lambda side=side: line_first(side).wait_send())
        own_pair().wait()
        keep().wait()

    return start, each(arrive), each(turn), each(hand), finish


def gather_kernel(shapes, line, *refs):
    count = len(shapes)
    sources = []
    at = 0
    for shape in shapes:
        sources.append(refs[at : at + len(shape.widths)])
        at += len(shape.widths)
    targets = refs[at : at + count]
    scratch = refs[at + count :]
    place = Place(line)
    place.greet()
    plans = []
    for index, shape in enumerate(shapes):
        own, *sems = scratch[4 * index : 4 * index + 4]
        plans.append(gather_steps(place, shape, sources[index], own, targets[index], sems))
    for plan in plans:
        plan[0]()
    for step in range(line + 1):
        for stage in range(3):
            hop = step - stage
            if 0 <= hop < line - 1:
                for plan in plans:
                    plan[1 + stage](hop)
    for plan in plans:
        plan[4]()


def fast_gather(groups, line, by_rows, collective_id):
    shapes = [GatherShape(group, flag) for group, flag in zip(groups, by_rows)]
    scratch = []
    for shape in shapes:
        scratch.append(pltpu.VMEM((shape.rows, shape.columns), BF16))
        scratch.extend(gather_sems(line))
    anywhere = pl.BlockSpec(memory_space=pl.ANY)
    blocks = [block for group in groups for block in group]
    return pl.pallas_call(
        functools.partial(gather_kernel, shapes, line),
        in_specs=[anywhere] * len(blocks),
        out_specs=[anywhere] * len(groups),
        out_shape=[
            jax.ShapeDtypeStruct((2 * line * s.rows, s.columns), BF16) for s in shapes
        ],
        scratch_shapes=scratch,
        compiler_params=pltpu.CompilerParams(collective_id=collective_id, has_side_effects=True),
        name="fast_gather",
    )(*blocks)


class ReduceShape:
    def __init__(self, kind, rows, columns, sources):
        self.kind = kind
        self.rows = rows
        self.sources = sources
        if kind == "rows":
            self.block = (rows // 8, columns)
        elif kind == "pair":
            self.block = (rows // 2, columns // 2)
        else:
            self.block = (rows // 2, columns)
        self.exchange = kind != "pair"
        self.part_rows = rows // 4 if kind == "rows" else rows
        self.part_columns = columns // 4

    def pieces(self, refs, owner, half, quarter):
        rows, columns = self.block
        if self.kind == "rows":
            base = owner * self.rows + quarter * (self.rows // 4) + half * rows
            return [(refs[0].at[pl.ds(pl.multiple_of(base, 16), rows)], 0, columns)]
        at = pl.ds(pl.multiple_of(owner * self.rows + half * rows, 16), rows)
        if self.kind == "four":
            return [(refs[quarter].at[at], 0, columns)]
        width = columns // 2
        cut = slice(quarter * width, (quarter + 1) * width)
        return [(refs[index].at[at, cut], index * width, width) for index in range(2)]

    def out_shape(self):
        if self.exchange:
            return jax.ShapeDtypeStruct((4, self.part_rows, self.part_columns), F32)
        return jax.ShapeDtypeStruct((self.rows, self.block[1]), F32)

    def total_shape(self, line):
        return (line, 2) + self.block

    def plane_scratch(self, line):
        rows, columns = self.block
        dma = pltpu.SemaphoreType.DMA
        return [
            pltpu.VMEM((line, 8, rows, columns), BF16),
            pltpu.VMEM((line, 8, rows, columns), BF16),
            pltpu.VMEM((line, 2, 2, rows, columns), BF16),
            pltpu.VMEM((line, 2, rows, columns), BF16),
            dma((line,)),
            dma((2, line)),
            dma((2, line, 2)),
            dma((2, line, 2)),
        ]

    def line_scratch(self, line):
        dma = pltpu.SemaphoreType.DMA
        return [
            pltpu.VMEM(self.total_shape(line), BF16),
            pltpu.VMEM((2,) + self.total_shape(line), BF16),
            pltpu.VMEM((4, self.part_rows, self.part_columns), F32),
            pltpu.VMEM((4, self.part_rows, self.part_columns), F32),
            dma((1,)),
            dma((2, 2, line)),
            dma((2, 3)),
        ]


PLANE_SCRATCH = 8
LINE_SCRATCH = 7


def reduce_order(line):
    return [line - 1, 0] + list(range(line - 2, 0, -1))


def added(left, right):
    return (left.astype(F32) + right.astype(F32)).astype(BF16)


def plane_steps(place, shape, refs, total, scratch):
    own, other, first_in, second_in, load_sem, pair_sem, first_sem, second_sem = scratch
    near = (place.x, place.y)
    far = (place.y, place.x)
    near_device = (place.at_x(), place.at_y())
    far_device = (place.at_y(), place.at_x())

    def quarter_of(half, index):
        high, low = index // 2, index % 2
        return low * 2 + high if half == 0 else high * 2 + low

    def start(z):
        for half in range(2):
            for index in range(4):
                quarter = quarter_of(half, index)
                slot = half * 4 + index
                mine = shape.pieces(refs, 2 * z + place.core, half, quarter)
                theirs = shape.pieces(refs, 2 * z + 1 - place.core, half, quarter)
                for (view, column, width), (view_two, _, _) in zip(mine, theirs):
                    cut = pl.ds(column, width)
                    remote(
                        view_two,
                        other.at[z, slot, :, cut],
                        pair_sem.at[0, z],
                        pair_sem.at[1, z],
                        place.at_partner(),
                    ).start()
                    pltpu.make_async_copy(
                        view, own.at[z, slot, :, cut], load_sem.at[z]
                    ).start()

    def pair_all(z):
        return remote(
            own.at[z], other.at[z], pair_sem.at[0, z], pair_sem.at[1, z], place.at_partner()
        )

    def first(z, half):
        return remote(
            own.at[z, pl.ds(half * 4 + (1 - near[half]) * 2, 2)],
            first_in.at[z, half],
            first_sem.at[0, z, half],
            first_sem.at[1, z, half],
            near_device[half],
        )

    def second(z, half):
        return remote(
            own.at[z, half * 4 + near[half] * 2 + 1 - far[half]],
            second_in.at[z, half],
            second_sem.at[0, z, half],
            second_sem.at[1, z, half],
            far_device[half],
        )

    def pair_add(z):
        pltpu.make_async_copy(own.at[z], own.at[z], load_sem.at[z]).wait()
        pair_all(z).wait_recv()

        @pl.loop(0, 8)
        def _(slot):
            own[z, slot] = added(own[z, slot], other[z, slot])

        for half in range(2):
            first(z, half).start()

    def first_add(z):
        for half in range(2):
            first(z, half).wait_recv()
            base = half * 4 + near[half] * 2

            @pl.loop(0, 2)
            def _(index):
                own[z, base + index] = added(own[z, base + index], first_in[z, half, index])

            second(z, half).start()

    def second_add(z):
        for half in range(2):
            second(z, half).wait_recv()
            mine = half * 4 + near[half] * 2 + far[half]
            total[z, half] = added(own[z, mine], second_in[z, half])

    def drain(z):
        pair_all(z).wait_send()
        for half in range(2):
            first(z, half).wait_send()
            second(z, half).wait_send()

    return start, pair_add, first_add, second_add, drain


def line_steps(place, shape, source, out, scratch):
    total, line_in, parts, gathered, load_sem, line_sem, swap_sem = scratch
    line = place.line

    def load():
        return pltpu.make_async_copy(source, total, load_sem.at[0])

    def along(z, side):
        return remote(
            total.at[z],
            line_in.at[side, z],
            line_sem.at[0, side, z],
            line_sem.at[1, side, z],
            place.at_line(side),
        )

    def line_send(z, side):
        ahead = place.z < z if side == 0 else place.z > z

        @pl.when(ahead)
        def _():
            @pl.when(place.has_last(side))
            def _():
                along(z, side).wait_recv()

                @pl.loop(0, 2)
                def _(half):
                    total[z, half] = added(total[z, half], line_in[side, z, half])

            along(z, side).start()

    def line_end(z):
        @pl.when(place.z == z)
        def _():
            for side in range(2):
                pl.when(place.has_last(side))(lambda: along(z, side).wait_recv())

    def swap(rep_slot, device, index):
        return remote(
            parts.at[rep_slot],
            gathered.at[place.rep],
            swap_sem.at[0, index],
            swap_sem.at[1, index],
            device,
        )

    def swaps():
        corner = 3 - place.rep
        return [
            swap(place.x_rep, place.at_x(), 0),
            swap(place.y_rep, place.at_y(), 1),
            swap(corner, {"rep": corner, "fsdp": place.fsdp}, 2),
        ]

    def finish():
        rows, columns = shape.block
        me = place.z
        for half in range(2):
            result = total[me, half].astype(F32)
            for side in range(2):
                extra = line_in[side, me, half].astype(F32)
                result = result + jnp.where(place.has_last(side), extra, 0.0)
            at = slice(half * rows, (half + 1) * rows)
            if shape.exchange:
                width = shape.part_columns
                for index in range(4):
                    parts[index, at, :] = result[:, index * width : (index + 1) * width]
            else:
                out[at, :] = result
        if shape.exchange:
            for copy in swaps():
                copy.start()
            gathered[place.rep] = parts[place.rep]

    def send(z):
        line_send(z, 0)
        line_send(z, 1)

    def close():
        for z in range(line):
            line_end(z)
        finish()

    def drain():
        if shape.exchange:
            for copy in swaps():
                copy.wait()
            out[...] = gathered[...]
        for z in range(line):
            for side in range(2):
                ahead = place.z < z if side == 0 else place.z > z
                pl.when(ahead)(lambda: along(z, side).wait_send())

    return load, send, close, drain


class VectorSum:
    def __init__(self, place, source, out, scratch):
        self.place = place
        self.source = source
        self.out = out
        self.current, self.incoming, self.sems = scratch
        side = place.z % 2
        near = place.fsdp + 2 - 4 * side
        self.devices = [
            place.at_partner(),
            place.at_x(),
            place.at_y(),
            {"rep": place.rep, "fsdp": near},
            place.at_far(),
        ]

    @staticmethod
    def scratch(shape):
        return [
            pltpu.VMEM((6,) + shape, F32),
            pltpu.VMEM((5,) + shape, F32),
            pltpu.SemaphoreType.DMA((2, 5)),
        ]

    def copy(self, index):
        return remote(
            self.current.at[index],
            self.incoming.at[index],
            self.sems.at[0, index],
            self.sems.at[1, index],
            self.devices[index],
        )

    def round(self, index):
        if index == 0:
            self.current[0] = self.source[...]
        else:
            self.copy(index - 1).wait_recv()
            self.current[index] = self.current[index - 1] + self.incoming[index - 1]
        if index < 5:
            self.copy(index).start()

    def finish(self):
        self.out[...] = self.current[5]
        for index in range(5):
            self.copy(index).wait_send()


def carried_kernel(shape, line, steps, inner, inputs, outputs, *refs):
    split = inputs + shape.sources
    local, sources = refs[:inputs], refs[inputs:split]
    outs = refs[split : split + outputs]
    total = refs[split + outputs]
    own = len(refs) - PLANE_SCRATCH
    place = Place(line)
    order = reduce_order(line)
    start, pair_add, first_add, second_add, drain = plane_steps(
        place, shape, sources, total, refs[own:]
    )
    step = pl.program_id(0) * pl.num_programs(1) + pl.program_id(1)

    @pl.when(step == 0)
    def _():
        place.greet()
        for z in order:
            start(z)

    @pl.when(step == 1)
    def _():
        for z in order:
            pair_add(z)

    for index, z in enumerate(order):
        pl.when(step == min(3 + 2 * index - index // 2, steps - 1))(
            functools.partial(first_add, z)
        )
    inner(*local, *outs, *refs[split + outputs + 1 : own])

    @pl.when(step == steps - 1)
    def _():
        for z in order:
            second_add(z)
        for z in order:
            drain(z)


def reduce_kernel(ready_shapes, shape, line, *refs):
    count = shape.sources
    many = len(ready_shapes)
    ready, sources = refs[:many], refs[many : many + count]
    vector_ref = refs[many + count]
    at = many + count + 1
    ready_outs, out, vector_out = refs[at : at + many], refs[at + many], refs[at + many + 1]
    scratch = refs[at + many + 2 :]
    place = Place(line)
    place.greet(wide=True)
    order = reduce_order(line)
    plans = []
    for index, ready_shape in enumerate(ready_shapes):
        own, scratch = scratch[:LINE_SCRATCH], scratch[LINE_SCRATCH:]
        plans.append(line_steps(place, ready_shape, ready[index], ready_outs[index], own))
    line_scratch, scratch = scratch[:LINE_SCRATCH], scratch[LINE_SCRATCH:]
    plane_scratch, scratch = scratch[:PLANE_SCRATCH], scratch[PLANE_SCRATCH:]
    start, pair_add, first_add, second_add, drain = plane_steps(
        place, shape, sources, line_scratch[0], plane_scratch
    )
    _, send, close, line_drain = line_steps(place, shape, None, out, line_scratch)
    vector = VectorSum(place, vector_ref, vector_out, scratch)
    for z in order:
        start(z)
    for load, *_ in plans:
        load().start()
    vector.round(0)
    for index, z in enumerate(order):
        pair_add(z)
    for load, *_ in plans:
        load().wait()
    vector.round(1)
    for index, z in enumerate(order):
        for _, ready_send, _, _ in plans:
            ready_send(z)
        first_add(z)
        if index == 1:
            vector.round(2)
    for _, _, ready_close, _ in plans:
        ready_close()
    vector.round(3)
    for index, z in enumerate(order):
        second_add(z)
        if index > 0:
            send(order[index - 1])
    send(order[-1])
    vector.round(4)
    close()
    vector.round(5)
    for _, _, _, ready_drain in plans:
        ready_drain()
    line_drain()
    for z in order:
        drain(z)
    vector.finish()


def group_shape(group, kind, line):
    rows, columns = group[0].shape
    return ReduceShape(kind, rows // (2 * line), columns, len(group))


def fast_reduce(ready, ready_shapes, group, line, collective_id, vector):
    shape = group_shape(group, "four", line)
    anywhere = pl.BlockSpec(memory_space=pl.ANY)
    local = pl.BlockSpec(memory_space=pltpu.VMEM)
    shapes = ready_shapes + [shape]
    scratch = []
    for item in shapes:
        scratch.extend(item.line_scratch(line))
    return pl.pallas_call(
        functools.partial(reduce_kernel, ready_shapes, shape, line),
        in_specs=[anywhere] * (len(ready) + len(group)) + [local],
        out_specs=[local] * (len(shapes) + 1),
        out_shape=[item.out_shape() for item in shapes]
        + [jax.ShapeDtypeStruct(vector.shape, F32)],
        scratch_shapes=scratch
        + shape.plane_scratch(line)
        + VectorSum.scratch(vector.shape),
        compiler_params=pltpu.CompilerParams(
            collective_id=collective_id, has_side_effects=True, vmem_limit_bytes=60 << 20
        ),
        name="fast_reduce",
    )(*ready, *group, vector)


PLANE = 4
CHIP = 2
LINE = 4


def small_plane():
    return lax.axis_size("rep") == PLANE and lax.axis_size("fsdp") == CHIP * LINE


def gather(block):
    return lax.all_gather(block, "fsdp", axis=0, tiled=True)


def gather_all(groups, by_rows, collective_id):
    if small_plane():
        return fast_gather(groups, LINE, by_rows, collective_id)
    return [gather(jnp.concatenate(group, axis=1)) for group in groups]


def scatter(block):
    return lax.psum_scatter(block.astype(BF16), "fsdp", scatter_dimension=0, tiled=True)


def column_blocks(block):
    rows = block.shape[0]
    return block.reshape(rows, lax.axis_size("rep"), -1).swapaxes(0, 1)


def scatter_columns(parts):
    count = lax.axis_size("rep")
    rows = parts[0].shape[0]
    split = [part.reshape(rows, count, -1) for part in parts]
    joined = jnp.concatenate(split, axis=2).reshape(rows, -1)
    own = lax.psum_scatter(joined, "rep", scatter_dimension=1, tiled=True)
    sizes = [part.shape[1] // count for part in parts]
    outs = []
    start = 0
    for size in sizes:
        outs.append(own[:, start : start + size].astype(F32))
        start += size
    return outs


def scatter_last(down, cross, group, vector, collective_id):
    down_term, down_sums = down
    cross_group, cross_sums = cross
    if small_plane():
        shapes = [
            group_shape(cross_group, "four", LINE),
            group_shape([down_term], "rows", LINE),
        ]
        cross_out, down_out, group_out, total = fast_reduce(
            [cross_sums[0], down_sums[0]], shapes, group, LINE, collective_id, vector
        )
        outs = [[out[index] for index in range(4)] for out in (cross_out, group_out)]
        return down_out.reshape(-1, down_out.shape[2]), outs, total
    (down_out,) = scatter_columns([scatter(down_term)])
    outs = [scatter_columns([scatter(item) for item in part]) for part in (cross_group, group)]
    return down_out, outs, lax.psum(vector, ("rep", "fsdp"))


def body(
    tokens,
    memory,
    prefix_len,
    bucket_table,
    rel_bias,
    gain_self,
    self_query,
    self_key,
    self_value,
    self_out,
    gain_cross,
    cross_query,
    cross_key,
    cross_value,
    cross_out,
    gain_feed,
    gate_weight,
    up_weight,
    down_weight,
    out_grad,
):
    nseq, length, width = tokens.shape
    shard = gain_self.shape[0]
    groups = width // shard
    entries = rel_bias.shape[0]
    small = jnp.stack(
        [gain_self, gain_cross, gain_feed, jnp.pad(rel_bias, (0, shard - entries))], axis=1
    )
    small = jnp.pad(small, ((0, 0), (0, 2 * LANES - 4)))
    first, second, down = gather_all(
        [
            [self_query, self_key, self_value, small],
            [self_out, cross_query, cross_key, cross_value, cross_out, small],
            [down_weight],
        ],
        [False, False, True],
        1,
    )
    gate_up_own = jnp.concatenate([gate_weight, up_weight], axis=1)
    gate_up_own, first, second, down = lax.optimization_barrier(
        (gate_up_own, first, second, down)
    )
    gate_up = gather(gate_up_own)
    qkv_proj = first[:, : 3 * width]
    picks = jnp.eye(8, LANES, dtype=BF16)
    vectors = back_term(picks, first[:, 3 * width : 3 * width + LANES])
    gain_first = vectors[0:1]
    gain_second = vectors[1:2]
    gain_third = vectors[2:3]
    table = vectors[3].astype(BF16).reshape(groups, shard)[:, :entries]
    table = table.reshape(NHEAD, BUCKETS)
    out_self = second[:, :width]
    query_cross = second[:, width : 2 * width]
    kv_cross = second[:, 2 * width : 4 * width]

    buckets_back = jnp.pad(bucket_table[::-1], (0, 1)).reshape(1, 2 * length)
    bias = skewed_bias(table, buckets_back, length)

    rows = nseq * length
    start_rows = tokens.reshape(rows, width).astype(F32)
    memory_rows = memory.reshape(-1, width)
    upstream = out_grad.reshape(rows, width)

    scale_first = inverse_rms(start_rows)
    normed_first = (start_rows * scale_first * gain_first).astype(BF16)
    qkv = matmul(normed_first, qkv_proj).astype(BF16)
    context, lse_self = run_self_forward(prefix_len, qkv, bias, nseq)
    middle = start_rows + matmul(context, out_self)
    scale_second = inverse_rms(middle)
    normed_second = (middle * scale_second * gain_second).astype(BF16)
    query_two = matmul(normed_second, query_cross).astype(BF16)
    kv_two = matmul(memory_rows, kv_cross).astype(BF16)
    context_two, lse_cross = run_cross_forward(query_two, kv_two, nseq)
    (
        result,
        later_grad,
        branch_two,
        context_two_grad,
        gain_third_grad,
        down_term,
        pair_term,
    ) = run_feed(middle, context_two, second, 4, gain_third, upstream, gate_up, down)
    carries = small_plane()
    pair_own = scatter(pair_term)
    query_two_grad, key_two_grad, value_two_grad, *down_sums = run_cross_backward(
        query_two,
        kv_two,
        context_two_grad,
        context_two,
        lse_cross,
        nseq,
        ([down_term], "rows", 4) if carries else None,
    )
    (
        middle_grad,
        gain_second_grad,
        query_term,
        out_term,
        branch_one,
        context_grad,
    ) = run_close(
        middle,
        later_grad,
        gain_second,
        context_two,
        branch_two,
        [query_two_grad],
        [(second, 1)],
        (second, 0),
        "cross_close",
    )
    memory_grad, key_term, value_term = run_memory(
        memory_rows, key_two_grad, value_two_grad, second, 2, 3
    )
    cross_terms = [query_term, key_term, value_term, out_term]
    query_grad, key_grad, value_grad, diagonal, *cross_sums = run_self_backward(
        prefix_len,
        qkv,
        context_grad,
        context,
        lse_self,
        bias,
        nseq,
        (cross_terms, "four", 2) if carries else None,
    )
    pair_split, query_grad = lax.optimization_barrier((column_blocks(pair_own), query_grad))
    tokens_grad, gain_first_grad, *self_terms = run_close(
        tokens.reshape(rows, width),
        middle_grad,
        gain_first,
        context,
        branch_one,
        [query_grad, key_grad, value_grad],
        [(first, 0), (first, 1), (first, 2)],
        None,
        "self_close",
    )

    onehot = (
        buckets_back.reshape(-1, 1) == jnp.arange(BUCKETS, dtype=jnp.int32)[None, :]
    ).astype(F32)
    onehot = onehot * (jnp.arange(2 * length) < 2 * length - 1)[:, None]
    bias_grad = jnp.dot(
        diagonal.reshape(NHEAD, 2 * length), onehot, precision=lax.Precision.HIGHEST
    )
    bias_rows = jnp.pad(
        bias_grad.reshape(groups, entries), ((0, 0), (0, shard - entries))
    ).reshape(width)
    vector_block = jnp.pad(
        jnp.concatenate(
            [gain_first_grad, gain_second_grad, gain_third_grad, bias_rows[None]], axis=0
        ),
        ((0, 4), (0, 0)),
    )
    pair_grad = lax.psum_scatter(pair_split, "rep").astype(F32)
    pair_grad = pair_grad.reshape(shard, -1, 2, FEED_BLOCK)
    gate_weight_grad = pair_grad[:, :, 0].reshape(shard, -1)
    up_weight_grad = pair_grad[:, :, 1].reshape(shard, -1)
    down_weight_grad, (cross_out_grads, self_out_grads), totals = scatter_last(
        (down_term, down_sums), (cross_terms, cross_sums), self_terms, vector_block, 3
    )
    own = lax.dynamic_slice(
        totals, (0, lax.axis_index("fsdp") * shard), (totals.shape[0], shard)
    )
    return (
        result.reshape(tokens.shape),
        tokens_grad.reshape(tokens.shape),
        memory_grad.reshape(memory.shape),
        own[3, :entries],
        own[0],
        *self_out_grads,
        own[1],
        *cross_out_grads,
        own[2],
        gate_weight_grad,
        up_weight_grad,
        down_weight_grad,
    )


def solution(mesh):
    batch = P(("rep", "fsdp"), None, None)
    matrix = P("fsdp", None)
    vector = P("fsdp")
    split = P("fsdp", "rep")
    in_specs = (
        (batch, batch, P(("rep", "fsdp")), P(), vector, vector)
        + (matrix,) * 4
        + (vector,)
        + (matrix,) * 4
        + (vector,)
        + (matrix,) * 3
        + (batch,)
    )
    out_specs = (
        (batch, batch, batch, vector, vector)
        + (split,) * 4
        + (vector,)
        + (split,) * 4
        + (vector,)
        + (split,) * 3
    )
    return jax.shard_map(body, mesh=mesh, in_specs=in_specs, out_specs=out_specs, check_vma=False)
```

```python
import functools

import jax
import jax.numpy as jnp
from jax import lax
from jax.experimental import pallas as pl
from jax.experimental.pallas import tpu as pltpu
from jax.sharding import PartitionSpec as P

NHEAD = 12
DHEAD = 64
BUCKETS = 32
PAIRS = NHEAD // 2
LANES = 2 * DHEAD
PREFIX_MAX = 256

EPSILON = 1e-06
CUBIC_TERM = 0.044715
SQRT_TWO_PI = 0.7978845608028654
NEGATIVE = -1000000000.0

F32 = jnp.float32
BF16 = jnp.bfloat16
LAST_DIMS = (((1,), (1,)), ((), ()))


def matmul(left_side, right_side):
    return jnp.dot(left_side, right_side, preferred_element_type=F32)


def back_term(gradient, weight):
    return lax.dot_general(gradient, weight, LAST_DIMS, preferred_element_type=F32)


def inverse_rms(values):
    return lax.rsqrt(jnp.mean(values * values, axis=-1, keepdims=True) + EPSILON)


def norm_back(values, scale_rows, gain_vec, upstream):
    weighted = upstream * gain_vec
    gain_grad = jnp.sum(upstream * values * scale_rows, axis=0)
    input_grad = scale_rows * weighted - values * scale_rows * scale_rows * scale_rows * jnp.mean(
        values * weighted, axis=-1, keepdims=True
    )
    return (input_grad, gain_grad)


def one_head(rows, head):
    lane = lax.broadcasted_iota(jnp.int32, rows.shape, 1)
    keep = lane < DHEAD if head == 0 else lane >= DHEAD
    return jnp.where(keep, rows, jnp.zeros_like(rows))


def flipped(rows):
    return rows.astype(F32).T.astype(BF16)


def tree(fold, rows, groups):
    step = rows.shape[0] // groups
    total = rows[:step]
    for index in range(1, groups):
        total = fold(total, rows[index * step : (index + 1) * step])
    return total


def column_max(rows, groups):
    return jnp.max(tree(jnp.maximum, rows, groups), axis=0, keepdims=True)


def column_sum(rows, groups):
    return jnp.sum(tree(jnp.add, rows, groups), axis=0, keepdims=True)


def allowed_at(shape, key_start, query_start, prefix):
    key = lax.broadcasted_iota(jnp.int32, shape, 0) + key_start
    query = lax.broadcasted_iota(jnp.int32, shape, 1) + query_start
    return (key <= query) | (key < prefix)


def skew_kernel(table_ref, buckets_ref, out_ref):
    bucket = lax.broadcasted_iota(jnp.int32, (BUCKETS, buckets_ref.shape[1]), 0)
    onehot = (bucket == buckets_ref[...]).astype(BF16)
    by_offset = matmul(table_ref[...], onehot)
    width = out_ref.shape[2]
    total = by_offset.shape[1]
    for head in range(NHEAD):
        rows = jnp.broadcast_to(by_offset[head : head + 1], (LANES, total))
        rolled = pltpu.roll(rows, total - (LANES - 1), 1, stride=1, stride_axis=0)
        out_ref[head] = rolled[:, :width]


def skewed_bias(table, buckets_back, length):
    total = 2 * length
    return pl.pallas_call(
        skew_kernel,
        out_shape=jax.ShapeDtypeStruct((NHEAD, LANES, total - LANES), F32),
        name="skewed_bias",
    )(jnp.pad(table, ((0, 4), (0, 0))), buckets_back)


HEADROOM = 70.0


def self_forward(prefix_ref, query_ref, key_ref, value_ref, bias_ref, out_ref, lse_ref):
    length = query_ref.shape[0]
    block = 256
    prefix = prefix_ref[pl.program_id(0)]
    queries = query_ref[...]
    keys = key_ref[...]
    values = flipped(value_ref[...])

    def run(exact):
        excess = jnp.zeros((1, block), F32)
        for start in range(0, length, block):
            stop = start + block
            count = max(PREFIX_MAX, stop)
            outs = []
            for head in range(2):
                scores = back_term(keys[:count], one_head(queries[start:stop], head))
                parts = []
                for base in range(0, count, LANES):
                    shift = length - LANES - base + start
                    part = scores[base : base + LANES] + bias_ref[head, :, shift : shift + block]
                    if base + LANES - 1 > start:
                        part = jnp.where(
                            allowed_at(part.shape, base, start, prefix), part, NEGATIVE
                        )
                    parts.append(part)
                top = parts[0]
                for part in parts[1:]:
                    top = jnp.maximum(top, part)
                top = column_max(top, 4)
                anchor = top if exact else column_max(parts[0], 4)
                if not exact:
                    excess = jnp.maximum(excess, top - anchor)
                shares = [jnp.exp(part - anchor) for part in parts]
                total = shares[0]
                for share in shares[1:]:
                    total = total + share
                total = column_sum(total, 4)
                share = jnp.concatenate([item.astype(BF16) for item in shares], axis=0)
                context = matmul(values[head * DHEAD : (head + 1) * DHEAD, :count], share)
                outs.append(context * (1.0 / total))
                lse_ref[head : head + 1, start:stop] = anchor + jnp.log(total)
            out_ref[start:stop, :] = jnp.concatenate(outs, axis=0).T.astype(BF16)
        return jnp.max(excess)

    excess = run(False)

    @pl.when(excess > HEADROOM)
    def _():
        run(True)


def cross_forward(query_ref, key_ref, value_ref, out_ref, lse_ref):
    keys = key_ref[...]
    values = flipped(value_ref[...])
    queries = query_ref[...]

    def run(exact):
        excess = jnp.zeros((1, queries.shape[0]), F32)
        ahead = [back_term(keys, one_head(queries, head)) for head in range(2)]
        outs = []
        for head in range(2):
            scores = ahead[head]
            top = column_max(scores, 16)
            anchor = top if exact else column_max(scores[: 2 * LANES], 8)
            if not exact:
                excess = jnp.maximum(excess, top - anchor)
            share = jnp.exp(scores - anchor)
            total = column_sum(share, 16)
            context = matmul(values[head * DHEAD : (head + 1) * DHEAD], share.astype(BF16))
            outs.append(context * (1.0 / total))
            lse_ref[head : head + 1, :] = anchor + jnp.log(total)
        out_ref[...] = jnp.concatenate(outs, axis=0).T.astype(BF16)
        return jnp.max(excess)

    excess = run(False)

    @pl.when(excess > HEADROOM)
    def _():
        run(True)


def cross_backward(
    query_ref, key_ref, value_ref, up_ref, context_ref, lse_ref, dq_ref, dk_ref, dv_ref
):
    length = query_ref.shape[0]
    block = 256
    keys = key_ref[...]
    values = value_ref[...]
    queries = query_ref[...]
    upstream = up_ref[...]
    keys_flipped = flipped(keys)
    inner = (upstream.astype(F32) * context_ref[...].astype(F32)).T
    key_grad = None
    value_grad = None
    for start in range(0, length, block):
        rows = slice(start, start + block)
        grads = []
        for head in range(2):
            sub = slice(head * DHEAD, (head + 1) * DHEAD)
            query = one_head(queries[rows], head)
            above = one_head(upstream[rows], head)
            row_inner = jnp.sum(inner[sub, rows], axis=0, keepdims=True)
            shares = jnp.exp(back_term(keys, query) - lse_ref[head : head + 1, rows])
            share_grad = back_term(values, above)
            score_grad = (shares * (share_grad - row_inner)).astype(BF16)
            value_part = matmul(shares.astype(BF16), above)
            key_part = matmul(score_grad, query)
            value_grad = value_part if value_grad is None else value_grad + value_part
            key_grad = key_part if key_grad is None else key_grad + key_part
            grads.append(matmul(keys_flipped[sub], score_grad))
        dq_ref[rows, :] = jnp.concatenate(grads, axis=0).T.astype(BF16)
    dk_ref[...] = key_grad.astype(BF16)
    dv_ref[...] = value_grad.astype(BF16)


def self_backward(
    prefix_ref,
    query_ref,
    key_ref,
    value_ref,
    up_ref,
    context_ref,
    lse_ref,
    bias_ref,
    dq_ref,
    dk_ref,
    dv_ref,
    diag_ref,
    acc_ref,
):
    length = query_ref.shape[0]
    block = 256
    step = pl.program_id(1)
    prefix = prefix_ref[step]

    @pl.when(step == 0)
    def _():
        acc_ref[...] = jnp.zeros_like(acc_ref)

    queries = query_ref[...]
    keys = key_ref[...]
    values = value_ref[...]
    upstream = up_ref[...]
    keys_flipped = flipped(keys)
    inner = (upstream.astype(F32) * context_ref[...].astype(F32)).T
    count_all = length // block
    key_grad = [None] * count_all
    value_grad = [None] * count_all
    for start in range(0, length, block):
        stop = start + block
        count = max(PREFIX_MAX, stop)
        rows = slice(start, stop)
        grads = []
        for head in range(2):
            sub = slice(head * DHEAD, (head + 1) * DHEAD)
            query = one_head(queries[rows], head)
            above = one_head(upstream[rows], head)
            row_inner = jnp.sum(inner[sub, rows], axis=0, keepdims=True)
            row_lse = lse_ref[head : head + 1, rows]
            scores = back_term(keys[:count], query)
            share_grad = back_term(values[:count], above)
            shares = []
            score_grads = []
            for base in range(0, count, LANES):
                part = slice(base, base + LANES)
                shift = length - LANES - base + start
                share = jnp.exp(
                    scores[part] + bias_ref[head, :, shift : shift + block] - row_lse
                )
                if base + LANES - 1 > start:
                    share = jnp.where(allowed_at(share.shape, base, start, prefix), share, 0.0)
                score_grad = share * (share_grad[part] - row_inner)
                acc_ref[head, :, shift : shift + block] += score_grad
                shares.append(share.astype(BF16))
                score_grads.append(score_grad.astype(BF16))
            share = jnp.concatenate(shares, axis=0)
            score_grad = jnp.concatenate(score_grads, axis=0)
            value_part = matmul(share, above)
            key_part = matmul(score_grad, query)
            for index in range(count // block):
                part = slice(index * block, (index + 1) * block)
                if value_grad[index] is None:
                    value_grad[index] = value_part[part]
                    key_grad[index] = key_part[part]
                else:
                    value_grad[index] = value_grad[index] + value_part[part]
                    key_grad[index] = key_grad[index] + key_part[part]
            grads.append(matmul(keys_flipped[sub, :count], score_grad))
        dq_ref[rows, :] = jnp.concatenate(grads, axis=0).T.astype(BF16)
    for index in range(count_all):
        part = slice(index * block, (index + 1) * block)
        dk_ref[part, :] = key_grad[index].astype(BF16)
        dv_ref[part, :] = value_grad[index].astype(BF16)

    @pl.when(step == pl.num_programs(1) - 1)
    def _():
        total = 2 * length
        for head in range(2):
            rows = jnp.concatenate([acc_ref[head], jnp.zeros((LANES, LANES), F32)], axis=1)
            half = LANES // 2
            while half >= 1:
                rows = rows[:half] + pltpu.roll(rows[half:], total - half, 1)
                half //= 2
            diag_ref[head : head + 1, :] = pltpu.roll(rows, LANES - 1, 1)


def spec(shape, index):
    return pl.BlockSpec(shape, index)


def run_self_forward(prefix, qkv, bias, nseq):
    length = qkv.shape[0] // nseq
    return pl.pallas_call(
        self_forward,
        grid_spec=pltpu.PrefetchScalarGridSpec(
            num_scalar_prefetch=1,
            grid=(nseq, PAIRS),
            in_specs=[
                spec((length, LANES), lambda s, p, _: (s, p)),
                spec((length, LANES), lambda s, p, _: (s, PAIRS + p)),
                spec((length, LANES), lambda s, p, _: (s, 2 * PAIRS + p)),
                spec((2, LANES, 2 * length - LANES), lambda s, p, _: (p, 0, 0)),
            ],
            out_specs=[
                spec((length, LANES), lambda s, p, _: (s, p)),
                spec((None, None, 2, length), lambda s, p, _: (s, p, 0, 0)),
            ],
        ),
        out_shape=[
            jax.ShapeDtypeStruct((qkv.shape[0], PAIRS * LANES), BF16),
            jax.ShapeDtypeStruct((nseq, PAIRS, 2, length), F32),
        ],
        cost_estimate=pl.CostEstimate(
            flops=20_000_000_000, bytes_accessed=12_000_000, transcendentals=0
        ),
        name="self_forward",
    )(prefix, qkv, qkv, qkv, bias)


def run_cross_forward(query, kv, nseq):
    length = query.shape[0] // nseq
    count = kv.shape[0] // nseq
    return pl.pallas_call(
        cross_forward,
        grid=(nseq, PAIRS),
        in_specs=[
            spec((length, LANES), lambda s, p: (s, p)),
            spec((count, LANES), lambda s, p: (s, p)),
            spec((count, LANES), lambda s, p: (s, PAIRS + p)),
        ],
        out_specs=[
            spec((length, LANES), lambda s, p: (s, p)),
            spec((None, None, 2, length), lambda s, p: (s, p, 0, 0)),
        ],
        out_shape=[
            jax.ShapeDtypeStruct(query.shape, BF16),
            jax.ShapeDtypeStruct((nseq, PAIRS, 2, length), F32),
        ],
        cost_estimate=pl.CostEstimate(
            flops=24_000_000_000, bytes_accessed=10_000_000, transcendentals=0
        ),
        name="cross_forward",
    )(query, kv, kv)


def carry(carried, steps, inner, inputs, outputs):
    if carried is None:
        return inner, [], [], [], [], None
    group, kind, collective_id = carried
    shape = group_shape(group, kind, LINE)
    kernel = functools.partial(
        carried_kernel, shape, LINE, steps, inner, inputs, outputs
    )
    total = shape.total_shape(LINE)
    params = pltpu.CompilerParams(
        collective_id=collective_id, has_side_effects=True, vmem_limit_bytes=60 << 20
    )
    return (
        kernel,
        group,
        [pl.BlockSpec(total, lambda *_: (0, 0, 0, 0))],
        [jax.ShapeDtypeStruct(total, BF16)],
        shape.plane_scratch(LINE),
        params,
    )


def run_cross_backward(query, kv, upstream, context, lse, nseq, carried=None):
    length = query.shape[0] // nseq
    count = kv.shape[0] // nseq
    rows = spec((length, LANES), lambda s, p: (s, p))
    wide = spec((count, LANES), lambda s, p: (s, p))
    kernel, group, total_specs, totals, scratch, params = carry(
        carried, PAIRS * nseq, cross_backward, 6, 3
    )
    return pl.pallas_call(
        kernel,
        grid=(nseq, PAIRS),
        in_specs=[
            rows,
            wide,
            spec((count, LANES), lambda s, p: (s, PAIRS + p)),
            rows,
            rows,
            spec((None, None, 2, length), lambda s, p: (s, p, 0, 0)),
        ]
        + [pl.BlockSpec(memory_space=pl.ANY)] * len(group),
        out_specs=[rows, wide, wide] + total_specs,
        out_shape=[
            jax.ShapeDtypeStruct(query.shape, BF16),
            jax.ShapeDtypeStruct((kv.shape[0], PAIRS * LANES), BF16),
            jax.ShapeDtypeStruct((kv.shape[0], PAIRS * LANES), BF16),
        ]
        + totals,
        scratch_shapes=scratch,
        cost_estimate=pl.CostEstimate(
            flops=36_000_000_000, bytes_accessed=20_000_000, transcendentals=0
        ),
        compiler_params=params,
        name="cross_backward",
    )(query, kv, kv, upstream, context, lse, *group)


def run_self_backward(prefix, qkv, upstream, context, lse, bias, nseq, carried=None):
    length = qkv.shape[0] // nseq
    rows = spec((length, LANES), lambda p, s, _: (s, p))
    kernel, group, total_specs, totals, scratch, params = carry(
        carried, PAIRS * nseq, self_backward, 8, 4
    )
    return pl.pallas_call(
        kernel,
        grid_spec=pltpu.PrefetchScalarGridSpec(
            num_scalar_prefetch=1,
            grid=(PAIRS, nseq),
            in_specs=[
                rows,
                spec((length, LANES), lambda p, s, _: (s, PAIRS + p)),
                spec((length, LANES), lambda p, s, _: (s, 2 * PAIRS + p)),
                rows,
                rows,
                spec((None, None, 2, length), lambda p, s, _: (s, p, 0, 0)),
                spec((2, LANES, 2 * length - LANES), lambda p, s, _: (p, 0, 0)),
            ]
            + [pl.BlockSpec(memory_space=pl.ANY)] * len(group),
            out_specs=[
                rows,
                rows,
                rows,
                spec((None, 2, 2 * length), lambda p, s, _: (p, 0, 0)),
            ]
            + total_specs,
            scratch_shapes=[pltpu.VMEM((2, LANES, 2 * length - LANES), F32)] + scratch,
        ),
        out_shape=[jax.ShapeDtypeStruct(upstream.shape, BF16)] * 3
        + [jax.ShapeDtypeStruct((PAIRS, 2, 2 * length), F32)]
        + totals,
        cost_estimate=pl.CostEstimate(
            flops=24_000_000_000, bytes_accessed=20_000_000, transcendentals=0
        ),
        compiler_params=params,
        name="self_backward",
    )(prefix, qkv, qkv, qkv, upstream, context, lse, bias, *group)


FEED_BLOCK = 512


def feed_kernel(
    middle_ref,
    context_ref,
    out_proj_ref,
    gain_ref,
    up_grad_ref,
    gate_ref,
    up_ref,
    down_ref,
    result_ref,
    later_grad_ref,
    branch_ref,
    context_grad_ref,
    gain_grad_ref,
    down_term_ref,
    pair_term_ref,
    later_ref,
    normed_ref,
    flipped_ref,
    result_acc,
    third_acc,
):
    step = pl.program_id(0)
    count = middle_ref.shape[0]
    chunk = 256
    chunks = [slice(start, start + chunk) for start in range(0, count, chunk)]

    @pl.when(step == 0)
    def _():
        for rows in chunks:
            later = middle_ref[rows] + matmul(context_ref[rows], out_proj_ref[...])
            normed = (later * inverse_rms(later) * gain_ref[...]).astype(BF16)
            later_ref[rows] = later
            normed_ref[rows] = normed
            flipped_ref[:, rows] = flipped(normed)
            result_acc[rows] = jnp.zeros_like(later)
            third_acc[rows] = jnp.zeros_like(later)

    gate_proj = gate_ref[...]
    up_proj = up_ref[...]
    down_proj = down_ref[...]
    hidden_flipped = []
    gate_grads = []
    lift_grads = []
    for rows in chunks:
        normed = normed_ref[rows]
        gate = matmul(normed, gate_proj)
        lift = matmul(normed, up_proj)
        hidden_grad = back_term(up_grad_ref[rows], down_proj)
        square = gate * gate
        tangent = jnp.tanh(SQRT_TWO_PI * gate * (1.0 + CUBIC_TERM * square))
        half = 0.5 * (1.0 + tangent)
        active = gate * half
        slope = half + 0.5 * gate * (1.0 - tangent * tangent) * (
            SQRT_TWO_PI + 3.0 * CUBIC_TERM * SQRT_TWO_PI * square
        )
        hidden = active * lift
        gate_grad = (hidden_grad * lift * slope).astype(BF16)
        lift_grad = (hidden_grad * active).astype(BF16)
        hidden_flipped.append(hidden.T.astype(BF16))
        gate_grads.append(gate_grad)
        lift_grads.append(lift_grad)
        result_acc[rows] += matmul(hidden.astype(BF16), down_proj)
        third_acc[rows] += back_term(gate_grad, gate_proj) + back_term(lift_grad, up_proj)
    hidden_flipped = jnp.concatenate(hidden_flipped, axis=1)
    down_term_ref[...] = matmul(hidden_flipped, up_grad_ref[...]).astype(BF16)
    gate_grads = jnp.concatenate(gate_grads, axis=0)
    lift_grads = jnp.concatenate(lift_grads, axis=0)
    pair_term_ref[:, :FEED_BLOCK] = matmul(flipped_ref[...], gate_grads).astype(BF16)
    pair_term_ref[:, FEED_BLOCK:] = matmul(flipped_ref[...], lift_grads).astype(BF16)

    @pl.when(step == pl.num_programs(0) - 1)
    def _():
        gain_grad = jnp.zeros(gain_ref.shape, F32)
        for rows in chunks:
            later = later_ref[rows]
            result_ref[rows] = (later + result_acc[rows]).astype(BF16)
            carry, part = norm_back(later, inverse_rms(later), gain_ref[...], third_acc[rows])
            gain_grad = gain_grad + part[None, :]
            later_grad = up_grad_ref[rows].astype(F32) + carry
            branch = later_grad.astype(BF16)
            later_grad_ref[rows] = later_grad
            branch_ref[rows] = branch
            context_grad_ref[rows] = back_term(branch, out_proj_ref[...]).astype(BF16)
        gain_grad_ref[...] = gain_grad


def run_feed(middle, context, out_proj, out_block, gain, upstream, gate_up, down):
    count, width = middle.shape
    ffn = down.shape[0]
    blocks = ffn // FEED_BLOCK

    def whole(shape, **extra):
        return pl.BlockSpec(shape, lambda j: (0, 0), **extra)

    once = {"pipeline_mode": pl.Buffered(1)}
    rows = (count, width)
    return pl.pallas_call(
        feed_kernel,
        grid=(blocks,),
        in_specs=[
            whole(rows, **once),
            whole(rows, **once),
            pl.BlockSpec((width, width), lambda j: (0, out_block), **once),
            whole((1, width)),
            whole(rows, **once),
            spec((width, FEED_BLOCK), lambda j: (0, j)),
            spec((width, FEED_BLOCK), lambda j: (0, blocks + j)),
            spec((FEED_BLOCK, width), lambda j: (j, 0)),
        ],
        out_specs=[
            whole(rows),
            whole(rows),
            whole(rows),
            whole(rows),
            whole((1, width)),
            spec((FEED_BLOCK, width), lambda j: (j, 0)),
            spec((width, 2 * FEED_BLOCK), lambda j: (0, j)),
        ],
        out_shape=[
            jax.ShapeDtypeStruct(rows, BF16),
            jax.ShapeDtypeStruct(rows, F32),
            jax.ShapeDtypeStruct(rows, BF16),
            jax.ShapeDtypeStruct(rows, BF16),
            jax.ShapeDtypeStruct((1, width), F32),
            jax.ShapeDtypeStruct((ffn, width), BF16),
            jax.ShapeDtypeStruct((width, 2 * ffn), BF16),
        ],
        scratch_shapes=[
            pltpu.VMEM(rows, F32),
            pltpu.VMEM(rows, BF16),
            pltpu.VMEM((width, count), BF16),
            pltpu.VMEM(rows, F32),
            pltpu.VMEM(rows, F32),
        ],
        cost_estimate=pl.CostEstimate(
            flops=32_000_000_000, bytes_accessed=40_000_000, transcendentals=0
        ),
        compiler_params=pltpu.CompilerParams(vmem_limit_bytes=60 << 20),
        name="feed",
    )(middle, context, out_proj, gain, upstream, gate_up, gate_up, down)


def close_kernel(count, project, *refs):
    values_ref, carry_ref, gain_ref, left_ref, right_ref = refs[:5]
    grad_refs = refs[5 : 5 + count]
    weight_refs = refs[5 + count : 5 + 2 * count]
    at = 5 + 2 * count
    if project:
        proj_ref = refs[at]
        at += 1
    out_ref, gain_grad_ref = refs[at : at + 2]
    term_refs = refs[at + 2 : at + 3 + count]
    at += 3 + count
    if project:
        branch_ref, projected_ref = refs[at : at + 2]
        at += 2
    sums = refs[at : at + 1 + count]
    gain_sum = refs[at + 1 + count]
    step = pl.program_id(0)

    @pl.when(step == 0)
    def _():
        gain_sum[...] = jnp.zeros_like(gain_sum)
        for total in sums:
            total[...] = jnp.zeros_like(total)

    values = values_ref[...].astype(F32)
    gain = gain_ref[...]
    scale = inverse_rms(values)
    normed = (values * scale * gain).T.astype(BF16)
    upstream = None
    for index in range(count):
        grad = grad_refs[index][...]
        sums[index][...] += matmul(normed, grad)
        part = back_term(grad, weight_refs[index][...])
        upstream = part if upstream is None else upstream + part
    sums[count][...] += matmul(flipped(left_ref[...]), right_ref[...])
    carry, part = norm_back(values, scale, gain, upstream)
    gain_sum[...] += part[None, :]
    result = carry_ref[...] + carry
    out_ref[...] = result
    if project:
        branch = result.astype(BF16)
        branch_ref[...] = branch
        projected_ref[...] = back_term(branch, proj_ref[...]).astype(BF16)

    @pl.when(step == pl.num_programs(0) - 1)
    def _():
        gain_grad_ref[...] = gain_sum[...]
        for term, total in zip(term_refs, sums):
            term[...] = total[...].astype(BF16)


def run_close(values, carry, gain, left, right, grads, weights, project, name):
    rows, width = values.shape
    count = len(grads)
    block = 256
    wide = spec((block, width), lambda i: (i, 0))

    def columns(index):
        return pl.BlockSpec((width, width), lambda i: (0, index), pipeline_mode=pl.Buffered(1))

    whole = [spec((1, width), lambda i: (0, 0))]
    square = [spec((width, width), lambda i: (0, 0))] * (count + 1)
    extra = [] if project is None else [project]
    out_shape = [
        jax.ShapeDtypeStruct((rows, width), F32),
        jax.ShapeDtypeStruct((1, width), F32),
    ] + [jax.ShapeDtypeStruct((width, width), BF16)] * (count + 1)
    out_shape += [jax.ShapeDtypeStruct((rows, width), BF16)] * (2 * len(extra))
    return pl.pallas_call(
        functools.partial(close_kernel, count, project is not None),
        grid=(rows // block,),
        in_specs=[wide, wide]
        + whole
        + [wide] * (2 + count)
        + [columns(index) for _, index in weights + extra],
        out_specs=[wide] + whole + square + [wide] * (2 * len(extra)),
        out_shape=out_shape,
        scratch_shapes=[pltpu.VMEM((width, width), F32)] * (count + 1)
        + [pltpu.VMEM((1, width), F32)],
        cost_estimate=pl.CostEstimate(
            flops=8_000_000_000, bytes_accessed=25_000_000, transcendentals=0
        ),
        compiler_params=pltpu.CompilerParams(vmem_limit_bytes=60 << 20),
        name=name,
    )(values, carry, gain, left, right, *grads, *[item for item, _ in weights + extra])


def memory_kernel(
    memory_ref, key_grad_ref, value_grad_ref, key_ref, value_ref, out_ref, *rest
):
    key_term_ref, value_term_ref, key_sum, value_sum = rest
    step = pl.program_id(0)

    @pl.when(step == 0)
    def _():
        key_sum[...] = jnp.zeros_like(key_sum)
        value_sum[...] = jnp.zeros_like(value_sum)

    rows = flipped(memory_ref[...])
    key_grad = key_grad_ref[...]
    value_grad = value_grad_ref[...]
    out_ref[...] = back_term(key_grad, key_ref[...]) + back_term(value_grad, value_ref[...])
    key_sum[...] += matmul(rows, key_grad)
    value_sum[...] += matmul(rows, value_grad)

    @pl.when(step == pl.num_programs(0) - 1)
    def _():
        key_term_ref[...] = key_sum[...].astype(BF16)
        value_term_ref[...] = value_sum[...].astype(BF16)


def run_memory(memory, key_grad, value_grad, weights, key_block, value_block):
    rows, width = memory.shape
    block = 512
    wide = spec((block, width), lambda i: (i, 0))
    square = spec((width, width), lambda i: (0, 0))

    def columns(index):
        return pl.BlockSpec((width, width), lambda i: (0, index), pipeline_mode=pl.Buffered(1))

    return pl.pallas_call(
        memory_kernel,
        grid=(rows // block,),
        in_specs=[wide, wide, wide, columns(key_block), columns(value_block)],
        out_specs=[wide, square, square],
        out_shape=[
            jax.ShapeDtypeStruct((rows, width), F32),
            jax.ShapeDtypeStruct((width, width), BF16),
            jax.ShapeDtypeStruct((width, width), BF16),
        ],
        scratch_shapes=[pltpu.VMEM((width, width), F32)] * 2,
        cost_estimate=pl.CostEstimate(
            flops=10_000_000_000, bytes_accessed=18_000_000, transcendentals=0
        ),
        compiler_params=pltpu.CompilerParams(vmem_limit_bytes=60 << 20),
        name="memory_close",
    )(memory, key_grad, value_grad, weights, weights)


MESH = pl.DeviceIdType.MESH


class Place:
    def __init__(self, line):
        self.line = line
        rep = lax.axis_index("rep")
        fsdp = lax.axis_index("fsdp")
        self.rep = rep
        self.fsdp = fsdp
        self.y = rep // 2
        self.x = rep % 2
        self.z = fsdp // 2
        self.core = fsdp % 2
        self.x_rep = self.y * 2 + 1 - self.x
        self.y_rep = (1 - self.y) * 2 + self.x

    def at_x(self):
        return {"rep": self.x_rep, "fsdp": self.fsdp}

    def at_y(self):
        return {"rep": self.y_rep, "fsdp": self.fsdp}

    def at_partner(self):
        return {"rep": self.rep, "fsdp": self.z * 2 + 1 - self.core}

    def at_line(self, side):
        return {"rep": self.rep, "fsdp": self.fsdp + (2 if side == 0 else -2)}

    def has_next(self, side):
        return self.z < self.line - 1 if side == 0 else self.z > 0

    def has_last(self, side):
        return self.has_next(1 - side)

    def arrives(self, side, hop):
        if side == 0:
            return self.z - 1 - hop >= 0
        return self.z + 1 + hop <= self.line - 1

    def source(self, side, hop):
        return self.z - 1 - hop if side == 0 else self.z + 1 + hop

    def at_far(self):
        half = self.line // 2
        return {"rep": self.rep, "fsdp": (self.z + half) % self.line * 2 + self.core}

    def greet(self, wide=False):
        barrier = pltpu.get_barrier_semaphore()
        targets = [self.at_x(), self.at_y(), self.at_partner()]
        if wide:
            targets.append({"rep": 3 - self.rep, "fsdp": self.fsdp})
            targets.append(self.at_far())
        for target in targets:
            pl.semaphore_signal(barrier, inc=1, device_id=target, device_id_type=MESH)
        for side in range(2):

            @pl.when(self.has_next(side))
            def _():
                pl.semaphore_signal(
                    barrier, inc=1, device_id=self.at_line(side), device_id_type=MESH
                )

        count = len(targets)
        for side in range(2):
            count = count + jnp.where(self.has_next(side), 1, 0)
        pl.semaphore_wait(barrier, count)


def remote(source, target, send, recv, device):
    return pltpu.make_async_remote_copy(
        src_ref=source,
        dst_ref=target,
        send_sem=send,
        recv_sem=recv,
        device_id=device,
        device_id_type=MESH,
    )


class GatherShape:
    def __init__(self, parts, by_rows):
        self.rows = parts[0].shape[0]
        self.widths = [part.shape[1] for part in parts]
        self.starts = [sum(self.widths[:index]) for index in range(len(parts))]
        self.columns = sum(self.widths)
        self.by_rows = by_rows

    def full(self, ref, owner):
        return ref.at[pl.ds(pl.multiple_of(owner * self.rows, 32), self.rows)]

    def piece(self, ref, owner, part, half=None):
        base = owner * self.rows
        if self.by_rows:
            rows = self.rows // 4
            base = base + part * rows
        else:
            rows = self.rows
        if half is not None:
            rows = rows // 2
            base = base + half * rows
        row_slice = pl.ds(pl.multiple_of(base, 16), rows)
        if self.by_rows:
            return ref.at[row_slice]
        width = self.columns // 4
        return ref.at[row_slice, pl.ds(pl.multiple_of(part * width, LANES), width)]


def gather_sems(line):
    hops = line - 1
    return [pltpu.SemaphoreType.DMA((5, 2, 2, hops)), pltpu.SemaphoreType.DMA((4,))] + [
        pltpu.SemaphoreType.DMA((2, 2, hops))
    ]


def gather_steps(place, shape, src, own, dst, sems):
    hop_sem, own_sem, pair_sem = sems
    hops = place.line - 1
    me = place.fsdp

    def load(index):
        at = pl.ds(shape.starts[index], shape.widths[index])
        return pltpu.make_async_copy(src[index], own.at[:, at], own_sem.at[0])

    def loaded():
        return pltpu.make_async_copy(own, own, own_sem.at[0])

    def keep():
        return pltpu.make_async_copy(own, shape.full(dst, me), own_sem.at[1])

    def own_pair():
        return remote(
            own, shape.full(dst, me), own_sem.at[2], own_sem.at[3], place.at_partner()
        )

    def owner(side, hop):
        return place.source(side, hop) * 2 + place.core

    def line_first(side):
        return remote(
            shape.piece(own, 0, place.rep),
            shape.piece(dst, me, place.rep),
            hop_sem.at[0, 0, side, 0],
            hop_sem.at[0, 1, side, 0],
            place.at_line(side),
        )

    def moved(kind, side, hop, block, device):
        return remote(
            block, block, hop_sem.at[kind, 0, side, hop], hop_sem.at[kind, 1, side, hop], device
        )

    def line_next(side, hop):
        block = shape.piece(dst, owner(side, hop - 1), place.rep)
        return moved(0, side, hop, block, place.at_line(side))

    def line_arrival(side, hop):
        block = shape.piece(dst, owner(side, hop), place.rep)
        return moved(0, side, hop, block, place.at_line(side))

    def plane(axis, side, hop):
        block = shape.piece(dst, owner(side, hop), place.rep)
        return moved(1 + axis, side, hop, block, place.at_x() if axis == 0 else place.at_y())

    def cross(axis, side, hop):
        part = place.x_rep if axis == 1 else place.y_rep
        block = shape.piece(dst, owner(side, hop), part, 1 - axis)
        return moved(3 + axis, side, hop, block, place.at_x() if axis == 0 else place.at_y())

    def pair(side, hop):
        block = shape.full(dst, owner(side, hop))
        return remote(
            block, block, pair_sem.at[0, side, hop], pair_sem.at[1, side, hop], place.at_partner()
        )

    def each(fn):
        def run(hop):
            for side in range(2):
                pl.when(place.arrives(side, hop))(functools.partial(fn, side, hop))

        return run

    def start():
        for index in range(len(src)):
            load(index).start()
        loaded().wait()
        for side in range(2):
            pl.when(place.has_next(side))(lambda side=side: line_first(side).start())
        own_pair().start()
        keep().start()

    def arrive(side, hop):
        line_arrival(side, hop).wait_recv()
        if hop + 1 < hops:
            pl.when(place.has_next(side))(lambda: line_next(side, hop + 1).start())
        plane(0, side, hop).start()
        plane(1, side, hop).start()

    def turn(side, hop):
        plane(0, side, hop).wait_recv()
        cross(1, side, hop).start()
        plane(1, side, hop).wait_recv()
        cross(0, side, hop).start()

    def hand(side, hop):
        cross(0, side, hop).wait_recv()
        cross(1, side, hop).wait_recv()
        pair(side, hop).start()

    def finish():
        def last(side, hop):
            pair(side, hop).wait()
            for axis in range(2):
                plane(axis, side, hop).wait_send()
                cross(axis, side, hop).wait_send()
            if hop + 1 < hops:
                pl.when(place.has_next(side))(lambda: line_next(side, hop + 1).wait_send())

        for hop in range(hops):
            each(last)(hop)
        for side in range(2):
            pl.when(place.has_next(side))(lambda side=side: line_first(side).wait_send())
        own_pair().wait()
        keep().wait()

    return start, each(arrive), each(turn), each(hand), finish


def gather_kernel(shapes, line, *refs):
    count = len(shapes)
    sources = []
    at = 0
    for shape in shapes:
        sources.append(refs[at : at + len(shape.widths)])
        at += len(shape.widths)
    targets = refs[at : at + count]
    scratch = refs[at + count :]
    place = Place(line)
    place.greet()
    plans = []
    for index, shape in enumerate(shapes):
        own, *sems = scratch[4 * index : 4 * index + 4]
        plans.append(gather_steps(place, shape, sources[index], own, targets[index], sems))
    for plan in plans:
        plan[0]()
    for step in range(line + 1):
        for stage in range(3):
            hop = step - stage
            if 0 <= hop < line - 1:
                for plan in plans:
                    plan[1 + stage](hop)
    for plan in plans:
        plan[4]()


def fast_gather(groups, line, by_rows, collective_id):
    shapes = [GatherShape(group, flag) for group, flag in zip(groups, by_rows)]
    scratch = []
    for shape in shapes:
        scratch.append(pltpu.VMEM((shape.rows, shape.columns), BF16))
        scratch.extend(gather_sems(line))
    anywhere = pl.BlockSpec(memory_space=pl.ANY)
    blocks = [block for group in groups for block in group]
    return pl.pallas_call(
        functools.partial(gather_kernel, shapes, line),
        in_specs=[anywhere] * len(blocks),
        out_specs=[anywhere] * len(groups),
        out_shape=[
            jax.ShapeDtypeStruct((2 * line * s.rows, s.columns), BF16) for s in shapes
        ],
        scratch_shapes=scratch,
        compiler_params=pltpu.CompilerParams(collective_id=collective_id, has_side_effects=True),
        name="fast_gather",
    )(*blocks)


class ReduceShape:
    def __init__(self, kind, rows, columns, sources):
        self.kind = kind
        self.rows = rows
        self.sources = sources
        if kind == "rows":
            self.block = (rows // 8, columns)
        elif kind == "pair":
            self.block = (rows // 2, columns // 2)
        else:
            self.block = (rows // 2, columns)
        self.exchange = kind != "pair"
        self.part_rows = rows // 4 if kind == "rows" else rows
        self.part_columns = columns // 4

    def pieces(self, refs, owner, half, quarter):
        rows, columns = self.block
        if self.kind == "rows":
            base = owner * self.rows + quarter * (self.rows // 4) + half * rows
            return [(refs[0].at[pl.ds(pl.multiple_of(base, 16), rows)], 0, columns)]
        at = pl.ds(pl.multiple_of(owner * self.rows + half * rows, 16), rows)
        if self.kind == "four":
            return [(refs[quarter].at[at], 0, columns)]
        width = columns // 2
        cut = slice(quarter * width, (quarter + 1) * width)
        return [(refs[index].at[at, cut], index * width, width) for index in range(2)]

    def out_shape(self):
        if self.exchange:
            return jax.ShapeDtypeStruct((4, self.part_rows, self.part_columns), F32)
        return jax.ShapeDtypeStruct((self.rows, self.block[1]), F32)

    def total_shape(self, line):
        return (line, 2) + self.block

    def plane_scratch(self, line):
        rows, columns = self.block
        dma = pltpu.SemaphoreType.DMA
        return [
            pltpu.VMEM((line, 8, rows, columns), BF16),
            pltpu.VMEM((line, 8, rows, columns), BF16),
            pltpu.VMEM((line, 2, 2, rows, columns), BF16),
            pltpu.VMEM((line, 2, rows, columns), BF16),
            dma((line,)),
            dma((2, line)),
            dma((2, line, 2)),
            dma((2, line, 2)),
        ]

    def line_scratch(self, line):
        dma = pltpu.SemaphoreType.DMA
        return [
            pltpu.VMEM(self.total_shape(line), BF16),
            pltpu.VMEM((2,) + self.total_shape(line), BF16),
            pltpu.VMEM((4, self.part_rows, self.part_columns), F32),
            pltpu.VMEM((4, self.part_rows, self.part_columns), F32),
            dma((1,)),
            dma((2, 2, line)),
            dma((2, 3)),
        ]


PLANE_SCRATCH = 8
LINE_SCRATCH = 7


def reduce_order(line):
    return [line - 1, 0] + list(range(line - 2, 0, -1))


def added(left, right):
    return (left.astype(F32) + right.astype(F32)).astype(BF16)


def plane_steps(place, shape, refs, total, scratch):
    own, other, first_in, second_in, load_sem, pair_sem, first_sem, second_sem = scratch
    near = (place.x, place.y)
    far = (place.y, place.x)
    near_device = (place.at_x(), place.at_y())
    far_device = (place.at_y(), place.at_x())

    def quarter_of(half, index):
        high, low = index // 2, index % 2
        return low * 2 + high if half == 0 else high * 2 + low

    def start(z):
        for half in range(2):
            for index in range(4):
                quarter = quarter_of(half, index)
                slot = half * 4 + index
                mine = shape.pieces(refs, 2 * z + place.core, half, quarter)
                theirs = shape.pieces(refs, 2 * z + 1 - place.core, half, quarter)
                for (view, column, width), (view_two, _, _) in zip(mine, theirs):
                    cut = pl.ds(column, width)
                    remote(
                        view_two,
                        other.at[z, slot, :, cut],
                        pair_sem.at[0, z],
                        pair_sem.at[1, z],
                        place.at_partner(),
                    ).start()
                    pltpu.make_async_copy(
                        view, own.at[z, slot, :, cut], load_sem.at[z]
                    ).start()

    def pair_all(z):
        return remote(
            own.at[z], other.at[z], pair_sem.at[0, z], pair_sem.at[1, z], place.at_partner()
        )

    def first(z, half):
        return remote(
            own.at[z, pl.ds(half * 4 + (1 - near[half]) * 2, 2)],
            first_in.at[z, half],
            first_sem.at[0, z, half],
            first_sem.at[1, z, half],
            near_device[half],
        )

    def second(z, half):
        return remote(
            own.at[z, half * 4 + near[half] * 2 + 1 - far[half]],
            second_in.at[z, half],
            second_sem.at[0, z, half],
            second_sem.at[1, z, half],
            far_device[half],
        )

    def pair_add(z):
        pltpu.make_async_copy(own.at[z], own.at[z], load_sem.at[z]).wait()
        pair_all(z).wait_recv()

        @pl.loop(0, 8)
        def _(slot):
            own[z, slot] = added(own[z, slot], other[z, slot])

        for half in range(2):
            first(z, half).start()

    def first_add(z):
        for half in range(2):
            first(z, half).wait_recv()
            base = half * 4 + near[half] * 2

            @pl.loop(0, 2)
            def _(index):
                own[z, base + index] = added(own[z, base + index], first_in[z, half, index])

            second(z, half).start()

    def second_add(z):
        for half in range(2):
            second(z, half).wait_recv()
            mine = half * 4 + near[half] * 2 + far[half]
            total[z, half] = added(own[z, mine], second_in[z, half])

    def drain(z):
        pair_all(z).wait_send()
        for half in range(2):
            first(z, half).wait_send()
            second(z, half).wait_send()

    return start, pair_add, first_add, second_add, drain


def line_steps(place, shape, source, out, scratch):
    total, line_in, parts, gathered, load_sem, line_sem, swap_sem = scratch
    line = place.line

    def load():
        return pltpu.make_async_copy(source, total, load_sem.at[0])

    def along(z, side):
        return remote(
            total.at[z],
            line_in.at[side, z],
            line_sem.at[0, side, z],
            line_sem.at[1, side, z],
            place.at_line(side),
        )

    def line_send(z, side):
        ahead = place.z < z if side == 0 else place.z > z

        @pl.when(ahead)
        def _():
            @pl.when(place.has_last(side))
            def _():
                along(z, side).wait_recv()

                @pl.loop(0, 2)
                def _(half):
                    total[z, half] = added(total[z, half], line_in[side, z, half])

            along(z, side).start()

    def line_end(z):
        @pl.when(place.z == z)
        def _():
            for side in range(2):
                pl.when(place.has_last(side))(lambda: along(z, side).wait_recv())

    def swap(rep_slot, device, index):
        return remote(
            parts.at[rep_slot],
            gathered.at[place.rep],
            swap_sem.at[0, index],
            swap_sem.at[1, index],
            device,
        )

    def swaps():
        corner = 3 - place.rep
        return [
            swap(place.x_rep, place.at_x(), 0),
            swap(place.y_rep, place.at_y(), 1),
            swap(corner, {"rep": corner, "fsdp": place.fsdp}, 2),
        ]

    def finish():
        rows, columns = shape.block
        me = place.z
        for half in range(2):
            result = total[me, half].astype(F32)
            for side in range(2):
                extra = line_in[side, me, half].astype(F32)
                result = result + jnp.where(place.has_last(side), extra, 0.0)
            at = slice(half * rows, (half + 1) * rows)
            if shape.exchange:
                width = shape.part_columns
                for index in range(4):
                    parts[index, at, :] = result[:, index * width : (index + 1) * width]
            else:
                out[at, :] = result
        if shape.exchange:
            for copy in swaps():
                copy.start()
            gathered[place.rep] = parts[place.rep]

    def head(z):
        if z > 0:
            pl.when(place.z == 0)(functools.partial(line_send, z, 0))
        if z < line - 1:
            pl.when(place.z == line - 1)(functools.partial(line_send, z, 1))

    def relay(hop, far):
        up = [line - 1] if far else range(line - 2, hop, -1)
        down = [0] if far else range(1, line - 1 - hop)
        for z in up:
            pl.when(place.z == hop)(functools.partial(line_send, z, 0))
        for z in down:
            pl.when(place.z == line - 1 - hop)(functools.partial(line_send, z, 1))

    def close():
        for z in range(line):
            line_end(z)
        finish()

    def drain():
        if shape.exchange:
            for copy in swaps():
                copy.wait()
            out[...] = gathered[...]
        for z in range(line):
            for side in range(2):
                ahead = place.z < z if side == 0 else place.z > z
                pl.when(ahead)(lambda: along(z, side).wait_send())

    return load, head, relay, close, drain


class VectorSum:
    def __init__(self, place, source, out, scratch):
        self.place = place
        self.source = source
        self.out = out
        self.current, self.incoming, self.sems = scratch
        side = place.z % 2
        near = place.fsdp + 2 - 4 * side
        self.devices = [
            place.at_partner(),
            place.at_x(),
            place.at_y(),
            {"rep": place.rep, "fsdp": near},
            place.at_far(),
        ]

    @staticmethod
    def scratch(shape):
        return [
            pltpu.VMEM((6,) + shape, F32),
            pltpu.VMEM((5,) + shape, F32),
            pltpu.SemaphoreType.DMA((2, 5)),
        ]

    def copy(self, index):
        return remote(
            self.current.at[index],
            self.incoming.at[index],
            self.sems.at[0, index],
            self.sems.at[1, index],
            self.devices[index],
        )

    def round(self, index):
        if index == 0:
            self.current[0] = self.source[...]
        else:
            self.copy(index - 1).wait_recv()
            self.current[index] = self.current[index - 1] + self.incoming[index - 1]
        if index < 5:
            self.copy(index).start()

    def finish(self):
        self.out[...] = self.current[5]
        for index in range(5):
            self.copy(index).wait_send()


def carried_kernel(shape, line, steps, inner, inputs, outputs, *refs):
    split = inputs + shape.sources
    local, sources = refs[:inputs], refs[inputs:split]
    outs = refs[split : split + outputs]
    total = refs[split + outputs]
    own = len(refs) - PLANE_SCRATCH
    place = Place(line)
    order = reduce_order(line)
    start, pair_add, first_add, second_add, drain = plane_steps(
        place, shape, sources, total, refs[own:]
    )
    step = pl.program_id(0) * pl.num_programs(1) + pl.program_id(1)

    @pl.when(step == 0)
    def _():
        place.greet()
        for z in order:
            start(z)

    @pl.when(step == 1)
    def _():
        for z in order:
            pair_add(z)

    for index, z in enumerate(order):
        pl.when(step == min(3 + 2 * index - index // 2, steps - 1))(
            functools.partial(first_add, z)
        )
    inner(*local, *outs, *refs[split + outputs + 1 : own])

    @pl.when(step == steps - 1)
    def _():
        for z in order:
            second_add(z)
        for z in order:
            drain(z)


def reduce_kernel(ready_shapes, shape, line, *refs):
    count = shape.sources
    many = len(ready_shapes)
    ready, sources = refs[:many], refs[many : many + count]
    vector_ref = refs[many + count]
    at = many + count + 1
    ready_outs, out, vector_out = refs[at : at + many], refs[at + many], refs[at + many + 1]
    scratch = refs[at + many + 2 :]
    place = Place(line)
    place.greet(wide=True)
    order = reduce_order(line)
    plans = []
    for index, ready_shape in enumerate(ready_shapes):
        own, scratch = scratch[:LINE_SCRATCH], scratch[LINE_SCRATCH:]
        plans.append(line_steps(place, ready_shape, ready[index], ready_outs[index], own))
    line_scratch, scratch = scratch[:LINE_SCRATCH], scratch[LINE_SCRATCH:]
    plane_scratch, scratch = scratch[:PLANE_SCRATCH], scratch[PLANE_SCRATCH:]
    start, pair_add, first_add, second_add, drain = plane_steps(
        place, shape, sources, line_scratch[0], plane_scratch
    )
    _, head, relay, close, line_drain = line_steps(place, shape, None, out, line_scratch)
    vector = VectorSum(place, vector_ref, vector_out, scratch)
    for z in order:
        start(z)
    for load, *_ in plans:
        load().start()
    vector.round(0)
    pair_add(order[0])
    for load, *_ in plans:
        load().wait()
    for z in order:
        for _, ready_head, *_ in plans:
            ready_head(z)
    for z in order[1:]:
        pair_add(z)
    vector.round(1)
    for z in order[:2]:
        first_add(z)
    for _, _, ready_relay, *_ in plans:
        ready_relay(1, True)
    vector.round(2)
    for z in order[2:]:
        first_add(z)
    for hop in range(2, line - 1):
        for _, _, ready_relay, *_ in plans:
            ready_relay(hop, True)
    for hop in range(1, line - 1):
        for _, _, ready_relay, *_ in plans:
            ready_relay(hop, False)
    vector.round(3)
    for z in order:
        second_add(z)
        head(z)
    relay(1, True)
    for _, _, _, ready_close, _ in plans:
        ready_close()
    for hop in range(2, line - 1):
        relay(hop, True)
    for hop in range(1, line - 1):
        relay(hop, False)
    vector.round(4)
    close()
    vector.round(5)
    for *_, ready_drain in plans:
        ready_drain()
    line_drain()
    for z in order:
        drain(z)
    vector.finish()


def group_shape(group, kind, line):
    rows, columns = group[0].shape
    return ReduceShape(kind, rows // (2 * line), columns, len(group))


def fast_reduce(ready, ready_shapes, group, line, collective_id, vector):
    shape = group_shape(group, "four", line)
    anywhere = pl.BlockSpec(memory_space=pl.ANY)
    local = pl.BlockSpec(memory_space=pltpu.VMEM)
    shapes = ready_shapes + [shape]
    scratch = []
    for item in shapes:
        scratch.extend(item.line_scratch(line))
    return pl.pallas_call(
        functools.partial(reduce_kernel, ready_shapes, shape, line),
        in_specs=[anywhere] * (len(ready) + len(group)) + [local],
        out_specs=[local] * (len(shapes) + 1),
        out_shape=[item.out_shape() for item in shapes]
        + [jax.ShapeDtypeStruct(vector.shape, F32)],
        scratch_shapes=scratch
        + shape.plane_scratch(line)
        + VectorSum.scratch(vector.shape),
        compiler_params=pltpu.CompilerParams(
            collective_id=collective_id, has_side_effects=True, vmem_limit_bytes=60 << 20
        ),
        name="fast_reduce",
    )(*ready, *group, vector)


PLANE = 4
CHIP = 2
LINE = 4


def small_plane():
    return lax.axis_size("rep") == PLANE and lax.axis_size("fsdp") == CHIP * LINE


def gather(block):
    return lax.all_gather(block, "fsdp", axis=0, tiled=True)


def gather_all(groups, by_rows, collective_id):
    if small_plane():
        return fast_gather(groups, LINE, by_rows, collective_id)
    return [gather(jnp.concatenate(group, axis=1)) for group in groups]


def scatter(block):
    return lax.psum_scatter(block.astype(BF16), "fsdp", scatter_dimension=0, tiled=True)


def column_blocks(block):
    rows = block.shape[0]
    return block.reshape(rows, lax.axis_size("rep"), -1).swapaxes(0, 1)


def scatter_columns(parts):
    count = lax.axis_size("rep")
    rows = parts[0].shape[0]
    split = [part.reshape(rows, count, -1) for part in parts]
    joined = jnp.concatenate(split, axis=2).reshape(rows, -1)
    own = lax.psum_scatter(joined, "rep", scatter_dimension=1, tiled=True)
    sizes = [part.shape[1] // count for part in parts]
    outs = []
    start = 0
    for size in sizes:
        outs.append(own[:, start : start + size].astype(F32))
        start += size
    return outs


def scatter_last(down, cross, group, vector, collective_id):
    down_term, down_sums = down
    cross_group, cross_sums = cross
    if small_plane():
        shapes = [
            group_shape(cross_group, "four", LINE),
            group_shape([down_term], "rows", LINE),
        ]
        cross_out, down_out, group_out, total = fast_reduce(
            [cross_sums[0], down_sums[0]], shapes, group, LINE, collective_id, vector
        )
        outs = [[out[index] for index in range(4)] for out in (cross_out, group_out)]
        return down_out.reshape(-1, down_out.shape[2]), outs, total
    (down_out,) = scatter_columns([scatter(down_term)])
    outs = [scatter_columns([scatter(item) for item in part]) for part in (cross_group, group)]
    return down_out, outs, lax.psum(vector, ("rep", "fsdp"))


def body(
    tokens,
    memory,
    prefix_len,
    bucket_table,
    rel_bias,
    gain_self,
    self_query,
    self_key,
    self_value,
    self_out,
    gain_cross,
    cross_query,
    cross_key,
    cross_value,
    cross_out,
    gain_feed,
    gate_weight,
    up_weight,
    down_weight,
    out_grad,
):
    nseq, length, width = tokens.shape
    shard = gain_self.shape[0]
    groups = width // shard
    entries = rel_bias.shape[0]
    small = jnp.stack(
        [gain_self, gain_cross, gain_feed, jnp.pad(rel_bias, (0, shard - entries))], axis=1
    )
    small = jnp.pad(small, ((0, 0), (0, 2 * LANES - 4)))
    first, second, down = gather_all(
        [
            [self_query, self_key, self_value, small],
            [self_out, cross_query, cross_key, cross_value, cross_out, small],
            [down_weight],
        ],
        [False, False, True],
        1,
    )
    gate_up_own = jnp.concatenate([gate_weight, up_weight], axis=1)
    gate_up_own, first, second, down = lax.optimization_barrier(
        (gate_up_own, first, second, down)
    )
    gate_up = gather(gate_up_own)
    qkv_proj = first[:, : 3 * width]
    picks = jnp.eye(8, LANES, dtype=BF16)
    vectors = back_term(picks, first[:, 3 * width : 3 * width + LANES])
    gain_first = vectors[0:1]
    gain_second = vectors[1:2]
    gain_third = vectors[2:3]
    table = vectors[3].astype(BF16).reshape(groups, shard)[:, :entries]
    table = table.reshape(NHEAD, BUCKETS)
    out_self = second[:, :width]
    query_cross = second[:, width : 2 * width]
    kv_cross = second[:, 2 * width : 4 * width]

    buckets_back = jnp.pad(bucket_table[::-1], (0, 1)).reshape(1, 2 * length)
    bias = skewed_bias(table, buckets_back, length)

    rows = nseq * length
    start_rows = tokens.reshape(rows, width).astype(F32)
    memory_rows = memory.reshape(-1, width)
    upstream = out_grad.reshape(rows, width)

    scale_first = inverse_rms(start_rows)
    normed_first = (start_rows * scale_first * gain_first).astype(BF16)
    qkv = matmul(normed_first, qkv_proj).astype(BF16)
    context, lse_self = run_self_forward(prefix_len, qkv, bias, nseq)
    middle = start_rows + matmul(context, out_self)
    scale_second = inverse_rms(middle)
    normed_second = (middle * scale_second * gain_second).astype(BF16)
    query_two = matmul(normed_second, query_cross).astype(BF16)
    kv_two = matmul(memory_rows, kv_cross).astype(BF16)
    context_two, lse_cross = run_cross_forward(query_two, kv_two, nseq)
    (
        result,
        later_grad,
        branch_two,
        context_two_grad,
        gain_third_grad,
        down_term,
        pair_term,
    ) = run_feed(middle, context_two, second, 4, gain_third, upstream, gate_up, down)
    carries = small_plane()
    pair_own = scatter(pair_term)
    query_two_grad, key_two_grad, value_two_grad, *down_sums = run_cross_backward(
        query_two,
        kv_two,
        context_two_grad,
        context_two,
        lse_cross,
        nseq,
        ([down_term], "rows", 4) if carries else None,
    )
    (
        middle_grad,
        gain_second_grad,
        query_term,
        out_term,
        branch_one,
        context_grad,
    ) = run_close(
        middle,
        later_grad,
        gain_second,
        context_two,
        branch_two,
        [query_two_grad],
        [(second, 1)],
        (second, 0),
        "cross_close",
    )
    memory_grad, key_term, value_term = run_memory(
        memory_rows, key_two_grad, value_two_grad, second, 2, 3
    )
    cross_terms = [query_term, key_term, value_term, out_term]
    query_grad, key_grad, value_grad, diagonal, *cross_sums = run_self_backward(
        prefix_len,
        qkv,
        context_grad,
        context,
        lse_self,
        bias,
        nseq,
        (cross_terms, "four", 2) if carries else None,
    )
    pair_split, query_grad = lax.optimization_barrier((column_blocks(pair_own), query_grad))
    tokens_grad, gain_first_grad, *self_terms = run_close(
        tokens.reshape(rows, width),
        middle_grad,
        gain_first,
        context,
        branch_one,
        [query_grad, key_grad, value_grad],
        [(first, 0), (first, 1), (first, 2)],
        None,
        "self_close",
    )

    onehot = (
        buckets_back.reshape(-1, 1) == jnp.arange(BUCKETS, dtype=jnp.int32)[None, :]
    ).astype(F32)
    onehot = onehot * (jnp.arange(2 * length) < 2 * length - 1)[:, None]
    bias_grad = jnp.dot(
        diagonal.reshape(NHEAD, 2 * length), onehot, precision=lax.Precision.HIGHEST
    )
    bias_rows = jnp.pad(
        bias_grad.reshape(groups, entries), ((0, 0), (0, shard - entries))
    ).reshape(width)
    vector_block = jnp.pad(
        jnp.concatenate(
            [gain_first_grad, gain_second_grad, gain_third_grad, bias_rows[None]], axis=0
        ),
        ((0, 4), (0, 0)),
    )
    pair_grad = lax.psum_scatter(pair_split, "rep").astype(F32)
    pair_grad = pair_grad.reshape(shard, -1, 2, FEED_BLOCK)
    gate_weight_grad = pair_grad[:, :, 0].reshape(shard, -1)
    up_weight_grad = pair_grad[:, :, 1].reshape(shard, -1)
    down_weight_grad, (cross_out_grads, self_out_grads), totals = scatter_last(
        (down_term, down_sums), (cross_terms, cross_sums), self_terms, vector_block, 3
    )
    own = lax.dynamic_slice(
        totals, (0, lax.axis_index("fsdp") * shard), (totals.shape[0], shard)
    )
    return (
        result.reshape(tokens.shape),
        tokens_grad.reshape(tokens.shape),
        memory_grad.reshape(memory.shape),
        own[3, :entries],
        own[0],
        *self_out_grads,
        own[1],
        *cross_out_grads,
        own[2],
        gate_weight_grad,
        up_weight_grad,
        down_weight_grad,
    )


def solution(mesh):
    batch = P(("rep", "fsdp"), None, None)
    matrix = P("fsdp", None)
    vector = P("fsdp")
    split = P("fsdp", "rep")
    in_specs = (
        (batch, batch, P(("rep", "fsdp")), P(), vector, vector)
        + (matrix,) * 4
        + (vector,)
        + (matrix,) * 4
        + (vector,)
        + (matrix,) * 3
        + (batch,)
    )
    out_specs = (
        (batch, batch, batch, vector, vector)
        + (split,) * 4
        + (vector,)
        + (split,) * 4
        + (vector,)
        + (split,) * 3
    )
    return jax.shard_map(body, mesh=mesh, in_specs=in_specs, out_specs=out_specs, check_vma=False)
```

```python
import functools

import jax
import jax.numpy as jnp
from jax import lax
from jax.experimental import pallas as pl
from jax.experimental.pallas import tpu as pltpu
from jax.sharding import PartitionSpec as P

NHEAD = 12
DHEAD = 64
BUCKETS = 32
PAIRS = NHEAD // 2
LANES = 2 * DHEAD
PREFIX_MAX = 256

EPSILON = 1e-06
CUBIC_TERM = 0.044715
SQRT_TWO_PI = 0.7978845608028654
NEGATIVE = -1000000000.0

F32 = jnp.float32
BF16 = jnp.bfloat16
LAST_DIMS = (((1,), (1,)), ((), ()))


def matmul(left_side, right_side):
    return jnp.dot(left_side, right_side, preferred_element_type=F32)


def back_term(gradient, weight):
    return lax.dot_general(gradient, weight, LAST_DIMS, preferred_element_type=F32)


def inverse_rms(values):
    return lax.rsqrt(jnp.mean(values * values, axis=-1, keepdims=True) + EPSILON)


def norm_back(values, scale_rows, gain_vec, upstream):
    weighted = upstream * gain_vec
    gain_grad = jnp.sum(upstream * values * scale_rows, axis=0)
    input_grad = scale_rows * weighted - values * scale_rows * scale_rows * scale_rows * jnp.mean(
        values * weighted, axis=-1, keepdims=True
    )
    return (input_grad, gain_grad)


def one_head(rows, head):
    lane = lax.broadcasted_iota(jnp.int32, rows.shape, 1)
    keep = lane < DHEAD if head == 0 else lane >= DHEAD
    return jnp.where(keep, rows, jnp.zeros_like(rows))


def flipped(rows):
    return rows.astype(F32).T.astype(BF16)


def tree(fold, rows, groups):
    step = rows.shape[0] // groups
    total = rows[:step]
    for index in range(1, groups):
        total = fold(total, rows[index * step : (index + 1) * step])
    return total


def column_max(rows, groups):
    return jnp.max(tree(jnp.maximum, rows, groups), axis=0, keepdims=True)


def column_sum(rows, groups):
    return jnp.sum(tree(jnp.add, rows, groups), axis=0, keepdims=True)


def allowed_at(shape, key_start, query_start, prefix):
    key = lax.broadcasted_iota(jnp.int32, shape, 0) + key_start
    query = lax.broadcasted_iota(jnp.int32, shape, 1) + query_start
    return (key <= query) | (key < prefix)


def skew_kernel(table_ref, buckets_ref, out_ref):
    bucket = lax.broadcasted_iota(jnp.int32, (BUCKETS, buckets_ref.shape[1]), 0)
    onehot = (bucket == buckets_ref[...]).astype(BF16)
    by_offset = matmul(table_ref[...], onehot)
    width = out_ref.shape[2]
    total = by_offset.shape[1]
    for head in range(NHEAD):
        rows = jnp.broadcast_to(by_offset[head : head + 1], (LANES, total))
        rolled = pltpu.roll(rows, total - (LANES - 1), 1, stride=1, stride_axis=0)
        out_ref[head] = rolled[:, :width]


def skewed_bias(table, buckets_back, length):
    total = 2 * length
    return pl.pallas_call(
        skew_kernel,
        out_shape=jax.ShapeDtypeStruct((NHEAD, LANES, total - LANES), F32),
        name="skewed_bias",
    )(jnp.pad(table, ((0, 4), (0, 0))), buckets_back)


HEADROOM = 70.0


def self_forward(prefix_ref, query_ref, key_ref, value_ref, bias_ref, out_ref, lse_ref):
    length = query_ref.shape[0]
    block = 256
    prefix = prefix_ref[pl.program_id(0)]
    queries = query_ref[...]
    keys = key_ref[...]
    values = flipped(value_ref[...])

    def run(exact):
        excess = jnp.zeros((1, block), F32)
        for start in range(0, length, block):
            stop = start + block
            count = max(PREFIX_MAX, stop)
            outs = []
            for head in range(2):
                scores = back_term(keys[:count], one_head(queries[start:stop], head))
                parts = []
                for base in range(0, count, LANES):
                    shift = length - LANES - base + start
                    part = scores[base : base + LANES] + bias_ref[head, :, shift : shift + block]
                    if base + LANES - 1 > start:
                        part = jnp.where(
                            allowed_at(part.shape, base, start, prefix), part, NEGATIVE
                        )
                    parts.append(part)
                top = parts[0]
                for part in parts[1:]:
                    top = jnp.maximum(top, part)
                top = column_max(top, 4)
                anchor = top if exact else column_max(parts[0], 4)
                if not exact:
                    excess = jnp.maximum(excess, top - anchor)
                shares = [jnp.exp(part - anchor) for part in parts]
                total = shares[0]
                for share in shares[1:]:
                    total = total + share
                total = column_sum(total, 4)
                share = jnp.concatenate([item.astype(BF16) for item in shares], axis=0)
                context = matmul(values[head * DHEAD : (head + 1) * DHEAD, :count], share)
                outs.append(context * (1.0 / total))
                lse_ref[head : head + 1, start:stop] = anchor + jnp.log(total)
            out_ref[start:stop, :] = jnp.concatenate(outs, axis=0).T.astype(BF16)
        return jnp.max(excess)

    excess = run(False)

    @pl.when(excess > HEADROOM)
    def _():
        run(True)


def cross_forward(query_ref, key_ref, value_ref, out_ref, lse_ref):
    keys = key_ref[...]
    values = flipped(value_ref[...])
    queries = query_ref[...]

    def run(exact):
        excess = jnp.zeros((1, queries.shape[0]), F32)
        ahead = [back_term(keys, one_head(queries, head)) for head in range(2)]
        outs = []
        for head in range(2):
            scores = ahead[head]
            top = column_max(scores, 16)
            anchor = top if exact else column_max(scores[: 2 * LANES], 8)
            if not exact:
                excess = jnp.maximum(excess, top - anchor)
            share = jnp.exp(scores - anchor)
            total = column_sum(share, 16)
            context = matmul(values[head * DHEAD : (head + 1) * DHEAD], share.astype(BF16))
            outs.append(context * (1.0 / total))
            lse_ref[head : head + 1, :] = anchor + jnp.log(total)
        out_ref[...] = jnp.concatenate(outs, axis=0).T.astype(BF16)
        return jnp.max(excess)

    excess = run(False)

    @pl.when(excess > HEADROOM)
    def _():
        run(True)


def cross_backward(
    query_ref, key_ref, value_ref, up_ref, context_ref, lse_ref, dq_ref, dk_ref, dv_ref
):
    length = query_ref.shape[0]
    block = 256
    keys = key_ref[...]
    values = value_ref[...]
    queries = query_ref[...]
    upstream = up_ref[...]
    keys_flipped = flipped(keys)
    inner = (upstream.astype(F32) * context_ref[...].astype(F32)).T
    key_grad = None
    value_grad = None
    for start in range(0, length, block):
        rows = slice(start, start + block)
        grads = []
        for head in range(2):
            sub = slice(head * DHEAD, (head + 1) * DHEAD)
            query = one_head(queries[rows], head)
            above = one_head(upstream[rows], head)
            row_inner = jnp.sum(inner[sub, rows], axis=0, keepdims=True)
            shares = jnp.exp(back_term(keys, query) - lse_ref[head : head + 1, rows])
            share_grad = back_term(values, above)
            score_grad = (shares * (share_grad - row_inner)).astype(BF16)
            value_part = matmul(shares.astype(BF16), above)
            key_part = matmul(score_grad, query)
            value_grad = value_part if value_grad is None else value_grad + value_part
            key_grad = key_part if key_grad is None else key_grad + key_part
            grads.append(matmul(keys_flipped[sub], score_grad))
        dq_ref[rows, :] = jnp.concatenate(grads, axis=0).T.astype(BF16)
    dk_ref[...] = key_grad.astype(BF16)
    dv_ref[...] = value_grad.astype(BF16)


def self_backward(
    prefix_ref,
    query_ref,
    key_ref,
    value_ref,
    up_ref,
    context_ref,
    lse_ref,
    bias_ref,
    dq_ref,
    dk_ref,
    dv_ref,
    diag_ref,
    acc_ref,
):
    length = query_ref.shape[0]
    block = 256
    step = pl.program_id(1)
    prefix = prefix_ref[step]

    @pl.when(step == 0)
    def _():
        acc_ref[...] = jnp.zeros_like(acc_ref)

    queries = query_ref[...]
    keys = key_ref[...]
    values = value_ref[...]
    upstream = up_ref[...]
    keys_flipped = flipped(keys)
    inner = (upstream.astype(F32) * context_ref[...].astype(F32)).T
    count_all = length // block
    key_grad = [None] * count_all
    value_grad = [None] * count_all
    for start in range(0, length, block):
        stop = start + block
        count = max(PREFIX_MAX, stop)
        rows = slice(start, stop)
        grads = []
        for head in range(2):
            sub = slice(head * DHEAD, (head + 1) * DHEAD)
            query = one_head(queries[rows], head)
            above = one_head(upstream[rows], head)
            row_inner = jnp.sum(inner[sub, rows], axis=0, keepdims=True)
            row_lse = lse_ref[head : head + 1, rows]
            scores = back_term(keys[:count], query)
            share_grad = back_term(values[:count], above)
            shares = []
            score_grads = []
            for base in range(0, count, LANES):
                part = slice(base, base + LANES)
                shift = length - LANES - base + start
                share = jnp.exp(
                    scores[part] + bias_ref[head, :, shift : shift + block] - row_lse
                )
                if base + LANES - 1 > start:
                    share = jnp.where(allowed_at(share.shape, base, start, prefix), share, 0.0)
                score_grad = share * (share_grad[part] - row_inner)
                acc_ref[head, :, shift : shift + block] += score_grad
                shares.append(share.astype(BF16))
                score_grads.append(score_grad.astype(BF16))
            share = jnp.concatenate(shares, axis=0)
            score_grad = jnp.concatenate(score_grads, axis=0)
            value_part = matmul(share, above)
            key_part = matmul(score_grad, query)
            for index in range(count // block):
                part = slice(index * block, (index + 1) * block)
                if value_grad[index] is None:
                    value_grad[index] = value_part[part]
                    key_grad[index] = key_part[part]
                else:
                    value_grad[index] = value_grad[index] + value_part[part]
                    key_grad[index] = key_grad[index] + key_part[part]
            grads.append(matmul(keys_flipped[sub, :count], score_grad))
        dq_ref[rows, :] = jnp.concatenate(grads, axis=0).T.astype(BF16)
    for index in range(count_all):
        part = slice(index * block, (index + 1) * block)
        dk_ref[part, :] = key_grad[index].astype(BF16)
        dv_ref[part, :] = value_grad[index].astype(BF16)

    @pl.when(step == pl.num_programs(1) - 1)
    def _():
        total = 2 * length
        for head in range(2):
            rows = jnp.concatenate([acc_ref[head], jnp.zeros((LANES, LANES), F32)], axis=1)
            half = LANES // 2
            while half >= 1:
                rows = rows[:half] + pltpu.roll(rows[half:], total - half, 1)
                half //= 2
            diag_ref[head : head + 1, :] = pltpu.roll(rows, LANES - 1, 1)


def spec(shape, index):
    return pl.BlockSpec(shape, index)


def run_self_forward(prefix, qkv, bias, nseq):
    length = qkv.shape[0] // nseq
    return pl.pallas_call(
        self_forward,
        grid_spec=pltpu.PrefetchScalarGridSpec(
            num_scalar_prefetch=1,
            grid=(nseq, PAIRS),
            in_specs=[
                spec((length, LANES), lambda s, p, _: (s, p)),
                spec((length, LANES), lambda s, p, _: (s, PAIRS + p)),
                spec((length, LANES), lambda s, p, _: (s, 2 * PAIRS + p)),
                spec((2, LANES, 2 * length - LANES), lambda s, p, _: (p, 0, 0)),
            ],
            out_specs=[
                spec((length, LANES), lambda s, p, _: (s, p)),
                spec((None, None, 2, length), lambda s, p, _: (s, p, 0, 0)),
            ],
        ),
        out_shape=[
            jax.ShapeDtypeStruct((qkv.shape[0], PAIRS * LANES), BF16),
            jax.ShapeDtypeStruct((nseq, PAIRS, 2, length), F32),
        ],
        cost_estimate=pl.CostEstimate(
            flops=20_000_000_000, bytes_accessed=12_000_000, transcendentals=0
        ),
        name="self_forward",
    )(prefix, qkv, qkv, qkv, bias)


def run_cross_forward(query, kv, nseq):
    length = query.shape[0] // nseq
    count = kv.shape[0] // nseq
    return pl.pallas_call(
        cross_forward,
        grid=(nseq, PAIRS),
        in_specs=[
            spec((length, LANES), lambda s, p: (s, p)),
            spec((count, LANES), lambda s, p: (s, p)),
            spec((count, LANES), lambda s, p: (s, PAIRS + p)),
        ],
        out_specs=[
            spec((length, LANES), lambda s, p: (s, p)),
            spec((None, None, 2, length), lambda s, p: (s, p, 0, 0)),
        ],
        out_shape=[
            jax.ShapeDtypeStruct(query.shape, BF16),
            jax.ShapeDtypeStruct((nseq, PAIRS, 2, length), F32),
        ],
        cost_estimate=pl.CostEstimate(
            flops=24_000_000_000, bytes_accessed=10_000_000, transcendentals=0
        ),
        name="cross_forward",
    )(query, kv, kv)


def carry(carried, steps, inner, inputs, outputs):
    if carried is None:
        return inner, [], [], [], [], None
    group, kind, collective_id = carried
    shape = group_shape(group, kind, LINE)
    kernel = functools.partial(
        carried_kernel, shape, LINE, steps, inner, inputs, outputs
    )
    total = shape.total_shape(LINE)
    params = pltpu.CompilerParams(
        collective_id=collective_id, has_side_effects=True, vmem_limit_bytes=60 << 20
    )
    return (
        kernel,
        group,
        [pl.BlockSpec(total, lambda *_: (0, 0, 0, 0))],
        [jax.ShapeDtypeStruct(total, BF16)],
        shape.plane_scratch(LINE),
        params,
    )


def run_cross_backward(query, kv, upstream, context, lse, nseq, carried=None):
    length = query.shape[0] // nseq
    count = kv.shape[0] // nseq
    rows = spec((length, LANES), lambda s, p: (s, p))
    wide = spec((count, LANES), lambda s, p: (s, p))
    kernel, group, total_specs, totals, scratch, params = carry(
        carried, PAIRS * nseq, cross_backward, 6, 3
    )
    return pl.pallas_call(
        kernel,
        grid=(nseq, PAIRS),
        in_specs=[
            rows,
            wide,
            spec((count, LANES), lambda s, p: (s, PAIRS + p)),
            rows,
            rows,
            spec((None, None, 2, length), lambda s, p: (s, p, 0, 0)),
        ]
        + [pl.BlockSpec(memory_space=pl.ANY)] * len(group),
        out_specs=[rows, wide, wide] + total_specs,
        out_shape=[
            jax.ShapeDtypeStruct(query.shape, BF16),
            jax.ShapeDtypeStruct((kv.shape[0], PAIRS * LANES), BF16),
            jax.ShapeDtypeStruct((kv.shape[0], PAIRS * LANES), BF16),
        ]
        + totals,
        scratch_shapes=scratch,
        cost_estimate=pl.CostEstimate(
            flops=36_000_000_000, bytes_accessed=20_000_000, transcendentals=0
        ),
        compiler_params=params,
        name="cross_backward",
    )(query, kv, kv, upstream, context, lse, *group)


def run_self_backward(prefix, qkv, upstream, context, lse, bias, nseq, carried=None):
    length = qkv.shape[0] // nseq
    rows = spec((length, LANES), lambda p, s, _: (s, p))
    kernel, group, total_specs, totals, scratch, params = carry(
        carried, PAIRS * nseq, self_backward, 8, 4
    )
    return pl.pallas_call(
        kernel,
        grid_spec=pltpu.PrefetchScalarGridSpec(
            num_scalar_prefetch=1,
            grid=(PAIRS, nseq),
            in_specs=[
                rows,
                spec((length, LANES), lambda p, s, _: (s, PAIRS + p)),
                spec((length, LANES), lambda p, s, _: (s, 2 * PAIRS + p)),
                rows,
                rows,
                spec((None, None, 2, length), lambda p, s, _: (s, p, 0, 0)),
                spec((2, LANES, 2 * length - LANES), lambda p, s, _: (p, 0, 0)),
            ]
            + [pl.BlockSpec(memory_space=pl.ANY)] * len(group),
            out_specs=[
                rows,
                rows,
                rows,
                spec((None, 2, 2 * length), lambda p, s, _: (p, 0, 0)),
            ]
            + total_specs,
            scratch_shapes=[pltpu.VMEM((2, LANES, 2 * length - LANES), F32)] + scratch,
        ),
        out_shape=[jax.ShapeDtypeStruct(upstream.shape, BF16)] * 3
        + [jax.ShapeDtypeStruct((PAIRS, 2, 2 * length), F32)]
        + totals,
        cost_estimate=pl.CostEstimate(
            flops=24_000_000_000, bytes_accessed=20_000_000, transcendentals=0
        ),
        compiler_params=params,
        name="self_backward",
    )(prefix, qkv, qkv, qkv, upstream, context, lse, bias, *group)


FEED_BLOCK = 512


def feed_kernel(
    middle_ref,
    context_ref,
    out_proj_ref,
    gain_ref,
    up_grad_ref,
    gate_ref,
    up_ref,
    down_ref,
    result_ref,
    later_grad_ref,
    branch_ref,
    context_grad_ref,
    gain_grad_ref,
    down_term_ref,
    pair_term_ref,
    later_ref,
    normed_ref,
    flipped_ref,
    result_acc,
    third_acc,
):
    step = pl.program_id(0)
    count = middle_ref.shape[0]
    chunk = 256
    chunks = [slice(start, start + chunk) for start in range(0, count, chunk)]

    @pl.when(step == 0)
    def _():
        for rows in chunks:
            later = middle_ref[rows] + matmul(context_ref[rows], out_proj_ref[...])
            normed = (later * inverse_rms(later) * gain_ref[...]).astype(BF16)
            later_ref[rows] = later
            normed_ref[rows] = normed
            flipped_ref[:, rows] = flipped(normed)
            result_acc[rows] = jnp.zeros_like(later)
            third_acc[rows] = jnp.zeros_like(later)

    gate_proj = gate_ref[...]
    up_proj = up_ref[...]
    down_proj = down_ref[...]
    hidden_flipped = []
    gate_grads = []
    lift_grads = []
    for rows in chunks:
        normed = normed_ref[rows]
        gate = matmul(normed, gate_proj)
        lift = matmul(normed, up_proj)
        hidden_grad = back_term(up_grad_ref[rows], down_proj)
        square = gate * gate
        tangent = jnp.tanh(SQRT_TWO_PI * gate * (1.0 + CUBIC_TERM * square))
        half = 0.5 * (1.0 + tangent)
        active = gate * half
        slope = half + 0.5 * gate * (1.0 - tangent * tangent) * (
            SQRT_TWO_PI + 3.0 * CUBIC_TERM * SQRT_TWO_PI * square
        )
        hidden = active * lift
        gate_grad = (hidden_grad * lift * slope).astype(BF16)
        lift_grad = (hidden_grad * active).astype(BF16)
        hidden_flipped.append(hidden.T.astype(BF16))
        gate_grads.append(gate_grad)
        lift_grads.append(lift_grad)
        result_acc[rows] += matmul(hidden.astype(BF16), down_proj)
        third_acc[rows] += back_term(gate_grad, gate_proj) + back_term(lift_grad, up_proj)
    hidden_flipped = jnp.concatenate(hidden_flipped, axis=1)
    down_term_ref[...] = matmul(hidden_flipped, up_grad_ref[...]).astype(BF16)
    gate_grads = jnp.concatenate(gate_grads, axis=0)
    lift_grads = jnp.concatenate(lift_grads, axis=0)
    pair_term_ref[:, :FEED_BLOCK] = matmul(flipped_ref[...], gate_grads).astype(BF16)
    pair_term_ref[:, FEED_BLOCK:] = matmul(flipped_ref[...], lift_grads).astype(BF16)

    @pl.when(step == pl.num_programs(0) - 1)
    def _():
        gain_grad = jnp.zeros(gain_ref.shape, F32)
        for rows in chunks:
            later = later_ref[rows]
            result_ref[rows] = (later + result_acc[rows]).astype(BF16)
            carry, part = norm_back(later, inverse_rms(later), gain_ref[...], third_acc[rows])
            gain_grad = gain_grad + part[None, :]
            later_grad = up_grad_ref[rows].astype(F32) + carry
            branch = later_grad.astype(BF16)
            later_grad_ref[rows] = later_grad
            branch_ref[rows] = branch
            context_grad_ref[rows] = back_term(branch, out_proj_ref[...]).astype(BF16)
        gain_grad_ref[...] = gain_grad


def run_feed(middle, context, out_proj, out_block, gain, upstream, gate_up, down):
    count, width = middle.shape
    ffn = down.shape[0]
    blocks = ffn // FEED_BLOCK

    def whole(shape, **extra):
        return pl.BlockSpec(shape, lambda j: (0, 0), **extra)

    once = {"pipeline_mode": pl.Buffered(1)}
    rows = (count, width)
    return pl.pallas_call(
        feed_kernel,
        grid=(blocks,),
        in_specs=[
            whole(rows, **once),
            whole(rows, **once),
            pl.BlockSpec((width, width), lambda j: (0, out_block), **once),
            whole((1, width)),
            whole(rows, **once),
            spec((width, FEED_BLOCK), lambda j: (0, j)),
            spec((width, FEED_BLOCK), lambda j: (0, blocks + j)),
            spec((FEED_BLOCK, width), lambda j: (j, 0)),
        ],
        out_specs=[
            whole(rows),
            whole(rows),
            whole(rows),
            whole(rows),
            whole((1, width)),
            spec((FEED_BLOCK, width), lambda j: (j, 0)),
            spec((width, 2 * FEED_BLOCK), lambda j: (0, j)),
        ],
        out_shape=[
            jax.ShapeDtypeStruct(rows, BF16),
            jax.ShapeDtypeStruct(rows, F32),
            jax.ShapeDtypeStruct(rows, BF16),
            jax.ShapeDtypeStruct(rows, BF16),
            jax.ShapeDtypeStruct((1, width), F32),
            jax.ShapeDtypeStruct((ffn, width), BF16),
            jax.ShapeDtypeStruct((width, 2 * ffn), BF16),
        ],
        scratch_shapes=[
            pltpu.VMEM(rows, F32),
            pltpu.VMEM(rows, BF16),
            pltpu.VMEM((width, count), BF16),
            pltpu.VMEM(rows, F32),
            pltpu.VMEM(rows, F32),
        ],
        cost_estimate=pl.CostEstimate(
            flops=32_000_000_000, bytes_accessed=40_000_000, transcendentals=0
        ),
        compiler_params=pltpu.CompilerParams(vmem_limit_bytes=60 << 20),
        name="feed",
    )(middle, context, out_proj, gain, upstream, gate_up, gate_up, down)


def close_kernel(count, project, *refs):
    values_ref, carry_ref, gain_ref, left_ref, right_ref = refs[:5]
    grad_refs = refs[5 : 5 + count]
    weight_refs = refs[5 + count : 5 + 2 * count]
    at = 5 + 2 * count
    if project:
        proj_ref = refs[at]
        at += 1
    out_ref, gain_grad_ref = refs[at : at + 2]
    term_refs = refs[at + 2 : at + 3 + count]
    at += 3 + count
    if project:
        branch_ref, projected_ref = refs[at : at + 2]
        at += 2
    sums = refs[at : at + 1 + count]
    gain_sum = refs[at + 1 + count]
    step = pl.program_id(0)

    @pl.when(step == 0)
    def _():
        gain_sum[...] = jnp.zeros_like(gain_sum)
        for total in sums:
            total[...] = jnp.zeros_like(total)

    values = values_ref[...].astype(F32)
    gain = gain_ref[...]
    scale = inverse_rms(values)
    normed = (values * scale * gain).T.astype(BF16)
    upstream = None
    for index in range(count):
        grad = grad_refs[index][...]
        sums[index][...] += matmul(normed, grad)
        part = back_term(grad, weight_refs[index][...])
        upstream = part if upstream is None else upstream + part
    sums[count][...] += matmul(flipped(left_ref[...]), right_ref[...])
    carry, part = norm_back(values, scale, gain, upstream)
    gain_sum[...] += part[None, :]
    result = carry_ref[...] + carry
    out_ref[...] = result
    if project:
        branch = result.astype(BF16)
        branch_ref[...] = branch
        projected_ref[...] = back_term(branch, proj_ref[...]).astype(BF16)

    @pl.when(step == pl.num_programs(0) - 1)
    def _():
        gain_grad_ref[...] = gain_sum[...]
        for term, total in zip(term_refs, sums):
            term[...] = total[...].astype(BF16)


def run_close(values, carry, gain, left, right, grads, weights, project, name):
    rows, width = values.shape
    count = len(grads)
    block = 256
    wide = spec((block, width), lambda i: (i, 0))

    def columns(index):
        return pl.BlockSpec((width, width), lambda i: (0, index), pipeline_mode=pl.Buffered(1))

    whole = [spec((1, width), lambda i: (0, 0))]
    square = [spec((width, width), lambda i: (0, 0))] * (count + 1)
    extra = [] if project is None else [project]
    out_shape = [
        jax.ShapeDtypeStruct((rows, width), F32),
        jax.ShapeDtypeStruct((1, width), F32),
    ] + [jax.ShapeDtypeStruct((width, width), BF16)] * (count + 1)
    out_shape += [jax.ShapeDtypeStruct((rows, width), BF16)] * (2 * len(extra))
    return pl.pallas_call(
        functools.partial(close_kernel, count, project is not None),
        grid=(rows // block,),
        in_specs=[wide, wide]
        + whole
        + [wide] * (2 + count)
        + [columns(index) for _, index in weights + extra],
        out_specs=[wide] + whole + square + [wide] * (2 * len(extra)),
        out_shape=out_shape,
        scratch_shapes=[pltpu.VMEM((width, width), F32)] * (count + 1)
        + [pltpu.VMEM((1, width), F32)],
        cost_estimate=pl.CostEstimate(
            flops=8_000_000_000, bytes_accessed=25_000_000, transcendentals=0
        ),
        compiler_params=pltpu.CompilerParams(vmem_limit_bytes=60 << 20),
        name=name,
    )(values, carry, gain, left, right, *grads, *[item for item, _ in weights + extra])


def memory_kernel(
    memory_ref, key_grad_ref, value_grad_ref, key_ref, value_ref, out_ref, *rest
):
    key_term_ref, value_term_ref, key_sum, value_sum = rest
    step = pl.program_id(0)

    @pl.when(step == 0)
    def _():
        key_sum[...] = jnp.zeros_like(key_sum)
        value_sum[...] = jnp.zeros_like(value_sum)

    rows = flipped(memory_ref[...])
    key_grad = key_grad_ref[...]
    value_grad = value_grad_ref[...]
    out_ref[...] = back_term(key_grad, key_ref[...]) + back_term(value_grad, value_ref[...])
    key_sum[...] += matmul(rows, key_grad)
    value_sum[...] += matmul(rows, value_grad)

    @pl.when(step == pl.num_programs(0) - 1)
    def _():
        key_term_ref[...] = key_sum[...].astype(BF16)
        value_term_ref[...] = value_sum[...].astype(BF16)


def run_memory(memory, key_grad, value_grad, weights, key_block, value_block):
    rows, width = memory.shape
    block = 512
    wide = spec((block, width), lambda i: (i, 0))
    square = spec((width, width), lambda i: (0, 0))

    def columns(index):
        return pl.BlockSpec((width, width), lambda i: (0, index), pipeline_mode=pl.Buffered(1))

    return pl.pallas_call(
        memory_kernel,
        grid=(rows // block,),
        in_specs=[wide, wide, wide, columns(key_block), columns(value_block)],
        out_specs=[wide, square, square],
        out_shape=[
            jax.ShapeDtypeStruct((rows, width), F32),
            jax.ShapeDtypeStruct((width, width), BF16),
            jax.ShapeDtypeStruct((width, width), BF16),
        ],
        scratch_shapes=[pltpu.VMEM((width, width), F32)] * 2,
        cost_estimate=pl.CostEstimate(
            flops=10_000_000_000, bytes_accessed=18_000_000, transcendentals=0
        ),
        compiler_params=pltpu.CompilerParams(vmem_limit_bytes=60 << 20),
        name="memory_close",
    )(memory, key_grad, value_grad, weights, weights)


MESH = pl.DeviceIdType.MESH


class Place:
    def __init__(self, line):
        self.line = line
        rep = lax.axis_index("rep")
        fsdp = lax.axis_index("fsdp")
        self.rep = rep
        self.fsdp = fsdp
        self.y = rep // 2
        self.x = rep % 2
        self.z = fsdp // 2
        self.core = fsdp % 2
        self.x_rep = self.y * 2 + 1 - self.x
        self.y_rep = (1 - self.y) * 2 + self.x

    def at_x(self):
        return {"rep": self.x_rep, "fsdp": self.fsdp}

    def at_y(self):
        return {"rep": self.y_rep, "fsdp": self.fsdp}

    def at_partner(self):
        return {"rep": self.rep, "fsdp": self.z * 2 + 1 - self.core}

    def at_line(self, side):
        return {"rep": self.rep, "fsdp": self.fsdp + (2 if side == 0 else -2)}

    def has_next(self, side):
        return self.z < self.line - 1 if side == 0 else self.z > 0

    def has_last(self, side):
        return self.has_next(1 - side)

    def arrives(self, side, hop):
        if side == 0:
            return self.z - 1 - hop >= 0
        return self.z + 1 + hop <= self.line - 1

    def source(self, side, hop):
        return self.z - 1 - hop if side == 0 else self.z + 1 + hop

    def at_far(self):
        half = self.line // 2
        return {"rep": self.rep, "fsdp": (self.z + half) % self.line * 2 + self.core}

    def greet(self, wide=False):
        barrier = pltpu.get_barrier_semaphore()
        targets = [self.at_x(), self.at_y(), self.at_partner()]
        if wide:
            targets.append({"rep": 3 - self.rep, "fsdp": self.fsdp})
            targets.append(self.at_far())
        for target in targets:
            pl.semaphore_signal(barrier, inc=1, device_id=target, device_id_type=MESH)
        for side in range(2):

            @pl.when(self.has_next(side))
            def _():
                pl.semaphore_signal(
                    barrier, inc=1, device_id=self.at_line(side), device_id_type=MESH
                )

        count = len(targets)
        for side in range(2):
            count = count + jnp.where(self.has_next(side), 1, 0)
        pl.semaphore_wait(barrier, count)


def remote(source, target, send, recv, device):
    return pltpu.make_async_remote_copy(
        src_ref=source,
        dst_ref=target,
        send_sem=send,
        recv_sem=recv,
        device_id=device,
        device_id_type=MESH,
    )


class GatherShape:
    def __init__(self, parts, by_rows):
        self.rows = parts[0].shape[0]
        self.widths = [part.shape[1] for part in parts]
        self.starts = [sum(self.widths[:index]) for index in range(len(parts))]
        self.columns = sum(self.widths)
        self.by_rows = by_rows

    def full(self, ref, owner):
        return ref.at[pl.ds(pl.multiple_of(owner * self.rows, 32), self.rows)]

    def piece(self, ref, owner, part, half=None):
        base = owner * self.rows
        if self.by_rows:
            rows = self.rows // 4
            base = base + part * rows
        else:
            rows = self.rows
        if half is not None:
            rows = rows // 2
            base = base + half * rows
        row_slice = pl.ds(pl.multiple_of(base, 16), rows)
        if self.by_rows:
            return ref.at[row_slice]
        width = self.columns // 4
        return ref.at[row_slice, pl.ds(pl.multiple_of(part * width, LANES), width)]


def gather_sems(line):
    hops = line - 1
    return [pltpu.SemaphoreType.DMA((5, 2, 2, hops)), pltpu.SemaphoreType.DMA((4,))] + [
        pltpu.SemaphoreType.DMA((2, 2, hops))
    ]


def gather_steps(place, shape, src, own, dst, sems):
    hop_sem, own_sem, pair_sem = sems
    hops = place.line - 1
    me = place.fsdp

    def load(index):
        at = pl.ds(shape.starts[index], shape.widths[index])
        return pltpu.make_async_copy(src[index], own.at[:, at], own_sem.at[0])

    def loaded():
        return pltpu.make_async_copy(own, own, own_sem.at[0])

    def keep():
        return pltpu.make_async_copy(own, shape.full(dst, me), own_sem.at[1])

    def own_pair():
        return remote(
            own, shape.full(dst, me), own_sem.at[2], own_sem.at[3], place.at_partner()
        )

    def owner(side, hop):
        return place.source(side, hop) * 2 + place.core

    def line_first(side):
        return remote(
            shape.piece(own, 0, place.rep),
            shape.piece(dst, me, place.rep),
            hop_sem.at[0, 0, side, 0],
            hop_sem.at[0, 1, side, 0],
            place.at_line(side),
        )

    def moved(kind, side, hop, block, device):
        return remote(
            block, block, hop_sem.at[kind, 0, side, hop], hop_sem.at[kind, 1, side, hop], device
        )

    def line_next(side, hop):
        block = shape.piece(dst, owner(side, hop - 1), place.rep)
        return moved(0, side, hop, block, place.at_line(side))

    def line_arrival(side, hop):
        block = shape.piece(dst, owner(side, hop), place.rep)
        return moved(0, side, hop, block, place.at_line(side))

    def plane(axis, side, hop):
        block = shape.piece(dst, owner(side, hop), place.rep)
        return moved(1 + axis, side, hop, block, place.at_x() if axis == 0 else place.at_y())

    def cross(axis, side, hop):
        part = place.x_rep if axis == 1 else place.y_rep
        block = shape.piece(dst, owner(side, hop), part, 1 - axis)
        return moved(3 + axis, side, hop, block, place.at_x() if axis == 0 else place.at_y())

    def pair(side, hop):
        block = shape.full(dst, owner(side, hop))
        return remote(
            block, block, pair_sem.at[0, side, hop], pair_sem.at[1, side, hop], place.at_partner()
        )

    def each(fn):
        def run(hop):
            for side in range(2):
                pl.when(place.arrives(side, hop))(functools.partial(fn, side, hop))

        return run

    def start():
        for index in range(len(src)):
            load(index).start()
        loaded().wait()
        for side in range(2):
            pl.when(place.has_next(side))(lambda side=side: line_first(side).start())
        own_pair().start()
        keep().start()

    def arrive(side, hop):
        line_arrival(side, hop).wait_recv()
        if hop + 1 < hops:
            pl.when(place.has_next(side))(lambda: line_next(side, hop + 1).start())
        plane(0, side, hop).start()
        plane(1, side, hop).start()

    def turn(side, hop):
        plane(0, side, hop).wait_recv()
        cross(1, side, hop).start()
        plane(1, side, hop).wait_recv()
        cross(0, side, hop).start()

    def hand(side, hop):
        cross(0, side, hop).wait_recv()
        cross(1, side, hop).wait_recv()
        pair(side, hop).start()

    def finish():
        def last(side, hop):
            pair(side, hop).wait()
            for axis in range(2):
                plane(axis, side, hop).wait_send()
                cross(axis, side, hop).wait_send()
            if hop + 1 < hops:
                pl.when(place.has_next(side))(lambda: line_next(side, hop + 1).wait_send())

        for hop in range(hops):
            each(last)(hop)
        for side in range(2):
            pl.when(place.has_next(side))(lambda side=side: line_first(side).wait_send())
        own_pair().wait()
        keep().wait()

    return start, each(arrive), each(turn), each(hand), finish


def gather_kernel(shapes, line, *refs):
    count = len(shapes)
    sources = []
    at = 0
    for shape in shapes:
        sources.append(refs[at : at + len(shape.widths)])
        at += len(shape.widths)
    targets = refs[at : at + count]
    scratch = refs[at + count :]
    place = Place(line)
    place.greet()
    plans = []
    for index, shape in enumerate(shapes):
        own, *sems = scratch[4 * index : 4 * index + 4]
        plans.append(gather_steps(place, shape, sources[index], own, targets[index], sems))
    for plan in plans:
        plan[0]()
    for step in range(line + 1):
        for stage in range(3):
            hop = step - stage
            if 0 <= hop < line - 1:
                for plan in plans:
                    plan[1 + stage](hop)
    for plan in plans:
        plan[4]()


def fast_gather(groups, line, by_rows, collective_id):
    shapes = [GatherShape(group, flag) for group, flag in zip(groups, by_rows)]
    scratch = []
    for shape in shapes:
        scratch.append(pltpu.VMEM((shape.rows, shape.columns), BF16))
        scratch.extend(gather_sems(line))
    anywhere = pl.BlockSpec(memory_space=pl.ANY)
    blocks = [block for group in groups for block in group]
    return pl.pallas_call(
        functools.partial(gather_kernel, shapes, line),
        in_specs=[anywhere] * len(blocks),
        out_specs=[anywhere] * len(groups),
        out_shape=[
            jax.ShapeDtypeStruct((2 * line * s.rows, s.columns), BF16) for s in shapes
        ],
        scratch_shapes=scratch,
        compiler_params=pltpu.CompilerParams(collective_id=collective_id, has_side_effects=True),
        name="fast_gather",
    )(*blocks)


class ReduceShape:
    def __init__(self, kind, rows, columns, sources):
        self.kind = kind
        self.rows = rows
        self.sources = sources
        if kind == "rows":
            self.block = (rows // 8, columns)
        elif kind == "pair":
            self.block = (rows // 2, columns // 2)
        else:
            self.block = (rows // 2, columns)
        self.exchange = kind != "pair"
        self.part_rows = rows // 4 if kind == "rows" else rows
        self.part_columns = columns // 4

    def pieces(self, refs, owner, half, quarter):
        rows, columns = self.block
        if self.kind == "rows":
            base = owner * self.rows + quarter * (self.rows // 4) + half * rows
            return [(refs[0].at[pl.ds(pl.multiple_of(base, 16), rows)], 0, columns)]
        at = pl.ds(pl.multiple_of(owner * self.rows + half * rows, 16), rows)
        if self.kind == "four":
            return [(refs[quarter].at[at], 0, columns)]
        width = columns // 2
        cut = slice(quarter * width, (quarter + 1) * width)
        return [(refs[index].at[at, cut], index * width, width) for index in range(2)]

    def out_shape(self):
        if self.exchange:
            return jax.ShapeDtypeStruct((4, self.part_rows, self.part_columns), F32)
        return jax.ShapeDtypeStruct((self.rows, self.block[1]), F32)

    def total_shape(self, line):
        return (line, 2) + self.block

    def plane_scratch(self, line):
        rows, columns = self.block
        dma = pltpu.SemaphoreType.DMA
        return [
            pltpu.VMEM((line, 8, rows, columns), BF16),
            pltpu.VMEM((line, 8, rows, columns), BF16),
            pltpu.VMEM((line, 2, 2, rows, columns), BF16),
            pltpu.VMEM((line, 2, rows, columns), BF16),
            dma((line,)),
            dma((2, line)),
            dma((2, line, 2)),
            dma((2, line, 2)),
        ]

    def line_scratch(self, line):
        dma = pltpu.SemaphoreType.DMA
        return [
            pltpu.VMEM(self.total_shape(line), BF16),
            pltpu.VMEM((2,) + self.total_shape(line), BF16),
            pltpu.VMEM((4, self.part_rows, self.part_columns), BF16),
            pltpu.VMEM((4, self.part_rows, self.part_columns), BF16),
            dma((1,)),
            dma((2, 2, line)),
            dma((2, 3)),
        ]


PLANE_SCRATCH = 8
LINE_SCRATCH = 7


def reduce_order(line):
    return [line - 1, 0] + list(range(line - 2, 0, -1))


def added(left, right):
    return (left.astype(F32) + right.astype(F32)).astype(BF16)


def plane_steps(place, shape, refs, total, scratch):
    own, other, first_in, second_in, load_sem, pair_sem, first_sem, second_sem = scratch
    near = (place.x, place.y)
    far = (place.y, place.x)
    near_device = (place.at_x(), place.at_y())
    far_device = (place.at_y(), place.at_x())

    def quarter_of(half, index):
        high, low = index // 2, index % 2
        return low * 2 + high if half == 0 else high * 2 + low

    def start(z):
        for half in range(2):
            for index in range(4):
                quarter = quarter_of(half, index)
                slot = half * 4 + index
                mine = shape.pieces(refs, 2 * z + place.core, half, quarter)
                theirs = shape.pieces(refs, 2 * z + 1 - place.core, half, quarter)
                for (view, column, width), (view_two, _, _) in zip(mine, theirs):
                    cut = pl.ds(column, width)
                    remote(
                        view_two,
                        other.at[z, slot, :, cut],
                        pair_sem.at[0, z],
                        pair_sem.at[1, z],
                        place.at_partner(),
                    ).start()
                    pltpu.make_async_copy(
                        view, own.at[z, slot, :, cut], load_sem.at[z]
                    ).start()

    def pair_all(z):
        return remote(
            own.at[z], other.at[z], pair_sem.at[0, z], pair_sem.at[1, z], place.at_partner()
        )

    def first(z, half):
        return remote(
            own.at[z, pl.ds(half * 4 + (1 - near[half]) * 2, 2)],
            first_in.at[z, half],
            first_sem.at[0, z, half],
            first_sem.at[1, z, half],
            near_device[half],
        )

    def second(z, half):
        return remote(
            own.at[z, half * 4 + near[half] * 2 + 1 - far[half]],
            second_in.at[z, half],
            second_sem.at[0, z, half],
            second_sem.at[1, z, half],
            far_device[half],
        )

    def pair_add(z):
        pltpu.make_async_copy(own.at[z], own.at[z], load_sem.at[z]).wait()
        pair_all(z).wait_recv()

        @pl.loop(0, 8)
        def _(slot):
            own[z, slot] = added(own[z, slot], other[z, slot])

        for half in range(2):
            first(z, half).start()

    def first_add(z):
        for half in range(2):
            first(z, half).wait_recv()
            base = half * 4 + near[half] * 2

            @pl.loop(0, 2)
            def _(index):
                own[z, base + index] = added(own[z, base + index], first_in[z, half, index])

            second(z, half).start()

    def second_add(z):
        for half in range(2):
            second(z, half).wait_recv()
            mine = half * 4 + near[half] * 2 + far[half]
            total[z, half] = added(own[z, mine], second_in[z, half])

    def drain(z):
        pair_all(z).wait_send()
        for half in range(2):
            first(z, half).wait_send()
            second(z, half).wait_send()

    return start, pair_add, first_add, second_add, drain


def line_steps(place, shape, source, out, scratch):
    total, line_in, parts, gathered, load_sem, line_sem, swap_sem = scratch
    line = place.line

    def load():
        return pltpu.make_async_copy(source, total, load_sem.at[0])

    def along(z, side):
        return remote(
            total.at[z],
            line_in.at[side, z],
            line_sem.at[0, side, z],
            line_sem.at[1, side, z],
            place.at_line(side),
        )

    def line_send(z, side):
        ahead = place.z < z if side == 0 else place.z > z

        @pl.when(ahead)
        def _():
            @pl.when(place.has_last(side))
            def _():
                along(z, side).wait_recv()

                @pl.loop(0, 2)
                def _(half):
                    total[z, half] = added(total[z, half], line_in[side, z, half])

            along(z, side).start()

    def line_end(z):
        @pl.when(place.z == z)
        def _():
            for side in range(2):
                pl.when(place.has_last(side))(lambda: along(z, side).wait_recv())

    def swap(rep_slot, device, index):
        return remote(
            parts.at[rep_slot],
            gathered.at[place.rep],
            swap_sem.at[0, index],
            swap_sem.at[1, index],
            device,
        )

    def swaps():
        corner = 3 - place.rep
        return [
            swap(place.x_rep, place.at_x(), 0),
            swap(place.y_rep, place.at_y(), 1),
            swap(corner, {"rep": corner, "fsdp": place.fsdp}, 2),
        ]

    def finish():
        rows, columns = shape.block
        me = place.z
        for half in range(2):
            result = total[me, half].astype(F32)
            for side in range(2):
                extra = line_in[side, me, half].astype(F32)
                result = result + jnp.where(place.has_last(side), extra, 0.0)
            at = slice(half * rows, (half + 1) * rows)
            if shape.exchange:
                width = shape.part_columns
                for index in range(4):
                    part = result[:, index * width : (index + 1) * width]
                    parts[index, at, :] = part.astype(BF16)
            else:
                out[at, :] = result
        if shape.exchange:
            for copy in swaps():
                copy.start()
            gathered[place.rep] = parts[place.rep]

    def head(z):
        if z > 0:
            pl.when(place.z == 0)(functools.partial(line_send, z, 0))
        if z < line - 1:
            pl.when(place.z == line - 1)(functools.partial(line_send, z, 1))

    def relay(hop, far):
        up = [line - 1] if far else range(line - 2, hop, -1)
        down = [0] if far else range(1, line - 1 - hop)
        for z in up:
            pl.when(place.z == hop)(functools.partial(line_send, z, 0))
        for z in down:
            pl.when(place.z == line - 1 - hop)(functools.partial(line_send, z, 1))

    def close():
        for z in range(line):
            line_end(z)
        finish()

    def drain():
        if shape.exchange:
            for copy in swaps():
                copy.wait()
            out[...] = gathered[...].astype(F32)
        for z in range(line):
            for side in range(2):
                ahead = place.z < z if side == 0 else place.z > z
                pl.when(ahead)(lambda: along(z, side).wait_send())

    return load, head, relay, close, drain


class VectorSum:
    def __init__(self, place, source, out, scratch):
        self.place = place
        self.source = source
        self.out = out
        self.current, self.incoming, self.sems = scratch
        side = place.z % 2
        near = place.fsdp + 2 - 4 * side
        self.devices = [
            place.at_partner(),
            place.at_x(),
            place.at_y(),
            {"rep": place.rep, "fsdp": near},
            place.at_far(),
        ]

    @staticmethod
    def scratch(shape):
        return [
            pltpu.VMEM((6,) + shape, F32),
            pltpu.VMEM((5,) + shape, F32),
            pltpu.SemaphoreType.DMA((2, 5)),
        ]

    def copy(self, index):
        return remote(
            self.current.at[index],
            self.incoming.at[index],
            self.sems.at[0, index],
            self.sems.at[1, index],
            self.devices[index],
        )

    def round(self, index):
        if index == 0:
            self.current[0] = self.source[...]
        else:
            self.copy(index - 1).wait_recv()
            self.current[index] = self.current[index - 1] + self.incoming[index - 1]
        if index < 5:
            self.copy(index).start()

    def finish(self):
        self.out[...] = self.current[5]
        for index in range(5):
            self.copy(index).wait_send()


def carried_kernel(shape, line, steps, inner, inputs, outputs, *refs):
    split = inputs + shape.sources
    local, sources = refs[:inputs], refs[inputs:split]
    outs = refs[split : split + outputs]
    total = refs[split + outputs]
    own = len(refs) - PLANE_SCRATCH
    place = Place(line)
    order = reduce_order(line)
    start, pair_add, first_add, second_add, drain = plane_steps(
        place, shape, sources, total, refs[own:]
    )
    step = pl.program_id(0) * pl.num_programs(1) + pl.program_id(1)

    @pl.when(step == 0)
    def _():
        place.greet()
        for z in order:
            start(z)

    @pl.when(step == 1)
    def _():
        for z in order:
            pair_add(z)

    for index, z in enumerate(order):
        pl.when(step == min(3 + 2 * index - index // 2, steps - 1))(
            functools.partial(first_add, z)
        )
    inner(*local, *outs, *refs[split + outputs + 1 : own])

    @pl.when(step == steps - 1)
    def _():
        for z in order:
            second_add(z)
        for z in order:
            drain(z)


def reduce_kernel(ready_shapes, shape, line, *refs):
    count = shape.sources
    many = len(ready_shapes)
    ready, sources = refs[:many], refs[many : many + count]
    vector_ref = refs[many + count]
    at = many + count + 1
    ready_outs, out, vector_out = refs[at : at + many], refs[at + many], refs[at + many + 1]
    scratch = refs[at + many + 2 :]
    place = Place(line)
    place.greet(wide=True)
    order = reduce_order(line)
    plans = []
    for index, ready_shape in enumerate(ready_shapes):
        own, scratch = scratch[:LINE_SCRATCH], scratch[LINE_SCRATCH:]
        plans.append(line_steps(place, ready_shape, ready[index], ready_outs[index], own))
    line_scratch, scratch = scratch[:LINE_SCRATCH], scratch[LINE_SCRATCH:]
    plane_scratch, scratch = scratch[:PLANE_SCRATCH], scratch[PLANE_SCRATCH:]
    start, pair_add, first_add, second_add, drain = plane_steps(
        place, shape, sources, line_scratch[0], plane_scratch
    )
    _, head, relay, close, line_drain = line_steps(place, shape, None, out, line_scratch)
    vector = VectorSum(place, vector_ref, vector_out, scratch)
    for z in order:
        start(z)
    for load, *_ in plans:
        load().start()
    vector.round(0)
    pair_add(order[0])
    for load, *_ in plans:
        load().wait()
    for z in order:
        for _, ready_head, *_ in plans:
            ready_head(z)
    for z in order[1:]:
        pair_add(z)
    vector.round(1)
    for z in order[:2]:
        first_add(z)
    for _, _, ready_relay, *_ in plans:
        ready_relay(1, True)
    vector.round(2)
    for z in order[2:]:
        first_add(z)
    for hop in range(2, line - 1):
        for _, _, ready_relay, *_ in plans:
            ready_relay(hop, True)
    for hop in range(1, line - 1):
        for _, _, ready_relay, *_ in plans:
            ready_relay(hop, False)
    vector.round(3)
    for z in order:
        second_add(z)
        head(z)
    relay(1, True)
    for _, _, _, ready_close, _ in plans:
        ready_close()
    for hop in range(2, line - 1):
        relay(hop, True)
    for hop in range(1, line - 1):
        relay(hop, False)
    vector.round(4)
    for *_, ready_drain in plans:
        ready_drain()
    close()
    vector.round(5)
    line_drain()
    for z in order:
        drain(z)
    vector.finish()


def group_shape(group, kind, line):
    rows, columns = group[0].shape
    return ReduceShape(kind, rows // (2 * line), columns, len(group))


def fast_reduce(ready, ready_shapes, group, line, collective_id, vector):
    shape = group_shape(group, "four", line)
    anywhere = pl.BlockSpec(memory_space=pl.ANY)
    local = pl.BlockSpec(memory_space=pltpu.VMEM)
    shapes = ready_shapes + [shape]
    scratch = []
    for item in shapes:
        scratch.extend(item.line_scratch(line))
    return pl.pallas_call(
        functools.partial(reduce_kernel, ready_shapes, shape, line),
        in_specs=[anywhere] * (len(ready) + len(group)) + [local],
        out_specs=[local] * (len(shapes) + 1),
        out_shape=[item.out_shape() for item in shapes]
        + [jax.ShapeDtypeStruct(vector.shape, F32)],
        scratch_shapes=scratch
        + shape.plane_scratch(line)
        + VectorSum.scratch(vector.shape),
        compiler_params=pltpu.CompilerParams(
            collective_id=collective_id, has_side_effects=True, vmem_limit_bytes=60 << 20
        ),
        name="fast_reduce",
    )(*ready, *group, vector)


PLANE = 4
CHIP = 2
LINE = 4


def small_plane():
    return lax.axis_size("rep") == PLANE and lax.axis_size("fsdp") == CHIP * LINE


def gather(block):
    return lax.all_gather(block, "fsdp", axis=0, tiled=True)


def gather_all(groups, by_rows, collective_id):
    if small_plane():
        return fast_gather(groups, LINE, by_rows, collective_id)
    return [gather(jnp.concatenate(group, axis=1)) for group in groups]


def scatter(block):
    return lax.psum_scatter(block.astype(BF16), "fsdp", scatter_dimension=0, tiled=True)


def column_blocks(block):
    rows = block.shape[0]
    return block.reshape(rows, lax.axis_size("rep"), -1).swapaxes(0, 1)


def scatter_columns(parts):
    count = lax.axis_size("rep")
    rows = parts[0].shape[0]
    split = [part.reshape(rows, count, -1) for part in parts]
    joined = jnp.concatenate(split, axis=2).reshape(rows, -1)
    own = lax.psum_scatter(joined, "rep", scatter_dimension=1, tiled=True)
    sizes = [part.shape[1] // count for part in parts]
    outs = []
    start = 0
    for size in sizes:
        outs.append(own[:, start : start + size].astype(F32))
        start += size
    return outs


def scatter_last(down, cross, group, vector, collective_id):
    down_term, down_sums = down
    cross_group, cross_sums = cross
    if small_plane():
        shapes = [
            group_shape(cross_group, "four", LINE),
            group_shape([down_term], "rows", LINE),
        ]
        cross_out, down_out, group_out, total = fast_reduce(
            [cross_sums[0], down_sums[0]], shapes, group, LINE, collective_id, vector
        )
        outs = [[out[index] for index in range(4)] for out in (cross_out, group_out)]
        return down_out.reshape(-1, down_out.shape[2]), outs, total
    (down_out,) = scatter_columns([scatter(down_term)])
    outs = [scatter_columns([scatter(item) for item in part]) for part in (cross_group, group)]
    return down_out, outs, lax.psum(vector, ("rep", "fsdp"))


def body(
    tokens,
    memory,
    prefix_len,
    bucket_table,
    rel_bias,
    gain_self,
    self_query,
    self_key,
    self_value,
    self_out,
    gain_cross,
    cross_query,
    cross_key,
    cross_value,
    cross_out,
    gain_feed,
    gate_weight,
    up_weight,
    down_weight,
    out_grad,
):
    nseq, length, width = tokens.shape
    shard = gain_self.shape[0]
    groups = width // shard
    entries = rel_bias.shape[0]
    small = jnp.stack(
        [gain_self, gain_cross, gain_feed, jnp.pad(rel_bias, (0, shard - entries))], axis=1
    )
    small = jnp.pad(small, ((0, 0), (0, 2 * LANES - 4)))
    first, second, down = gather_all(
        [
            [self_query, self_key, self_value, small],
            [self_out, cross_query, cross_key, cross_value, cross_out, small],
            [down_weight],
        ],
        [False, False, True],
        1,
    )
    gate_up_own = jnp.concatenate([gate_weight, up_weight], axis=1)
    gate_up_own, first, second, down = lax.optimization_barrier(
        (gate_up_own, first, second, down)
    )
    gate_up = gather(gate_up_own)
    qkv_proj = first[:, : 3 * width]
    picks = jnp.eye(8, LANES, dtype=BF16)
    vectors = back_term(picks, first[:, 3 * width : 3 * width + LANES])
    gain_first = vectors[0:1]
    gain_second = vectors[1:2]
    gain_third = vectors[2:3]
    table = vectors[3].astype(BF16).reshape(groups, shard)[:, :entries]
    table = table.reshape(NHEAD, BUCKETS)
    out_self = second[:, :width]
    query_cross = second[:, width : 2 * width]
    kv_cross = second[:, 2 * width : 4 * width]

    buckets_back = jnp.pad(bucket_table[::-1], (0, 1)).reshape(1, 2 * length)
    bias = skewed_bias(table, buckets_back, length)

    rows = nseq * length
    start_rows = tokens.reshape(rows, width).astype(F32)
    memory_rows = memory.reshape(-1, width)
    upstream = out_grad.reshape(rows, width)

    scale_first = inverse_rms(start_rows)
    normed_first = (start_rows * scale_first * gain_first).astype(BF16)
    qkv = matmul(normed_first, qkv_proj).astype(BF16)
    context, lse_self = run_self_forward(prefix_len, qkv, bias, nseq)
    middle = start_rows + matmul(context, out_self)
    scale_second = inverse_rms(middle)
    normed_second = (middle * scale_second * gain_second).astype(BF16)
    query_two = matmul(normed_second, query_cross).astype(BF16)
    kv_two = matmul(memory_rows, kv_cross).astype(BF16)
    context_two, lse_cross = run_cross_forward(query_two, kv_two, nseq)
    (
        result,
        later_grad,
        branch_two,
        context_two_grad,
        gain_third_grad,
        down_term,
        pair_term,
    ) = run_feed(middle, context_two, second, 4, gain_third, upstream, gate_up, down)
    carries = small_plane()
    pair_own = scatter(pair_term)
    query_two_grad, key_two_grad, value_two_grad, *down_sums = run_cross_backward(
        query_two,
        kv_two,
        context_two_grad,
        context_two,
        lse_cross,
        nseq,
        ([down_term], "rows", 4) if carries else None,
    )
    (
        middle_grad,
        gain_second_grad,
        query_term,
        out_term,
        branch_one,
        context_grad,
    ) = run_close(
        middle,
        later_grad,
        gain_second,
        context_two,
        branch_two,
        [query_two_grad],
        [(second, 1)],
        (second, 0),
        "cross_close",
    )
    memory_grad, key_term, value_term = run_memory(
        memory_rows, key_two_grad, value_two_grad, second, 2, 3
    )
    cross_terms = [query_term, key_term, value_term, out_term]
    query_grad, key_grad, value_grad, diagonal, *cross_sums = run_self_backward(
        prefix_len,
        qkv,
        context_grad,
        context,
        lse_self,
        bias,
        nseq,
        (cross_terms, "four", 2) if carries else None,
    )
    pair_split, query_grad = lax.optimization_barrier((column_blocks(pair_own), query_grad))
    tokens_grad, gain_first_grad, *self_terms = run_close(
        tokens.reshape(rows, width),
        middle_grad,
        gain_first,
        context,
        branch_one,
        [query_grad, key_grad, value_grad],
        [(first, 0), (first, 1), (first, 2)],
        None,
        "self_close",
    )

    onehot = (
        buckets_back.reshape(-1, 1) == jnp.arange(BUCKETS, dtype=jnp.int32)[None, :]
    ).astype(F32)
    onehot = onehot * (jnp.arange(2 * length) < 2 * length - 1)[:, None]
    bias_grad = jnp.dot(
        diagonal.reshape(NHEAD, 2 * length), onehot, precision=lax.Precision.HIGHEST
    )
    bias_rows = jnp.pad(
        bias_grad.reshape(groups, entries), ((0, 0), (0, shard - entries))
    ).reshape(width)
    vector_block = jnp.pad(
        jnp.concatenate(
            [gain_first_grad, gain_second_grad, gain_third_grad, bias_rows[None]], axis=0
        ),
        ((0, 4), (0, 0)),
    )
    pair_grad = lax.psum_scatter(pair_split, "rep").astype(F32)
    pieces = [
        pair_grad[:, start : start + FEED_BLOCK]
        for start in range(0, pair_grad.shape[1], FEED_BLOCK)
    ]
    gate_weight_grad = jnp.concatenate(pieces[0::2], axis=1)
    up_weight_grad = jnp.concatenate(pieces[1::2], axis=1)
    down_weight_grad, (cross_out_grads, self_out_grads), totals = scatter_last(
        (down_term, down_sums), (cross_terms, cross_sums), self_terms, vector_block, 3
    )
    own = lax.dynamic_slice(
        totals, (0, lax.axis_index("fsdp") * shard), (totals.shape[0], shard)
    )
    return (
        result.reshape(tokens.shape),
        tokens_grad.reshape(tokens.shape),
        memory_grad.reshape(memory.shape),
        own[3, :entries],
        own[0],
        *self_out_grads,
        own[1],
        *cross_out_grads,
        own[2],
        gate_weight_grad,
        up_weight_grad,
        down_weight_grad,
    )


def solution(mesh):
    batch = P(("rep", "fsdp"), None, None)
    matrix = P("fsdp", None)
    vector = P("fsdp")
    split = P("fsdp", "rep")
    in_specs = (
        (batch, batch, P(("rep", "fsdp")), P(), vector, vector)
        + (matrix,) * 4
        + (vector,)
        + (matrix,) * 4
        + (vector,)
        + (matrix,) * 3
        + (batch,)
    )
    out_specs = (
        (batch, batch, batch, vector, vector)
        + (split,) * 4
        + (vector,)
        + (split,) * 4
        + (vector,)
        + (split,) * 3
    )
    return jax.shard_map(body, mesh=mesh, in_specs=in_specs, out_specs=out_specs, check_vma=False)
```
